32 devices in a mesh: dp: 8 (over y, x, core), tensor: 4 (over z).
Axes of the slice: x: 2, y: 2, z: 4, core: 2. Of those that a mesh axis runs over, the one named last changes fastest.
Arguments:
- inputs: bfloat16 [16, 1024, 1024], P('dp', 'tensor'), may hold values from -6 to 6
- lengths: int32 [16], P('dp'), may hold values from 256 to 1024, as said below
- w_query: bfloat16 [1024, 1024], P('dp', 'tensor'), may hold values from -0.1875 to 0.1875
- w_key: bfloat16 [1024, 1024], P('dp', 'tensor'), may hold values from -0.1875 to 0.1875
- w_value: bfloat16 [1024, 1024], P('dp', 'tensor'), may hold values from -0.1875 to 0.1875
- b_query: bfloat16 [1024], P('tensor'), may hold values from -3 to 3
- b_value: bfloat16 [1024], P('tensor'), may hold values from -0.29882812 to 0.29882812
- w_out: bfloat16 [1024, 1024], P('tensor', 'dp'), may hold values from -1.5 to 1.5
- b_out: bfloat16 [1024], replicated, may hold values from -3 to 3
- gain_one: bfloat16 [1024], replicated, may hold values from 0.099609375 to 1.8984375
- shift_one: bfloat16 [1024], replicated, may hold values from -3 to 3
- w_in: bfloat16 [1024, 4096], P('dp', 'tensor'), may hold values from -0.1875 to 0.1875
- b_in: bfloat16 [4096], P('tensor'), may hold values from -3 to 3
- w_back: bfloat16 [4096, 1024], P('tensor', 'dp'), may hold values from -0.09375 to 0.09375
- b_back: bfloat16 [1024], replicated, may hold values from -3 to 3
- gain_two: bfloat16 [1024], replicated, may hold values from 0.099609375 to 1.8984375
- shift_two: bfloat16 [1024], replicated, may hold values from -3 to 3
- cotangent: bfloat16 [16, 1024, 1024], P('dp', 'tensor'), may hold values from -6 to 6
Outputs:
- layer_out: bfloat16 [16, 1024, 1024], P('dp', 'tensor')
- grad_inputs: float32 [16, 1024, 1024], P('dp', 'tensor')
- grad_w_query: float32 [1024, 1024], P('dp', 'tensor')
- grad_w_key: float32 [1024, 1024], P('dp', 'tensor')
- grad_w_value: float32 [1024, 1024], P('dp', 'tensor')
- grad_b_query: float32 [1024], P('tensor')
- grad_b_value: float32 [1024], P('tensor')
- grad_w_out: float32 [1024, 1024], P('tensor', 'dp')
- grad_b_out: float32 [1024], replicated
- grad_gain_one: float32 [1024], replicated
- grad_shift_one: float32 [1024], replicated
- grad_w_in: float32 [1024, 4096], P('dp', 'tensor')
- grad_b_in: float32 [4096], P('tensor')
- grad_w_back: float32 [4096, 1024], P('tensor', 'dp')
- grad_b_back: float32 [1024], replicated
- grad_gain_two: float32 [1024], replicated
- grad_shift_two: float32 [1024], replicated
The draws below stay inside these ranges and needn't reach their ends.
Inputs may be any that keep to these rules, and one draw needn't show every extreme that they name: The first lengths[s] slots of sequence s are real tokens; one sequence has 1024 and another 1024 // 4.
All inputs are finite; a program needn't handle non-finite values.
Results may differ from the reference program's by a relative error of at most 0.015.
The reference program's roundings to bfloat16 on the way count: a program that leaves them out, or rounds other values in their place, can miss the bound.
Values may be sent and summed in bfloat16 or wider, within the bound.
A program may use at most 192 MiB of HBM per device.

```python
import jax
import jax.numpy as jnp
from jax import lax

D = 1024
HEADS = 16
HD = 64
FF = 4096
SLOTS = 1024
SEQS = 16


def draw_lengths(key, part):
    key_draw, key_long, key_short = jax.random.split(key, 3)
    values = jax.random.randint(key_draw, (SEQS,), SLOTS // 4, SLOTS + 1)
    longest = jax.random.randint(key_long, (), 0, SEQS)
    shortest = (longest + 1 + jax.random.randint(key_short, (), 0, SEQS - 1)) % SEQS
    values = values.at[longest].set(SLOTS)
    values = values.at[shortest].set(SLOTS // 4)
    return values.astype(jnp.int32)


def with_spikes(values, stream_key, source, target, shards_of, factor):
    def block_of(dim):
        return (jnp.arange(values.shape[dim]) // (values.shape[dim] // shards_of)).reshape((-1,) + (1,) * (values.ndim - 1 - dim))

    first = jax.random.permutation(stream_key, shards_of)[block_of(target)]
    other_side = (block_of(target) + shards_of // 2) % shards_of
    return jnp.where((block_of(source) == first) | (block_of(source) == other_side), factor * values, values)


def shard_levels(own_key, extent, pieces, smallest, high):
    loudness = 1.0
    for axis_at, shards_of in pieces:
        draws = jax.random.uniform(jax.random.fold_in(jax.random.fold_in(own_key, 6), axis_at), (shards_of,), jnp.float32, smallest / len(pieces), high / len(pieces))
        loudness = loudness * jnp.repeat(jnp.exp(draws), extent[axis_at] // shards_of).reshape((-1,) + (1,) * (len(extent) - 1 - axis_at))
    return loudness


def normal_values(own_key, shape, spread, bound, cuts=(), dtype=jnp.bfloat16):
    values = spread * jax.random.normal(own_key, shape, jnp.float32)
    if cuts:
        values = values * shard_levels(own_key, shape, cuts, -0.22, 0.18)
    return jnp.clip(values, -bound, bound).astype(dtype)


def gaussian_with(own_key, extent, spread, reach, shards, heavy, kind=jnp.bfloat16):
    values = spread * jax.random.normal(own_key, extent, jnp.float32)
    if shards:
        values = values * shard_levels(own_key, extent, shards, -0.22, 0.18)
    return jnp.clip(with_spikes(values, jax.random.fold_in(own_key, 3), *heavy), -reach, reach).astype(kind)


def setup_inputs(seed: int = 0) -> dict:
    streams_of = jax.random.split(jax.random.key(seed), 19)
    return {
        "inputs": gaussian_with(streams_of[0], (SEQS, SLOTS, D), 1.0, 6.0, ((0, 8), (1, 4)), (0, 2, 8, 2.0)),
        "lengths": draw_lengths(jax.random.fold_in(streams_of[18], 71), 0),
        "w_query": normal_values(streams_of[2], (D, D), D ** -0.5, 0.1875, ((0, 8), (1, 4))),
        "w_key": normal_values(streams_of[3], (D, D), D ** -0.5, 0.1875, ((0, 8), (1, 4))),
        "w_value": normal_values(streams_of[4], (D, D), D ** -0.5, 0.1875, ((0, 8), (1, 4))),
        "b_query": normal_values(streams_of[5], (D,), 0.5, 3.0, ((0, 4),)),
        "b_value": normal_values(streams_of[6], (D,), 0.05, 0.29882812, ((0, 4),)),
        "w_out": normal_values(streams_of[7], (D, D), (D // 64) ** -0.5, 1.5, ((0, 4), (1, 8))),
        "b_out": normal_values(streams_of[8], (D,), 0.5, 3.0),
        "gain_one": jnp.clip(1.0 + 0.18 * jax.random.normal(streams_of[9], (D,), jnp.float32), 0.099609375, 1.8984375).astype(jnp.bfloat16),
        "shift_one": normal_values(streams_of[10], (D,), 0.5, 3.0),
        "w_in": normal_values(streams_of[11], (D, FF), D ** -0.5, 0.1875, ((0, 8), (1, 4))),
        "b_in": normal_values(streams_of[12], (FF,), 0.5, 3.0, ((0, 4),)),
        "w_back": normal_values(streams_of[13], (FF, D), FF ** -0.5, 0.09375, ((0, 4), (1, 8))),
        "b_back": normal_values(streams_of[14], (D,), 0.5, 3.0),
        "gain_two": jnp.clip(1.0 + 0.18 * jax.random.normal(streams_of[15], (D,), jnp.float32), 0.099609375, 1.8984375).astype(jnp.bfloat16),
        "shift_two": normal_values(streams_of[16], (D,), 0.5, 3.0),
        "cotangent": gaussian_with(streams_of[17], (SEQS, SLOTS, D), 1.0, 6.0, ((0, 8), (1, 4)), (0, 2, 8, 2.0)),
    }


EPSILON = 1e-05
NEGATIVE = -1e+30
HIGHEST = lax.Precision.HIGHEST

@jax.custom_vjp
def low(v):
    return lax.optimization_barrier(v.astype(jnp.bfloat16)).astype(jnp.float32)

@jax.custom_vjp
def low_back(v):
    return v

def low_keep(v):
    return (low(v), None)

def low_pass(kept, grad):
    return (grad,)

def back_keep(v):
    return (v, None)

def back_low(kept, grad):
    return (low(grad),)
low.defvjp(low_keep, low_pass)
low_back.defvjp(back_keep, back_low)

def norm_rows(values, norm_gain, norm_shift):
    average = lax.optimization_barrier(jnp.mean(values, axis=-1, keepdims=True))
    centered = values - average
    variance = lax.optimization_barrier(jnp.mean(centered * centered, axis=-1, keepdims=True))
    return centered * lax.rsqrt(variance + EPSILON) * norm_gain + norm_shift

def layer_sequence(inputs, length, params):
    w_query, w_key, w_value, b_query, b_value, w_out, b_out, gain_one, shift_one, w_in, b_in, w_back, b_back, gain_two, shift_two = params
    slots = inputs.shape[0]
    key_valid = jnp.arange(slots) < length
    query_scale = HD ** (-0.5)
    query_rows = low_back(low((jnp.dot(inputs, w_query, precision=HIGHEST) + b_query) * query_scale))
    key_rows = low_back(low(jnp.dot(inputs, w_key, precision=HIGHEST)))
    value_rows = low_back(low(jnp.dot(inputs, w_value, precision=HIGHEST) + b_value))
    query_heads = query_rows.reshape(slots, HEADS, HD)
    key_heads = key_rows.reshape(slots, HEADS, HD)
    value_heads = value_rows.reshape(slots, HEADS, HD)
    scores = low_back(jnp.einsum('qhd,khd->hqk', query_heads, key_heads, precision=HIGHEST))
    scores = jnp.where(key_valid[None, None, :], scores, NEGATIVE)
    chances = low(jax.nn.softmax(scores, axis=-1))
    context = jnp.einsum('hqk,khd->qhd', chances, value_heads, precision=HIGHEST).reshape(slots, D)
    context = low_back(low(context))
    attended = low_back(jnp.dot(context, w_out, precision=HIGHEST))
    first_norm = norm_rows(inputs + attended + b_out, gain_one, shift_one)
    pre_act = low_back(jnp.dot(low(first_norm), w_in, precision=HIGHEST) + b_in)
    hidden = low(jax.nn.gelu(pre_act, approximate=False))
    mixed_rows = low_back(jnp.dot(hidden, w_back, precision=HIGHEST))
    second = norm_rows(first_norm + mixed_rows + b_back, gain_two, shift_two)
    return jnp.where(key_valid[:, None], second, 0.0)

def reference(inputs, lengths, w_query, w_key, w_value, b_query, b_value, w_out, b_out, gain_one, shift_one, w_in, b_in, w_back, b_back, gain_two, shift_two, cotangent):
    params = tuple((weight_arg.astype(jnp.float32) for weight_arg in (w_query, w_key, w_value, b_query, b_value, w_out, b_out, gain_one, shift_one, w_in, b_in, w_back, b_back, gain_two, shift_two)))

    def forward(activations, weights):

        def one_sequence(sequence_pair):
            return layer_sequence(sequence_pair[0], sequence_pair[1], weights)
        return lax.map(jax.checkpoint(one_sequence), (activations, lengths))
    layer_out, pullback = jax.vjp(forward, inputs.astype(jnp.float32), params)
    grad_inputs, weight_grads = pullback(cotangent.astype(jnp.float32))
    return (layer_out.astype(jnp.bfloat16), grad_inputs, weight_grads[0], weight_grads[1], weight_grads[2], weight_grads[3], weight_grads[4], weight_grads[5], weight_grads[6], weight_grads[7], weight_grads[8], weight_grads[9], weight_grads[10], weight_grads[11], weight_grads[12], weight_grads[13], weight_grads[14])
```

```python
import jax
import jax.numpy as jnp
from jax import lax
from jax.experimental import pallas as pl
from jax.experimental.pallas import tpu as pltpu
from jax.sharding import Mesh, PartitionSpec as P

HD = 64
EPSILON = 1e-05
NEGATIVE = -1e30
f32 = jnp.float32
bf16 = jnp.bfloat16
SWAP = [(0, 1), (1, 0)]


def nt(a, b):
    return lax.dot_general(a, b, (((1,), (1,)), ((), ())), preferred_element_type=f32)


def tn(a, b):
    return lax.dot_general(a, b, (((0,), (0,)), ((), ())), preferred_element_type=f32)


def nn(a, b):
    return lax.dot_general(a, b, (((1,), (0,)), ((), ())), preferred_element_type=f32)


def attend_fwd_kernel(block, qkv_ref, kb_ref, ctx_ref, lse_ref):
    rows = qkv_ref.shape[0]
    lane = lax.broadcasted_iota(jnp.int32, (1, 2 * HD), 1)
    keys = qkv_ref[:, 2 * HD : 4 * HD]
    values_t = qkv_ref[:, 4 * HD : 6 * HD].T
    key_bias = kb_ref[...]
    for start in range(0, rows, block):
        query = qkv_ref[start : start + block, 0 : 2 * HD]
        parts = []
        for h in range(2):
            query_h = jnp.where(lane // HD == h, query, jnp.zeros_like(query))
            scores = nt(keys, query_h) + key_bias
            largest = jnp.max(scores, axis=0, keepdims=True)
            weights = jnp.exp(scores - largest)
            total = jnp.sum(weights, axis=0, keepdims=True)
            part = nn(values_t[h * HD : (h + 1) * HD], weights.astype(bf16))
            parts.append(part / total)
            lse_ref[0, h : h + 1, start : start + block] = largest + jnp.log(total)
        ctx_ref[start : start + block, :] = jnp.concatenate(parts, axis=0).T.astype(bf16)


def attend_fwd(qkv, key_bias):
    rows = qkv.shape[0]
    groups = qkv.shape[1] // (6 * HD)
    block = min(512, rows)
    return pl.pallas_call(
        lambda *refs: attend_fwd_kernel(block, *refs),
        grid=(groups,),
        in_specs=[
            pl.BlockSpec((rows, 6 * HD), lambda j: (0, j)),
            pl.BlockSpec((rows, 1), lambda j: (0, 0)),
        ],
        out_specs=[
            pl.BlockSpec((rows, 2 * HD), lambda j: (0, j)),
            pl.BlockSpec((1, 2, rows), lambda j: (j, 0, 0)),
        ],
        out_shape=[
            jax.ShapeDtypeStruct((rows, groups * 2 * HD), bf16),
            jax.ShapeDtypeStruct((groups, 2, rows), f32),
        ],
        compiler_params=pltpu.CompilerParams(vmem_limit_bytes=48 << 20),
        cost_estimate=pl.CostEstimate(
            flops=groups * 8 * rows * rows * HD * 4,
            bytes_accessed=rows * groups * 8 * HD * 2,
            transcendentals=groups * 2 * rows * rows,
        ),
        name="attend_fwd",
    )(qkv, key_bias)


def attend_bwd_kernel(block, qkv_ref, g_ref, lse_ref, kb_ref, d_ref, dk_acc, dv_acc):
    rows = qkv_ref.shape[0]
    lane = lax.broadcasted_iota(jnp.int32, (1, 2 * HD), 1)
    keys = qkv_ref[:, 2 * HD : 4 * HD]
    keys_t = keys.T
    values = qkv_ref[:, 4 * HD : 6 * HD]
    key_bias = kb_ref[...]
    for start in range(0, rows, block):
        query = qkv_ref[start : start + block, 0 : 2 * HD]
        grad = g_ref[start : start + block, :]
        parts = []
        for h in range(2):
            here = lane // HD == h
            query_h = jnp.where(here, query, jnp.zeros_like(query))
            grad_h = jnp.where(here, grad, jnp.zeros_like(grad))
            scores = nt(keys, query_h) + key_bias
            chances = jnp.exp(scores - lse_ref[0, h : h + 1, start : start + block])
            grad_chances = nt(values, grad_h)
            inner = jnp.sum(chances * grad_chances, axis=0, keepdims=True)
            grad_scores = (chances * (grad_chances - inner)).astype(bf16)
            dv = nn(chances.astype(bf16), grad_h)
            dk = nn(grad_scores, query_h)
            if start == 0 and h == 0:
                dv_acc[...] = dv
                dk_acc[...] = dk
            else:
                dv_acc[...] += dv
                dk_acc[...] += dk
            parts.append(nn(keys_t[h * HD : (h + 1) * HD], grad_scores))
        d_ref[start : start + block, 0 : 2 * HD] = jnp.concatenate(parts, axis=0).T.astype(bf16)
    d_ref[:, 2 * HD : 4 * HD] = dk_acc[...].astype(bf16)
    d_ref[:, 4 * HD : 6 * HD] = dv_acc[...].astype(bf16)


def attend_bwd(qkv, grad_context, lse, key_bias):
    rows = qkv.shape[0]
    groups = qkv.shape[1] // (6 * HD)
    block = min(512, rows)
    return pl.pallas_call(
        lambda *refs: attend_bwd_kernel(block, *refs),
        grid=(groups,),
        in_specs=[
            pl.BlockSpec((rows, 6 * HD), lambda j: (0, j)),
            pl.BlockSpec((rows, 2 * HD), lambda j: (0, j)),
            pl.BlockSpec((1, 2, rows), lambda j: (j, 0, 0)),
            pl.BlockSpec((rows, 1), lambda j: (0, 0)),
        ],
        out_specs=pl.BlockSpec((rows, 6 * HD), lambda j: (0, j)),
        out_shape=jax.ShapeDtypeStruct((rows, groups * 6 * HD), bf16),
        scratch_shapes=[pltpu.VMEM((rows, 2 * HD), f32), pltpu.VMEM((rows, 2 * HD), f32)],
        compiler_params=pltpu.CompilerParams(vmem_limit_bytes=48 << 20),
        cost_estimate=pl.CostEstimate(
            flops=groups * 20 * rows * rows * HD * 4,
            bytes_accessed=rows * groups * 14 * HD * 2,
            transcendentals=groups * 2 * rows * rows,
        ),
        name="attend_bwd",
    )(qkv, grad_context, lse, key_bias)


def swap_cores(value):
    return lax.ppermute(value, "core", SWAP)


def on_device(
    inputs,
    lengths,
    w_query,
    w_key,
    w_value,
    b_query,
    b_value,
    w_out,
    b_out,
    gain_one,
    shift_one,
    w_in,
    b_in,
    w_back,
    b_back,
    gain_two,
    shift_two,
    cotangent,
):
    planes = lax.axis_size("plane")
    n_t = lax.axis_size("tensor")
    plane = lax.axis_index("plane")
    core = lax.axis_index("core")
    place = lax.axis_index("tensor")
    seqs, slots_here, width = inputs.shape
    slots = slots_here * n_t
    half_slots = slots_here // 2
    own = slots // 2
    assert seqs * 2 == n_t
    head_cols = w_query.shape[1] // 2
    ff_cols = w_in.shape[1] // 2
    scale = HD ** (-0.5)
    quad = planes == 4
    ring = [(i, (i + 1) % n_t) for i in range(n_t)]
    x_pairs = [(i, i ^ 1) for i in range(planes)]
    y_pairs = [(i, i ^ 2) for i in range(planes)]

    def reorder(value, axis):
        if not quad:
            return value
        size = value.shape[axis] // 4
        return jnp.concatenate(
            [lax.dynamic_slice_in_dim(value, (plane ^ k) * size, size, axis) for k in range(4)],
            axis=axis,
        )

    def by_core(mine, theirs, axis=0):
        first = jnp.where(core == 0, mine, theirs)
        second = jnp.where(core == 0, theirs, mine)
        return jnp.concatenate([first, second], axis=axis)

    def to_chip(rows_here):
        value = reorder(rows_here, 2).reshape(seqs, 2, half_slots, width)
        mine = lax.dynamic_index_in_dim(value, core, 1, keepdims=False)
        other = lax.dynamic_index_in_dim(value, 1 - core, 1, keepdims=False)
        both = by_core(mine, swap_cores(other))
        return lax.all_to_all(both, "tensor", 0, 0, tiled=True).reshape(own, width)

    def from_chip(rows_own):
        value = rows_own.reshape(n_t, half_slots, width)
        value = lax.all_to_all(value, "tensor", 0, 0, tiled=True)
        value = value.reshape(2, seqs, half_slots, width)
        mine = lax.dynamic_index_in_dim(value, core, 0, keepdims=False)
        other = lax.dynamic_index_in_dim(value, 1 - core, 0, keepdims=False)
        got = swap_cores(other)
        value = jnp.stack(
            [jnp.where(core == 0, mine, got), jnp.where(core == 0, got, mine)], axis=1
        )
        return reorder(value.reshape(seqs, slots_here, width), 2)

    own_x = to_chip(inputs)
    their_lengths = swap_cores(lengths)
    all_lengths = by_core(lengths, their_lengths)
    length = lax.dynamic_index_in_dim(all_lengths, place, 0, keepdims=False)
    index = jnp.arange(slots)
    position = (
        (index % own) // half_slots * slots_here
        + ((index // own) ^ core) * half_slots
        + index % half_slots
    )
    valid = position < length
    key_bias = jnp.where(valid, 0.0, NEGATIVE).astype(f32)[:, None]
    own_valid = valid[:own, None]

    def halves(value, cols):
        return (
            lax.dynamic_slice_in_dim(value, core * cols, cols, 1),
            lax.dynamic_slice_in_dim(value, (1 - core) * cols, cols, 1),
        )

    pieces = [
        halves(w_query, head_cols),
        halves(w_key, head_cols),
        halves(w_value, head_cols),
        halves(w_out.T, head_cols),
        halves(w_in, ff_cols),
        halves(w_back.T, ff_cols),
    ]
    keep = jnp.concatenate([piece[0] for piece in pieces], axis=1)
    give = jnp.concatenate([piece[1] for piece in pieces], axis=1)
    packed = by_core(keep, swap_cores(give))
    cuts = (4 * head_cols, 4 * head_cols + ff_cols)
    bundle_a = packed[:, : cuts[0]]
    bundle_b = packed[:, cuts[0] : cuts[1]]
    bundle_c = packed[:, cuts[1] :]

    def gather_z(own_piece):
        got = [own_piece]
        for _ in range(n_t - 1):
            got.append(lax.ppermute(got[-1], "tensor", ring))
        return jnp.stack(got)

    def gather_planes(mine):
        if not quad:
            return lax.all_gather(mine, "plane", axis=1, tiled=True)
        half = n_t // 2
        from_x = lax.ppermute(mine, "plane", x_pairs)
        from_y = lax.ppermute(mine, "plane", y_pairs)
        low = lax.ppermute(from_y[:half], "plane", x_pairs)
        high = lax.ppermute(from_x[half:], "plane", y_pairs)
        return jnp.concatenate([mine, from_x, from_y, jnp.concatenate([low, high])], axis=1)

    def flat(gathered):
        return jnp.concatenate([gathered[j] for j in range(n_t)], axis=1)

    bias_row = jnp.concatenate(
        [
            lax.dynamic_slice_in_dim(b_query, core * head_cols, head_cols),
            lax.dynamic_slice_in_dim(b_value, core * head_cols, head_cols),
            lax.dynamic_slice_in_dim(b_in, core * ff_cols, ff_cols),
        ]
    )[None]
    biases = gather_z(bias_row)[:, 0].astype(f32)
    z_a = gather_z(bundle_a)
    full_a = gather_planes(z_a)
    w_qkv = flat(full_a[:, :, : 3 * head_cols])
    w_o = flat(full_a[:, :, 3 * head_cols :])
    w_1 = flat(gather_planes(gather_z(bundle_b)))
    w_2 = flat(gather_planes(gather_z(bundle_c)))

    zeros_k = jnp.zeros((n_t, head_cols), f32)
    qkv_bias = jnp.concatenate(
        [biases[:, :head_cols], zeros_k, biases[:, head_cols : 2 * head_cols]], axis=1
    ).reshape(1, -1)
    qkv_scale = jnp.tile(
        jnp.concatenate([jnp.full((head_cols,), scale, f32), jnp.ones((2 * head_cols,), f32)]), n_t
    )[None]
    in_bias = biases[:, 2 * head_cols :].reshape(1, -1)
    out_bias = reorder(b_out, 0).astype(f32)
    back_bias = reorder(b_back, 0).astype(f32)
    gain_first = reorder(gain_one, 0).astype(f32)
    shift_first = reorder(shift_one, 0).astype(f32)
    gain_second = reorder(gain_two, 0).astype(f32)
    shift_second = reorder(shift_two, 0).astype(f32)

    def both_rows(value):
        return jnp.concatenate([value, swap_cores(value)], axis=0)

    def own_sum(partial):
        return partial[:own] + swap_cores(partial[own:])

    def normalize(value):
        average = jnp.mean(value, axis=-1, keepdims=True)
        centered = value - average
        variance = jnp.mean(centered * centered, axis=-1, keepdims=True)
        inverse = lax.rsqrt(variance + EPSILON)
        return centered * inverse, inverse

    def normalize_back(grad, gain, normed, inverse):
        e = grad * gain
        return (
            e
            - jnp.mean(e, axis=-1, keepdims=True)
            - normed * jnp.mean(e * normed, axis=-1, keepdims=True)
        ) * inverse

    x_full = both_rows(own_x)
    qkv = ((nn(x_full, w_qkv) + qkv_bias) * qkv_scale).astype(bf16)
    context, lse = attend_fwd(qkv, key_bias)
    attended = own_sum(nt(context, w_o))
    normed_one, inverse_one = normalize(own_x.astype(f32) + attended + out_bias)
    first_norm = normed_one * gain_first + shift_first
    first_full = both_rows(first_norm.astype(bf16))
    pre_act = nn(first_full, w_1) + in_bias
    activated, gelu_back = jax.vjp(lambda v: jax.nn.gelu(v, approximate=False), pre_act)
    hidden = activated.astype(bf16)
    mixed = own_sum(nt(hidden, w_2))
    normed_two, inverse_two = normalize(first_norm + mixed + back_bias)
    second = normed_two * gain_second + shift_second
    layer_out = from_chip(jnp.where(own_valid, second, 0.0).astype(bf16))

    grad_second = jnp.where(own_valid, to_chip(cotangent).astype(f32), 0.0)
    grad_mixed = normalize_back(grad_second, gain_second, normed_two, inverse_two)
    grad_mixed_full = both_rows(grad_mixed.astype(bf16))
    grad_w2 = tn(grad_mixed_full, hidden)
    (grad_pre,) = gelu_back(nn(grad_mixed_full, w_2))
    grad_pre_low = grad_pre.astype(bf16)
    grad_w1 = tn(first_full, grad_pre_low)
    grad_first = grad_mixed + own_sum(nt(grad_pre_low, w_1))
    grad_att = normalize_back(grad_first, gain_first, normed_one, inverse_one)
    grad_att_full = both_rows(grad_att.astype(bf16))
    grad_context = nn(grad_att_full, w_o).astype(bf16)
    grad_wo = tn(grad_att_full, context)
    grad_qkv = attend_bwd(qkv, grad_context, lse, key_bias)
    grad_qkv = grad_qkv * qkv_scale.astype(bf16)
    grad_wqkv = tn(x_full, grad_qkv)
    grad_rows = grad_att + own_sum(nt(grad_qkv, w_qkv))
    grad_inputs = from_chip(grad_rows.astype(bf16)).astype(f32)

    def scatter(grad):
        cols = grad.shape[1] // n_t
        if quad:
            rows = width // 4
            blocks = grad.reshape(4, rows, n_t, cols).transpose(0, 2, 1, 3)
            half = n_t // 2
            low = lax.ppermute(blocks[3, :half].astype(bf16), "plane", x_pairs)
            high = lax.ppermute(blocks[3, half:].astype(bf16), "plane", y_pairs)
            for_y = jnp.concatenate([blocks[2, :half] + low.astype(f32), blocks[2, half:]])
            for_x = jnp.concatenate([blocks[1, :half], blocks[1, half:] + high.astype(f32)])
            from_x = lax.ppermute(for_x.astype(bf16), "plane", x_pairs)
            from_y = lax.ppermute(for_y.astype(bf16), "plane", y_pairs)
            mine = blocks[0] + from_x.astype(f32) + from_y.astype(f32)
        else:
            blocks = grad.reshape(width, n_t, cols).transpose(1, 0, 2)
            mine = lax.psum_scatter(
                blocks.astype(bf16), "plane", scatter_dimension=1, tiled=True
            ).astype(f32)
        back = [(b, a) for a, b in ring]
        total = mine[n_t - 1]
        for j in range(n_t - 2, -1, -1):
            total = mine[j] + lax.ppermute(total.astype(bf16), "tensor", back).astype(f32)
        return total

    home_c = scatter(grad_w2)
    home_b = scatter(grad_w1)
    grad_a = jnp.concatenate(
        [
            grad_wqkv.reshape(width, n_t, 3 * head_cols),
            grad_wo.reshape(width, n_t, head_cols),
        ],
        axis=2,
    ).reshape(width, -1)
    home_a = scatter(grad_a)
    home = jnp.concatenate([home_a, home_b, home_c], axis=1)
    home = home.reshape(2, -1, home.shape[1])
    mine = lax.dynamic_index_in_dim(home, core, 0, keepdims=False)
    other = lax.dynamic_index_in_dim(home, 1 - core, 0, keepdims=False)
    got = swap_cores(other)

    def columns(start, cols):
        return by_core(mine[:, start : start + cols], got[:, start : start + cols], axis=1)

    grad_w_query = columns(0, head_cols)
    grad_w_key = columns(head_cols, head_cols)
    grad_w_value = columns(2 * head_cols, head_cols)
    grad_w_out = columns(3 * head_cols, head_cols).T
    grad_w_in = columns(cuts[0], ff_cols)
    grad_w_back = columns(cuts[1], ff_cols).T

    def row_sum(value):
        return reorder(jnp.sum(value, axis=0), 0)

    norm_sums = jnp.concatenate(
        [
            row_sum(grad_att),
            row_sum(grad_first * normed_one),
            row_sum(grad_first),
            row_sum(grad_mixed),
            row_sum(grad_second * normed_two),
            row_sum(grad_second),
        ]
    )
    qkv_sum = jnp.sum(grad_qkv.astype(f32), axis=0).reshape(n_t, 3 * head_cols)
    pre_sum = jnp.sum(grad_pre_low.astype(f32), axis=0).reshape(n_t, ff_cols)
    bias_sum = jnp.concatenate([qkv_sum[:, :head_cols], qkv_sum[:, 2 * head_cols :], pre_sum], axis=1)
    at_home = lax.rem(place - jnp.arange(n_t) + n_t, n_t)
    spread = (at_home[:, None] == jnp.arange(n_t)[None]).astype(f32)
    by_place = jnp.sum(spread[:, :, None] * bias_sum[:, None, :], axis=0)
    both = jnp.where(
        (jnp.arange(2) == core)[None, :, None], by_place[:, None, :], 0.0
    )
    sums = lax.psum(jnp.concatenate([norm_sums, both.reshape(-1)]), ("plane", "core", "tensor"))
    norms = sums[: 6 * width].reshape(6, width)
    biases_out = lax.dynamic_index_in_dim(
        sums[6 * width :].reshape(n_t, 2, -1), place, 0, keepdims=False
    )
    grad_b_query = biases_out[:, :head_cols].reshape(-1)
    grad_b_value = biases_out[:, head_cols : 2 * head_cols].reshape(-1)
    grad_b_in = biases_out[:, 2 * head_cols :].reshape(-1)
    return (
        layer_out,
        grad_inputs,
        grad_w_query,
        grad_w_key,
        grad_w_value,
        grad_b_query,
        grad_b_value,
        grad_w_out,
        norms[0],
        norms[1],
        norms[2],
        grad_w_in,
        grad_b_in,
        grad_w_back,
        norms[3],
        norms[4],
        norms[5],
    )


def solution(mesh):
    devices = mesh.devices.reshape(mesh.shape["dp"] // 2, 2, mesh.shape["tensor"])
    inner = Mesh(devices, ("plane", "core", "tensor"))
    dp = ("plane", "core")
    row = P(dp, "tensor")
    column = P("tensor", dp)
    rows3 = P(dp, "tensor", None)
    shard = P("tensor")
    whole = P()
    return jax.shard_map(
        on_device,
        mesh=inner,
        in_specs=(
            rows3, P(dp), row, row, row, shard, shard, column, whole, whole, whole,
            row, shard, column, whole, whole, whole, rows3,
        ),
        out_specs=(
            rows3, rows3, row, row, row, shard, shard, column, whole, whole, whole,
            row, shard, column, whole, whole, whole,
        ),
        check_vma=False,
    )
```

```python
import jax
import jax.numpy as jnp
from jax import lax
from jax.experimental import pallas as pl
from jax.experimental.pallas import tpu as pltpu
from jax.sharding import Mesh, PartitionSpec as P

HD = 64
EPSILON = 1e-05
NEGATIVE = -1e30
f32 = jnp.float32
bf16 = jnp.bfloat16
SWAP = [(0, 1), (1, 0)]


def nt(a, b):
    return lax.dot_general(a, b, (((1,), (1,)), ((), ())), preferred_element_type=f32)


def tn(a, b):
    return lax.dot_general(a, b, (((0,), (0,)), ((), ())), preferred_element_type=f32)


def nn(a, b):
    return lax.dot_general(a, b, (((1,), (0,)), ((), ())), preferred_element_type=f32)


def attend_fwd_kernel(block, qkv_ref, kb_ref, ctx_ref, lse_ref):
    rows = qkv_ref.shape[0]
    lane = lax.broadcasted_iota(jnp.int32, (1, 2 * HD), 1)
    keys = qkv_ref[:, 2 * HD : 4 * HD]
    values_t = qkv_ref[:, 4 * HD : 6 * HD].T
    key_bias = kb_ref[...]
    for start in range(0, rows, block):
        query = qkv_ref[start : start + block, 0 : 2 * HD]
        parts = []
        for h in range(2):
            query_h = jnp.where(lane // HD == h, query, jnp.zeros_like(query))
            scores = nt(keys, query_h) + key_bias
            largest = jnp.max(scores, axis=0, keepdims=True)
            weights = jnp.exp(scores - largest)
            total = jnp.sum(weights, axis=0, keepdims=True)
            part = nn(values_t[h * HD : (h + 1) * HD], weights.astype(bf16))
            parts.append(part / total)
            lse_ref[0, h : h + 1, start : start + block] = largest + jnp.log(total)
        ctx_ref[start : start + block, :] = jnp.concatenate(parts, axis=0).T.astype(bf16)


def attend_fwd(qkv, key_bias):
    rows = qkv.shape[0]
    groups = qkv.shape[1] // (6 * HD)
    block = min(512, rows)
    return pl.pallas_call(
        lambda *refs: attend_fwd_kernel(block, *refs),
        grid=(groups,),
        in_specs=[
            pl.BlockSpec((rows, 6 * HD), lambda j: (0, j)),
            pl.BlockSpec((rows, 1), lambda j: (0, 0)),
        ],
        out_specs=[
            pl.BlockSpec((rows, 2 * HD), lambda j: (0, j)),
            pl.BlockSpec((1, 2, rows), lambda j: (j, 0, 0)),
        ],
        out_shape=[
            jax.ShapeDtypeStruct((rows, groups * 2 * HD), bf16),
            jax.ShapeDtypeStruct((groups, 2, rows), f32),
        ],
        compiler_params=pltpu.CompilerParams(vmem_limit_bytes=48 << 20),
        cost_estimate=pl.CostEstimate(
            flops=groups * 8 * rows * rows * HD * 4,
            bytes_accessed=rows * groups * 8 * HD * 2,
            transcendentals=groups * 2 * rows * rows,
        ),
        name="attend_fwd",
    )(qkv, key_bias)


def attend_bwd_kernel(block, qkv_ref, g_ref, lse_ref, kb_ref, d_ref, dk_acc, dv_acc):
    rows = qkv_ref.shape[0]
    lane = lax.broadcasted_iota(jnp.int32, (1, 2 * HD), 1)
    keys = qkv_ref[:, 2 * HD : 4 * HD]
    keys_t = keys.T
    values = qkv_ref[:, 4 * HD : 6 * HD]
    key_bias = kb_ref[...]
    for start in range(0, rows, block):
        query = qkv_ref[start : start + block, 0 : 2 * HD]
        grad = g_ref[start : start + block, :]
        parts = []
        for h in range(2):
            here = lane // HD == h
            query_h = jnp.where(here, query, jnp.zeros_like(query))
            grad_h = jnp.where(here, grad, jnp.zeros_like(grad))
            scores = nt(keys, query_h) + key_bias
            chances = jnp.exp(scores - lse_ref[0, h : h + 1, start : start + block])
            grad_chances = nt(values, grad_h)
            inner = jnp.sum(chances * grad_chances, axis=0, keepdims=True)
            grad_scores = (chances * (grad_chances - inner)).astype(bf16)
            dv = nn(chances.astype(bf16), grad_h)
            dk = nn(grad_scores, query_h)
            if start == 0 and h == 0:
                dv_acc[...] = dv
                dk_acc[...] = dk
            else:
                dv_acc[...] += dv
                dk_acc[...] += dk
            parts.append(nn(keys_t[h * HD : (h + 1) * HD], grad_scores))
        d_ref[start : start + block, 0 : 2 * HD] = jnp.concatenate(parts, axis=0).T.astype(bf16)
    d_ref[:, 2 * HD : 4 * HD] = dk_acc[...].astype(bf16)
    d_ref[:, 4 * HD : 6 * HD] = dv_acc[...].astype(bf16)


def attend_bwd(qkv, grad_context, lse, key_bias):
    rows = qkv.shape[0]
    groups = qkv.shape[1] // (6 * HD)
    block = min(512, rows)
    return pl.pallas_call(
        lambda *refs: attend_bwd_kernel(block, *refs),
        grid=(groups,),
        in_specs=[
            pl.BlockSpec((rows, 6 * HD), lambda j: (0, j)),
            pl.BlockSpec((rows, 2 * HD), lambda j: (0, j)),
            pl.BlockSpec((1, 2, rows), lambda j: (j, 0, 0)),
            pl.BlockSpec((rows, 1), lambda j: (0, 0)),
        ],
        out_specs=pl.BlockSpec((rows, 6 * HD), lambda j: (0, j)),
        out_shape=jax.ShapeDtypeStruct((rows, groups * 6 * HD), bf16),
        scratch_shapes=[pltpu.VMEM((rows, 2 * HD), f32), pltpu.VMEM((rows, 2 * HD), f32)],
        compiler_params=pltpu.CompilerParams(vmem_limit_bytes=48 << 20),
        cost_estimate=pl.CostEstimate(
            flops=groups * 20 * rows * rows * HD * 4,
            bytes_accessed=rows * groups * 14 * HD * 2,
            transcendentals=groups * 2 * rows * rows,
        ),
        name="attend_bwd",
    )(qkv, grad_context, lse, key_bias)

POLY = (
    0.30995978221815235,
    0.31100346478903146,
    0.2699660979585953,
    0.2765467936611628,
    -0.03831584737802812,
    0.38967711658103854,
    -0.3554874111653827,
    0.08996434684501212,
)
POLY_AT = 0.31
DENSITY = 0.3989422804014327
MESH = pl.DeviceIdType.MESH


def gelu_and_slope(v):
    density = jnp.exp(-0.5 * v * v) * DENSITY
    t = 1.0 / (1.0 + POLY_AT * jnp.abs(v))
    tail = jnp.full_like(v, POLY[-1])
    for coefficient in POLY[-2::-1]:
        tail = tail * t + coefficient
    tail = tail * t * density
    below = jnp.where(v > 0, 1.0 - tail, tail)
    return v * below, below + v * density


def forward_kernel(
    length_ref, xp_ref, cp_ref, keep_ref, give_ref, bias_in_ref, vec_ref,
    w_out, xf_out, qkv_out, lse_ref, ctx_out, ff_out, hid_out, dg_out, n1_out, inv1_ref, gm_ref,
    lo_ref, sums_ref,
    w, xf, bias, qkv, ctx, ff, hid, dg, n1, first, other_part, own_part, att_got, mix_got, cot, lo_own,
    z_s, z_r, x_s, x_r, y_s, y_r, f_s, f_r, pre_l, pre_s, pre_r, b_s, b_r,
    xa_s, xa_r, ca_s, ca_r, la_s, la_r, e_s, e_r, o_s,
):
    plane = lax.axis_index("plane")
    core = lax.axis_index("core")
    place = lax.axis_index("tensor")
    partner = {"core": 1 - core}
    x_side = {"plane": plane + 1 - 2 * (plane % 2)}
    y_side = {"plane": (plane + 2) % 4}
    z_next = {"tensor": (place + 1) % 4}
    rows = xf.shape[0]
    own = rows // 2
    part = own // 4
    piece = w.shape[2] // 4

    def remote(source, target, send, recv, to):
        return pltpu.make_async_remote_copy(
            source, target, send, recv, device_id=to, device_id_type=MESH
        )

    def z_copy(b, s):
        return remote(
            w.at[b, s, 0:piece], w.at[b, s + 1, 0:piece], z_s.at[b, s], z_r.at[b, s], z_next
        )

    def x_copy(b, j):
        return remote(
            w.at[b, j, 0:piece], w.at[b, j, piece : 2 * piece], x_s.at[b, j], x_r.at[b, j], x_side
        )

    def y_copy(b, j):
        return remote(
            w.at[b, j, 0:piece], w.at[b, j, 2 * piece : 3 * piece], y_s.at[b, j], y_r.at[b, j], y_side
        )

    def f_copy(b, j):
        start = 2 * piece if j < 2 else piece
        return remote(
            w.at[b, j, start : start + piece],
            w.at[b, j, 3 * piece : 4 * piece],
            f_s.at[b, j],
            f_r.at[b, j],
            x_side if j < 2 else y_side,
        )

    def pre_copy(b):
        rows_at = pl.ds(core * (piece // 2), piece // 2)
        return remote(give_ref.at[b], w.at[b, 0, rows_at], pre_s.at[b], pre_r.at[b], partner)

    def pre_got(b):
        rows_at = pl.ds((1 - core) * (piece // 2), piece // 2)
        return remote(give_ref.at[b], w.at[b, 0, rows_at], pre_s.at[b], pre_r.at[b], partner)

    def keep_copy(b):
        rows_at = pl.ds(core * (piece // 2), piece // 2)
        return pltpu.make_async_copy(keep_ref.at[b], w.at[b, 0, rows_at], pre_l.at[b])

    def bias_copy(s):
        return remote(
            bias.at[0], bias.at[s], b_s.at[s], b_r.at[s], {"tensor": (place + s) % 4}
        )

    def spread(source, target, send, recv, l, h):
        at = pl.ds(place * part, part)
        to = {"core": h, "tensor": 2 * core + l}
        return remote(
            source.at[2 * l + h], target.at[at], send.at[2 * l + h], recv.at[place], to
        )

    def spread_local(source, target, recv, l, h):
        at = pl.ds(place * part, part)
        return pltpu.make_async_copy(source.at[2 * l + h], target.at[at], recv.at[place])

    def is_here(l, h):
        return jnp.logical_and(core == h, place == 2 * core + l)

    def spread_start(source, target, send, recv):
        for l in range(2):
            for h in range(2):
                @pl.when(is_here(l, h))
                def _():
                    spread_local(source, target, recv, l, h).start()

                @pl.when(jnp.logical_not(is_here(l, h)))
                def _():
                    spread(source, target, send, recv, l, h).start()

    def spread_wait(source, target, recv):
        for s in range(4):
            pltpu.make_async_copy(
                source.at[s], target.at[s * part : (s + 1) * part], recv.at[s]
            ).wait()

    def spread_sent(source, target, send, recv):
        for l in range(2):
            for h in range(2):
                @pl.when(jnp.logical_not(is_here(l, h)))
                def _():
                    spread(source, target, send, recv, l, h).wait_send()

    def home(s):
        to = {"core": place // 2, "tensor": s}
        return remote(
            lo_own.at[s * part : (s + 1) * part],
            lo_ref.at[2 * (place % 2) + core],
            la_s.at[s],
            la_r.at[2 * (place % 2) + core],
            to,
        )

    def home_local(s):
        return pltpu.make_async_copy(
            lo_own.at[s * part : (s + 1) * part],
            lo_ref.at[2 * (place % 2) + core],
            la_r.at[2 * (place % 2) + core],
        )

    def is_home(s):
        return jnp.logical_and(core == place // 2, place == s)

    def exchange(source, target, n):
        return remote(source, target, e_s.at[n], e_r.at[n], partner)

    outs = []

    def save(source, target):
        copy = pltpu.make_async_copy(source, target, o_s.at[len(outs)])
        copy.start()
        outs.append(copy)

    barrier = pltpu.get_barrier_semaphore()
    friends = [x_side, y_side, partner]
    for s in range(1, 4):
        friends.append({"tensor": (place + s) % 4})
        friends.append({"tensor": (place + s) % 4, "core": 1 - core})
    for friend in friends:
        pl.semaphore_signal(barrier, inc=1, device_id=friend, device_id_type=MESH)
    keep_all = [keep_copy(b) for b in range(3)]
    for copy in keep_all:
        copy.start()
    pl.semaphore_wait(barrier, len(friends))

    for b in range(3):
        pre_copy(b).start()
    bias[0] = bias_in_ref[...]
    spread_start(xp_ref, xf, xa_s, xa_r)
    keep_all[0].wait()
    pre_got(0).wait_recv()
    z_copy(0, 0).start()
    x_copy(0, 0).start()
    y_copy(0, 0).start()
    for s in range(1, 4):
        bias_copy(s).start()
    for b in (1, 2):
        keep_all[b].wait()
        pre_got(b).wait_recv()
        x_copy(b, 0).start()
        y_copy(b, 0).start()
    z_copy(0, 0).wait_recv()
    z_copy(0, 1).start()
    x_copy(0, 1).start()
    y_copy(0, 1).start()
    y_copy(0, 0).wait_recv()
    f_copy(0, 0).start()
    z_copy(0, 1).wait_recv()
    z_copy(0, 2).start()
    x_copy(0, 2).start()
    y_copy(0, 2).start()
    z_copy(0, 2).wait_recv()
    z_copy(1, 0).start()
    z_copy(2, 0).start()
    x_copy(0, 3).start()
    y_copy(0, 3).start()

    spread_wait(xp_ref, xf, xa_r)
    share_x = exchange(xf.at[0:own], xf.at[own : 2 * own], 0)
    share_x.start()
    y_copy(0, 1).wait_recv()
    f_copy(0, 1).start()
    y_copy(1, 0).wait_recv()
    f_copy(1, 0).start()
    y_copy(2, 0).wait_recv()
    f_copy(2, 0).start()
    for s in range(1, 4):
        bias_copy(s).wait_recv()
    share_x.wait_recv()
    save(xf, xf_out)

    index = lax.broadcasted_iota(jnp.int32, (rows, 1), 0)
    length = length_ref[0]
    half = jnp.where(index < own, core, 1 - core)
    inside = index % own
    position = (inside // part) * (2 * part) + half * part + inside % part
    key_bias = jnp.where(position < length, 0.0, NEGATIVE).astype(f32)
    lane = lax.broadcasted_iota(jnp.int32, (1, 2 * HD), 1)
    head_cols = 2 * HD
    tile = 256

    def project(j):
        columns = lax.broadcasted_iota(jnp.int32, (1, 3 * head_cols), 1)
        zero = jnp.zeros((1, head_cols), f32)
        add = jnp.concatenate(
            [bias[j, 0:1, 0:head_cols], zero, bias[j, 0:1, head_cols : 2 * head_cols]], axis=1
        )
        times = jnp.where(columns < head_cols, HD ** (-0.5), 1.0).astype(f32)

        def body(i, _):
            at = pl.ds(pl.multiple_of(i * tile, tile), tile)
            value = nn(xf[at, :], w[0, j, :, 0 : 3 * head_cols])
            qkv[j, at, :] = ((value + add) * times).astype(bf16)
            return 0

        lax.fori_loop(0, rows // tile, body, 0)
        save(qkv.at[j], qkv_out.at[j])

    def attend(j):
        keys = qkv[j, :, head_cols : 2 * head_cols]
        values_t = qkv[j, :, 2 * head_cols : 3 * head_cols].T

        def body(i, _):
            at = pl.ds(pl.multiple_of(i * tile, tile), tile)
            query = qkv[j, at, 0:head_cols]
            parts = []
            for h in range(2):
                query_h = jnp.where(lane // HD == h, query, jnp.zeros_like(query))
                scores = nt(keys, query_h) + key_bias
                largest = jnp.max(scores, axis=0, keepdims=True)
                weights = jnp.exp(scores - largest)
                total = jnp.sum(weights, axis=0, keepdims=True)
                out = nn(values_t[h * HD : (h + 1) * HD], weights.astype(bf16))
                parts.append(out / total)
                lse_ref[2 * j + h, :, at] = largest + jnp.log(total)
            ctx[j, at, :] = jnp.concatenate(parts, axis=0).T.astype(bf16)
            return 0

        lax.fori_loop(0, rows // tile, body, 0)
        save(ctx.at[j], ctx_out.at[j])

    def ready(b, j):
        x_copy(b, j).wait_recv() if not (b, j, "x") in seen else None
        seen.add((b, j, "x"))
        y_copy(b, j).wait_recv() if not (b, j, "y") in seen else None
        seen.add((b, j, "y"))
        f_copy(b, j).wait_recv()
        save(w.at[b, j], w_out.at[b, j])

    seen = {(0, 0, "y"), (0, 1, "y"), (1, 0, "y"), (2, 0, "y")}

    def forward_on(b, j):
        side = "y" if j < 2 else "x"
        (y_copy if j < 2 else x_copy)(b, j).wait_recv()
        seen.add((b, j, side))
        f_copy(b, j).start()

    ready(0, 0)
    project(0)
    attend(0)
    forward_on(0, 2)
    z_copy(1, 0).wait_recv()
    z_copy(1, 1).start()
    x_copy(1, 1).start()
    y_copy(1, 1).start()
    forward_on(0, 3)
    z_copy(2, 0).wait_recv()
    z_copy(2, 1).start()
    ready(0, 1)
    project(1)
    attend(1)
    z_copy(1, 1).wait_recv()
    z_copy(1, 2).start()
    x_copy(1, 2).start()
    y_copy(1, 2).start()
    ready(0, 2)
    project(2)
    attend(2)
    z_copy(2, 1).wait_recv()
    z_copy(2, 2).start()
    forward_on(1, 1)
    ready(0, 3)
    project(3)
    attend(3)
    z_copy(1, 2).wait_recv()
    x_copy(1, 3).start()
    y_copy(1, 3).start()
    forward_on(1, 2)

    def out_rows(start, target):
        def body(i, _):
            at = pl.ds(pl.multiple_of(start + i * tile, tile), tile)
            to = pl.ds(pl.multiple_of(i * tile, tile), tile)
            total = nt(ctx[0, at, :], w[0, 0, :, 3 * head_cols :])
            for j in range(1, 4):
                total += nt(ctx[j, at, :], w[0, j, :, 3 * head_cols :])
            target[to, :] = total
            return 0

        lax.fori_loop(0, own // tile, body, 0)

    out_rows(own, other_part)
    share_att = exchange(other_part, att_got, 1)
    share_att.start()
    out_rows(0, own_part)
    x_copy(2, 1).start()
    y_copy(2, 1).start()
    spread_start(cp_ref, cot, ca_s, ca_r)
    share_att.wait_recv()
    small = 32

    def mean(value):
        return jnp.sum(value, axis=-1, keepdims=True) * (1.0 / value.shape[-1])

    def first_body(i, _):
        at = pl.ds(pl.multiple_of(i * small, small), small)
        total = xf[at, :].astype(f32) + (own_part[at, :] + att_got[at, :]) + vec_ref[0:1, :]
        centered = total - mean(total)
        inverse = lax.rsqrt(mean(centered * centered) + EPSILON)
        normed = centered * inverse
        n1[at, :] = normed
        inv1_ref[at, :] = inverse
        value = normed * vec_ref[1:2, :] + vec_ref[2:3, :]
        first[at, :] = value
        ff[at, :] = value.astype(bf16)
        return 0

    lax.fori_loop(0, own // small, first_body, 0)
    share_first = exchange(ff.at[0:own], ff.at[own : 2 * own], 2)
    share_first.start()
    save(n1, n1_out)
    forward_on(1, 3)
    z_copy(2, 2).wait_recv()
    for j in (2, 3):
        x_copy(2, j).start()
        y_copy(2, j).start()
    share_first.wait_recv()
    save(ff, ff_out)

    def expand(j):
        add = bias[j, 0:1, 2 * head_cols :]

        def body(i, _):
            at = pl.ds(pl.multiple_of(i * tile, tile), tile)
            value = nn(ff[at, :], w[1, j]) + add
            active, slope = gelu_and_slope(value)
            hid[j, at, :] = active.astype(bf16)
            dg[j, at, :] = slope.astype(bf16)
            return 0

        lax.fori_loop(0, rows // tile, body, 0)
        save(hid.at[j], hid_out.at[j])
        save(dg.at[j], dg_out.at[j])

    ready(1, 0)
    expand(0)
    ready(1, 1)
    expand(1)
    forward_on(2, 1)
    ready(1, 2)
    expand(2)
    forward_on(2, 2)
    ready(1, 3)
    expand(3)
    share_att.wait_send()

    def contract(js, start, target, fresh):
        def body(i, _):
            at = pl.ds(pl.multiple_of(start + i * tile, tile), tile)
            to = pl.ds(pl.multiple_of(i * tile, tile), tile)
            total = nt(hid[js[0], at, :], w[2, js[0]])
            for j in js[1:]:
                total += nt(hid[j, at, :], w[2, j])
            target[to, :] = total if fresh else target[to, :] + total
            return 0

        lax.fori_loop(0, own // tile, body, 0)

    ready(2, 0)
    ready(2, 1)
    contract((0, 1), own, other_part, True)
    contract((0, 1), 0, own_part, True)
    forward_on(2, 3)
    ready(2, 2)
    contract((2,), own, other_part, False)
    contract((2,), 0, own_part, False)
    ready(2, 3)
    contract((3,), own, other_part, False)
    share_mix = exchange(other_part, mix_got, 3)
    share_mix.start()
    contract((3,), 0, own_part, False)
    spread_wait(cp_ref, cot, ca_r)
    share_mix.wait_recv()
    sums_ref[...] = jnp.zeros_like(sums_ref)

    def second_body(i, _):
        at = pl.ds(pl.multiple_of(i * small, small), small)
        spot = i * small + lax.broadcasted_iota(jnp.int32, (small, 1), 0)
        where = (spot // part) * (2 * part) + core * part + spot % part
        alive = where < length
        total = first[at, :] + (own_part[at, :] + mix_got[at, :]) + vec_ref[3:4, :]
        centered = total - mean(total)
        inverse = lax.rsqrt(mean(centered * centered) + EPSILON)
        normed = centered * inverse
        value = normed * vec_ref[4:5, :] + vec_ref[5:6, :]
        lo_own[at, :] = jnp.where(alive, value, 0.0).astype(bf16)
        grad = jnp.where(alive, cot[at, :].astype(f32), 0.0)
        e = grad * vec_ref[4:5, :]
        back = (e - mean(e) - normed * mean(e * normed)) * inverse
        gm_ref[at, :] = back
        sums_ref[0:1, :] += jnp.sum(back, axis=0, keepdims=True)
        sums_ref[1:2, :] += jnp.sum(grad * normed, axis=0, keepdims=True)
        sums_ref[2:3, :] += jnp.sum(grad, axis=0, keepdims=True)
        return 0

    lax.fori_loop(0, own // small, second_body, 0)
    for s in range(4):
        @pl.when(is_home(s))
        def _():
            home_local(s).start()

        @pl.when(jnp.logical_not(is_home(s)))
        def _():
            home(s).start()

    for b in range(3):
        pre_copy(b).wait_send()
        for s in range(3):
            z_copy(b, s).wait_send()
        for j in range(4):
            x_copy(b, j).wait_send()
            y_copy(b, j).wait_send()
            f_copy(b, j).wait_send()
    for s in range(1, 4):
        bias_copy(s).wait_send()
    spread_sent(xp_ref, xf, xa_s, xa_r)
    spread_sent(cp_ref, cot, ca_s, ca_r)
    share_x.wait_send()
    share_first.wait_send()
    share_mix.wait_send()
    for copy in outs:
        copy.wait()
    for s in range(4):
        @pl.when(jnp.logical_not(is_home(s)))
        def _():
            home(s).wait_send()
    for s in range(4):
        pltpu.make_async_copy(lo_own.at[0:part], lo_ref.at[s], la_r.at[s]).wait()


def forward(length, xp, cp, keep, give, bias, vec):
    part, width = xp.shape[1:]
    own = 4 * part
    rows = 2 * own
    cols = keep.shape[2]
    head_cols = 2 * HD
    any_ = pl.BlockSpec(memory_space=pltpu.HBM)
    vm = pl.BlockSpec(memory_space=pltpu.VMEM)
    sm = pl.BlockSpec(memory_space=pltpu.SMEM)
    shape = jax.ShapeDtypeStruct
    dma = pltpu.SemaphoreType.DMA
    flops = 2 * rows * width * cols * 12 + 16 * rows * rows * HD * 4
    return pl.pallas_call(
        forward_kernel,
        in_specs=[sm, any_, any_, any_, any_, vm, vm],
        out_specs=[any_, any_, any_, vm, any_, any_, any_, any_, any_, vm, vm, any_, vm],
        out_shape=[
            shape((3, 4, width, cols), bf16),
            shape((rows, width), bf16),
            shape((4, rows, 3 * head_cols), bf16),
            shape((8, 1, rows), f32),
            shape((4, rows, head_cols), bf16),
            shape((rows, width), bf16),
            shape((4, rows, cols), bf16),
            shape((4, rows, cols), bf16),
            shape((own, width), f32),
            shape((own, 1), f32),
            shape((own, width), f32),
            shape((4, part, width), bf16),
            shape((8, width), f32),
        ],
        scratch_shapes=[
            pltpu.VMEM((3, 4, width, cols), bf16),
            pltpu.VMEM((rows, width), bf16),
            pltpu.VMEM((4, 8, bias.shape[1]), f32),
            pltpu.VMEM((4, rows, 3 * head_cols), bf16),
            pltpu.VMEM((4, rows, head_cols), bf16),
            pltpu.VMEM((rows, width), bf16),
            pltpu.VMEM((4, rows, cols), bf16),
            pltpu.VMEM((4, rows, cols), bf16),
            pltpu.VMEM((own, width), f32),
            pltpu.VMEM((own, width), f32),
            pltpu.VMEM((own, width), f32),
            pltpu.VMEM((own, width), f32),
            pltpu.VMEM((own, width), f32),
            pltpu.VMEM((own, width), f32),
            pltpu.VMEM((own, width), bf16),
            pltpu.VMEM((own, width), bf16),
            dma((3, 3)), dma((3, 3)), dma((3, 4)), dma((3, 4)), dma((3, 4)), dma((3, 4)),
            dma((3, 4)), dma((3, 4)), dma((3,)), dma((3,)), dma((3,)), dma((4,)), dma((4,)),
            dma((4,)), dma((4,)), dma((4,)), dma((4,)), dma((4,)), dma((4,)),
            dma((4,)), dma((4,)), dma((32,)),
        ],
        compiler_params=pltpu.CompilerParams(
            collective_id=0, has_side_effects=True, vmem_limit_bytes=60 << 20
        ),
        cost_estimate=pl.CostEstimate(
            flops=flops, bytes_accessed=60 << 20, transcendentals=8 * rows * rows
        ),
        name="forward_layer",
    )(length, xp, cp, keep, give, bias, vec)


def swap_cores(value):
    return lax.ppermute(value, "core", SWAP)


def on_device(
    inputs,
    lengths,
    w_query,
    w_key,
    w_value,
    b_query,
    b_value,
    w_out,
    b_out,
    gain_one,
    shift_one,
    w_in,
    b_in,
    w_back,
    b_back,
    gain_two,
    shift_two,
    cotangent,
):
    planes = lax.axis_size("plane")
    n_t = lax.axis_size("tensor")
    plane = lax.axis_index("plane")
    core = lax.axis_index("core")
    place = lax.axis_index("tensor")
    seqs, slots_here, width = inputs.shape
    slots = slots_here * n_t
    half_slots = slots_here // 2
    own = slots // 2
    assert seqs * 2 == n_t
    head_cols = w_query.shape[1] // 2
    ff_cols = w_in.shape[1] // 2
    scale = HD ** (-0.5)
    quad = planes == 4
    ring = [(i, (i + 1) % n_t) for i in range(n_t)]
    x_pairs = [(i, i ^ 1) for i in range(planes)]
    y_pairs = [(i, i ^ 2) for i in range(planes)]

    def reorder(value, axis):
        if not quad:
            return value
        size = value.shape[axis] // 4
        return jnp.concatenate(
            [lax.dynamic_slice_in_dim(value, (plane ^ k) * size, size, axis) for k in range(4)],
            axis=axis,
        )

    def by_core(mine, theirs, axis=0):
        first = jnp.where(core == 0, mine, theirs)
        second = jnp.where(core == 0, theirs, mine)
        return jnp.concatenate([first, second], axis=axis)

    def to_chip(rows_here):
        value = reorder(rows_here, 2).reshape(seqs, 2, half_slots, width)
        mine = lax.dynamic_index_in_dim(value, core, 1, keepdims=False)
        other = lax.dynamic_index_in_dim(value, 1 - core, 1, keepdims=False)
        both = by_core(mine, swap_cores(other))
        return lax.all_to_all(both, "tensor", 0, 0, tiled=True).reshape(own, width)

    def from_chip(rows_own):
        value = rows_own.reshape(n_t, half_slots, width)
        value = lax.all_to_all(value, "tensor", 0, 0, tiled=True)
        value = value.reshape(2, seqs, half_slots, width)
        mine = lax.dynamic_index_in_dim(value, core, 0, keepdims=False)
        other = lax.dynamic_index_in_dim(value, 1 - core, 0, keepdims=False)
        got = swap_cores(other)
        value = jnp.stack(
            [jnp.where(core == 0, mine, got), jnp.where(core == 0, got, mine)], axis=1
        )
        return reorder(value.reshape(seqs, slots_here, width), 2)

    their_lengths = swap_cores(lengths)
    all_lengths = by_core(lengths, their_lengths)
    length = lax.dynamic_index_in_dim(all_lengths, place, 0, keepdims=False)
    index = jnp.arange(slots)
    position = (
        (index % own) // half_slots * slots_here
        + ((index // own) ^ core) * half_slots
        + index % half_slots
    )
    valid = position < length
    key_bias = jnp.where(valid, 0.0, NEGATIVE).astype(f32)[:, None]
    own_valid = valid[:own, None]

    def halves(value, cols):
        return (
            lax.dynamic_slice_in_dim(value, core * cols, cols, 1),
            lax.dynamic_slice_in_dim(value, (1 - core) * cols, cols, 1),
        )

    pieces = [
        halves(w_query, head_cols),
        halves(w_key, head_cols),
        halves(w_value, head_cols),
        halves(w_out.T, head_cols),
        halves(w_in, ff_cols),
        halves(w_back.T, ff_cols),
    ]
    keep = jnp.concatenate([piece[0] for piece in pieces], axis=1)
    give = jnp.concatenate([piece[1] for piece in pieces], axis=1)
    cuts = (4 * head_cols, 4 * head_cols + ff_cols)

    def flat(gathered):
        return jnp.concatenate([gathered[j] for j in range(n_t)], axis=1)

    out_bias = reorder(b_out, 0).astype(f32)
    back_bias = reorder(b_back, 0).astype(f32)
    gain_first = reorder(gain_one, 0).astype(f32)
    shift_first = reorder(shift_one, 0).astype(f32)
    gain_second = reorder(gain_two, 0).astype(f32)
    shift_second = reorder(shift_two, 0).astype(f32)
    bias_row = jnp.concatenate(
        [
            lax.dynamic_slice_in_dim(b_query, core * head_cols, head_cols),
            lax.dynamic_slice_in_dim(b_value, core * head_cols, head_cols),
            lax.dynamic_slice_in_dim(b_in, core * ff_cols, ff_cols),
        ]
    )[None]
    qkv_scale = jnp.tile(
        jnp.concatenate([jnp.full((head_cols,), scale, f32), jnp.ones((2 * head_cols,), f32)]), n_t
    )[None]
    def both_rows(value):
        return jnp.concatenate([value, swap_cores(value)], axis=0)

    def own_sum(partial):
        return partial[:own] + swap_cores(partial[own:])

    def normalize(value):
        average = jnp.mean(value, axis=-1, keepdims=True)
        centered = value - average
        variance = jnp.mean(centered * centered, axis=-1, keepdims=True)
        inverse = lax.rsqrt(variance + EPSILON)
        return centered * inverse, inverse

    def normalize_back(grad, gain, normed, inverse):
        e = grad * gain
        return (
            e
            - jnp.mean(e, axis=-1, keepdims=True)
            - normed * jnp.mean(e * normed, axis=-1, keepdims=True)
        ) * inverse

    if quad:
        def blocks_of(value):
            return reorder(value, 2).reshape(4, half_slots, width)

        pack = lambda value: jnp.stack(
            [value[:, : cuts[0]], value[:, cuts[0] : cuts[1]], value[:, cuts[1] :]]
        )
        vec = jnp.stack(
            [out_bias, gain_first, shift_first, back_bias, gain_second, shift_second,
             out_bias, out_bias]
        )
        (w_all, x_full, qkv4, lse8, ctx4, first_full, hid4, dg4, normed_one, inverse_one,
         grad_mixed, lo_blocks, second_sums) = forward(
            length.reshape(1), blocks_of(inputs), blocks_of(cotangent), pack(keep), pack(give),
            jnp.broadcast_to(bias_row.astype(f32), (8, bias_row.shape[1])), vec,
        )
        layer_out = reorder(lo_blocks.reshape(seqs, slots_here, width), 2)
        w_qkv = flat(w_all[0][:, :, : 3 * head_cols])
        w_o = flat(w_all[0][:, :, 3 * head_cols :])
        w_1 = flat(w_all[1])
        w_2 = flat(w_all[2])
        qkv = flat(qkv4)
        lse = lse8.reshape(n_t, 2, slots)
        context = flat(ctx4)
        hidden = flat(hid4)
        slope = flat(dg4)
    else:
        packed = by_core(keep, swap_cores(give))
        bundle_a = packed[:, : cuts[0]]
        bundle_b = packed[:, cuts[0] : cuts[1]]
        bundle_c = packed[:, cuts[1] :]
        def gather_z(own_piece):
            got = [own_piece]
            for _ in range(n_t - 1):
                got.append(lax.ppermute(got[-1], "tensor", ring))
            return jnp.stack(got)

        def gather_planes(mine):
            if not quad:
                return lax.all_gather(mine, "plane", axis=1, tiled=True)
            half = n_t // 2
            from_x = lax.ppermute(mine, "plane", x_pairs)
            from_y = lax.ppermute(mine, "plane", y_pairs)
            low = lax.ppermute(from_y[:half], "plane", x_pairs)
            high = lax.ppermute(from_x[half:], "plane", y_pairs)
            return jnp.concatenate([mine, from_x, from_y, jnp.concatenate([low, high])], axis=1)

        biases = gather_z(bias_row)[:, 0].astype(f32)
        z_a = gather_z(bundle_a)
        full_a = gather_planes(z_a)
        w_qkv = flat(full_a[:, :, : 3 * head_cols])
        w_o = flat(full_a[:, :, 3 * head_cols :])
        w_1 = flat(gather_planes(gather_z(bundle_b)))
        w_2 = flat(gather_planes(gather_z(bundle_c)))

        zeros_k = jnp.zeros((n_t, head_cols), f32)
        qkv_bias = jnp.concatenate(
            [biases[:, :head_cols], zeros_k, biases[:, head_cols : 2 * head_cols]], axis=1
        ).reshape(1, -1)
        in_bias = biases[:, 2 * head_cols :].reshape(1, -1)

        own_x = to_chip(inputs)
        x_full = both_rows(own_x)
        qkv = ((nn(x_full, w_qkv) + qkv_bias) * qkv_scale).astype(bf16)
        context, lse = attend_fwd(qkv, key_bias)
        attended = own_sum(nt(context, w_o))
        normed_one, inverse_one = normalize(own_x.astype(f32) + attended + out_bias)
        first_norm = normed_one * gain_first + shift_first
        first_full = both_rows(first_norm.astype(bf16))
        pre_act = nn(first_full, w_1) + in_bias
        activated, slope = gelu_and_slope(pre_act)
        hidden = activated.astype(bf16)
        mixed = own_sum(nt(hidden, w_2))
        normed_two, inverse_two = normalize(first_norm + mixed + back_bias)
        second = normed_two * gain_second + shift_second
        layer_out = from_chip(jnp.where(own_valid, second, 0.0).astype(bf16))

        grad_second = jnp.where(own_valid, to_chip(cotangent).astype(f32), 0.0)
        grad_mixed = normalize_back(grad_second, gain_second, normed_two, inverse_two)

    grad_mixed_full = both_rows(grad_mixed.astype(bf16))
    grad_w2 = tn(grad_mixed_full, hidden)
    grad_pre_low = (nn(grad_mixed_full, w_2) * slope.astype(f32)).astype(bf16)
    grad_w1 = tn(first_full, grad_pre_low)
    grad_first = grad_mixed + own_sum(nt(grad_pre_low, w_1))
    grad_att = normalize_back(grad_first, gain_first, normed_one, inverse_one)
    grad_att_full = both_rows(grad_att.astype(bf16))
    grad_context = nn(grad_att_full, w_o).astype(bf16)
    grad_wo = tn(grad_att_full, context)
    grad_qkv = attend_bwd(qkv, grad_context, lse, key_bias)
    grad_qkv = grad_qkv * qkv_scale.astype(bf16)
    grad_wqkv = tn(x_full, grad_qkv)
    grad_rows = grad_att + own_sum(nt(grad_qkv, w_qkv))
    grad_inputs = from_chip(grad_rows.astype(bf16)).astype(f32)

    def scatter(grad):
        cols = grad.shape[1] // n_t
        if quad:
            rows = width // 4
            blocks = grad.reshape(4, rows, n_t, cols).transpose(0, 2, 1, 3)
            half = n_t // 2
            low = lax.ppermute(blocks[3, :half].astype(bf16), "plane", x_pairs)
            high = lax.ppermute(blocks[3, half:].astype(bf16), "plane", y_pairs)
            for_y = jnp.concatenate([blocks[2, :half] + low.astype(f32), blocks[2, half:]])
            for_x = jnp.concatenate([blocks[1, :half], blocks[1, half:] + high.astype(f32)])
            from_x = lax.ppermute(for_x.astype(bf16), "plane", x_pairs)
            from_y = lax.ppermute(for_y.astype(bf16), "plane", y_pairs)
            mine = blocks[0] + from_x.astype(f32) + from_y.astype(f32)
        else:
            blocks = grad.reshape(width, n_t, cols).transpose(1, 0, 2)
            mine = lax.psum_scatter(
                blocks.astype(bf16), "plane", scatter_dimension=1, tiled=True
            ).astype(f32)
        back = [(b, a) for a, b in ring]
        total = mine[n_t - 1]
        for j in range(n_t - 2, -1, -1):
            total = mine[j] + lax.ppermute(total.astype(bf16), "tensor", back).astype(f32)
        return total

    home_c = scatter(grad_w2)
    home_b = scatter(grad_w1)
    grad_a = jnp.concatenate(
        [
            grad_wqkv.reshape(width, n_t, 3 * head_cols),
            grad_wo.reshape(width, n_t, head_cols),
        ],
        axis=2,
    ).reshape(width, -1)
    home_a = scatter(grad_a)
    home = jnp.concatenate([home_a, home_b, home_c], axis=1)
    home = home.reshape(2, -1, home.shape[1])
    mine = lax.dynamic_index_in_dim(home, core, 0, keepdims=False)
    other = lax.dynamic_index_in_dim(home, 1 - core, 0, keepdims=False)
    got = swap_cores(other)

    def columns(start, cols):
        return by_core(mine[:, start : start + cols], got[:, start : start + cols], axis=1)

    grad_w_query = columns(0, head_cols)
    grad_w_key = columns(head_cols, head_cols)
    grad_w_value = columns(2 * head_cols, head_cols)
    grad_w_out = columns(3 * head_cols, head_cols).T
    grad_w_in = columns(cuts[0], ff_cols)
    grad_w_back = columns(cuts[1], ff_cols).T

    def row_sum(value):
        return reorder(jnp.sum(value, axis=0), 0)

    if quad:
        second_rows = [reorder(second_sums[i], 0) for i in range(3)]
    else:
        second_rows = [
            row_sum(grad_mixed), row_sum(grad_second * normed_two), row_sum(grad_second)
        ]
    norm_sums = jnp.concatenate(
        [
            row_sum(grad_att),
            row_sum(grad_first * normed_one),
            row_sum(grad_first),
            *second_rows,
        ]
    )
    qkv_sum = jnp.sum(grad_qkv.astype(f32), axis=0).reshape(n_t, 3 * head_cols)
    pre_sum = jnp.sum(grad_pre_low.astype(f32), axis=0).reshape(n_t, ff_cols)
    bias_sum = jnp.concatenate([qkv_sum[:, :head_cols], qkv_sum[:, 2 * head_cols :], pre_sum], axis=1)
    at_home = lax.rem(place - jnp.arange(n_t) + n_t, n_t)
    spread = (at_home[:, None] == jnp.arange(n_t)[None]).astype(f32)
    by_place = jnp.sum(spread[:, :, None] * bias_sum[:, None, :], axis=0)
    both = jnp.where(
        (jnp.arange(2) == core)[None, :, None], by_place[:, None, :], 0.0
    )
    sums = lax.psum(jnp.concatenate([norm_sums, both.reshape(-1)]), ("plane", "core", "tensor"))
    norms = sums[: 6 * width].reshape(6, width)
    biases_out = lax.dynamic_index_in_dim(
        sums[6 * width :].reshape(n_t, 2, -1), place, 0, keepdims=False
    )
    grad_b_query = biases_out[:, :head_cols].reshape(-1)
    grad_b_value = biases_out[:, head_cols : 2 * head_cols].reshape(-1)
    grad_b_in = biases_out[:, 2 * head_cols :].reshape(-1)
    return (
        layer_out,
        grad_inputs,
        grad_w_query,
        grad_w_key,
        grad_w_value,
        grad_b_query,
        grad_b_value,
        grad_w_out,
        norms[0],
        norms[1],
        norms[2],
        grad_w_in,
        grad_b_in,
        grad_w_back,
        norms[3],
        norms[4],
        norms[5],
    )


def solution(mesh):
    devices = mesh.devices.reshape(mesh.shape["dp"] // 2, 2, mesh.shape["tensor"])
    inner = Mesh(devices, ("plane", "core", "tensor"))
    dp = ("plane", "core")
    row = P(dp, "tensor")
    column = P("tensor", dp)
    rows3 = P(dp, "tensor", None)
    shard = P("tensor")
    whole = P()
    return jax.shard_map(
        on_device,
        mesh=inner,
        in_specs=(
            rows3, P(dp), row, row, row, shard, shard, column, whole, whole, whole,
            row, shard, column, whole, whole, whole, rows3,
        ),
        out_specs=(
            rows3, rows3, row, row, row, shard, shard, column, whole, whole, whole,
            row, shard, column, whole, whole, whole,
        ),
        check_vma=False,
    )
```

```python
import jax
import jax.numpy as jnp
from jax import lax
from jax.experimental import pallas as pl
from jax.experimental.pallas import tpu as pltpu
from jax.sharding import Mesh, PartitionSpec as P

HD = 64
EPSILON = 1e-05
NEGATIVE = -1e30
f32 = jnp.float32
bf16 = jnp.bfloat16
SWAP = [(0, 1), (1, 0)]


def nt(a, b):
    return lax.dot_general(a, b, (((1,), (1,)), ((), ())), preferred_element_type=f32)


def tn(a, b):
    return lax.dot_general(a, b, (((0,), (0,)), ((), ())), preferred_element_type=f32)


def nn(a, b):
    return lax.dot_general(a, b, (((1,), (0,)), ((), ())), preferred_element_type=f32)


def attend_fwd_kernel(block, qkv_ref, kb_ref, ctx_ref, lse_ref):
    rows = qkv_ref.shape[0]
    lane = lax.broadcasted_iota(jnp.int32, (1, 2 * HD), 1)
    keys = qkv_ref[:, 2 * HD : 4 * HD]
    values_t = qkv_ref[:, 4 * HD : 6 * HD].T
    key_bias = kb_ref[...]
    for start in range(0, rows, block):
        query = qkv_ref[start : start + block, 0 : 2 * HD]
        parts = []
        for h in range(2):
            query_h = jnp.where(lane // HD == h, query, jnp.zeros_like(query))
            scores = nt(keys, query_h) + key_bias
            largest = jnp.max(scores, axis=0, keepdims=True)
            weights = jnp.exp(scores - largest)
            total = jnp.sum(weights, axis=0, keepdims=True)
            part = nn(values_t[h * HD : (h + 1) * HD], weights.astype(bf16))
            parts.append(part / total)
            lse_ref[0, h : h + 1, start : start + block] = largest + jnp.log(total)
        ctx_ref[start : start + block, :] = jnp.concatenate(parts, axis=0).T.astype(bf16)


def attend_fwd(qkv, key_bias):
    rows = qkv.shape[0]
    groups = qkv.shape[1] // (6 * HD)
    block = min(512, rows)
    return pl.pallas_call(
        lambda *refs: attend_fwd_kernel(block, *refs),
        grid=(groups,),
        in_specs=[
            pl.BlockSpec((rows, 6 * HD), lambda j: (0, j)),
            pl.BlockSpec((rows, 1), lambda j: (0, 0)),
        ],
        out_specs=[
            pl.BlockSpec((rows, 2 * HD), lambda j: (0, j)),
            pl.BlockSpec((1, 2, rows), lambda j: (j, 0, 0)),
        ],
        out_shape=[
            jax.ShapeDtypeStruct((rows, groups * 2 * HD), bf16),
            jax.ShapeDtypeStruct((groups, 2, rows), f32),
        ],
        compiler_params=pltpu.CompilerParams(vmem_limit_bytes=48 << 20),
        cost_estimate=pl.CostEstimate(
            flops=groups * 8 * rows * rows * HD * 4,
            bytes_accessed=rows * groups * 8 * HD * 2,
            transcendentals=groups * 2 * rows * rows,
        ),
        name="attend_fwd",
    )(qkv, key_bias)


def attend_bwd_kernel(block, qkv_ref, g_ref, lse_ref, kb_ref, d_ref, dk_acc, dv_acc):
    rows = qkv_ref.shape[0]
    lane = lax.broadcasted_iota(jnp.int32, (1, 2 * HD), 1)
    keys = qkv_ref[:, 2 * HD : 4 * HD]
    keys_t = keys.T
    values = qkv_ref[:, 4 * HD : 6 * HD]
    key_bias = kb_ref[...]
    for start in range(0, rows, block):
        query = qkv_ref[start : start + block, 0 : 2 * HD]
        grad = g_ref[start : start + block, :]
        parts = []
        for h in range(2):
            here = lane // HD == h
            query_h = jnp.where(here, query, jnp.zeros_like(query))
            grad_h = jnp.where(here, grad, jnp.zeros_like(grad))
            scores = nt(keys, query_h) + key_bias
            chances = jnp.exp(scores - lse_ref[0, h : h + 1, start : start + block])
            grad_chances = nt(values, grad_h)
            inner = jnp.sum(chances * grad_chances, axis=0, keepdims=True)
            grad_scores = (chances * (grad_chances - inner)).astype(bf16)
            dv = nn(chances.astype(bf16), grad_h)
            dk = nn(grad_scores, query_h)
            if start == 0 and h == 0:
                dv_acc[...] = dv
                dk_acc[...] = dk
            else:
                dv_acc[...] += dv
                dk_acc[...] += dk
            parts.append(nn(keys_t[h * HD : (h + 1) * HD], grad_scores))
        d_ref[start : start + block, 0 : 2 * HD] = jnp.concatenate(parts, axis=0).T.astype(bf16)
    d_ref[:, 2 * HD : 4 * HD] = dk_acc[...].astype(bf16)
    d_ref[:, 4 * HD : 6 * HD] = dv_acc[...].astype(bf16)


def attend_bwd(qkv, grad_context, lse, key_bias):
    rows = qkv.shape[0]
    groups = qkv.shape[1] // (6 * HD)
    block = min(512, rows)
    return pl.pallas_call(
        lambda *refs: attend_bwd_kernel(block, *refs),
        grid=(groups,),
        in_specs=[
            pl.BlockSpec((rows, 6 * HD), lambda j: (0, j)),
            pl.BlockSpec((rows, 2 * HD), lambda j: (0, j)),
            pl.BlockSpec((1, 2, rows), lambda j: (j, 0, 0)),
            pl.BlockSpec((rows, 1), lambda j: (0, 0)),
        ],
        out_specs=pl.BlockSpec((rows, 6 * HD), lambda j: (0, j)),
        out_shape=jax.ShapeDtypeStruct((rows, groups * 6 * HD), bf16),
        scratch_shapes=[pltpu.VMEM((rows, 2 * HD), f32), pltpu.VMEM((rows, 2 * HD), f32)],
        compiler_params=pltpu.CompilerParams(vmem_limit_bytes=48 << 20),
        cost_estimate=pl.CostEstimate(
            flops=groups * 20 * rows * rows * HD * 4,
            bytes_accessed=rows * groups * 14 * HD * 2,
            transcendentals=groups * 2 * rows * rows,
        ),
        name="attend_bwd",
    )(qkv, grad_context, lse, key_bias)

POLY = (
    0.30995978221815235,
    0.31100346478903146,
    0.2699660979585953,
    0.2765467936611628,
    -0.03831584737802812,
    0.38967711658103854,
    -0.3554874111653827,
    0.08996434684501212,
)
POLY_AT = 0.31
DENSITY = 0.3989422804014327
MESH = pl.DeviceIdType.MESH


def gelu_and_slope(v):
    density = jnp.exp(-0.5 * v * v) * DENSITY
    t = 1.0 / (1.0 + POLY_AT * jnp.abs(v))
    tail = jnp.full_like(v, POLY[-1])
    for coefficient in POLY[-2::-1]:
        tail = tail * t + coefficient
    tail = tail * t * density
    below = jnp.where(v > 0, 1.0 - tail, tail)
    return v * below, below + v * density


def forward_kernel(
    length_ref, xp_ref, cp_ref, keep_ref, give_ref, bias_in_ref, vec_ref,
    w_out, xf_out, qkv_out, lse_ref, ctx_out, ff_out, hid_out, dg_out, n1_out, inv1_ref, gm_ref,
    lo_ref, sums_ref,
    w, xf, bias, qkv, ctx, ff, hid, dg, n1, first, other_part, own_part, att_got, mix_got, cot, lo_own,
    z_s, z_r, x_s, x_r, y_s, y_r, f_s, f_r, pre_l, pre_s, pre_r, b_s, b_r,
    xa_s, xa_r, ca_s, ca_r, la_s, la_r, e_s, e_r, o_s,
):
    plane = lax.axis_index("plane")
    core = lax.axis_index("core")
    place = lax.axis_index("tensor")
    partner = {"core": 1 - core}
    x_side = {"plane": plane + 1 - 2 * (plane % 2)}
    y_side = {"plane": (plane + 2) % 4}
    z_next = {"tensor": (place + 1) % 4}
    rows = xf.shape[0]
    own = rows // 2
    part = own // 4
    piece = w.shape[2] // 4

    def remote(source, target, send, recv, to):
        return pltpu.make_async_remote_copy(
            source, target, send, recv, device_id=to, device_id_type=MESH
        )

    def z_copy(b, s):
        return remote(
            w.at[b, s, 0:piece], w.at[b, s + 1, 0:piece], z_s.at[b, s], z_r.at[b, s], z_next
        )

    def x_copy(b, j):
        return remote(
            w.at[b, j, 0:piece], w.at[b, j, piece : 2 * piece], x_s.at[b, j], x_r.at[b, j], x_side
        )

    def y_copy(b, j):
        return remote(
            w.at[b, j, 0:piece], w.at[b, j, 2 * piece : 3 * piece], y_s.at[b, j], y_r.at[b, j], y_side
        )

    def f_copy(b, j):
        start = 2 * piece if j < 2 else piece
        return remote(
            w.at[b, j, start : start + piece],
            w.at[b, j, 3 * piece : 4 * piece],
            f_s.at[b, j],
            f_r.at[b, j],
            x_side if j < 2 else y_side,
        )

    def pre_copy(b):
        rows_at = pl.ds(core * (piece // 2), piece // 2)
        return remote(give_ref.at[b], w.at[b, 0, rows_at], pre_s.at[b], pre_r.at[b], partner)

    def pre_got(b):
        rows_at = pl.ds((1 - core) * (piece // 2), piece // 2)
        return remote(give_ref.at[b], w.at[b, 0, rows_at], pre_s.at[b], pre_r.at[b], partner)

    def keep_copy(b):
        rows_at = pl.ds(core * (piece // 2), piece // 2)
        return pltpu.make_async_copy(keep_ref.at[b], w.at[b, 0, rows_at], pre_l.at[b])

    def bias_copy(s):
        return remote(
            bias.at[0], bias.at[s], b_s.at[s], b_r.at[s], {"tensor": (place + s) % 4}
        )

    def spread(source, target, send, recv, l, h):
        at = pl.ds(place * part, part)
        to = {"core": h, "tensor": 2 * core + l}
        return remote(
            source.at[2 * l + h], target.at[at], send.at[2 * l + h], recv.at[place], to
        )

    def spread_local(source, target, recv, l, h):
        at = pl.ds(place * part, part)
        return pltpu.make_async_copy(source.at[2 * l + h], target.at[at], recv.at[place])

    def is_here(l, h):
        return jnp.logical_and(core == h, place == 2 * core + l)

    def spread_start(source, target, send, recv):
        for l in range(2):
            for h in range(2):
                @pl.when(is_here(l, h))
                def _():
                    spread_local(source, target, recv, l, h).start()

                @pl.when(jnp.logical_not(is_here(l, h)))
                def _():
                    spread(source, target, send, recv, l, h).start()

    def spread_wait(source, target, recv):
        for s in range(4):
            pltpu.make_async_copy(
                source.at[s], target.at[s * part : (s + 1) * part], recv.at[s]
            ).wait()

    def spread_sent(source, target, send, recv):
        for l in range(2):
            for h in range(2):
                @pl.when(jnp.logical_not(is_here(l, h)))
                def _():
                    spread(source, target, send, recv, l, h).wait_send()

    def home(s):
        to = {"core": place // 2, "tensor": s}
        return remote(
            lo_own.at[s * part : (s + 1) * part],
            lo_ref.at[2 * (place % 2) + core],
            la_s.at[s],
            la_r.at[2 * (place % 2) + core],
            to,
        )

    def home_local(s):
        return pltpu.make_async_copy(
            lo_own.at[s * part : (s + 1) * part],
            lo_ref.at[2 * (place % 2) + core],
            la_r.at[2 * (place % 2) + core],
        )

    def is_home(s):
        return jnp.logical_and(core == place // 2, place == s)

    def exchange(source, target, n):
        return remote(source, target, e_s.at[n], e_r.at[n], partner)

    outs = []

    def save(source, target):
        copy = pltpu.make_async_copy(source, target, o_s.at[len(outs)])
        copy.start()
        outs.append(copy)

    barrier = pltpu.get_barrier_semaphore()
    friends = [x_side, y_side, partner]
    for s in range(1, 4):
        friends.append({"tensor": (place + s) % 4})
        friends.append({"tensor": (place + s) % 4, "core": 1 - core})
    for friend in friends:
        pl.semaphore_signal(barrier, inc=1, device_id=friend, device_id_type=MESH)
    keep_all = [keep_copy(b) for b in range(3)]
    for copy in keep_all:
        copy.start()
    pl.semaphore_wait(barrier, len(friends))

    for b in range(3):
        pre_copy(b).start()
    bias[0] = bias_in_ref[...]
    spread_start(xp_ref, xf, xa_s, xa_r)
    keep_all[0].wait()
    pre_got(0).wait_recv()
    z_copy(0, 0).start()
    x_copy(0, 0).start()
    y_copy(0, 0).start()
    for s in range(1, 4):
        bias_copy(s).start()
    for b in (1, 2):
        keep_all[b].wait()
        pre_got(b).wait_recv()
        x_copy(b, 0).start()
        y_copy(b, 0).start()
    z_copy(0, 0).wait_recv()
    z_copy(0, 1).start()
    x_copy(0, 1).start()
    y_copy(0, 1).start()
    y_copy(0, 0).wait_recv()
    f_copy(0, 0).start()
    z_copy(0, 1).wait_recv()
    z_copy(0, 2).start()
    x_copy(0, 2).start()
    y_copy(0, 2).start()
    z_copy(0, 2).wait_recv()
    z_copy(1, 0).start()
    z_copy(2, 0).start()
    x_copy(0, 3).start()
    y_copy(0, 3).start()

    spread_wait(xp_ref, xf, xa_r)
    share_x = exchange(xf.at[0:own], xf.at[own : 2 * own], 0)
    share_x.start()
    y_copy(0, 1).wait_recv()
    f_copy(0, 1).start()
    y_copy(1, 0).wait_recv()
    f_copy(1, 0).start()
    y_copy(2, 0).wait_recv()
    f_copy(2, 0).start()
    for s in range(1, 4):
        bias_copy(s).wait_recv()
    share_x.wait_recv()
    save(xf, xf_out)

    index = lax.broadcasted_iota(jnp.int32, (rows, 1), 0)
    length = length_ref[0]
    half = jnp.where(index < own, core, 1 - core)
    inside = index % own
    position = (inside // part) * (2 * part) + half * part + inside % part
    key_bias = jnp.where(position < length, 0.0, NEGATIVE).astype(f32)
    lane = lax.broadcasted_iota(jnp.int32, (1, 2 * HD), 1)
    head_cols = 2 * HD
    tile = 256

    def project(j):
        columns = lax.broadcasted_iota(jnp.int32, (1, 3 * head_cols), 1)
        zero = jnp.zeros((1, head_cols), f32)
        add = jnp.concatenate(
            [bias[j, 0:1, 0:head_cols], zero, bias[j, 0:1, head_cols : 2 * head_cols]], axis=1
        )
        times = jnp.where(columns < head_cols, HD ** (-0.5), 1.0).astype(f32)

        def body(i, _):
            at = pl.ds(pl.multiple_of(i * tile, tile), tile)
            value = nn(xf[at, :], w[0, j, :, 0 : 3 * head_cols])
            qkv[j, at, :] = ((value + add) * times).astype(bf16)
            return 0

        lax.fori_loop(0, rows // tile, body, 0)
        save(qkv.at[j], qkv_out.at[j])

    def attend(j):
        keys = qkv[j, :, head_cols : 2 * head_cols]
        values_t = qkv[j, :, 2 * head_cols : 3 * head_cols].T

        def body(i, _):
            at = pl.ds(pl.multiple_of(i * tile, tile), tile)
            query = qkv[j, at, 0:head_cols]
            parts = []
            for h in range(2):
                query_h = jnp.where(lane // HD == h, query, jnp.zeros_like(query))
                scores = nt(keys, query_h) + key_bias
                largest = jnp.max(scores, axis=0, keepdims=True)
                weights = jnp.exp(scores - largest)
                total = jnp.sum(weights, axis=0, keepdims=True)
                out = nn(values_t[h * HD : (h + 1) * HD], weights.astype(bf16))
                parts.append(out / total)
                lse_ref[2 * j + h, :, at] = largest + jnp.log(total)
            ctx[j, at, :] = jnp.concatenate(parts, axis=0).T.astype(bf16)
            return 0

        lax.fori_loop(0, rows // tile, body, 0)
        save(ctx.at[j], ctx_out.at[j])

    def ready(b, j):
        x_copy(b, j).wait_recv() if not (b, j, "x") in seen else None
        seen.add((b, j, "x"))
        y_copy(b, j).wait_recv() if not (b, j, "y") in seen else None
        seen.add((b, j, "y"))
        f_copy(b, j).wait_recv()
        save(w.at[b, j], w_out.at[b, j])

    seen = {(0, 0, "y"), (0, 1, "y"), (1, 0, "y"), (2, 0, "y")}

    def forward_on(b, j):
        side = "y" if j < 2 else "x"
        (y_copy if j < 2 else x_copy)(b, j).wait_recv()
        seen.add((b, j, side))
        f_copy(b, j).start()

    ready(0, 0)
    project(0)
    attend(0)
    forward_on(0, 2)
    z_copy(1, 0).wait_recv()
    z_copy(1, 1).start()
    x_copy(1, 1).start()
    y_copy(1, 1).start()
    forward_on(0, 3)
    z_copy(2, 0).wait_recv()
    z_copy(2, 1).start()
    ready(0, 1)
    project(1)
    attend(1)
    z_copy(1, 1).wait_recv()
    z_copy(1, 2).start()
    x_copy(1, 2).start()
    y_copy(1, 2).start()
    ready(0, 2)
    project(2)
    attend(2)
    z_copy(2, 1).wait_recv()
    z_copy(2, 2).start()
    forward_on(1, 1)
    ready(0, 3)
    project(3)
    attend(3)
    z_copy(1, 2).wait_recv()
    x_copy(1, 3).start()
    y_copy(1, 3).start()
    forward_on(1, 2)

    def out_rows(start, target):
        def body(i, _):
            at = pl.ds(pl.multiple_of(start + i * tile, tile), tile)
            to = pl.ds(pl.multiple_of(i * tile, tile), tile)
            total = nt(ctx[0, at, :], w[0, 0, :, 3 * head_cols :])
            for j in range(1, 4):
                total += nt(ctx[j, at, :], w[0, j, :, 3 * head_cols :])
            target[to, :] = total
            return 0

        lax.fori_loop(0, own // tile, body, 0)

    out_rows(own, other_part)
    share_att = exchange(other_part, att_got, 1)
    share_att.start()
    out_rows(0, own_part)
    x_copy(2, 1).start()
    y_copy(2, 1).start()
    spread_start(cp_ref, cot, ca_s, ca_r)
    share_att.wait_recv()
    small = 32

    def mean(value):
        return jnp.sum(value, axis=-1, keepdims=True) * (1.0 / value.shape[-1])

    def first_body(i, _):
        at = pl.ds(pl.multiple_of(i * small, small), small)
        total = xf[at, :].astype(f32) + (own_part[at, :] + att_got[at, :]) + vec_ref[0:1, :]
        centered = total - mean(total)
        inverse = lax.rsqrt(mean(centered * centered) + EPSILON)
        normed = centered * inverse
        n1[at, :] = normed
        inv1_ref[at, :] = inverse
        value = normed * vec_ref[1:2, :] + vec_ref[2:3, :]
        first[at, :] = value
        ff[at, :] = value.astype(bf16)
        return 0

    lax.fori_loop(0, own // small, first_body, 0)
    share_first = exchange(ff.at[0:own], ff.at[own : 2 * own], 2)
    share_first.start()
    save(n1, n1_out)
    forward_on(1, 3)
    z_copy(2, 2).wait_recv()
    for j in (2, 3):
        x_copy(2, j).start()
        y_copy(2, j).start()
    share_first.wait_recv()
    save(ff, ff_out)

    def expand(j):
        add = bias[j, 0:1, 2 * head_cols :]

        def body(i, _):
            at = pl.ds(pl.multiple_of(i * tile, tile), tile)
            value = nn(ff[at, :], w[1, j]) + add
            active, slope = gelu_and_slope(value)
            hid[j, at, :] = active.astype(bf16)
            dg[j, at, :] = slope.astype(bf16)
            return 0

        lax.fori_loop(0, rows // tile, body, 0)
        save(hid.at[j], hid_out.at[j])
        save(dg.at[j], dg_out.at[j])

    ready(1, 0)
    expand(0)
    ready(1, 1)
    expand(1)
    forward_on(2, 1)
    ready(1, 2)
    expand(2)
    forward_on(2, 2)
    ready(1, 3)
    expand(3)
    share_att.wait_send()

    def contract(js, start, target, fresh):
        def body(i, _):
            at = pl.ds(pl.multiple_of(start + i * tile, tile), tile)
            to = pl.ds(pl.multiple_of(i * tile, tile), tile)
            total = nt(hid[js[0], at, :], w[2, js[0]])
            for j in js[1:]:
                total += nt(hid[j, at, :], w[2, j])
            target[to, :] = total if fresh else target[to, :] + total
            return 0

        lax.fori_loop(0, own // tile, body, 0)

    ready(2, 0)
    ready(2, 1)
    contract((0, 1), own, other_part, True)
    contract((0, 1), 0, own_part, True)
    forward_on(2, 3)
    ready(2, 2)
    contract((2,), own, other_part, False)
    contract((2,), 0, own_part, False)
    ready(2, 3)
    contract((3,), own, other_part, False)
    share_mix = exchange(other_part, mix_got, 3)
    share_mix.start()
    contract((3,), 0, own_part, False)
    spread_wait(cp_ref, cot, ca_r)
    share_mix.wait_recv()
    sums_ref[...] = jnp.zeros_like(sums_ref)

    def second_body(i, _):
        at = pl.ds(pl.multiple_of(i * small, small), small)
        spot = i * small + lax.broadcasted_iota(jnp.int32, (small, 1), 0)
        where = (spot // part) * (2 * part) + core * part + spot % part
        alive = where < length
        total = first[at, :] + (own_part[at, :] + mix_got[at, :]) + vec_ref[3:4, :]
        centered = total - mean(total)
        inverse = lax.rsqrt(mean(centered * centered) + EPSILON)
        normed = centered * inverse
        value = normed * vec_ref[4:5, :] + vec_ref[5:6, :]
        lo_own[at, :] = jnp.where(alive, value, 0.0).astype(bf16)
        grad = jnp.where(alive, cot[at, :].astype(f32), 0.0)
        e = grad * vec_ref[4:5, :]
        back = (e - mean(e) - normed * mean(e * normed)) * inverse
        gm_ref[at, :] = back
        sums_ref[0:1, :] += jnp.sum(back, axis=0, keepdims=True)
        sums_ref[1:2, :] += jnp.sum(grad * normed, axis=0, keepdims=True)
        sums_ref[2:3, :] += jnp.sum(grad, axis=0, keepdims=True)
        return 0

    lax.fori_loop(0, own // small, second_body, 0)
    for s in range(4):
        @pl.when(is_home(s))
        def _():
            home_local(s).start()

        @pl.when(jnp.logical_not(is_home(s)))
        def _():
            home(s).start()

    for b in range(3):
        pre_copy(b).wait_send()
        for s in range(3):
            z_copy(b, s).wait_send()
        for j in range(4):
            x_copy(b, j).wait_send()
            y_copy(b, j).wait_send()
            f_copy(b, j).wait_send()
    for s in range(1, 4):
        bias_copy(s).wait_send()
    spread_sent(xp_ref, xf, xa_s, xa_r)
    spread_sent(cp_ref, cot, ca_s, ca_r)
    share_x.wait_send()
    share_first.wait_send()
    share_mix.wait_send()
    for copy in outs:
        copy.wait()
    for s in range(4):
        @pl.when(jnp.logical_not(is_home(s)))
        def _():
            home(s).wait_send()
    for s in range(4):
        pltpu.make_async_copy(lo_own.at[0:part], lo_ref.at[s], la_r.at[s]).wait()


def forward(length, xp, cp, keep, give, bias, vec):
    part, width = xp.shape[1:]
    own = 4 * part
    rows = 2 * own
    cols = keep.shape[2]
    head_cols = 2 * HD
    any_ = pl.BlockSpec(memory_space=pltpu.HBM)
    vm = pl.BlockSpec(memory_space=pltpu.VMEM)
    sm = pl.BlockSpec(memory_space=pltpu.SMEM)
    shape = jax.ShapeDtypeStruct
    dma = pltpu.SemaphoreType.DMA
    flops = 2 * rows * width * cols * 12 + 16 * rows * rows * HD * 4
    return pl.pallas_call(
        forward_kernel,
        in_specs=[sm, any_, any_, any_, any_, vm, vm],
        out_specs=[any_, any_, any_, vm, any_, any_, any_, any_, any_, vm, vm, any_, vm],
        out_shape=[
            shape((3, 4, width, cols), bf16),
            shape((rows, width), bf16),
            shape((4, rows, 3 * head_cols), bf16),
            shape((8, 1, rows), f32),
            shape((4, rows, head_cols), bf16),
            shape((rows, width), bf16),
            shape((4, rows, cols), bf16),
            shape((4, rows, cols), bf16),
            shape((own, width), f32),
            shape((own, 1), f32),
            shape((own, width), f32),
            shape((4, part, width), bf16),
            shape((8, width), f32),
        ],
        scratch_shapes=[
            pltpu.VMEM((3, 4, width, cols), bf16),
            pltpu.VMEM((rows, width), bf16),
            pltpu.VMEM((4, 8, bias.shape[1]), f32),
            pltpu.VMEM((4, rows, 3 * head_cols), bf16),
            pltpu.VMEM((4, rows, head_cols), bf16),
            pltpu.VMEM((rows, width), bf16),
            pltpu.VMEM((4, rows, cols), bf16),
            pltpu.VMEM((4, rows, cols), bf16),
            pltpu.VMEM((own, width), f32),
            pltpu.VMEM((own, width), f32),
            pltpu.VMEM((own, width), f32),
            pltpu.VMEM((own, width), f32),
            pltpu.VMEM((own, width), f32),
            pltpu.VMEM((own, width), f32),
            pltpu.VMEM((own, width), bf16),
            pltpu.VMEM((own, width), bf16),
            dma((3, 3)), dma((3, 3)), dma((3, 4)), dma((3, 4)), dma((3, 4)), dma((3, 4)),
            dma((3, 4)), dma((3, 4)), dma((3,)), dma((3,)), dma((3,)), dma((4,)), dma((4,)),
            dma((4,)), dma((4,)), dma((4,)), dma((4,)), dma((4,)), dma((4,)),
            dma((4,)), dma((4,)), dma((32,)),
        ],
        compiler_params=pltpu.CompilerParams(
            collective_id=0, has_side_effects=True, vmem_limit_bytes=60 << 20
        ),
        cost_estimate=pl.CostEstimate(
            flops=flops, bytes_accessed=60 << 20, transcendentals=8 * rows * rows
        ),
        name="forward_layer",
    )(length, xp, cp, keep, give, bias, vec)


def backward_kernel(
    w_ref, xf_ref, qkv_ref, lse_ref, ctx_ref, ff_ref, hid_ref, dg_ref, n1_ref, inv1_ref, gm_ref,
    vec_ref, sums_ref, length_ref,
    gi_ref, mine_ref, got_ref, total_ref,
    w, grad_c, pad, pre, gmf, gaf, act, turned, gm, n1, own_part, other, got, gi_own,
    d_got, rx, ry, rz, home, dk_acc, dv_acc, vz, zg, xg, yg, cg, tot,
    d_s, d_r, x_s, x_r, y_s, y_r, z_s, z_r, h_s, h_r, h_l, e_s, e_r, g_s, g_r, v_s, v_r, l_s,
):
    plane = lax.axis_index("plane")
    core = lax.axis_index("core")
    place = lax.axis_index("tensor")
    partner = {"core": 1 - core}
    x_side = {"plane": plane + 1 - 2 * (plane % 2)}
    y_side = {"plane": (plane + 2) % 4}
    z_back = {"tensor": (place + 3) % 4}
    rows, width = gmf.shape
    own = rows // 2
    part = own // 4
    piece = width // 4
    head_cols = 2 * HD
    tile = 256
    small = 32

    def remote(source, target, send, recv, to):
        return pltpu.make_async_remote_copy(
            source, target, send, recv, device_id=to, device_id_type=MESH
        )

    def block(b, j, k):
        at = slice(k * piece, (k + 1) * piece)
        if b == 2:
            return grad_c.at[j, at]
        return w.at[b + 1, j, at]

    def d_copy(b, j):
        to = x_side if j < 2 else y_side
        return remote(block(b, j, 3), d_got.at[b, j], d_s.at[b, j], d_r.at[b, j], to)

    def x_copy(b, j):
        return remote(block(b, j, 1), rx.at[b, j], x_s.at[b, j], x_r.at[b, j], x_side)

    def y_copy(b, j):
        return remote(block(b, j, 2), ry.at[b, j], y_s.at[b, j], y_r.at[b, j], y_side)

    def z_copy(b, j):
        return remote(
            block(b, j, 0), rz.at[b, j - 1], z_s.at[b, j - 1], z_r.at[b, j - 1], z_back
        )

    def home_copy(b):
        at = pl.ds((1 - core) * (piece // 2), piece // 2)
        return remote(home.at[b, at], got_ref.at[b], h_s.at[b], h_r.at[b], partner)

    def home_keep(b):
        at = pl.ds(core * (piece // 2), piece // 2)
        return pltpu.make_async_copy(home.at[b, at], mine_ref.at[b], h_l.at[b])

    def send_first(b, j):
        d_copy(b, j).start()
        (x_copy if j < 2 else y_copy)(b, j).start()

    def send_second(b, j):
        d_copy(b, j).wait_recv()
        here = block(b, j, 2 if j < 2 else 1)
        here[...] = (here[...].astype(f32) + d_got[b, j].astype(f32)).astype(bf16)
        (y_copy if j < 2 else x_copy)(b, j).start()

    def send_third(b, j):
        x_copy(b, j).wait_recv()
        y_copy(b, j).wait_recv()
        total = block(b, j, 0)[...].astype(f32) + rx[b, j].astype(f32) + ry[b, j].astype(f32)
        if j < 3:
            z_copy(b, j + 1).wait_recv()
            total = total + rz[b, j].astype(f32)
        if j > 0:
            block(b, j, 0)[...] = total.astype(bf16)
            z_copy(b, j).start()
        else:
            home[b] = total
            home_copy(b).start()
            home_keep(b).start()

    def exchange(source, target, n):
        return remote(source, target, e_s.at[n], e_r.at[n], partner)

    def back(s):
        to = {"core": place // 2, "tensor": s}
        slot = 2 * (place % 2) + core
        return remote(
            gi_own.at[s * part : (s + 1) * part], gi_ref.at[slot], g_s.at[s], g_r.at[slot], to
        )

    def back_local(s):
        slot = 2 * (place % 2) + core
        return pltpu.make_async_copy(
            gi_own.at[s * part : (s + 1) * part], gi_ref.at[slot], g_r.at[slot]
        )

    def is_home(s):
        return jnp.logical_and(core == place // 2, place == s)

    def v_copy(j):
        to = {"tensor": (place + 4 - j) % 4}
        return remote(vz.at[j], zg.at[place], v_s.at[j - 1], v_r.at[place], to)

    def v_got(j):
        source = (place + j) % 4
        return remote(vz.at[j], zg.at[source], v_s.at[j - 1], v_r.at[source], z_back)

    coming = {}

    def fetch(name, source, target):
        copy = pltpu.make_async_copy(source, target, l_s.at[len(coming)])
        copy.start()
        coming[name] = copy

    fetch("gm", gm_ref, gm)
    for j in (3, 2, 1, 0):
        fetch(("hid", j), hid_ref.at[j], pad.at[j])
    for j in range(4):
        fetch(("w2", j), w_ref.at[2, j], w.at[2, j])
        fetch(("dg", j), dg_ref.at[j], pre.at[j])
    fetch("w1", w_ref.at[1], w.at[1])
    fetch("n1", n1_ref, n1)
    fetch("ff", ff_ref, act)
    fetch("w0", w_ref.at[0], w.at[0])

    barrier = pltpu.get_barrier_semaphore()
    friends = [x_side, y_side, partner]
    for s in range(1, 4):
        friends.append({"tensor": (place + s) % 4})
        friends.append({"tensor": (place + s) % 4, "core": 1 - core})
    for friend in friends:
        pl.semaphore_signal(barrier, inc=1, device_id=friend, device_id_type=MESH)

    coming["gm"].wait()

    def round_body(i, _):
        at = pl.ds(pl.multiple_of(i * 128, 128), 128)
        gmf[at, :] = gm[at, :].astype(bf16)
        return 0

    lax.fori_loop(0, own // 128, round_body, 0)
    pl.semaphore_wait(barrier, len(friends))
    share_gm = exchange(gmf.at[0:own], gmf.at[own : 2 * own], 0)
    share_gm.start()
    vz[...] = jnp.zeros_like(vz)

    def turn(source, first, last):
        def body(i, _):
            at = pl.ds(pl.multiple_of(i * tile, tile), tile)
            turned[:, at] = source[at, :].T
            return 0

        lax.fori_loop(first, last, body, 0)

    def weight_grad(b, j, right, columns):
        def body(k, _):
            at = pl.ds(pl.multiple_of(k * tile, tile), tile)
            value = nn(turned[at, :], right()).astype(bf16)
            if b == 2:
                grad_c[j, at, columns] = value
            else:
                w[b + 1, j, at, columns] = value
            return 0

        lax.fori_loop(0, width // tile, body, 0)

    every = slice(None)
    turn(gmf, 0, own // tile)
    share_gm.wait_recv()
    turn(gmf, own // tile, rows // tile)
    for j in (3, 2, 1, 0):
        coming[("hid", j)].wait()
        weight_grad(2, j, lambda: pad[j], every)
        send_first(2, j)

    def slope_rows(j):
        coming[("w2", j)].wait()
        coming[("dg", j)].wait()

        def body(i, _):
            at = pl.ds(pl.multiple_of(i * tile, tile), tile)
            value = (nn(gmf[at, :], w[2, j]) * pre[j, at, :].astype(f32)).astype(bf16)
            pre[j, at, :] = value
            vz[j, 8:9, 2 * head_cols : 2 * head_cols + value.shape[1]] += jnp.sum(
                value.astype(f32), axis=0, keepdims=True
            )
            return 0

        lax.fori_loop(0, rows // tile, body, 0)

    slope_rows(0)
    slope_rows(1)
    send_second(2, 3)
    slope_rows(2)
    send_second(2, 2)
    slope_rows(3)
    send_second(2, 1)
    for j in range(4):
        fetch(("ctx", j), ctx_ref.at[j], pad.at[j, :, pl.ds(3 * head_cols, head_cols)])
    coming["w1"].wait()

    def first_rows(start, target):
        def body(i, _):
            at = pl.ds(pl.multiple_of(start + i * tile, tile), tile)
            to = pl.ds(pl.multiple_of(i * tile, tile), tile)
            total = nt(pre[0, at, :], w[1, 0])
            for j in range(1, 4):
                total += nt(pre[j, at, :], w[1, j])
            target[to, :] = total.astype(target.dtype)
            return 0

        lax.fori_loop(0, own // tile, body, 0)

    first_rows(own, other)
    share_first = exchange(other, got, 1)
    share_first.start()
    first_rows(0, own_part)
    send_second(2, 0)
    coming["n1"].wait()
    share_first.wait_recv()

    def mean(value):
        return jnp.sum(value, axis=-1, keepdims=True) * (1.0 / value.shape[-1])

    def norm_body(i, _):
        at = pl.ds(pl.multiple_of(i * small, small), small)
        grad = gm[at, :] + (own_part[at, :] + got[at, :].astype(f32))
        normed = n1[at, :]
        e = grad * vec_ref[1:2, :]
        value = (e - mean(e) - normed * mean(e * normed)) * inv1_ref[at, :]
        gm[at, :] = value
        gaf[at, :] = value.astype(bf16)
        vz[0, 0:1, :] += jnp.sum(value, axis=0, keepdims=True)
        vz[0, 1:2, :] += jnp.sum(grad * normed, axis=0, keepdims=True)
        vz[0, 2:3, :] += jnp.sum(grad, axis=0, keepdims=True)
        return 0

    lax.fori_loop(0, own // small, norm_body, 0)
    share_att = exchange(gaf.at[0:own], gaf.at[own : 2 * own], 2)
    share_att.start()
    vz[0, 3:6, :] = sums_ref[0:3, :]
    for j in range(1, 4):
        vz[j, 0:8, :] = vz[0, 0:8, :]
    coming["ff"].wait()
    turn(act, 0, rows // tile)
    fetch("xf", xf_ref, act)
    weight_grad(1, 3, lambda: pre[3], every)
    send_first(1, 3)
    weight_grad(1, 2, lambda: pre[2], every)
    send_first(1, 2)
    send_third(2, 3)
    weight_grad(1, 1, lambda: pre[1], every)
    send_first(1, 1)
    weight_grad(1, 0, lambda: pre[0], every)
    send_first(1, 0)
    for j in range(4):
        fetch(("qkv", j), qkv_ref.at[j], pre.at[j, :, pl.ds(0, 3 * head_cols)])
    send_third(2, 2)
    share_att.wait_recv()
    turn(gaf, 0, rows // tile)
    coming["w0"].wait()
    last = slice(3 * head_cols, 4 * head_cols)

    def context_rows(j):
        def body(i, _):
            at = pl.ds(pl.multiple_of(i * tile, tile), tile)
            pre[j, at, last] = nn(gaf[at, :], w[0, j, :, last]).astype(bf16)
            return 0

        lax.fori_loop(0, rows // tile, body, 0)

    for j in (3, 2, 1, 0):
        context_rows(j)
        coming[("ctx", j)].wait()
        weight_grad(0, j, lambda: pad[j, :, last], last)
        if j == 2:
            send_third(2, 1)
    send_third(2, 0)
    coming["xf"].wait()
    turn(act, 0, rows // tile)
    send_second(1, 3)
    send_second(1, 2)

    index = lax.broadcasted_iota(jnp.int32, (rows, 1), 0)
    half = jnp.where(index < own, core, 1 - core)
    inside = index % own
    position = (inside // part) * (2 * part) + half * part + inside % part
    key_bias = jnp.where(position < length_ref[0], 0.0, NEGATIVE).astype(f32)
    lane = lax.broadcasted_iota(jnp.int32, (1, head_cols), 1)
    front = slice(0, 3 * head_cols)

    def attend_back(j):
        keys = pre[j, :, head_cols : 2 * head_cols]
        keys_t = keys.T
        values = pre[j, :, 2 * head_cols : 3 * head_cols]
        dk_acc[...] = jnp.zeros_like(dk_acc)
        dv_acc[...] = jnp.zeros_like(dv_acc)

        def body(i, _):
            at = pl.ds(pl.multiple_of(i * tile, tile), tile)
            query = pre[j, at, 0:head_cols]
            grad = pre[j, at, last]
            parts = []
            for h in range(2):
                here = lane // HD == h
                query_h = jnp.where(here, query, jnp.zeros_like(query))
                grad_h = jnp.where(here, grad, jnp.zeros_like(grad))
                scores = nt(keys, query_h) + key_bias
                chances = jnp.exp(scores - lse_ref[2 * j + h, :, at])
                grad_chances = nt(values, grad_h)
                inner = jnp.sum(chances * grad_chances, axis=0, keepdims=True)
                grad_scores = (chances * (grad_chances - inner)).astype(bf16)
                dv_acc[...] += nn(chances.astype(bf16), grad_h)
                dk_acc[...] += nn(grad_scores, query_h)
                parts.append(nn(keys_t[h * HD : (h + 1) * HD], grad_scores))
            low = jnp.concatenate(parts, axis=0).T.astype(bf16).astype(f32) * HD ** (-0.5)
            pad[j, at, 0:head_cols] = low.astype(bf16)
            vz[j, 8:9, 0:head_cols] += jnp.sum(low, axis=0, keepdims=True)
            return 0

        lax.fori_loop(0, rows // tile, body, 0)
        pad[j, :, head_cols : 2 * head_cols] = dk_acc[...].astype(bf16)
        low = dv_acc[...].astype(bf16)
        pad[j, :, 2 * head_cols : 3 * head_cols] = low
        vz[j, 8:9, head_cols : 2 * head_cols] = jnp.sum(low.astype(f32), axis=0, keepdims=True)

    for j in (3, 2, 1, 0):
        coming[("qkv", j)].wait()
        attend_back(j)
        if j == 3:
            send_second(1, 1)
            send_second(1, 0)
        weight_grad(0, j, lambda: pad[j, :, front], front)
        send_first(0, j)
        if j == 1:
            send_third(1, 3)
    for j in range(1, 4):
        v_copy(j).start()
    zg[place] = vz[0]
    send_third(1, 2)

    def input_rows(start, target):
        def body(i, _):
            at = pl.ds(pl.multiple_of(start + i * tile, tile), tile)
            to = pl.ds(pl.multiple_of(i * tile, tile), tile)
            total = nt(pad[0, at, front], w[0, 0, :, front])
            for j in range(1, 4):
                total += nt(pad[j, at, front], w[0, j, :, front])
            target[to, :] = total.astype(target.dtype)
            return 0

        lax.fori_loop(0, own // tile, body, 0)

    share_first.wait_send()
    input_rows(own, other)
    share_in = exchange(other, got, 3)
    share_in.start()
    send_third(1, 1)
    send_second(0, 3)
    send_second(0, 2)
    input_rows(0, own_part)
    send_third(1, 0)
    share_in.wait_recv()

    def input_body(i, _):
        at = pl.ds(pl.multiple_of(i * small, small), small)
        value = gm[at, :] + (own_part[at, :] + got[at, :].astype(f32))
        gi_own[at, :] = value.astype(bf16)
        return 0

    lax.fori_loop(0, own // small, input_body, 0)
    for s in range(4):
        @pl.when(is_home(s))
        def _():
            back_local(s).start()

        @pl.when(jnp.logical_not(is_home(s)))
        def _():
            back(s).start()

    def fold(n, m, arrived, flip):
        for k in range(4):
            here = slice(k * piece, (k + 1) * piece)
            there = slice((k ^ flip) * piece, ((k ^ flip) + 1) * piece)
            tot[n, 0:8, here] = tot[m, 0:8, here] + arrived[0:8, there]
        tot[n, 8:16, :] = tot[m, 8:16, :] + arrived[8:16, :]

    for j in range(1, 4):
        v_got(j).wait_recv()
    tot[0] = ((zg[0] + zg[1]) + zg[2]) + zg[3]
    v_x = remote(tot.at[0], xg, e_s.at[4], e_r.at[4], x_side)
    v_x.start()
    send_second(0, 1)
    send_second(0, 0)
    v_x.wait_recv()
    fold(1, 0, xg, 1)
    v_y = remote(tot.at[1], yg, e_s.at[5], e_r.at[5], y_side)
    v_y.start()
    send_third(0, 3)
    v_y.wait_recv()
    fold(2, 1, yg, 2)
    v_c = exchange(tot.at[2], cg, 6)
    v_c.start()
    send_third(0, 2)
    send_third(0, 1)
    send_third(0, 0)
    v_c.wait_recv()
    total_ref[0] = tot[2]
    total_ref[1] = cg[...]

    for b in range(3):
        for j in range(4):
            d_copy(b, j).wait_send()
            x_copy(b, j).wait_send()
            y_copy(b, j).wait_send()
            if j > 0:
                z_copy(b, j).wait_send()
        home_keep(b).wait()
        home_copy(b).wait_send()
        home_copy(b).wait_recv()
    for j in range(1, 4):
        v_copy(j).wait_send()
    for copy in (share_gm, share_att, share_in, v_x, v_y, v_c):
        copy.wait_send()
    for s in range(4):
        @pl.when(jnp.logical_not(is_home(s)))
        def _():
            back(s).wait_send()
    for s in range(4):
        pltpu.make_async_copy(gi_own.at[0:part], gi_ref.at[s], g_r.at[s]).wait()


def backward(w_all, xf, qkv, lse, ctx, ff, hid, dg, n1, inv1, gm, vec, sums, length):
    rows, width = xf.shape
    own = rows // 2
    part = own // 4
    piece = width // 4
    cols = hid.shape[2]
    head_cols = 2 * HD
    any_ = pl.BlockSpec(memory_space=pltpu.HBM)
    vm = pl.BlockSpec(memory_space=pltpu.VMEM)
    sm = pl.BlockSpec(memory_space=pltpu.SMEM)
    shape = jax.ShapeDtypeStruct
    dma = pltpu.SemaphoreType.DMA
    flops = 2 * rows * width * cols * 24 + 40 * rows * rows * HD * 4
    return pl.pallas_call(
        backward_kernel,
        in_specs=[any_, any_, any_, vm, any_, any_, any_, any_, any_, vm, any_, vm, vm, sm],
        out_specs=[any_, any_, any_, vm],
        out_shape=[
            shape((4, part, width), bf16),
            shape((3, piece // 2, cols), f32),
            shape((3, piece // 2, cols), f32),
            shape((2, 16, width), f32),
        ],
        scratch_shapes=[
            pltpu.VMEM((3, 4, width, cols), bf16),
            pltpu.VMEM((4, width, cols), bf16),
            pltpu.VMEM((4, rows, cols), bf16),
            pltpu.VMEM((4, rows, cols), bf16),
            pltpu.VMEM((rows, width), bf16),
            pltpu.VMEM((rows, width), bf16),
            pltpu.VMEM((rows, width), bf16),
            pltpu.VMEM((width, rows), bf16),
            pltpu.VMEM((own, width), f32),
            pltpu.VMEM((own, width), f32),
            pltpu.VMEM((own, width), f32),
            pltpu.VMEM((own, width), bf16),
            pltpu.VMEM((own, width), bf16),
            pltpu.VMEM((own, width), bf16),
            pltpu.VMEM((3, 4, piece, cols), bf16),
            pltpu.VMEM((3, 4, piece, cols), bf16),
            pltpu.VMEM((3, 4, piece, cols), bf16),
            pltpu.VMEM((3, 3, piece, cols), bf16),
            pltpu.VMEM((3, piece, cols), f32),
            pltpu.VMEM((rows, head_cols), f32),
            pltpu.VMEM((rows, head_cols), f32),
            pltpu.VMEM((4, 16, width), f32),
            pltpu.VMEM((4, 16, width), f32),
            pltpu.VMEM((16, width), f32),
            pltpu.VMEM((16, width), f32),
            pltpu.VMEM((16, width), f32),
            pltpu.VMEM((3, 16, width), f32),
            dma((3, 4)), dma((3, 4)), dma((3, 4)), dma((3, 4)), dma((3, 4)), dma((3, 4)),
            dma((3, 3)), dma((3, 3)), dma((3,)), dma((3,)), dma((3,)), dma((8,)), dma((8,)),
            dma((4,)), dma((4,)), dma((3,)), dma((4,)), dma((32,)),
        ],
        compiler_params=pltpu.CompilerParams(
            collective_id=1, has_side_effects=True, vmem_limit_bytes=60 << 20
        ),
        cost_estimate=pl.CostEstimate(
            flops=flops, bytes_accessed=60 << 20, transcendentals=8 * rows * rows
        ),
        name="backward_layer",
    )(w_all, xf, qkv, lse, ctx, ff, hid, dg, n1, inv1, gm, vec, sums, length)


def swap_cores(value):
    return lax.ppermute(value, "core", SWAP)


def on_device(
    inputs,
    lengths,
    w_query,
    w_key,
    w_value,
    b_query,
    b_value,
    w_out,
    b_out,
    gain_one,
    shift_one,
    w_in,
    b_in,
    w_back,
    b_back,
    gain_two,
    shift_two,
    cotangent,
):
    planes = lax.axis_size("plane")
    n_t = lax.axis_size("tensor")
    plane = lax.axis_index("plane")
    core = lax.axis_index("core")
    place = lax.axis_index("tensor")
    seqs, slots_here, width = inputs.shape
    slots = slots_here * n_t
    half_slots = slots_here // 2
    own = slots // 2
    assert seqs * 2 == n_t
    head_cols = w_query.shape[1] // 2
    ff_cols = w_in.shape[1] // 2
    scale = HD ** (-0.5)
    quad = planes == 4
    ring = [(i, (i + 1) % n_t) for i in range(n_t)]
    x_pairs = [(i, i ^ 1) for i in range(planes)]
    y_pairs = [(i, i ^ 2) for i in range(planes)]

    def reorder(value, axis):
        if not quad:
            return value
        size = value.shape[axis] // 4
        return jnp.concatenate(
            [lax.dynamic_slice_in_dim(value, (plane ^ k) * size, size, axis) for k in range(4)],
            axis=axis,
        )

    def by_core(mine, theirs, axis=0):
        first = jnp.where(core == 0, mine, theirs)
        second = jnp.where(core == 0, theirs, mine)
        return jnp.concatenate([first, second], axis=axis)

    def to_chip(rows_here):
        value = reorder(rows_here, 2).reshape(seqs, 2, half_slots, width)
        mine = lax.dynamic_index_in_dim(value, core, 1, keepdims=False)
        other = lax.dynamic_index_in_dim(value, 1 - core, 1, keepdims=False)
        both = by_core(mine, swap_cores(other))
        return lax.all_to_all(both, "tensor", 0, 0, tiled=True).reshape(own, width)

    def from_chip(rows_own):
        value = rows_own.reshape(n_t, half_slots, width)
        value = lax.all_to_all(value, "tensor", 0, 0, tiled=True)
        value = value.reshape(2, seqs, half_slots, width)
        mine = lax.dynamic_index_in_dim(value, core, 0, keepdims=False)
        other = lax.dynamic_index_in_dim(value, 1 - core, 0, keepdims=False)
        got = swap_cores(other)
        value = jnp.stack(
            [jnp.where(core == 0, mine, got), jnp.where(core == 0, got, mine)], axis=1
        )
        return reorder(value.reshape(seqs, slots_here, width), 2)

    their_lengths = swap_cores(lengths)
    all_lengths = by_core(lengths, their_lengths)
    length = lax.dynamic_index_in_dim(all_lengths, place, 0, keepdims=False)
    index = jnp.arange(slots)
    position = (
        (index % own) // half_slots * slots_here
        + ((index // own) ^ core) * half_slots
        + index % half_slots
    )
    valid = position < length
    key_bias = jnp.where(valid, 0.0, NEGATIVE).astype(f32)[:, None]
    own_valid = valid[:own, None]

    def halves(value, cols):
        return (
            lax.dynamic_slice_in_dim(value, core * cols, cols, 1),
            lax.dynamic_slice_in_dim(value, (1 - core) * cols, cols, 1),
        )

    pieces = [
        halves(w_query, head_cols),
        halves(w_key, head_cols),
        halves(w_value, head_cols),
        halves(w_out.T, head_cols),
        halves(w_in, ff_cols),
        halves(w_back.T, ff_cols),
    ]
    keep = jnp.concatenate([piece[0] for piece in pieces], axis=1)
    give = jnp.concatenate([piece[1] for piece in pieces], axis=1)
    cuts = (4 * head_cols, 4 * head_cols + ff_cols)

    def flat(gathered):
        return jnp.concatenate([gathered[j] for j in range(n_t)], axis=1)

    out_bias = reorder(b_out, 0).astype(f32)
    back_bias = reorder(b_back, 0).astype(f32)
    gain_first = reorder(gain_one, 0).astype(f32)
    shift_first = reorder(shift_one, 0).astype(f32)
    gain_second = reorder(gain_two, 0).astype(f32)
    shift_second = reorder(shift_two, 0).astype(f32)
    bias_row = jnp.concatenate(
        [
            lax.dynamic_slice_in_dim(b_query, core * head_cols, head_cols),
            lax.dynamic_slice_in_dim(b_value, core * head_cols, head_cols),
            lax.dynamic_slice_in_dim(b_in, core * ff_cols, ff_cols),
        ]
    )[None]
    qkv_scale = jnp.tile(
        jnp.concatenate([jnp.full((head_cols,), scale, f32), jnp.ones((2 * head_cols,), f32)]), n_t
    )[None]
    def both_rows(value):
        return jnp.concatenate([value, swap_cores(value)], axis=0)

    def own_sum(partial):
        return partial[:own] + swap_cores(partial[own:])

    def normalize(value):
        average = jnp.mean(value, axis=-1, keepdims=True)
        centered = value - average
        variance = jnp.mean(centered * centered, axis=-1, keepdims=True)
        inverse = lax.rsqrt(variance + EPSILON)
        return centered * inverse, inverse

    def normalize_back(grad, gain, normed, inverse):
        e = grad * gain
        return (
            e
            - jnp.mean(e, axis=-1, keepdims=True)
            - normed * jnp.mean(e * normed, axis=-1, keepdims=True)
        ) * inverse

    if quad:
        def blocks_of(value):
            return reorder(value, 2).reshape(4, half_slots, width)

        pack = lambda value: jnp.stack(
            [value[:, : cuts[0]], value[:, cuts[0] : cuts[1]], value[:, cuts[1] :]]
        )
        vec = jnp.stack(
            [out_bias, gain_first, shift_first, back_bias, gain_second, shift_second,
             out_bias, out_bias]
        )
        (w_all, x_full, qkv4, lse8, ctx4, first_full, hid4, dg4, normed_one, inverse_one,
         grad_mixed, lo_blocks, second_sums) = forward(
            length.reshape(1), blocks_of(inputs), blocks_of(cotangent), pack(keep), pack(give),
            jnp.broadcast_to(bias_row.astype(f32), (8, bias_row.shape[1])), vec,
        )
        layer_out = reorder(lo_blocks.reshape(seqs, slots_here, width), 2)
        gi_blocks, mine, got, totals = backward(
            w_all, x_full, qkv4, lse8, ctx4, first_full, hid4, dg4, normed_one, inverse_one,
            grad_mixed, vec, second_sums, length.reshape(1),
        )
        grad_inputs = reorder(gi_blocks.reshape(seqs, slots_here, width), 2).astype(f32)
        mine = jnp.concatenate([mine[0], mine[1], mine[2]], axis=1)
        got = jnp.concatenate([got[0], got[1], got[2]], axis=1)
        norms = reorder(totals[0, :6] + totals[1, :6], 1)
        n_bias = 2 * head_cols + ff_cols
        biases_out = by_core(totals[0, 8:9, :n_bias], totals[1, 8:9, :n_bias])
    else:
        packed = by_core(keep, swap_cores(give))
        bundle_a = packed[:, : cuts[0]]
        bundle_b = packed[:, cuts[0] : cuts[1]]
        bundle_c = packed[:, cuts[1] :]
        def gather_z(own_piece):
            got = [own_piece]
            for _ in range(n_t - 1):
                got.append(lax.ppermute(got[-1], "tensor", ring))
            return jnp.stack(got)

        def gather_planes(mine):
            if not quad:
                return lax.all_gather(mine, "plane", axis=1, tiled=True)
            half = n_t // 2
            from_x = lax.ppermute(mine, "plane", x_pairs)
            from_y = lax.ppermute(mine, "plane", y_pairs)
            low = lax.ppermute(from_y[:half], "plane", x_pairs)
            high = lax.ppermute(from_x[half:], "plane", y_pairs)
            return jnp.concatenate([mine, from_x, from_y, jnp.concatenate([low, high])], axis=1)

        biases = gather_z(bias_row)[:, 0].astype(f32)
        z_a = gather_z(bundle_a)
        full_a = gather_planes(z_a)
        w_qkv = flat(full_a[:, :, : 3 * head_cols])
        w_o = flat(full_a[:, :, 3 * head_cols :])
        w_1 = flat(gather_planes(gather_z(bundle_b)))
        w_2 = flat(gather_planes(gather_z(bundle_c)))

        zeros_k = jnp.zeros((n_t, head_cols), f32)
        qkv_bias = jnp.concatenate(
            [biases[:, :head_cols], zeros_k, biases[:, head_cols : 2 * head_cols]], axis=1
        ).reshape(1, -1)
        in_bias = biases[:, 2 * head_cols :].reshape(1, -1)

        own_x = to_chip(inputs)
        x_full = both_rows(own_x)
        qkv = ((nn(x_full, w_qkv) + qkv_bias) * qkv_scale).astype(bf16)
        context, lse = attend_fwd(qkv, key_bias)
        attended = own_sum(nt(context, w_o))
        normed_one, inverse_one = normalize(own_x.astype(f32) + attended + out_bias)
        first_norm = normed_one * gain_first + shift_first
        first_full = both_rows(first_norm.astype(bf16))
        pre_act = nn(first_full, w_1) + in_bias
        activated, slope = gelu_and_slope(pre_act)
        hidden = activated.astype(bf16)
        mixed = own_sum(nt(hidden, w_2))
        normed_two, inverse_two = normalize(first_norm + mixed + back_bias)
        second = normed_two * gain_second + shift_second
        layer_out = from_chip(jnp.where(own_valid, second, 0.0).astype(bf16))

        grad_second = jnp.where(own_valid, to_chip(cotangent).astype(f32), 0.0)
        grad_mixed = normalize_back(grad_second, gain_second, normed_two, inverse_two)

        grad_mixed_full = both_rows(grad_mixed.astype(bf16))
        grad_w2 = tn(grad_mixed_full, hidden)
        grad_pre_low = (nn(grad_mixed_full, w_2) * slope.astype(f32)).astype(bf16)
        grad_w1 = tn(first_full, grad_pre_low)
        grad_first = grad_mixed + own_sum(nt(grad_pre_low, w_1))
        grad_att = normalize_back(grad_first, gain_first, normed_one, inverse_one)
        grad_att_full = both_rows(grad_att.astype(bf16))
        grad_context = nn(grad_att_full, w_o).astype(bf16)
        grad_wo = tn(grad_att_full, context)
        grad_qkv = attend_bwd(qkv, grad_context, lse, key_bias)
        grad_qkv = grad_qkv * qkv_scale.astype(bf16)
        grad_wqkv = tn(x_full, grad_qkv)
        grad_rows = grad_att + own_sum(nt(grad_qkv, w_qkv))
        grad_inputs = from_chip(grad_rows.astype(bf16)).astype(f32)

        def scatter(grad):
            cols = grad.shape[1] // n_t
            if quad:
                rows = width // 4
                blocks = grad.reshape(4, rows, n_t, cols).transpose(0, 2, 1, 3)
                half = n_t // 2
                low = lax.ppermute(blocks[3, :half].astype(bf16), "plane", x_pairs)
                high = lax.ppermute(blocks[3, half:].astype(bf16), "plane", y_pairs)
                for_y = jnp.concatenate([blocks[2, :half] + low.astype(f32), blocks[2, half:]])
                for_x = jnp.concatenate([blocks[1, :half], blocks[1, half:] + high.astype(f32)])
                from_x = lax.ppermute(for_x.astype(bf16), "plane", x_pairs)
                from_y = lax.ppermute(for_y.astype(bf16), "plane", y_pairs)
                mine = blocks[0] + from_x.astype(f32) + from_y.astype(f32)
            else:
                blocks = grad.reshape(width, n_t, cols).transpose(1, 0, 2)
                mine = lax.psum_scatter(
                    blocks.astype(bf16), "plane", scatter_dimension=1, tiled=True
                ).astype(f32)
            back = [(b, a) for a, b in ring]
            total = mine[n_t - 1]
            for j in range(n_t - 2, -1, -1):
                total = mine[j] + lax.ppermute(total.astype(bf16), "tensor", back).astype(f32)
            return total

        home_c = scatter(grad_w2)
        home_b = scatter(grad_w1)
        grad_a = jnp.concatenate(
            [
                grad_wqkv.reshape(width, n_t, 3 * head_cols),
                grad_wo.reshape(width, n_t, head_cols),
            ],
            axis=2,
        ).reshape(width, -1)
        home_a = scatter(grad_a)
        home = jnp.concatenate([home_a, home_b, home_c], axis=1)
        home = home.reshape(2, -1, home.shape[1])
        mine = lax.dynamic_index_in_dim(home, core, 0, keepdims=False)
        other = lax.dynamic_index_in_dim(home, 1 - core, 0, keepdims=False)
        got = swap_cores(other)

        def row_sum(value):
            return reorder(jnp.sum(value, axis=0), 0)

        second_rows = [row_sum(grad_mixed), row_sum(grad_second * normed_two), row_sum(grad_second)]
        norm_sums = jnp.concatenate(
            [
                row_sum(grad_att),
                row_sum(grad_first * normed_one),
                row_sum(grad_first),
                *second_rows,
            ]
        )
        qkv_sum = jnp.sum(grad_qkv.astype(f32), axis=0).reshape(n_t, 3 * head_cols)
        pre_sum = jnp.sum(grad_pre_low.astype(f32), axis=0).reshape(n_t, ff_cols)
        bias_sum = jnp.concatenate([qkv_sum[:, :head_cols], qkv_sum[:, 2 * head_cols :], pre_sum], axis=1)
        at_home = lax.rem(place - jnp.arange(n_t) + n_t, n_t)
        spread = (at_home[:, None] == jnp.arange(n_t)[None]).astype(f32)
        by_place = jnp.sum(spread[:, :, None] * bias_sum[:, None, :], axis=0)
        both = jnp.where(
            (jnp.arange(2) == core)[None, :, None], by_place[:, None, :], 0.0
        )
        sums = lax.psum(jnp.concatenate([norm_sums, both.reshape(-1)]), ("plane", "core", "tensor"))
        norms = sums[: 6 * width].reshape(6, width)
        biases_out = lax.dynamic_index_in_dim(
            sums[6 * width :].reshape(n_t, 2, -1), place, 0, keepdims=False
        )
    def columns(start, cols):
        return by_core(mine[:, start : start + cols], got[:, start : start + cols], axis=1)

    grad_w_query = columns(0, head_cols)
    grad_w_key = columns(head_cols, head_cols)
    grad_w_value = columns(2 * head_cols, head_cols)
    grad_w_out = columns(3 * head_cols, head_cols).T
    grad_w_in = columns(cuts[0], ff_cols)
    grad_w_back = columns(cuts[1], ff_cols).T

    grad_b_query = biases_out[:, :head_cols].reshape(-1)
    grad_b_value = biases_out[:, head_cols : 2 * head_cols].reshape(-1)
    grad_b_in = biases_out[:, 2 * head_cols :].reshape(-1)
    return (
        layer_out,
        grad_inputs,
        grad_w_query,
        grad_w_key,
        grad_w_value,
        grad_b_query,
        grad_b_value,
        grad_w_out,
        norms[0],
        norms[1],
        norms[2],
        grad_w_in,
        grad_b_in,
        grad_w_back,
        norms[3],
        norms[4],
        norms[5],
    )


def solution(mesh):
    devices = mesh.devices.reshape(mesh.shape["dp"] // 2, 2, mesh.shape["tensor"])
    inner = Mesh(devices, ("plane", "core", "tensor"))
    dp = ("plane", "core")
    row = P(dp, "tensor")
    column = P("tensor", dp)
    rows3 = P(dp, "tensor", None)
    shard = P("tensor")
    whole = P()
    return jax.shard_map(
        on_device,
        mesh=inner,
        in_specs=(
            rows3, P(dp), row, row, row, shard, shard, column, whole, whole, whole,
            row, shard, column, whole, whole, whole, rows3,
        ),
        out_specs=(
            rows3, rows3, row, row, row, shard, shard, column, whole, whole, whole,
            row, shard, column, whole, whole, whole,
        ),
        check_vma=False,
    )
```

```python
import jax
import jax.numpy as jnp
from jax import lax
from jax.experimental import pallas as pl
from jax.experimental.pallas import tpu as pltpu
from jax.sharding import Mesh, PartitionSpec as P

HD = 64
EPSILON = 1e-05
NEGATIVE = -1e30
f32 = jnp.float32
bf16 = jnp.bfloat16
SWAP = [(0, 1), (1, 0)]


def nt(a, b):
    return lax.dot_general(a, b, (((1,), (1,)), ((), ())), preferred_element_type=f32)


def tn(a, b):
    return lax.dot_general(a, b, (((0,), (0,)), ((), ())), preferred_element_type=f32)


def nn(a, b):
    return lax.dot_general(a, b, (((1,), (0,)), ((), ())), preferred_element_type=f32)


def attend_fwd_kernel(block, qkv_ref, kb_ref, ctx_ref, lse_ref):
    rows = qkv_ref.shape[0]
    lane = lax.broadcasted_iota(jnp.int32, (1, 2 * HD), 1)
    keys = qkv_ref[:, 2 * HD : 4 * HD]
    values_t = qkv_ref[:, 4 * HD : 6 * HD].T
    key_bias = kb_ref[...]
    for start in range(0, rows, block):
        query = qkv_ref[start : start + block, 0 : 2 * HD]
        parts = []
        for h in range(2):
            query_h = jnp.where(lane // HD == h, query, jnp.zeros_like(query))
            scores = nt(keys, query_h) + key_bias
            largest = jnp.max(scores, axis=0, keepdims=True)
            weights = jnp.exp(scores - largest)
            total = jnp.sum(weights, axis=0, keepdims=True)
            part = nn(values_t[h * HD : (h + 1) * HD], weights.astype(bf16))
            parts.append(part / total)
            lse_ref[0, h : h + 1, start : start + block] = largest + jnp.log(total)
        ctx_ref[start : start + block, :] = jnp.concatenate(parts, axis=0).T.astype(bf16)


def attend_fwd(qkv, key_bias):
    rows = qkv.shape[0]
    groups = qkv.shape[1] // (6 * HD)
    block = min(512, rows)
    return pl.pallas_call(
        lambda *refs: attend_fwd_kernel(block, *refs),
        grid=(groups,),
        in_specs=[
            pl.BlockSpec((rows, 6 * HD), lambda j: (0, j)),
            pl.BlockSpec((rows, 1), lambda j: (0, 0)),
        ],
        out_specs=[
            pl.BlockSpec((rows, 2 * HD), lambda j: (0, j)),
            pl.BlockSpec((1, 2, rows), lambda j: (j, 0, 0)),
        ],
        out_shape=[
            jax.ShapeDtypeStruct((rows, groups * 2 * HD), bf16),
            jax.ShapeDtypeStruct((groups, 2, rows), f32),
        ],
        compiler_params=pltpu.CompilerParams(vmem_limit_bytes=48 << 20),
        cost_estimate=pl.CostEstimate(
            flops=groups * 8 * rows * rows * HD * 4,
            bytes_accessed=rows * groups * 8 * HD * 2,
            transcendentals=groups * 2 * rows * rows,
        ),
        name="attend_fwd",
    )(qkv, key_bias)


def attend_bwd_kernel(block, qkv_ref, g_ref, lse_ref, kb_ref, d_ref, dk_acc, dv_acc):
    rows = qkv_ref.shape[0]
    lane = lax.broadcasted_iota(jnp.int32, (1, 2 * HD), 1)
    keys = qkv_ref[:, 2 * HD : 4 * HD]
    keys_t = keys.T
    values = qkv_ref[:, 4 * HD : 6 * HD]
    key_bias = kb_ref[...]
    for start in range(0, rows, block):
        query = qkv_ref[start : start + block, 0 : 2 * HD]
        grad = g_ref[start : start + block, :]
        parts = []
        for h in range(2):
            here = lane // HD == h
            query_h = jnp.where(here, query, jnp.zeros_like(query))
            grad_h = jnp.where(here, grad, jnp.zeros_like(grad))
            scores = nt(keys, query_h) + key_bias
            chances = jnp.exp(scores - lse_ref[0, h : h + 1, start : start + block])
            grad_chances = nt(values, grad_h)
            inner = jnp.sum(chances * grad_chances, axis=0, keepdims=True)
            grad_scores = (chances * (grad_chances - inner)).astype(bf16)
            dv = nn(chances.astype(bf16), grad_h)
            dk = nn(grad_scores, query_h)
            if start == 0 and h == 0:
                dv_acc[...] = dv
                dk_acc[...] = dk
            else:
                dv_acc[...] += dv
                dk_acc[...] += dk
            parts.append(nn(keys_t[h * HD : (h + 1) * HD], grad_scores))
        d_ref[start : start + block, 0 : 2 * HD] = jnp.concatenate(parts, axis=0).T.astype(bf16)
    d_ref[:, 2 * HD : 4 * HD] = dk_acc[...].astype(bf16)
    d_ref[:, 4 * HD : 6 * HD] = dv_acc[...].astype(bf16)


def attend_bwd(qkv, grad_context, lse, key_bias):
    rows = qkv.shape[0]
    groups = qkv.shape[1] // (6 * HD)
    block = min(512, rows)
    return pl.pallas_call(
        lambda *refs: attend_bwd_kernel(block, *refs),
        grid=(groups,),
        in_specs=[
            pl.BlockSpec((rows, 6 * HD), lambda j: (0, j)),
            pl.BlockSpec((rows, 2 * HD), lambda j: (0, j)),
            pl.BlockSpec((1, 2, rows), lambda j: (j, 0, 0)),
            pl.BlockSpec((rows, 1), lambda j: (0, 0)),
        ],
        out_specs=pl.BlockSpec((rows, 6 * HD), lambda j: (0, j)),
        out_shape=jax.ShapeDtypeStruct((rows, groups * 6 * HD), bf16),
        scratch_shapes=[pltpu.VMEM((rows, 2 * HD), f32), pltpu.VMEM((rows, 2 * HD), f32)],
        compiler_params=pltpu.CompilerParams(vmem_limit_bytes=48 << 20),
        cost_estimate=pl.CostEstimate(
            flops=groups * 20 * rows * rows * HD * 4,
            bytes_accessed=rows * groups * 14 * HD * 2,
            transcendentals=groups * 2 * rows * rows,
        ),
        name="attend_bwd",
    )(qkv, grad_context, lse, key_bias)

POLY = (
    0.30995978221815235,
    0.31100346478903146,
    0.2699660979585953,
    0.2765467936611628,
    -0.03831584737802812,
    0.38967711658103854,
    -0.3554874111653827,
    0.08996434684501212,
)
POLY_AT = 0.31
DENSITY = 0.3989422804014327
MESH = pl.DeviceIdType.MESH


def gelu_and_slope(v):
    density = jnp.exp(-0.5 * v * v) * DENSITY
    t = 1.0 / (1.0 + POLY_AT * jnp.abs(v))
    tail = jnp.full_like(v, POLY[-1])
    for coefficient in POLY[-2::-1]:
        tail = tail * t + coefficient
    tail = tail * t * density
    below = jnp.where(v > 0, 1.0 - tail, tail)
    return v * below, below + v * density


def forward_kernel(
    lens_ref, row_ref, x_ref, c_ref, wq_ref, wk_ref, wv_ref, wo_ref, wi_ref, wb_ref,
    w_out, xf_out, qkv_out, lse_ref, ctx_out, ff_out, hid_out, dg_out, n1_out, inv1_ref, gm_ref,
    lo_ref, sums_ref, vec_ref, length_ref,
    w, xs, xf, bias, qkv, ctx, ff, hid, dg, n1, first, other_acc, other_part, own_part, att_got, mix_got, cot,
    wo_here, wb_here, wo_give, wb_give, lens,
    z_s, z_r, zl_s, zl_r, x_s, x_r, y_s, y_r, f_s, f_r, pre_l, pre_s, pre_r, b_s, b_r,
    xa_s, xa_r, ca_s, ca_r, e_s, e_r, o_s,
):
    plane = lax.axis_index("plane")
    core = lax.axis_index("core")
    place = lax.axis_index("tensor")
    partner = {"core": 1 - core}
    x_side = {"plane": plane + 1 - 2 * (plane % 2)}
    y_side = {"plane": (plane + 2) % 4}
    z_right = {"tensor": (place + 1) % 4}
    z_left = {"tensor": (place + 3) % 4}
    first_end = (3 - place) // 3
    last_end = place // 3
    turns = (0, 1 + 2 * first_end, 3 - first_end - last_end, 2 - first_end + last_end)
    rows = xf.shape[0]
    own = rows // 2
    part = own // 4
    piece = w.shape[2] // 4

    def remote(source, target, send, recv, to):
        return pltpu.make_async_remote_copy(
            source, target, send, recv, device_id=to, device_id_type=MESH
        )

    def right_copy(b, n):
        return remote(
            w.at[b, n - 1, 0:piece], w.at[b, n, 0:piece], z_s.at[b, n - 1], z_r.at[b, n - 1], z_right
        )

    def left_copy(b, n):
        return remote(
            w.at[b, (5 - n) % 4, 0:piece], w.at[b, 4 - n, 0:piece],
            zl_s.at[b, n - 1], zl_r.at[b, n - 1], z_left,
        )

    def line_do(b, n, act):
        @pl.when(jnp.logical_and(place <= 2, place >= n - 1))
        def _():
            act(right_copy(b, n))

        @pl.when(jnp.logical_and(place >= 1, place + n <= 4))
        def _():
            act(left_copy(b, n))

    def line_start(b, n):
        line_do(b, n, lambda copy: copy.start())

    def line_wait(b, n):
        @pl.when(place >= n)
        def _():
            right_copy(b, n).wait_recv()

        @pl.when(place + n <= 3)
        def _():
            left_copy(b, n).wait_recv()

    def x_copy(b, n):
        j = turns[n]
        return remote(
            w.at[b, j, 0:piece], w.at[b, j, piece : 2 * piece], x_s.at[b, n], x_r.at[b, n], x_side
        )

    def y_copy(b, n):
        j = turns[n]
        return remote(
            w.at[b, j, 0:piece], w.at[b, j, 2 * piece : 3 * piece], y_s.at[b, n], y_r.at[b, n], y_side
        )

    def fx_copy(b, n):
        j, half = turns[n], piece // 2
        return remote(
            w.at[b, j, 2 * piece : 2 * piece + half], w.at[b, j, 3 * piece : 3 * piece + half],
            f_s.at[b, n, 0], f_r.at[b, n, 0], x_side,
        )

    def fy_copy(b, n):
        j, half = turns[n], piece // 2
        return remote(
            w.at[b, j, piece + half : 2 * piece], w.at[b, j, 3 * piece + half : 4 * piece],
            f_s.at[b, n, 1], f_r.at[b, n, 1], y_side,
        )

    def cross(b, n):
        x_copy(b, n).start()
        y_copy(b, n).start()

    def forward_on(b, n):
        y_copy(b, n).wait_recv()
        fx_copy(b, n).start()
        x_copy(b, n).wait_recv()
        fy_copy(b, n).start()

    def ready(b, n):
        fx_copy(b, n).wait_recv()
        fy_copy(b, n).wait_recv()
        save(w.at[b, turns[n]], w_out.at[b, turns[n]])

    half_piece = piece // 2
    head_cols = 2 * HD
    mine_at = pl.ds(core * half_piece, half_piece)
    theirs_at = pl.ds((1 - core) * half_piece, half_piece)
    cols = w.shape[3]

    def head_half(which):
        return pl.ds(pl.multiple_of(which * head_cols, head_cols), head_cols)

    def wide_half(which):
        return pl.ds(pl.multiple_of(which * cols, cols), cols)

    def keep_copy(n):
        if n < 3:
            source = (wq_ref, wk_ref, wv_ref)[n].at[:, head_half(core)]
            target = w.at[0, 0, mine_at, n * head_cols : (n + 1) * head_cols]
        elif n == 3:
            source, target = wo_ref, wo_here
        elif n == 4:
            source, target = wi_ref.at[:, wide_half(core)], w.at[1, 0, mine_at]
        else:
            source, target = wb_ref, wb_here
        return pltpu.make_async_copy(source, target, pre_l.at[n])

    def pre_copy(n, at):
        if n < 3:
            source = (wq_ref, wk_ref, wv_ref)[n].at[:, head_half(1 - core)]
            target = w.at[0, 0, at, n * head_cols : (n + 1) * head_cols]
        elif n == 3:
            source, target = wo_give, w.at[0, 0, at, 3 * head_cols : 4 * head_cols]
        elif n == 4:
            source, target = wi_ref.at[:, wide_half(1 - core)], w.at[1, 0, at]
        else:
            source, target = wb_give, w.at[2, 0, at]
        return remote(source, target, pre_s.at[n], pre_r.at[n], partner)

    def bias_copy(s):
        return remote(
            bias.at[0], bias.at[s], b_s.at[s], b_r.at[s], {"tensor": (place + s) % 4}
        )

    def spread(source, target, send, recv, l, h):
        at = pl.ds(place * part, part)
        to = {"core": h, "tensor": 2 * core + l}
        return remote(
            source.at[l, h * part : (h + 1) * part], target.at[at], send.at[2 * l + h],
            recv.at[place], to,
        )

    def spread_local(source, target, recv, l, h):
        at = pl.ds(place * part, part)
        return pltpu.make_async_copy(
            source.at[l, h * part : (h + 1) * part], target.at[at], recv.at[place]
        )

    def is_here(l, h):
        return jnp.logical_and(core == h, place == 2 * core + l)

    def spread_start(source, target, send, recv):
        for l in range(2):
            for h in range(2):
                @pl.when(is_here(l, h))
                def _():
                    spread_local(source, target, recv, l, h).start()

                @pl.when(jnp.logical_not(is_here(l, h)))
                def _():
                    spread(source, target, send, recv, l, h).start()

    def spread_wait(source, target, recv):
        for s in range(4):
            pltpu.make_async_copy(
                source.at[0, 0:part], target.at[s * part : (s + 1) * part], recv.at[s]
            ).wait()

    def spread_sent(source, target, send, recv):
        for l in range(2):
            for h in range(2):
                @pl.when(jnp.logical_not(is_here(l, h)))
                def _():
                    spread(source, target, send, recv, l, h).wait_send()

    def exchange(source, target, n):
        return remote(source, target, e_s.at[n], e_r.at[n], partner)

    outs = []

    def save(source, target):
        copy = pltpu.make_async_copy(source, target, o_s.at[len(outs)])
        copy.start()
        outs.append(copy)

    barrier = pltpu.get_barrier_semaphore()
    friends = [x_side, y_side, partner]
    for s in range(1, 4):
        friends.append({"tensor": (place + s) % 4})
        friends.append({"tensor": (place + s) % 4, "core": 1 - core})
    for friend in friends:
        pl.semaphore_signal(barrier, inc=1, device_id=friend, device_id_type=MESH)
    for n in (3, 0, 1, 2, 4, 5):
        keep_copy(n).start()
    pl.semaphore_wait(barrier, len(friends))

    def block_at(k):
        number = (plane, plane + 1 - 2 * (plane % 2), (plane + 2) % 4, 3 - plane)[k]
        return pl.ds(pl.multiple_of(number * piece, piece), piece)

    for n in range(3):
        pre_copy(n, mine_at).start()
    keep_copy(3).wait()
    wo_give[...] = wo_here[head_half(1 - core), :].T
    pre_copy(3, mine_at).start()
    w[0, 0, mine_at, 3 * head_cols : 4 * head_cols] = wo_here[head_half(core), :].T
    pre_copy(4, mine_at).start()
    for n in range(3):
        keep_copy(n).wait()
    for n in range(4):
        pre_copy(n, theirs_at).wait_recv()
    line_start(0, 1)
    cross(0, 0)
    spread_start(x_ref, xs, xa_s, xa_r)
    keep_copy(5).wait()
    wb_give[...] = wb_here[wide_half(1 - core), :].T
    pre_copy(5, mine_at).start()
    w[2, 0, mine_at, :] = wb_here[wide_half(core), :].T
    keep_copy(4).wait()
    pre_copy(4, theirs_at).wait_recv()
    cross(1, 0)
    pre_copy(5, theirs_at).wait_recv()
    cross(2, 0)

    zero_row = jnp.zeros((1, head_cols), f32)
    heads_q = jnp.where(core == 0, row_ref[7:8, 0:head_cols], row_ref[7:8, head_cols : 2 * head_cols])
    heads_v = jnp.where(
        core == 0, row_ref[7:8, 2 * head_cols : 3 * head_cols], row_ref[7:8, 3 * head_cols : 4 * head_cols]
    )
    wide = jnp.where(core == 0, row_ref[6:7, 0:cols], row_ref[6:7, cols : 2 * cols])
    bias[0, 0:1, :] = jnp.concatenate([heads_q, zero_row, heads_v, zero_row, wide], axis=1)
    for k in range(4):
        vec_ref[:, k * piece : (k + 1) * piece] = row_ref[:, block_at(k)]
    for s in range(1, 4):
        bias_copy(s).start()
    lens[core] = lens_ref[...]
    share_len = remote(lens_ref, lens.at[core], e_s.at[4], e_r.at[4], partner)
    share_len.start()

    line_wait(0, 1)
    line_start(0, 2)
    line_start(1, 1)
    forward_on(0, 0)
    cross(0, 1)
    forward_on(1, 0)
    forward_on(2, 0)
    for s in range(1, 4):
        bias_copy(s).wait_recv()
    remote(lens_ref, lens.at[1 - core], e_s.at[4], e_r.at[4], partner).wait_recv()

    spread_wait(x_ref, xs, xa_r)
    for k in range(4):
        xf[0:own, k * piece : (k + 1) * piece] = xs[:, block_at(k)]
    share_x = exchange(xf.at[0:own], xf.at[own : 2 * own], 0)
    share_x.start()
    share_x.wait_recv()
    save(xf, xf_out)

    index = lax.broadcasted_iota(jnp.int32, (rows, 1), 0)
    length_ref[...] = lens[place // 2]
    length = length_ref[pl.ds(place % 2, 1), 0:1]
    half = jnp.where(index < own, core, 1 - core)
    inside = index % own
    position = (inside // part) * (2 * part) + half * part + inside % part
    key_bias = jnp.where(position.astype(f32) < length, 0.0, NEGATIVE).astype(f32)
    lane = lax.broadcasted_iota(jnp.int32, (1, 2 * HD), 1)
    tile = 256

    def project(n):
        j = turns[n]
        columns = lax.broadcasted_iota(jnp.int32, (1, 3 * head_cols), 1)
        zero = jnp.zeros((1, head_cols), f32)
        add = jnp.concatenate(
            [bias[j, 0:1, 0:head_cols], zero, bias[j, 0:1, 2 * head_cols : 3 * head_cols]], axis=1
        )
        times = jnp.where(columns < head_cols, HD ** (-0.5), 1.0).astype(f32)

        def body(i, _):
            at = pl.ds(pl.multiple_of(i * tile, tile), tile)
            value = nn(xf[at, :], w[0, j, :, 0 : 3 * head_cols])
            qkv[j, at, :] = ((value + add) * times).astype(bf16)
            return 0

        lax.fori_loop(0, rows // tile, body, 0)
        save(qkv.at[j], qkv_out.at[j])

    def attend(n):
        j = turns[n]
        keys = qkv[j, :, head_cols : 2 * head_cols]
        values_t = qkv[j, :, 2 * head_cols : 3 * head_cols].T

        def body(i, _):
            at = pl.ds(pl.multiple_of(i * tile, tile), tile)
            query = qkv[j, at, 0:head_cols]
            parts = []
            for h in range(2):
                query_h = jnp.where(lane // HD == h, query, jnp.zeros_like(query))
                scores = nt(keys, query_h) + key_bias
                largest = jnp.max(scores, axis=0, keepdims=True)
                weights = jnp.exp(scores - largest)
                total = jnp.sum(weights, axis=0, keepdims=True)
                out = nn(values_t[h * HD : (h + 1) * HD], weights.astype(bf16))
                parts.append(out / total)
                lse_ref[2 * j + h, :, at] = largest + jnp.log(total)
            ctx[j, at, :] = jnp.concatenate(parts, axis=0).T.astype(bf16)
            return 0

        lax.fori_loop(0, rows // tile, body, 0)
        save(ctx.at[j], ctx_out.at[j])

    ready(0, 0)
    project(0)
    line_wait(0, 2)
    line_start(0, 3)
    line_start(2, 1)
    cross(0, 2)
    attend(0)
    forward_on(0, 1)
    line_wait(1, 1)
    line_start(1, 2)
    ready(0, 1)
    project(1)
    line_wait(0, 3)
    cross(0, 3)
    cross(1, 1)
    attend(1)
    forward_on(0, 2)
    line_wait(2, 1)
    line_start(2, 2)
    ready(0, 2)
    project(2)
    line_wait(1, 2)
    line_start(1, 3)
    cross(1, 2)
    attend(2)
    forward_on(0, 3)
    forward_on(1, 1)
    ready(0, 3)
    project(3)
    line_wait(2, 2)
    line_start(2, 3)
    attend(3)
    line_wait(1, 3)
    cross(1, 3)
    cross(2, 1)
    forward_on(1, 2)

    def out_rows(start, target):
        def body(i, _):
            at = pl.ds(pl.multiple_of(start + i * tile, tile), tile)
            to = pl.ds(pl.multiple_of(i * tile, tile), tile)
            total = nt(ctx[0, at, :], w[0, 0, :, 3 * head_cols :])
            for j in range(1, 4):
                total += nt(ctx[j, at, :], w[0, j, :, 3 * head_cols :])
            target[to, :] = total.astype(target.dtype)
            return 0

        lax.fori_loop(0, own // tile, body, 0)

    out_rows(own, other_part)
    share_att = exchange(other_part, att_got, 1)
    share_att.start()
    out_rows(0, own_part)
    line_wait(2, 3)
    spread_start(c_ref, cot, ca_s, ca_r)
    cross(2, 2)
    cross(2, 3)
    share_att.wait_recv()
    small = 32

    def mean(value):
        return jnp.sum(value, axis=-1, keepdims=True) * (1.0 / value.shape[-1])

    def first_body(i, _):
        at = pl.ds(pl.multiple_of(i * small, small), small)
        total = xf[at, :].astype(f32) + (own_part[at, :] + att_got[at, :].astype(f32)) + vec_ref[0:1, :]
        centered = total - mean(total)
        inverse = lax.rsqrt(mean(centered * centered) + EPSILON)
        normed = centered * inverse
        n1[at, :] = normed
        inv1_ref[at, :] = inverse
        value = normed * vec_ref[1:2, :] + vec_ref[2:3, :]
        first[at, :] = value
        ff[at, :] = value.astype(bf16)
        return 0

    lax.fori_loop(0, own // small, first_body, 0)
    share_first = exchange(ff.at[0:own], ff.at[own : 2 * own], 2)
    share_first.start()
    save(n1, n1_out)
    forward_on(1, 3)
    share_first.wait_recv()
    save(ff, ff_out)

    def expand(n):
        j = turns[n]
        add = bias[j, 0:1, 4 * head_cols : 4 * head_cols + cols]

        def body(i, _):
            at = pl.ds(pl.multiple_of(i * tile, tile), tile)
            value = nn(ff[at, :], w[1, j]) + add
            active, slope = gelu_and_slope(value)
            hid[j, at, :] = active.astype(bf16)
            dg[j, at, :] = slope.astype(bf16)
            return 0

        lax.fori_loop(0, rows // tile, body, 0)
        save(hid.at[j], hid_out.at[j])
        save(dg.at[j], dg_out.at[j])

    ready(1, 0)
    expand(0)
    ready(1, 1)
    expand(1)
    forward_on(2, 1)
    ready(1, 2)
    expand(2)
    ready(1, 3)
    expand(3)
    forward_on(2, 2)
    share_att.wait_send()

    def contract(ns, start, target, source):
        def body(i, _):
            at = pl.ds(pl.multiple_of(start + i * tile, tile), tile)
            to = pl.ds(pl.multiple_of(i * tile, tile), tile)
            total = nt(hid[turns[ns[0]], at, :], w[2, turns[ns[0]]])
            for n in ns[1:]:
                total += nt(hid[turns[n], at, :], w[2, turns[n]])
            if source is not None:
                total += source[to, :]
            target[to, :] = total.astype(target.dtype)
            return 0

        lax.fori_loop(0, own // tile, body, 0)

    ready(2, 0)
    ready(2, 1)
    contract((0, 1), own, other_acc, None)
    contract((0, 1), 0, own_part, None)
    forward_on(2, 3)
    ready(2, 2)
    contract((2,), own, other_acc, other_acc)
    contract((2,), 0, own_part, own_part)
    ready(2, 3)
    contract((3,), own, other_part, other_acc)
    share_mix = exchange(other_part, mix_got, 3)
    share_mix.start()
    contract((3,), 0, own_part, own_part)
    spread_wait(c_ref, cot, ca_r)
    share_mix.wait_recv()
    sums_ref[...] = jnp.zeros_like(sums_ref)

    def second_body(i, _):
        at = pl.ds(pl.multiple_of(i * small, small), small)
        spot = i * small + lax.broadcasted_iota(jnp.int32, (small, 1), 0)
        where = (spot // part) * (2 * part) + core * part + spot % part
        alive = where.astype(f32) < length
        total = first[at, :] + (own_part[at, :] + mix_got[at, :].astype(f32)) + vec_ref[3:4, :]
        centered = total - mean(total)
        inverse = lax.rsqrt(mean(centered * centered) + EPSILON)
        normed = centered * inverse
        value = normed * vec_ref[4:5, :] + vec_ref[5:6, :]
        shown = jnp.where(alive, value, 0.0).astype(bf16)
        for k in range(4):
            lo_ref[at, block_at(k)] = shown[:, k * piece : (k + 1) * piece]
        given = jnp.concatenate([cot[at, block_at(k)] for k in range(4)], axis=1)
        grad = jnp.where(alive, given.astype(f32), 0.0)
        e = grad * vec_ref[4:5, :]
        back = (e - mean(e) - normed * mean(e * normed)) * inverse
        gm_ref[at, :] = back
        sums_ref[0:1, :] += jnp.sum(back, axis=0, keepdims=True)
        sums_ref[1:2, :] += jnp.sum(grad * normed, axis=0, keepdims=True)
        sums_ref[2:3, :] += jnp.sum(grad, axis=0, keepdims=True)
        return 0

    lax.fori_loop(0, own // small, second_body, 0)
    for n in range(6):
        pre_copy(n, mine_at).wait_send()
    share_len.wait_send()
    for b in range(3):
        for n in range(1, 4):
            line_do(b, n, lambda copy: copy.wait_send())
        for n in range(4):
            x_copy(b, n).wait_send()
            y_copy(b, n).wait_send()
            fx_copy(b, n).wait_send()
            fy_copy(b, n).wait_send()
    for s in range(1, 4):
        bias_copy(s).wait_send()
    spread_sent(x_ref, xs, xa_s, xa_r)
    spread_sent(c_ref, cot, ca_s, ca_r)
    share_x.wait_send()
    share_first.wait_send()
    share_mix.wait_send()
    for copy in outs:
        copy.wait()


def forward(lens, row, inputs, cotangent, w_query, w_key, w_value, w_out, w_in, w_back):
    part, width = inputs.shape[1] // 2, inputs.shape[2]
    own = 4 * part
    rows = 2 * own
    cols = w_in.shape[1] // 2
    head_cols = 2 * HD
    any_ = pl.BlockSpec(memory_space=pltpu.HBM)
    vm = pl.BlockSpec(memory_space=pltpu.VMEM)
    shape = jax.ShapeDtypeStruct
    dma = pltpu.SemaphoreType.DMA
    flops = 2 * rows * width * cols * 12 + 16 * rows * rows * HD * 4
    return pl.pallas_call(
        forward_kernel,
        in_specs=[vm, vm] + [any_] * 8,
        out_specs=[
            any_, any_, any_, vm, any_, any_, any_, any_, any_, vm, vm, vm, vm, vm, vm
        ],
        out_shape=[
            shape((3, 4, width, cols), bf16),
            shape((rows, width), bf16),
            shape((4, rows, 3 * head_cols), bf16),
            shape((8, 1, rows), f32),
            shape((4, rows, head_cols), bf16),
            shape((rows, width), bf16),
            shape((4, rows, cols), bf16),
            shape((4, rows, cols), bf16),
            shape((own, width), f32),
            shape((own, 1), f32),
            shape((own, width), f32),
            shape((own, width), bf16),
            shape((8, width), f32),
            shape((8, width), f32),
            shape((8, 128), f32),
        ],
        scratch_shapes=[
            pltpu.VMEM((3, 4, width, cols), bf16),
            pltpu.VMEM((own, width), bf16),
            pltpu.VMEM((rows, width), bf16),
            pltpu.VMEM((4, 8, 4 * head_cols + cols), f32),
            pltpu.VMEM((4, rows, 3 * head_cols), bf16),
            pltpu.VMEM((4, rows, head_cols), bf16),
            pltpu.VMEM((rows, width), bf16),
            pltpu.VMEM((4, rows, cols), bf16),
            pltpu.VMEM((4, rows, cols), bf16),
            pltpu.VMEM((own, width), f32),
            pltpu.VMEM((own, width), f32),
            pltpu.VMEM((own, width), f32),
            pltpu.VMEM((own, width), bf16),
            pltpu.VMEM((own, width), f32),
            pltpu.VMEM((own, width), bf16),
            pltpu.VMEM((own, width), bf16),
            pltpu.VMEM((own, width), bf16),
            pltpu.VMEM(w_out.shape, bf16),
            pltpu.VMEM(w_back.shape, bf16),
            pltpu.VMEM((w_out.shape[1], head_cols), bf16),
            pltpu.VMEM((w_back.shape[1], cols), bf16),
            pltpu.VMEM((2, 8, 128), f32),
            dma((3, 3)), dma((3, 3)), dma((3, 3)), dma((3, 3)),
            dma((3, 4)), dma((3, 4)), dma((3, 4)), dma((3, 4)),
            dma((3, 4, 2)), dma((3, 4, 2)), dma((6,)), dma((6,)), dma((6,)), dma((4,)), dma((4,)),
            dma((4,)), dma((4,)), dma((4,)), dma((4,)),
            dma((5,)), dma((5,)), dma((32,)),
        ],
        compiler_params=pltpu.CompilerParams(
            collective_id=0, has_side_effects=True, vmem_limit_bytes=60 << 20
        ),
        cost_estimate=pl.CostEstimate(
            flops=flops, bytes_accessed=60 << 20, transcendentals=8 * rows * rows
        ),
        name="forward_layer",
    )(lens, row, inputs, cotangent, w_query, w_key, w_value, w_out, w_in, w_back)


def backward_kernel(
    w_ref, xf_ref, qkv_ref, lse_ref, ctx_ref, ff_ref, hid_ref, dg_ref, n1_ref, inv1_ref, gm_ref,
    vec_ref, sums_ref, length_ref, lo_own,
    lo_ref, gi_ref, gq_ref, gk_ref, gv_ref, go_ref, gw_ref, gb_ref, total_ref,
    w, grad_c, pad, pre, gmf, gaf, act, turned, gm, n1, own_part, other, got,
    d_got, rx, ry, rz, home, dk_acc, dv_acc, vz, zg, xg, yg, cg, tot, go_turned, gb_turned,
    d_s, d_r, x_s, x_r, y_s, y_r, z_s, z_r, h_s, h_r, h_l, e_s, e_r, g_s, g_r, v_s, v_r, l_s,
    lo_s, lo_r,
):
    plane = lax.axis_index("plane")
    core = lax.axis_index("core")
    place = lax.axis_index("tensor")
    partner = {"core": 1 - core}
    x_side = {"plane": plane + 1 - 2 * (plane % 2)}
    y_side = {"plane": (plane + 2) % 4}
    z_back = {"tensor": (place + 3) % 4}
    rows, width = gmf.shape
    own = rows // 2
    part = own // 4
    piece = width // 4
    head_cols = 2 * HD
    tile = 256
    small = 32
    gi_own = gmf

    def remote(source, target, send, recv, to):
        return pltpu.make_async_remote_copy(
            source, target, send, recv, device_id=to, device_id_type=MESH
        )

    def block(b, j, k):
        at = slice(k * piece, (k + 1) * piece)
        if b == 2:
            return grad_c.at[j, at]
        return w.at[b + 1, j, at]

    def d_copy(b, j):
        to = x_side if j < 2 else y_side
        return remote(block(b, j, 3), d_got.at[b, j], d_s.at[b, j], d_r.at[b, j], to)

    def x_copy(b, j):
        return remote(block(b, j, 1), rx.at[b, j], x_s.at[b, j], x_r.at[b, j], x_side)

    def y_copy(b, j):
        return remote(block(b, j, 2), ry.at[b, j], y_s.at[b, j], y_r.at[b, j], y_side)

    def z_copy(b, j):
        return remote(
            block(b, j, 0), rz.at[b, j - 1], z_s.at[b, j - 1], z_r.at[b, j - 1], z_back
        )

    half_piece = piece // 2
    cols = w.shape[3]
    mine_at = pl.ds(core * half_piece, half_piece)
    theirs_at = pl.ds((1 - core) * half_piece, half_piece)

    def home_parts(n, at):
        heads = pl.ds(pl.multiple_of(core * head_cols, head_cols), head_cols)
        wide = pl.ds(pl.multiple_of(core * cols, cols), cols)
        if n < 3:
            return home.at[0, at, n * head_cols : (n + 1) * head_cols], (gq_ref, gk_ref, gv_ref)[n].at[:, heads]
        if n == 3:
            return go_turned.at[:, at], go_ref.at[heads]
        if n == 4:
            return home.at[1, at], gw_ref.at[:, wide]
        return gb_turned.at[:, at], gb_ref.at[wide]

    def home_copy(n):
        source, target = home_parts(n, theirs_at)
        return remote(source, target, h_s.at[n], h_r.at[n], partner)

    def home_keep(n):
        source, target = home_parts(n, mine_at)
        return pltpu.make_async_copy(source, target, h_l.at[n])

    def send_first(b, j):
        d_copy(b, j).start()

    def send_second(b, j):
        (x_copy if j < 2 else y_copy)(b, j).start()
        d_copy(b, j).wait_recv()
        here = block(b, j, 2 if j < 2 else 1)
        here[...] = (here[...].astype(f32) + d_got[b, j].astype(f32)).astype(bf16)
        (y_copy if j < 2 else x_copy)(b, j).start()

    def send_third(b, j):
        x_copy(b, j).wait_recv()
        y_copy(b, j).wait_recv()
        total = block(b, j, 0)[...].astype(f32) + rx[b, j].astype(f32) + ry[b, j].astype(f32)
        if j < 3:
            z_copy(b, j + 1).wait_recv()
            total = total + rz[b, j].astype(f32)
        if j > 0:
            block(b, j, 0)[...] = total.astype(bf16)
            z_copy(b, j).start()
        else:
            home[b] = total
            if b == 0:
                go_turned[...] = total[:, 3 * head_cols : 4 * head_cols].T
            if b == 2:
                gb_turned[...] = total.T
            for n in ((0, 1, 2, 3), (4,), (5,))[b]:
                home_copy(n).start()
                home_keep(n).start()

    def exchange(source, target, n):
        return remote(source, target, e_s.at[n], e_r.at[n], partner)

    def back_parts(source, target, s):
        at = pl.ds(core * part, part)
        return source.at[s * part : (s + 1) * part], target.at[place % 2, at]

    def back(source, target, send, recv, s):
        here, there = back_parts(source, target, s)
        to = {"core": place // 2, "tensor": s}
        return remote(here, there, send.at[s], recv.at[2 * (place % 2) + core], to)

    def back_local(source, target, recv, s):
        here, there = back_parts(source, target, s)
        return pltpu.make_async_copy(here, there, recv.at[2 * (place % 2) + core])

    def is_home(s):
        return jnp.logical_and(core == place // 2, place == s)

    def back_start(source, target, send, recv):
        for s in range(4):
            @pl.when(is_home(s))
            def _():
                back_local(source, target, recv, s).start()

            @pl.when(jnp.logical_not(is_home(s)))
            def _():
                back(source, target, send, recv, s).start()

    def back_end(source, target, send, recv):
        for s in range(4):
            @pl.when(jnp.logical_not(is_home(s)))
            def _():
                back(source, target, send, recv, s).wait_send()
        for s in range(4):
            pltpu.make_async_copy(
                source.at[0:part], target.at[s // 2, pl.ds((s % 2) * part, part)], recv.at[s]
            ).wait()

    def v_copy(j):
        to = {"tensor": (place + 4 - j) % 4}
        return remote(vz.at[j], zg.at[place], v_s.at[j - 1], v_r.at[place], to)

    def v_got(j):
        source = (place + j) % 4
        return remote(vz.at[j], zg.at[source], v_s.at[j - 1], v_r.at[source], z_back)

    coming = {}

    def fetch(name, source, target):
        copy = pltpu.make_async_copy(source, target, l_s.at[len(coming)])
        copy.start()
        coming[name] = copy

    fetch("gm", gm_ref, gm)
    for j in (3, 2, 1, 0):
        fetch(("hid", j), hid_ref.at[j], pad.at[j])
    for j in range(4):
        fetch(("w2", j), w_ref.at[2, j], w.at[2, j])
        fetch(("dg", j), dg_ref.at[j], pre.at[j])
    fetch("w1", w_ref.at[1], w.at[1])
    fetch("n1", n1_ref, n1)
    fetch("ff", ff_ref, act)
    fetch("w0", w_ref.at[0], w.at[0])

    barrier = pltpu.get_barrier_semaphore()
    friends = [x_side, y_side, partner]
    for s in range(1, 4):
        friends.append({"tensor": (place + s) % 4})
        friends.append({"tensor": (place + s) % 4, "core": 1 - core})
    for friend in friends:
        pl.semaphore_signal(barrier, inc=1, device_id=friend, device_id_type=MESH)

    coming["gm"].wait()

    def round_body(i, _):
        at = pl.ds(pl.multiple_of(i * 128, 128), 128)
        gmf[at, :] = gm[at, :].astype(bf16)
        return 0

    lax.fori_loop(0, own // 128, round_body, 0)
    pl.semaphore_wait(barrier, len(friends))
    share_gm = exchange(gmf.at[0:own], gmf.at[own : 2 * own], 0)
    share_gm.start()
    back_start(lo_own, lo_ref, lo_s, lo_r)
    vz[...] = jnp.zeros_like(vz)

    def turn(source, first, last):
        def body(i, _):
            at = pl.ds(pl.multiple_of(i * tile, tile), tile)
            turned[:, at] = source[at, :].T
            return 0

        lax.fori_loop(first, last, body, 0)

    def weight_grad(b, j, right, columns):
        def body(k, _):
            at = pl.ds(pl.multiple_of(k * tile, tile), tile)
            value = nn(turned[at, :], right()).astype(bf16)
            if b == 2:
                grad_c[j, at, columns] = value
            else:
                w[b + 1, j, at, columns] = value
            return 0

        lax.fori_loop(0, width // tile, body, 0)

    every = slice(None)
    turn(gmf, 0, own // tile)
    share_gm.wait_recv()
    turn(gmf, own // tile, rows // tile)
    for j in (3, 1, 2, 0):
        coming[("hid", j)].wait()
        weight_grad(2, j, lambda: pad[j], every)
        send_first(2, j)

    def slope_rows(j):
        coming[("w2", j)].wait()
        coming[("dg", j)].wait()

        def body(i, _):
            at = pl.ds(pl.multiple_of(i * tile, tile), tile)
            value = (nn(gmf[at, :], w[2, j]) * pre[j, at, :].astype(f32)).astype(bf16)
            pre[j, at, :] = value
            vz[j, 8:9, 2 * head_cols : 2 * head_cols + value.shape[1]] += jnp.sum(
                value.astype(f32), axis=0, keepdims=True
            )
            return 0

        lax.fori_loop(0, rows // tile, body, 0)

    slope_rows(0)
    slope_rows(1)
    send_second(2, 3)
    slope_rows(2)
    slope_rows(3)
    send_second(2, 2)
    for j in range(4):
        fetch(("ctx", j), ctx_ref.at[j], pad.at[j, :, pl.ds(3 * head_cols, head_cols)])
    coming["w1"].wait()

    def first_rows(start, target):
        def body(i, _):
            at = pl.ds(pl.multiple_of(start + i * tile, tile), tile)
            to = pl.ds(pl.multiple_of(i * tile, tile), tile)
            total = nt(pre[0, at, :], w[1, 0])
            for j in range(1, 4):
                total += nt(pre[j, at, :], w[1, j])
            target[to, :] = total.astype(target.dtype)
            return 0

        lax.fori_loop(0, own // tile, body, 0)

    first_rows(own, other)
    share_first = exchange(other, got, 1)
    share_first.start()
    send_second(2, 1)
    first_rows(0, own_part)
    send_second(2, 0)
    coming["n1"].wait()
    share_first.wait_recv()

    def mean(value):
        return jnp.sum(value, axis=-1, keepdims=True) * (1.0 / value.shape[-1])

    def norm_body(i, _):
        at = pl.ds(pl.multiple_of(i * small, small), small)
        grad = gm[at, :] + (own_part[at, :] + got[at, :].astype(f32))
        normed = n1[at, :]
        e = grad * vec_ref[1:2, :]
        value = (e - mean(e) - normed * mean(e * normed)) * inv1_ref[at, :]
        gm[at, :] = value
        gaf[at, :] = value.astype(bf16)
        vz[0, 0:1, :] += jnp.sum(value, axis=0, keepdims=True)
        vz[0, 1:2, :] += jnp.sum(grad * normed, axis=0, keepdims=True)
        vz[0, 2:3, :] += jnp.sum(grad, axis=0, keepdims=True)
        return 0

    lax.fori_loop(0, own // small, norm_body, 0)
    share_att = exchange(gaf.at[0:own], gaf.at[own : 2 * own], 2)
    share_att.start()
    vz[0, 3:6, :] = sums_ref[0:3, :]
    for j in range(1, 4):
        vz[j, 0:8, :] = vz[0, 0:8, :]
    coming["ff"].wait()
    turn(act, 0, rows // tile)
    fetch("xf", xf_ref, act)
    weight_grad(1, 3, lambda: pre[3], every)
    send_first(1, 3)
    weight_grad(1, 1, lambda: pre[1], every)
    send_first(1, 1)
    send_third(2, 3)
    weight_grad(1, 2, lambda: pre[2], every)
    send_first(1, 2)
    weight_grad(1, 0, lambda: pre[0], every)
    send_first(1, 0)
    for j in range(4):
        fetch(("qkv", j), qkv_ref.at[j], pre.at[j, :, pl.ds(0, 3 * head_cols)])
    send_third(2, 2)
    share_att.wait_recv()
    turn(gaf, 0, rows // tile)
    coming["w0"].wait()
    last = slice(3 * head_cols, 4 * head_cols)

    def context_rows(j):
        def body(i, _):
            at = pl.ds(pl.multiple_of(i * tile, tile), tile)
            pre[j, at, last] = nn(gaf[at, :], w[0, j, :, last]).astype(bf16)
            return 0

        lax.fori_loop(0, rows // tile, body, 0)

    for j in (3, 2, 1, 0):
        context_rows(j)
        coming[("ctx", j)].wait()
        weight_grad(0, j, lambda: pad[j, :, last], last)
        if j == 2:
            send_third(2, 1)
    send_third(2, 0)
    coming["xf"].wait()
    turn(act, 0, rows // tile)
    send_second(1, 3)

    index = lax.broadcasted_iota(jnp.int32, (rows, 1), 0)
    half = jnp.where(index < own, core, 1 - core)
    inside = index % own
    position = (inside // part) * (2 * part) + half * part + inside % part
    length = length_ref[pl.ds(place % 2, 1), 0:1]
    key_bias = jnp.where(position.astype(f32) < length, 0.0, NEGATIVE).astype(f32)
    lane = lax.broadcasted_iota(jnp.int32, (1, head_cols), 1)
    front = slice(0, 3 * head_cols)

    def attend_back(j):
        keys = pre[j, :, head_cols : 2 * head_cols]
        keys_t = keys.T
        values = pre[j, :, 2 * head_cols : 3 * head_cols]
        dk_acc[...] = jnp.zeros_like(dk_acc)
        dv_acc[...] = jnp.zeros_like(dv_acc)

        def body(i, _):
            at = pl.ds(pl.multiple_of(i * tile, tile), tile)
            query = pre[j, at, 0:head_cols]
            grad = pre[j, at, last]
            parts = []
            for h in range(2):
                here = lane // HD == h
                query_h = jnp.where(here, query, jnp.zeros_like(query))
                grad_h = jnp.where(here, grad, jnp.zeros_like(grad))
                scores = nt(keys, query_h) + key_bias
                chances = jnp.exp(scores - lse_ref[2 * j + h, :, at])
                grad_chances = nt(values, grad_h)
                inner = jnp.sum(chances * grad_chances, axis=0, keepdims=True)
                grad_scores = (chances * (grad_chances - inner)).astype(bf16)
                dv_acc[...] += nn(chances.astype(bf16), grad_h)
                dk_acc[...] += nn(grad_scores, query_h)
                parts.append(nn(keys_t[h * HD : (h + 1) * HD], grad_scores))
            low = jnp.concatenate(parts, axis=0).T.astype(bf16).astype(f32) * HD ** (-0.5)
            pad[j, at, 0:head_cols] = low.astype(bf16)
            vz[j, 8:9, 0:head_cols] += jnp.sum(low, axis=0, keepdims=True)
            return 0

        lax.fori_loop(0, rows // tile, body, 0)
        pad[j, :, head_cols : 2 * head_cols] = dk_acc[...].astype(bf16)
        low = dv_acc[...].astype(bf16)
        pad[j, :, 2 * head_cols : 3 * head_cols] = low
        vz[j, 8:9, head_cols : 2 * head_cols] = jnp.sum(low.astype(f32), axis=0, keepdims=True)

    for n, j in enumerate((3, 1, 2, 0)):
        coming[("qkv", j)].wait()
        attend_back(j)
        if n == 0:
            send_second(1, 2)
            send_second(1, 1)
            send_second(1, 0)
        else:
            send_third(1, 4 - n)
        weight_grad(0, j, lambda: pad[j, :, front], front)
        send_first(0, j)
    for j in range(1, 4):
        v_copy(j).start()
    zg[place] = vz[0]
    send_second(0, 3)

    def input_rows(start, target):
        def body(i, _):
            at = pl.ds(pl.multiple_of(start + i * tile, tile), tile)
            to = pl.ds(pl.multiple_of(i * tile, tile), tile)
            total = nt(pad[0, at, front], w[0, 0, :, front])
            for j in range(1, 4):
                total += nt(pad[j, at, front], w[0, j, :, front])
            target[to, :] = total.astype(target.dtype)
            return 0

        lax.fori_loop(0, own // tile, body, 0)

    share_gm.wait_send()
    share_first.wait_send()
    input_rows(own, other)
    share_in = exchange(other, got, 3)
    share_in.start()
    send_second(0, 2)
    input_rows(0, own_part)
    send_third(1, 0)
    send_second(0, 1)
    share_in.wait_recv()

    def input_body(i, _):
        at = pl.ds(pl.multiple_of(i * small, small), small)
        value = gm[at, :] + (own_part[at, :] + got[at, :].astype(f32))
        low = value.astype(bf16)
        for k in range(4):
            number = (plane, plane + 1 - 2 * (plane % 2), (plane + 2) % 4, 3 - plane)[k]
            to = pl.ds(pl.multiple_of(number * piece, piece), piece)
            gi_own[at, to] = low[:, k * piece : (k + 1) * piece]
        return 0

    lax.fori_loop(0, own // small, input_body, 0)
    back_start(gi_own, gi_ref, g_s, g_r)

    def fold(n, m, arrived, flip):
        for k in range(4):
            here = slice(k * piece, (k + 1) * piece)
            there = slice((k ^ flip) * piece, ((k ^ flip) + 1) * piece)
            tot[n, 0:8, here] = tot[m, 0:8, here] + arrived[0:8, there]
        tot[n, 8:16, :] = tot[m, 8:16, :] + arrived[8:16, :]

    for j in range(1, 4):
        v_got(j).wait_recv()
    tot[0] = ((zg[0] + zg[1]) + zg[2]) + zg[3]
    v_x = remote(tot.at[0], xg, e_s.at[4], e_r.at[4], x_side)
    v_x.start()
    send_second(0, 0)
    v_x.wait_recv()
    fold(1, 0, xg, 1)
    v_y = remote(tot.at[1], yg, e_s.at[5], e_r.at[5], y_side)
    v_y.start()
    send_third(0, 3)
    v_y.wait_recv()
    fold(2, 1, yg, 2)
    v_c = exchange(tot.at[2], cg, 6)
    v_c.start()
    send_third(0, 2)
    send_third(0, 1)
    send_third(0, 0)
    v_c.wait_recv()
    for k in range(4):
        number = (plane, plane + 1 - 2 * (plane % 2), (plane + 2) % 4, 3 - plane)[k]
        to = pl.ds(pl.multiple_of(number * piece, piece), piece)
        here = slice(k * piece, (k + 1) * piece)
        total_ref[0:8, to] = tot[2, 0:8, here] + cg[0:8, here]
    own_row = tot[2, 8:9, :]
    their_row = cg[8:9, :]
    total_ref[8:9, :] = jnp.where(core == 0, own_row, their_row)
    total_ref[9:10, :] = jnp.where(core == 0, their_row, own_row)

    for b in range(3):
        for j in range(4):
            d_copy(b, j).wait_send()
            x_copy(b, j).wait_send()
            y_copy(b, j).wait_send()
            if j > 0:
                z_copy(b, j).wait_send()
    for n in range(6):
        home_keep(n).wait()
        home_copy(n).wait_send()
        home_copy(n).wait_recv()
    for j in range(1, 4):
        v_copy(j).wait_send()
    for copy in (share_att, share_in, v_x, v_y, v_c):
        copy.wait_send()
    back_end(lo_own, lo_ref, lo_s, lo_r)
    back_end(gi_own, gi_ref, g_s, g_r)


def backward(w_all, xf, qkv, lse, ctx, ff, hid, dg, n1, inv1, gm, vec, sums, length, lo):
    rows, width = xf.shape
    own = rows // 2
    part = own // 4
    piece = width // 4
    cols = hid.shape[2]
    head_cols = 2 * HD
    any_ = pl.BlockSpec(memory_space=pltpu.HBM)
    vm = pl.BlockSpec(memory_space=pltpu.VMEM)
    shape = jax.ShapeDtypeStruct
    dma = pltpu.SemaphoreType.DMA
    flops = 2 * rows * width * cols * 24 + 40 * rows * rows * HD * 4
    return pl.pallas_call(
        backward_kernel,
        in_specs=[
            any_, any_, any_, vm, any_, any_, any_, any_, any_, vm, any_, vm, vm, vm, any_
        ],
        out_specs=[any_] * 8 + [vm],
        out_shape=[
            shape((2, 2 * part, width), bf16),
            shape((2, 2 * part, width), bf16),
            shape((piece // 2, 2 * head_cols), f32),
            shape((piece // 2, 2 * head_cols), f32),
            shape((piece // 2, 2 * head_cols), f32),
            shape((2 * head_cols, piece // 2), f32),
            shape((piece // 2, 2 * cols), f32),
            shape((2 * cols, piece // 2), f32),
            shape((16, width), f32),
        ],
        scratch_shapes=[
            pltpu.VMEM((3, 4, width, cols), bf16),
            pltpu.VMEM((4, width, cols), bf16),
            pltpu.VMEM((4, rows, cols), bf16),
            pltpu.VMEM((4, rows, cols), bf16),
            pltpu.VMEM((rows, width), bf16),
            pltpu.VMEM((rows, width), bf16),
            pltpu.VMEM((rows, width), bf16),
            pltpu.VMEM((width, rows), bf16),
            pltpu.VMEM((own, width), f32),
            pltpu.VMEM((own, width), f32),
            pltpu.VMEM((own, width), f32),
            pltpu.VMEM((own, width), bf16),
            pltpu.VMEM((own, width), bf16),
            pltpu.VMEM((3, 4, piece, cols), bf16),
            pltpu.VMEM((3, 4, piece, cols), bf16),
            pltpu.VMEM((3, 4, piece, cols), bf16),
            pltpu.VMEM((3, 3, piece, cols), bf16),
            pltpu.VMEM((3, piece, cols), f32),
            pltpu.VMEM((rows, head_cols), f32),
            pltpu.VMEM((rows, head_cols), f32),
            pltpu.VMEM((4, 16, width), f32),
            pltpu.VMEM((4, 16, width), f32),
            pltpu.VMEM((16, width), f32),
            pltpu.VMEM((16, width), f32),
            pltpu.VMEM((16, width), f32),
            pltpu.VMEM((3, 16, width), f32),
            pltpu.VMEM((head_cols, piece), f32),
            pltpu.VMEM((cols, piece), f32),
            dma((3, 4)), dma((3, 4)), dma((3, 4)), dma((3, 4)), dma((3, 4)), dma((3, 4)),
            dma((3, 3)), dma((3, 3)), dma((6,)), dma((6,)), dma((6,)), dma((8,)), dma((8,)),
            dma((4,)), dma((4,)), dma((3,)), dma((4,)), dma((32,)),
            dma((4,)), dma((4,)),
        ],
        compiler_params=pltpu.CompilerParams(
            collective_id=1, has_side_effects=True, vmem_limit_bytes=60 << 20
        ),
        cost_estimate=pl.CostEstimate(
            flops=flops, bytes_accessed=60 << 20, transcendentals=8 * rows * rows
        ),
        name="backward_layer",
    )(w_all, xf, qkv, lse, ctx, ff, hid, dg, n1, inv1, gm, vec, sums, length, lo)


def swap_cores(value):
    return lax.ppermute(value, "core", SWAP)


def on_device(
    inputs,
    lengths,
    w_query,
    w_key,
    w_value,
    b_query,
    b_value,
    w_out,
    b_out,
    gain_one,
    shift_one,
    w_in,
    b_in,
    w_back,
    b_back,
    gain_two,
    shift_two,
    cotangent,
):
    planes = lax.axis_size("plane")
    n_t = lax.axis_size("tensor")
    plane = lax.axis_index("plane")
    core = lax.axis_index("core")
    place = lax.axis_index("tensor")
    seqs, slots_here, width = inputs.shape
    slots = slots_here * n_t
    half_slots = slots_here // 2
    own = slots // 2
    assert seqs * 2 == n_t
    head_cols = w_query.shape[1] // 2
    ff_cols = w_in.shape[1] // 2
    scale = HD ** (-0.5)
    quad = planes == 4
    if quad:
        row = jnp.stack(
            [
                value.astype(f32)
                for value in (
                    b_out, gain_one, shift_one, b_back, gain_two, shift_two, b_in,
                    jnp.concatenate([b_query, b_value, jnp.zeros((width // 2,), bf16)]),
                )
            ]
        )
        lens = jnp.broadcast_to(
            jnp.concatenate([lengths.astype(f32)] * (8 // seqs))[:, None], (8, 128)
        )
        (w_all, x_full, qkv4, lse8, ctx4, first_full, hid4, dg4, normed_one, inverse_one,
         grad_mixed, lo, second_sums, vec, length_rows) = forward(
            lens, row, inputs, cotangent, w_query, w_key, w_value, w_out, w_in, w_back
        )
        (layer_out, gi, grad_w_query, grad_w_key, grad_w_value, grad_w_out, grad_w_in,
         grad_w_back, totals) = backward(
            w_all, x_full, qkv4, lse8, ctx4, first_full, hid4, dg4, normed_one, inverse_one,
            grad_mixed, vec, second_sums, length_rows, lo,
        )
        n_bias = 2 * head_cols + ff_cols
        biases_out = totals[8:10, :n_bias]
        return (
            layer_out,
            gi.astype(f32),
            grad_w_query,
            grad_w_key,
            grad_w_value,
            biases_out[:, :head_cols].reshape(-1),
            biases_out[:, head_cols : 2 * head_cols].reshape(-1),
            grad_w_out,
            totals[0],
            totals[1],
            totals[2],
            grad_w_in,
            biases_out[:, 2 * head_cols :].reshape(-1),
            grad_w_back,
            totals[3],
            totals[4],
            totals[5],
        )

    ring = [(i, (i + 1) % n_t) for i in range(n_t)]
    x_pairs = [(i, i ^ 1) for i in range(planes)]
    y_pairs = [(i, i ^ 2) for i in range(planes)]

    def reorder(value, axis):
        if not quad:
            return value
        size = value.shape[axis] // 4
        return jnp.concatenate(
            [lax.dynamic_slice_in_dim(value, (plane ^ k) * size, size, axis) for k in range(4)],
            axis=axis,
        )

    def by_core(mine, theirs, axis=0):
        first = jnp.where(core == 0, mine, theirs)
        second = jnp.where(core == 0, theirs, mine)
        return jnp.concatenate([first, second], axis=axis)

    def to_chip(rows_here):
        value = reorder(rows_here, 2).reshape(seqs, 2, half_slots, width)
        mine = lax.dynamic_index_in_dim(value, core, 1, keepdims=False)
        other = lax.dynamic_index_in_dim(value, 1 - core, 1, keepdims=False)
        both = by_core(mine, swap_cores(other))
        return lax.all_to_all(both, "tensor", 0, 0, tiled=True).reshape(own, width)

    def from_chip(rows_own):
        value = rows_own.reshape(n_t, half_slots, width)
        value = lax.all_to_all(value, "tensor", 0, 0, tiled=True)
        value = value.reshape(2, seqs, half_slots, width)
        mine = lax.dynamic_index_in_dim(value, core, 0, keepdims=False)
        other = lax.dynamic_index_in_dim(value, 1 - core, 0, keepdims=False)
        got = swap_cores(other)
        value = jnp.stack(
            [jnp.where(core == 0, mine, got), jnp.where(core == 0, got, mine)], axis=1
        )
        return reorder(value.reshape(seqs, slots_here, width), 2)

    their_lengths = swap_cores(lengths)
    all_lengths = by_core(lengths, their_lengths)
    length = lax.dynamic_index_in_dim(all_lengths, place, 0, keepdims=False)
    index = jnp.arange(slots)
    position = (
        (index % own) // half_slots * slots_here
        + ((index // own) ^ core) * half_slots
        + index % half_slots
    )
    valid = position < length
    key_bias = jnp.where(valid, 0.0, NEGATIVE).astype(f32)[:, None]
    own_valid = valid[:own, None]

    def halves(value, cols):
        return (
            lax.dynamic_slice_in_dim(value, core * cols, cols, 1),
            lax.dynamic_slice_in_dim(value, (1 - core) * cols, cols, 1),
        )

    pieces = [
        halves(w_query, head_cols),
        halves(w_key, head_cols),
        halves(w_value, head_cols),
        halves(w_out.T, head_cols),
        halves(w_in, ff_cols),
        halves(w_back.T, ff_cols),
    ]
    keep = jnp.concatenate([piece[0] for piece in pieces], axis=1)
    give = jnp.concatenate([piece[1] for piece in pieces], axis=1)
    cuts = (4 * head_cols, 4 * head_cols + ff_cols)

    def flat(gathered):
        return jnp.concatenate([gathered[j] for j in range(n_t)], axis=1)

    out_bias = reorder(b_out, 0).astype(f32)
    back_bias = reorder(b_back, 0).astype(f32)
    gain_first = reorder(gain_one, 0).astype(f32)
    shift_first = reorder(shift_one, 0).astype(f32)
    gain_second = reorder(gain_two, 0).astype(f32)
    shift_second = reorder(shift_two, 0).astype(f32)
    bias_row = jnp.concatenate(
        [
            lax.dynamic_slice_in_dim(b_query, core * head_cols, head_cols),
            lax.dynamic_slice_in_dim(b_value, core * head_cols, head_cols),
            lax.dynamic_slice_in_dim(b_in, core * ff_cols, ff_cols),
        ]
    )[None]
    qkv_scale = jnp.tile(
        jnp.concatenate([jnp.full((head_cols,), scale, f32), jnp.ones((2 * head_cols,), f32)]), n_t
    )[None]
    def both_rows(value):
        return jnp.concatenate([value, swap_cores(value)], axis=0)

    def own_sum(partial):
        return partial[:own] + swap_cores(partial[own:])

    def normalize(value):
        average = jnp.mean(value, axis=-1, keepdims=True)
        centered = value - average
        variance = jnp.mean(centered * centered, axis=-1, keepdims=True)
        inverse = lax.rsqrt(variance + EPSILON)
        return centered * inverse, inverse

    def normalize_back(grad, gain, normed, inverse):
        e = grad * gain
        return (
            e
            - jnp.mean(e, axis=-1, keepdims=True)
            - normed * jnp.mean(e * normed, axis=-1, keepdims=True)
        ) * inverse

    packed = by_core(keep, swap_cores(give))
    bundle_a = packed[:, : cuts[0]]
    bundle_b = packed[:, cuts[0] : cuts[1]]
    bundle_c = packed[:, cuts[1] :]
    def gather_z(own_piece):
        got = [own_piece]
        for _ in range(n_t - 1):
            got.append(lax.ppermute(got[-1], "tensor", ring))
        return jnp.stack(got)

    def gather_planes(mine):
        if not quad:
            return lax.all_gather(mine, "plane", axis=1, tiled=True)
        half = n_t // 2
        from_x = lax.ppermute(mine, "plane", x_pairs)
        from_y = lax.ppermute(mine, "plane", y_pairs)
        low = lax.ppermute(from_y[:half], "plane", x_pairs)
        high = lax.ppermute(from_x[half:], "plane", y_pairs)
        return jnp.concatenate([mine, from_x, from_y, jnp.concatenate([low, high])], axis=1)

    biases = gather_z(bias_row)[:, 0].astype(f32)
    z_a = gather_z(bundle_a)
    full_a = gather_planes(z_a)
    w_qkv = flat(full_a[:, :, : 3 * head_cols])
    w_o = flat(full_a[:, :, 3 * head_cols :])
    w_1 = flat(gather_planes(gather_z(bundle_b)))
    w_2 = flat(gather_planes(gather_z(bundle_c)))

    zeros_k = jnp.zeros((n_t, head_cols), f32)
    qkv_bias = jnp.concatenate(
        [biases[:, :head_cols], zeros_k, biases[:, head_cols : 2 * head_cols]], axis=1
    ).reshape(1, -1)
    in_bias = biases[:, 2 * head_cols :].reshape(1, -1)

    own_x = to_chip(inputs)
    x_full = both_rows(own_x)
    qkv = ((nn(x_full, w_qkv) + qkv_bias) * qkv_scale).astype(bf16)
    context, lse = attend_fwd(qkv, key_bias)
    attended = own_sum(nt(context, w_o))
    normed_one, inverse_one = normalize(own_x.astype(f32) + attended + out_bias)
    first_norm = normed_one * gain_first + shift_first
    first_full = both_rows(first_norm.astype(bf16))
    pre_act = nn(first_full, w_1) + in_bias
    activated, slope = gelu_and_slope(pre_act)
    hidden = activated.astype(bf16)
    mixed = own_sum(nt(hidden, w_2))
    normed_two, inverse_two = normalize(first_norm + mixed + back_bias)
    second = normed_two * gain_second + shift_second
    layer_out = from_chip(jnp.where(own_valid, second, 0.0).astype(bf16))

    grad_second = jnp.where(own_valid, to_chip(cotangent).astype(f32), 0.0)
    grad_mixed = normalize_back(grad_second, gain_second, normed_two, inverse_two)

    grad_mixed_full = both_rows(grad_mixed.astype(bf16))
    grad_w2 = tn(grad_mixed_full, hidden)
    grad_pre_low = (nn(grad_mixed_full, w_2) * slope.astype(f32)).astype(bf16)
    grad_w1 = tn(first_full, grad_pre_low)
    grad_first = grad_mixed + own_sum(nt(grad_pre_low, w_1))
    grad_att = normalize_back(grad_first, gain_first, normed_one, inverse_one)
    grad_att_full = both_rows(grad_att.astype(bf16))
    grad_context = nn(grad_att_full, w_o).astype(bf16)
    grad_wo = tn(grad_att_full, context)
    grad_qkv = attend_bwd(qkv, grad_context, lse, key_bias)
    grad_qkv = grad_qkv * qkv_scale.astype(bf16)
    grad_wqkv = tn(x_full, grad_qkv)
    grad_rows = grad_att + own_sum(nt(grad_qkv, w_qkv))
    grad_inputs = from_chip(grad_rows.astype(bf16)).astype(f32)

    def scatter(grad):
        cols = grad.shape[1] // n_t
        if quad:
            rows = width // 4
            blocks = grad.reshape(4, rows, n_t, cols).transpose(0, 2, 1, 3)
            half = n_t // 2
            low = lax.ppermute(blocks[3, :half].astype(bf16), "plane", x_pairs)
            high = lax.ppermute(blocks[3, half:].astype(bf16), "plane", y_pairs)
            for_y = jnp.concatenate([blocks[2, :half] + low.astype(f32), blocks[2, half:]])
            for_x = jnp.concatenate([blocks[1, :half], blocks[1, half:] + high.astype(f32)])
            from_x = lax.ppermute(for_x.astype(bf16), "plane", x_pairs)
            from_y = lax.ppermute(for_y.astype(bf16), "plane", y_pairs)
            mine = blocks[0] + from_x.astype(f32) + from_y.astype(f32)
        else:
            blocks = grad.reshape(width, n_t, cols).transpose(1, 0, 2)
            mine = lax.psum_scatter(
                blocks.astype(bf16), "plane", scatter_dimension=1, tiled=True
            ).astype(f32)
        back = [(b, a) for a, b in ring]
        total = mine[n_t - 1]
        for j in range(n_t - 2, -1, -1):
            total = mine[j] + lax.ppermute(total.astype(bf16), "tensor", back).astype(f32)
        return total

    home_c = scatter(grad_w2)
    home_b = scatter(grad_w1)
    grad_a = jnp.concatenate(
        [
            grad_wqkv.reshape(width, n_t, 3 * head_cols),
            grad_wo.reshape(width, n_t, head_cols),
        ],
        axis=2,
    ).reshape(width, -1)
    home_a = scatter(grad_a)
    home = jnp.concatenate([home_a, home_b, home_c], axis=1)
    home = home.reshape(2, -1, home.shape[1])
    mine = lax.dynamic_index_in_dim(home, core, 0, keepdims=False)
    other = lax.dynamic_index_in_dim(home, 1 - core, 0, keepdims=False)
    got = swap_cores(other)

    def row_sum(value):
        return reorder(jnp.sum(value, axis=0), 0)

    second_rows = [row_sum(grad_mixed), row_sum(grad_second * normed_two), row_sum(grad_second)]
    norm_sums = jnp.concatenate(
        [
            row_sum(grad_att),
            row_sum(grad_first * normed_one),
            row_sum(grad_first),
            *second_rows,
        ]
    )
    qkv_sum = jnp.sum(grad_qkv.astype(f32), axis=0).reshape(n_t, 3 * head_cols)
    pre_sum = jnp.sum(grad_pre_low.astype(f32), axis=0).reshape(n_t, ff_cols)
    bias_sum = jnp.concatenate([qkv_sum[:, :head_cols], qkv_sum[:, 2 * head_cols :], pre_sum], axis=1)
    at_home = lax.rem(place - jnp.arange(n_t) + n_t, n_t)
    spread = (at_home[:, None] == jnp.arange(n_t)[None]).astype(f32)
    by_place = jnp.sum(spread[:, :, None] * bias_sum[:, None, :], axis=0)
    both = jnp.where(
        (jnp.arange(2) == core)[None, :, None], by_place[:, None, :], 0.0
    )
    sums = lax.psum(jnp.concatenate([norm_sums, both.reshape(-1)]), ("plane", "core", "tensor"))
    norms = sums[: 6 * width].reshape(6, width)
    biases_out = lax.dynamic_index_in_dim(
        sums[6 * width :].reshape(n_t, 2, -1), place, 0, keepdims=False
    )
    def columns(start, cols):
        return by_core(mine[:, start : start + cols], got[:, start : start + cols], axis=1)

    grad_w_query = columns(0, head_cols)
    grad_w_key = columns(head_cols, head_cols)
    grad_w_value = columns(2 * head_cols, head_cols)
    grad_w_out = columns(3 * head_cols, head_cols).T
    grad_w_in = columns(cuts[0], ff_cols)
    grad_w_back = columns(cuts[1], ff_cols).T

    grad_b_query = biases_out[:, :head_cols].reshape(-1)
    grad_b_value = biases_out[:, head_cols : 2 * head_cols].reshape(-1)
    grad_b_in = biases_out[:, 2 * head_cols :].reshape(-1)
    return (
        layer_out,
        grad_inputs,
        grad_w_query,
        grad_w_key,
        grad_w_value,
        grad_b_query,
        grad_b_value,
        grad_w_out,
        norms[0],
        norms[1],
        norms[2],
        grad_w_in,
        grad_b_in,
        grad_w_back,
        norms[3],
        norms[4],
        norms[5],
    )


def solution(mesh):
    devices = mesh.devices.reshape(mesh.shape["dp"] // 2, 2, mesh.shape["tensor"])
    inner = Mesh(devices, ("plane", "core", "tensor"))
    dp = ("plane", "core")
    row = P(dp, "tensor")
    column = P("tensor", dp)
    rows3 = P(dp, "tensor", None)
    shard = P("tensor")
    whole = P()
    return jax.shard_map(
        on_device,
        mesh=inner,
        in_specs=(
            rows3, P(dp), row, row, row, shard, shard, column, whole, whole, whole,
            row, shard, column, whole, whole, whole, rows3,
        ),
        out_specs=(
            rows3, rows3, row, row, row, shard, shard, column, whole, whole, whole,
            row, shard, column, whole, whole, whole,
        ),
        check_vma=False,
    )
```

```python
import jax
import jax.numpy as jnp
from jax import lax
from jax.experimental import pallas as pl
from jax.experimental.pallas import tpu as pltpu
from jax.sharding import Mesh, PartitionSpec as P

HD = 64
EPSILON = 1e-05
NEGATIVE = -1e30
f32 = jnp.float32
bf16 = jnp.bfloat16
SWAP = [(0, 1), (1, 0)]


def nt(a, b):
    return lax.dot_general(a, b, (((1,), (1,)), ((), ())), preferred_element_type=f32)


def tn(a, b):
    return lax.dot_general(a, b, (((0,), (0,)), ((), ())), preferred_element_type=f32)


def nn(a, b):
    return lax.dot_general(a, b, (((1,), (0,)), ((), ())), preferred_element_type=f32)


def attend_fwd_kernel(block, qkv_ref, kb_ref, ctx_ref, lse_ref):
    rows = qkv_ref.shape[0]
    lane = lax.broadcasted_iota(jnp.int32, (1, 2 * HD), 1)
    keys = qkv_ref[:, 2 * HD : 4 * HD]
    values_t = qkv_ref[:, 4 * HD : 6 * HD].T
    key_bias = kb_ref[...]
    for start in range(0, rows, block):
        query = qkv_ref[start : start + block, 0 : 2 * HD]
        parts = []
        for h in range(2):
            query_h = jnp.where(lane // HD == h, query, jnp.zeros_like(query))
            scores = nt(keys, query_h) + key_bias
            largest = jnp.max(scores, axis=0, keepdims=True)
            weights = jnp.exp(scores - largest)
            total = jnp.sum(weights, axis=0, keepdims=True)
            part = nn(values_t[h * HD : (h + 1) * HD], weights.astype(bf16))
            parts.append(part / total)
            lse_ref[0, h : h + 1, start : start + block] = largest + jnp.log(total)
        ctx_ref[start : start + block, :] = jnp.concatenate(parts, axis=0).T.astype(bf16)


def attend_fwd(qkv, key_bias):
    rows = qkv.shape[0]
    groups = qkv.shape[1] // (6 * HD)
    block = min(512, rows)
    return pl.pallas_call(
        lambda *refs: attend_fwd_kernel(block, *refs),
        grid=(groups,),
        in_specs=[
            pl.BlockSpec((rows, 6 * HD), lambda j: (0, j)),
            pl.BlockSpec((rows, 1), lambda j: (0, 0)),
        ],
        out_specs=[
            pl.BlockSpec((rows, 2 * HD), lambda j: (0, j)),
            pl.BlockSpec((1, 2, rows), lambda j: (j, 0, 0)),
        ],
        out_shape=[
            jax.ShapeDtypeStruct((rows, groups * 2 * HD), bf16),
            jax.ShapeDtypeStruct((groups, 2, rows), f32),
        ],
        compiler_params=pltpu.CompilerParams(vmem_limit_bytes=48 << 20),
        cost_estimate=pl.CostEstimate(
            flops=groups * 8 * rows * rows * HD * 4,
            bytes_accessed=rows * groups * 8 * HD * 2,
            transcendentals=groups * 2 * rows * rows,
        ),
        name="attend_fwd",
    )(qkv, key_bias)


def attend_bwd_kernel(block, qkv_ref, g_ref, lse_ref, kb_ref, d_ref, dk_acc, dv_acc):
    rows = qkv_ref.shape[0]
    lane = lax.broadcasted_iota(jnp.int32, (1, 2 * HD), 1)
    keys = qkv_ref[:, 2 * HD : 4 * HD]
    keys_t = keys.T
    values = qkv_ref[:, 4 * HD : 6 * HD]
    key_bias = kb_ref[...]
    for start in range(0, rows, block):
        query = qkv_ref[start : start + block, 0 : 2 * HD]
        grad = g_ref[start : start + block, :]
        parts = []
        for h in range(2):
            here = lane // HD == h
            query_h = jnp.where(here, query, jnp.zeros_like(query))
            grad_h = jnp.where(here, grad, jnp.zeros_like(grad))
            scores = nt(keys, query_h) + key_bias
            chances = jnp.exp(scores - lse_ref[0, h : h + 1, start : start + block])
            grad_chances = nt(values, grad_h)
            inner = jnp.sum(chances * grad_chances, axis=0, keepdims=True)
            grad_scores = (chances * (grad_chances - inner)).astype(bf16)
            dv = nn(chances.astype(bf16), grad_h)
            dk = nn(grad_scores, query_h)
            if start == 0 and h == 0:
                dv_acc[...] = dv
                dk_acc[...] = dk
            else:
                dv_acc[...] += dv
                dk_acc[...] += dk
            parts.append(nn(keys_t[h * HD : (h + 1) * HD], grad_scores))
        d_ref[start : start + block, 0 : 2 * HD] = jnp.concatenate(parts, axis=0).T.astype(bf16)
    d_ref[:, 2 * HD : 4 * HD] = dk_acc[...].astype(bf16)
    d_ref[:, 4 * HD : 6 * HD] = dv_acc[...].astype(bf16)


def attend_bwd(qkv, grad_context, lse, key_bias):
    rows = qkv.shape[0]
    groups = qkv.shape[1] // (6 * HD)
    block = min(512, rows)
    return pl.pallas_call(
        lambda *refs: attend_bwd_kernel(block, *refs),
        grid=(groups,),
        in_specs=[
            pl.BlockSpec((rows, 6 * HD), lambda j: (0, j)),
            pl.BlockSpec((rows, 2 * HD), lambda j: (0, j)),
            pl.BlockSpec((1, 2, rows), lambda j: (j, 0, 0)),
            pl.BlockSpec((rows, 1), lambda j: (0, 0)),
        ],
        out_specs=pl.BlockSpec((rows, 6 * HD), lambda j: (0, j)),
        out_shape=jax.ShapeDtypeStruct((rows, groups * 6 * HD), bf16),
        scratch_shapes=[pltpu.VMEM((rows, 2 * HD), f32), pltpu.VMEM((rows, 2 * HD), f32)],
        compiler_params=pltpu.CompilerParams(vmem_limit_bytes=48 << 20),
        cost_estimate=pl.CostEstimate(
            flops=groups * 20 * rows * rows * HD * 4,
            bytes_accessed=rows * groups * 14 * HD * 2,
            transcendentals=groups * 2 * rows * rows,
        ),
        name="attend_bwd",
    )(qkv, grad_context, lse, key_bias)

POLY = (
    0.30995978221815235,
    0.31100346478903146,
    0.2699660979585953,
    0.2765467936611628,
    -0.03831584737802812,
    0.38967711658103854,
    -0.3554874111653827,
    0.08996434684501212,
)
POLY_AT = 0.31
DENSITY = 0.3989422804014327
MESH = pl.DeviceIdType.MESH


def gelu_and_slope(v):
    density = jnp.exp(-0.5 * v * v) * DENSITY
    t = 1.0 / (1.0 + POLY_AT * jnp.abs(v))
    tail = jnp.full_like(v, POLY[-1])
    for coefficient in POLY[-2::-1]:
        tail = tail * t + coefficient
    tail = tail * t * density
    below = jnp.where(v > 0, 1.0 - tail, tail)
    return v * below, below + v * density


def forward_kernel(
    lens_ref, row_ref, x_ref, c_ref, wq_ref, wk_ref, wv_ref, wo_ref, wi_ref, wb_ref,
    w_out, xf_out, qkv_out, lse_ref, ctx_out, ff_out, hid_out, dg_out, n1_out, inv1_ref, gm_ref,
    lo_ref, sums_ref, vec_ref, length_ref,
    w, xs, xf, bias, qkv, ctx, ff, hid, dg, n1, first, other_acc, other_part, own_part, att_got, mix_got, cot,
    wo_here, wb_here, wo_give, wb_give, lens, parts_of,
    z_s, z_r, zl_s, zl_r, x_s, x_r, y_s, y_r, f_s, f_r, pre_l, pre_s, pre_r, b_s, b_r,
    xa_s, xa_r, ca_s, ca_r, e_s, e_r, o_s,
):
    plane = lax.axis_index("plane")
    core = lax.axis_index("core")
    place = lax.axis_index("tensor")
    partner = {"core": 1 - core}
    x_side = {"plane": plane + 1 - 2 * (plane % 2)}
    y_side = {"plane": (plane + 2) % 4}
    z_right = {"tensor": (place + 1) % 4}
    z_left = {"tensor": (place + 3) % 4}
    first_end = (3 - place) // 3
    last_end = place // 3
    turns = (0, 1 + 2 * first_end, 3 - first_end - last_end, 2 - first_end + last_end)
    rows = xf.shape[0]
    own = rows // 2
    part = own // 4
    piece = w.shape[2] // 4

    def remote(source, target, send, recv, to):
        return pltpu.make_async_remote_copy(
            source, target, send, recv, device_id=to, device_id_type=MESH
        )

    def right_copy(b, n):
        return remote(
            w.at[b, n - 1, 0:piece], w.at[b, n, 0:piece], z_s.at[b, n - 1], z_r.at[b, n - 1], z_right
        )

    def left_copy(b, n):
        return remote(
            w.at[b, (5 - n) % 4, 0:piece], w.at[b, 4 - n, 0:piece],
            zl_s.at[b, n - 1], zl_r.at[b, n - 1], z_left,
        )

    def line_do(b, n, act):
        @pl.when(jnp.logical_and(place <= 2, place >= n - 1))
        def _():
            act(right_copy(b, n))

        @pl.when(jnp.logical_and(place >= 1, place + n <= 4))
        def _():
            act(left_copy(b, n))

    def line_start(b, n):
        line_do(b, n, lambda copy: copy.start())

    def line_wait(b, n):
        @pl.when(place >= n)
        def _():
            right_copy(b, n).wait_recv()

        @pl.when(place + n <= 3)
        def _():
            left_copy(b, n).wait_recv()

    def x_copy(b, n):
        j = turns[n]
        return remote(
            w.at[b, j, 0:piece], w.at[b, j, piece : 2 * piece], x_s.at[b, n], x_r.at[b, n], x_side
        )

    def y_copy(b, n):
        j = turns[n]
        return remote(
            w.at[b, j, 0:piece], w.at[b, j, 2 * piece : 3 * piece], y_s.at[b, n], y_r.at[b, n], y_side
        )

    def fx_copy(b, n):
        j, half = turns[n], piece // 2
        return remote(
            w.at[b, j, 2 * piece : 2 * piece + half], w.at[b, j, 3 * piece : 3 * piece + half],
            f_s.at[b, n, 0], f_r.at[b, n, 0], x_side,
        )

    def fy_copy(b, n):
        j, half = turns[n], piece // 2
        return remote(
            w.at[b, j, piece + half : 2 * piece], w.at[b, j, 3 * piece + half : 4 * piece],
            f_s.at[b, n, 1], f_r.at[b, n, 1], y_side,
        )

    def cross(b, n):
        x_copy(b, n).start()
        y_copy(b, n).start()

    def forward_on(b, n):
        y_copy(b, n).wait_recv()
        fx_copy(b, n).start()
        x_copy(b, n).wait_recv()
        fy_copy(b, n).start()

    def ready(b, n):
        fx_copy(b, n).wait_recv()
        fy_copy(b, n).wait_recv()
        save(w.at[b, turns[n]], w_out.at[b, turns[n]])

    half_piece = piece // 2
    head_cols = 2 * HD
    mine_at = pl.ds(core * half_piece, half_piece)
    theirs_at = pl.ds((1 - core) * half_piece, half_piece)
    cols = w.shape[3]

    def head_half(which):
        return pl.ds(pl.multiple_of(which * head_cols, head_cols), head_cols)

    def wide_half(which):
        return pl.ds(pl.multiple_of(which * cols, cols), cols)

    def keep_copy(n):
        if n < 3:
            source = (wq_ref, wk_ref, wv_ref)[n].at[:, head_half(core)]
            target = w.at[0, 0, mine_at, n * head_cols : (n + 1) * head_cols]
        elif n == 3:
            source, target = wo_ref, wo_here
        elif n == 4:
            source, target = wi_ref.at[:, wide_half(core)], w.at[1, 0, mine_at]
        else:
            source, target = wb_ref, wb_here
        return pltpu.make_async_copy(source, target, pre_l.at[n])

    def pre_copy(n, at):
        if n < 3:
            source = (wq_ref, wk_ref, wv_ref)[n].at[:, head_half(1 - core)]
            target = w.at[0, 0, at, n * head_cols : (n + 1) * head_cols]
        elif n == 3:
            source, target = wo_give, w.at[0, 0, at, 3 * head_cols : 4 * head_cols]
        elif n == 4:
            source, target = wi_ref.at[:, wide_half(1 - core)], w.at[1, 0, at]
        else:
            source, target = wb_give, w.at[2, 0, at]
        return remote(source, target, pre_s.at[n], pre_r.at[n], partner)

    def bias_copy(s):
        return remote(
            bias.at[0], bias.at[s], b_s.at[s], b_r.at[s], {"tensor": (place + s) % 4}
        )

    def spread(source, target, send, recv, l, h):
        at = pl.ds(place * part, part)
        to = {"core": h, "tensor": 2 * core + l}
        return remote(
            source.at[l, h * part : (h + 1) * part], target.at[at], send.at[2 * l + h],
            recv.at[place], to,
        )

    def spread_local(source, target, recv, l, h):
        at = pl.ds(place * part, part)
        return pltpu.make_async_copy(
            source.at[l, h * part : (h + 1) * part], target.at[at], recv.at[place]
        )

    def is_here(l, h):
        return jnp.logical_and(core == h, place == 2 * core + l)

    def spread_start(source, target, send, recv):
        for l in range(2):
            for h in range(2):
                @pl.when(is_here(l, h))
                def _():
                    spread_local(source, target, recv, l, h).start()

                @pl.when(jnp.logical_not(is_here(l, h)))
                def _():
                    spread(source, target, send, recv, l, h).start()

    def spread_wait(source, target, recv):
        for s in range(4):
            pltpu.make_async_copy(
                source.at[0, 0:part], target.at[s * part : (s + 1) * part], recv.at[s]
            ).wait()

    def spread_sent(source, target, send, recv):
        for l in range(2):
            for h in range(2):
                @pl.when(jnp.logical_not(is_here(l, h)))
                def _():
                    spread(source, target, send, recv, l, h).wait_send()

    def exchange(source, target, n):
        return remote(source, target, e_s.at[n], e_r.at[n], partner)

    outs = []

    def save(source, target):
        copy = pltpu.make_async_copy(source, target, o_s.at[len(outs)])
        copy.start()
        outs.append(copy)

    barrier = pltpu.get_barrier_semaphore()
    friends = [x_side, y_side, partner]
    for s in range(1, 4):
        friends.append({"tensor": (place + s) % 4})
        friends.append({"tensor": (place + s) % 4, "core": 1 - core})
    for friend in friends:
        pl.semaphore_signal(barrier, inc=1, device_id=friend, device_id_type=MESH)
    for n in (3, 0, 1, 2, 4, 5):
        keep_copy(n).start()
    pl.semaphore_wait(barrier, len(friends))

    def block_at(k):
        number = (plane, plane + 1 - 2 * (plane % 2), (plane + 2) % 4, 3 - plane)[k]
        return pl.ds(pl.multiple_of(number * piece, piece), piece)

    for n in range(3):
        pre_copy(n, mine_at).start()
    keep_copy(3).wait()
    wo_give[...] = wo_here[head_half(1 - core), :].T
    pre_copy(3, mine_at).start()
    w[0, 0, mine_at, 3 * head_cols : 4 * head_cols] = wo_here[head_half(core), :].T
    pre_copy(4, mine_at).start()
    for n in range(3):
        keep_copy(n).wait()
    for n in range(4):
        pre_copy(n, theirs_at).wait_recv()
    line_start(0, 1)
    cross(0, 0)
    spread_start(x_ref, xs, xa_s, xa_r)
    keep_copy(5).wait()
    wb_give[...] = wb_here[wide_half(1 - core), :].T
    pre_copy(5, mine_at).start()
    w[2, 0, mine_at, :] = wb_here[wide_half(core), :].T
    keep_copy(4).wait()
    pre_copy(4, theirs_at).wait_recv()
    cross(1, 0)
    pre_copy(5, theirs_at).wait_recv()
    cross(2, 0)

    zero_row = jnp.zeros((1, head_cols), f32)
    heads_q = jnp.where(core == 0, row_ref[7:8, 0:head_cols], row_ref[7:8, head_cols : 2 * head_cols])
    heads_v = jnp.where(
        core == 0, row_ref[7:8, 2 * head_cols : 3 * head_cols], row_ref[7:8, 3 * head_cols : 4 * head_cols]
    )
    wide = jnp.where(core == 0, row_ref[6:7, 0:cols], row_ref[6:7, cols : 2 * cols])
    bias[0, 0:1, :] = jnp.concatenate([heads_q, zero_row, heads_v, zero_row, wide], axis=1)
    for k in range(4):
        vec_ref[:, k * piece : (k + 1) * piece] = row_ref[:, block_at(k)]
    for s in range(1, 4):
        bias_copy(s).start()
    lens[core] = lens_ref[...]
    share_len = remote(lens_ref, lens.at[core], e_s.at[4], e_r.at[4], partner)
    share_len.start()

    line_wait(0, 1)
    line_start(0, 2)
    line_start(1, 1)
    forward_on(0, 0)
    cross(0, 1)
    forward_on(1, 0)
    forward_on(2, 0)
    for s in range(1, 4):
        bias_copy(s).wait_recv()
    remote(lens_ref, lens.at[1 - core], e_s.at[4], e_r.at[4], partner).wait_recv()

    spread_wait(x_ref, xs, xa_r)
    for k in range(4):
        xf[0:own, k * piece : (k + 1) * piece] = xs[:, block_at(k)]
    share_x = exchange(xf.at[0:own], xf.at[own : 2 * own], 0)
    share_x.start()
    share_x.wait_recv()
    save(xf, xf_out)

    index = lax.broadcasted_iota(jnp.int32, (rows, 1), 0)
    length_ref[...] = lens[place // 2]
    length = length_ref[pl.ds(place % 2, 1), 0:1]
    half = jnp.where(index < own, core, 1 - core)
    inside = index % own
    position = (inside // part) * (2 * part) + half * part + inside % part
    key_bias = jnp.where(position.astype(f32) < length, 0.0, NEGATIVE).astype(f32)
    lane = lax.broadcasted_iota(jnp.int32, (1, 2 * HD), 1)
    tile = 512

    def project(n):
        j = turns[n]
        columns = lax.broadcasted_iota(jnp.int32, (1, 3 * head_cols), 1)
        zero = jnp.zeros((1, head_cols), f32)
        add = jnp.concatenate(
            [bias[j, 0:1, 0:head_cols], zero, bias[j, 0:1, 2 * head_cols : 3 * head_cols]], axis=1
        )
        times = jnp.where(columns < head_cols, HD ** (-0.5), 1.0).astype(f32)

        def body(i, _):
            at = pl.ds(pl.multiple_of(i * tile, tile), tile)
            value = nn(xf[at, :], w[0, j, :, 0 : 3 * head_cols])
            qkv[j, at, :] = ((value + add) * times).astype(bf16)
            return 0

        lax.fori_loop(0, rows // tile, body, 0)
        save(qkv.at[j], qkv_out.at[j])

    def attend(n, midway):
        j = turns[n]
        keys = qkv[j, :, head_cols : 2 * head_cols]
        values_t = qkv[j, :, 2 * head_cols : 3 * head_cols].T

        def body(start):
            at = slice(start, start + 512)
            query = qkv[j, at, 0:head_cols]
            parts = []
            for h in range(2):
                query_h = jnp.where(lane // HD == h, query, jnp.zeros_like(query))
                scores = nt(keys, query_h) + key_bias
                largest = jnp.max(scores, axis=0, keepdims=True)
                weights = jnp.exp(scores - largest)
                total = jnp.sum(weights, axis=0, keepdims=True)
                out = nn(values_t[h * HD : (h + 1) * HD], weights.astype(bf16))
                parts.append(out / total)
                lse_ref[2 * j + h, :, at] = largest + jnp.log(total)
            ctx[j, at, :] = jnp.concatenate(parts, axis=0).T.astype(bf16)

        for start in range(0, rows, 512):
            if start:
                midway()
            body(start)
        save(ctx.at[j], ctx_out.at[j])

    def between_1():
        line_wait(0, 3)
        cross(0, 3)
        forward_on(0, 2)

    def between_2():
        line_wait(1, 2)
        line_start(1, 3)

    def between_3():
        line_wait(2, 2)
        line_start(2, 3)

    ready(0, 0)
    project(0)
    line_wait(0, 2)
    line_start(0, 3)
    line_start(2, 1)
    cross(0, 2)
    forward_on(0, 1)
    attend(0, lambda: None)
    line_wait(1, 1)
    line_start(1, 2)
    ready(0, 1)
    project(1)
    attend(1, between_1)
    cross(1, 1)
    line_wait(2, 1)
    line_start(2, 2)
    forward_on(0, 3)
    ready(0, 2)
    project(2)
    attend(2, between_2)
    cross(1, 2)
    forward_on(1, 1)
    ready(0, 3)
    project(3)
    attend(3, between_3)
    line_wait(1, 3)
    cross(1, 3)
    forward_on(1, 2)

    def out_rows(start, target):
        def body(i, _):
            at = pl.ds(pl.multiple_of(start + i * tile, tile), tile)
            to = pl.ds(pl.multiple_of(i * tile, tile), tile)
            total = nt(ctx[0, at, :], w[0, 0, :, 3 * head_cols :])
            for j in range(1, 4):
                total += nt(ctx[j, at, :], w[0, j, :, 3 * head_cols :])
            target[to, :] = total.astype(target.dtype)
            return 0

        lax.fori_loop(0, own // tile, body, 0)

    out_rows(own, other_part)
    share_att = exchange(other_part, att_got, 1)
    share_att.start()
    out_rows(0, own_part)
    cross(2, 1)
    line_wait(2, 3)
    spread_start(c_ref, cot, ca_s, ca_r)
    share_att.wait_recv()
    small = 32

    def mean(value):
        return jnp.sum(value, axis=-1, keepdims=True) * (1.0 / value.shape[-1])

    def first_body(i, _):
        at = pl.ds(pl.multiple_of(i * small, small), small)
        total = xf[at, :].astype(f32) + (own_part[at, :] + att_got[at, :].astype(f32)) + vec_ref[0:1, :]
        centered = total - mean(total)
        inverse = lax.rsqrt(mean(centered * centered) + EPSILON)
        normed = centered * inverse
        n1[at, :] = normed
        inv1_ref[at, :] = inverse
        value = normed * vec_ref[1:2, :] + vec_ref[2:3, :]
        first[at, :] = value
        ff[at, :] = value.astype(bf16)
        return 0

    lax.fori_loop(0, own // small, first_body, 0)
    share_first = exchange(ff.at[0:own], ff.at[own : 2 * own], 2)
    share_first.start()
    save(n1, n1_out)
    share_first.wait_recv()
    save(ff, ff_out)

    def expand(n):
        j = turns[n]
        add = bias[j, 0:1, 4 * head_cols : 4 * head_cols + cols]

        def body(i, _):
            at = pl.ds(pl.multiple_of(i * tile, tile), tile)
            value = nn(ff[at, :], w[1, j]) + add
            active, slope = gelu_and_slope(value)
            hid[j, at, :] = active.astype(bf16)
            dg[j, at, :] = slope.astype(bf16)
            return 0

        lax.fori_loop(0, rows // tile, body, 0)
        save(hid.at[j], hid_out.at[j])
        save(dg.at[j], dg_out.at[j])

    ready(1, 0)
    expand(0)
    cross(2, 2)
    forward_on(1, 3)
    ready(1, 1)
    expand(1)
    ready(1, 2)
    expand(2)
    cross(2, 3)
    forward_on(2, 1)
    ready(1, 3)
    expand(3)
    forward_on(2, 2)
    share_att.wait_send()

    def contract(ns, start, target, source):
        def body(i, _):
            at = pl.ds(pl.multiple_of(start + i * tile, tile), tile)
            to = pl.ds(pl.multiple_of(i * tile, tile), tile)
            total = nt(hid[turns[ns[0]], at, :], w[2, turns[ns[0]]])
            for n in ns[1:]:
                total += nt(hid[turns[n], at, :], w[2, turns[n]])
            if source is not None:
                total += source[to, :]
            target[to, :] = total.astype(target.dtype)
            return 0

        lax.fori_loop(0, own // tile, body, 0)

    ready(2, 0)
    ready(2, 1)
    contract((0, 1), own, other_acc, None)
    contract((0, 1), 0, own_part, None)
    forward_on(2, 3)
    ready(2, 2)
    contract((2,), own, other_acc, other_acc)
    contract((2,), 0, own_part, own_part)
    ready(2, 3)
    contract((3,), own, other_part, other_acc)
    share_mix = exchange(other_part, mix_got, 3)
    share_mix.start()
    contract((3,), 0, own_part, own_part)
    spread_wait(c_ref, cot, ca_r)
    share_mix.wait_recv()
    sums_ref[...] = jnp.zeros_like(sums_ref)

    def second_body(i, _):
        at = pl.ds(pl.multiple_of(i * small, small), small)
        spot = i * small + lax.broadcasted_iota(jnp.int32, (small, 1), 0)
        where = (spot // part) * (2 * part) + core * part + spot % part
        alive = where.astype(f32) < length
        total = first[at, :] + (own_part[at, :] + mix_got[at, :].astype(f32)) + vec_ref[3:4, :]
        centered = total - mean(total)
        inverse = lax.rsqrt(mean(centered * centered) + EPSILON)
        normed = centered * inverse
        value = normed * vec_ref[4:5, :] + vec_ref[5:6, :]
        shown = jnp.where(alive, value, 0.0).astype(bf16)
        for k in range(4):
            lo_ref[at, block_at(k)] = shown[:, k * piece : (k + 1) * piece]
        given = jnp.concatenate([cot[at, block_at(k)] for k in range(4)], axis=1)
        grad = jnp.where(alive, given.astype(f32), 0.0)
        e = grad * vec_ref[4:5, :]
        back = (e - mean(e) - normed * mean(e * normed)) * inverse
        gm_ref[at, :] = back
        for m, value in enumerate((back, grad * normed, grad)):
            eights = value[0:8, :]
            for q in range(8, small, 8):
                eights += value[q : q + 8, :]
            parts_of[m] += eights
        return 0

    parts_of[...] = jnp.zeros_like(parts_of)
    lax.fori_loop(0, own // small, second_body, 0)
    for m in range(3):
        sums_ref[m : m + 1, :] = jnp.sum(parts_of[m], axis=0, keepdims=True)
    for n in range(6):
        pre_copy(n, mine_at).wait_send()
    share_len.wait_send()
    for b in range(3):
        for n in range(1, 4):
            line_do(b, n, lambda copy: copy.wait_send())
        for n in range(4):
            x_copy(b, n).wait_send()
            y_copy(b, n).wait_send()
            fx_copy(b, n).wait_send()
            fy_copy(b, n).wait_send()
    for s in range(1, 4):
        bias_copy(s).wait_send()
    spread_sent(x_ref, xs, xa_s, xa_r)
    spread_sent(c_ref, cot, ca_s, ca_r)
    share_x.wait_send()
    share_first.wait_send()
    share_mix.wait_send()
    for copy in outs:
        copy.wait()


def forward(lens, row, inputs, cotangent, w_query, w_key, w_value, w_out, w_in, w_back):
    part, width = inputs.shape[1] // 2, inputs.shape[2]
    own = 4 * part
    rows = 2 * own
    cols = w_in.shape[1] // 2
    head_cols = 2 * HD
    any_ = pl.BlockSpec(memory_space=pltpu.HBM)
    vm = pl.BlockSpec(memory_space=pltpu.VMEM)
    shape = jax.ShapeDtypeStruct
    dma = pltpu.SemaphoreType.DMA
    flops = 2 * rows * width * cols * 12 + 16 * rows * rows * HD * 4
    return pl.pallas_call(
        forward_kernel,
        in_specs=[vm, vm] + [any_] * 8,
        out_specs=[
            any_, any_, any_, vm, any_, any_, any_, any_, any_, vm, vm, vm, vm, vm, vm
        ],
        out_shape=[
            shape((3, 4, width, cols), bf16),
            shape((rows, width), bf16),
            shape((4, rows, 3 * head_cols), bf16),
            shape((8, 1, rows), f32),
            shape((4, rows, head_cols), bf16),
            shape((rows, width), bf16),
            shape((4, rows, cols), bf16),
            shape((4, rows, cols), bf16),
            shape((own, width), f32),
            shape((own, 1), f32),
            shape((own, width), f32),
            shape((own, width), bf16),
            shape((8, width), f32),
            shape((8, width), f32),
            shape((8, 128), f32),
        ],
        scratch_shapes=[
            pltpu.VMEM((3, 4, width, cols), bf16),
            pltpu.VMEM((own, width), bf16),
            pltpu.VMEM((rows, width), bf16),
            pltpu.VMEM((4, 8, 4 * head_cols + cols), f32),
            pltpu.VMEM((4, rows, 3 * head_cols), bf16),
            pltpu.VMEM((4, rows, head_cols), bf16),
            pltpu.VMEM((rows, width), bf16),
            pltpu.VMEM((4, rows, cols), bf16),
            pltpu.VMEM((4, rows, cols), bf16),
            pltpu.VMEM((own, width), f32),
            pltpu.VMEM((own, width), f32),
            pltpu.VMEM((own, width), f32),
            pltpu.VMEM((own, width), bf16),
            pltpu.VMEM((own, width), f32),
            pltpu.VMEM((own, width), bf16),
            pltpu.VMEM((own, width), bf16),
            pltpu.VMEM((own, width), bf16),
            pltpu.VMEM(w_out.shape, bf16),
            pltpu.VMEM(w_back.shape, bf16),
            pltpu.VMEM((w_out.shape[1], head_cols), bf16),
            pltpu.VMEM((w_back.shape[1], cols), bf16),
            pltpu.VMEM((2, 8, 128), f32),
            pltpu.VMEM((3, 8, width), f32),
            dma((3, 3)), dma((3, 3)), dma((3, 3)), dma((3, 3)),
            dma((3, 4)), dma((3, 4)), dma((3, 4)), dma((3, 4)),
            dma((3, 4, 2)), dma((3, 4, 2)), dma((6,)), dma((6,)), dma((6,)), dma((4,)), dma((4,)),
            dma((4,)), dma((4,)), dma((4,)), dma((4,)),
            dma((5,)), dma((5,)), dma((32,)),
        ],
        compiler_params=pltpu.CompilerParams(
            collective_id=0, has_side_effects=True, vmem_limit_bytes=60 << 20
        ),
        cost_estimate=pl.CostEstimate(
            flops=flops, bytes_accessed=60 << 20, transcendentals=8 * rows * rows
        ),
        name="forward_layer",
    )(lens, row, inputs, cotangent, w_query, w_key, w_value, w_out, w_in, w_back)


def backward_kernel(
    w_ref, xf_ref, qkv_ref, lse_ref, ctx_ref, ff_ref, hid_ref, dg_ref, n1_ref, inv1_ref, gm_ref,
    vec_ref, sums_ref, length_ref, lo_own,
    lo_ref, gi_ref, gq_ref, gk_ref, gv_ref, go_ref, gw_ref, gb_ref, total_ref,
    w, grad_c, pad, pre, gmf, act, turned, gm, n1, own_part, other, got,
    d_got, rx, ry, rz, home, dk_acc, dv_acc, vz, zg, xg, yg, cg, tot,
    d_s, d_r, x_s, x_r, y_s, y_r, z_s, z_r, h_s, h_r, h_l, e_s, e_r, g_s, g_r, v_s, v_r, l_s,
    lo_s, lo_r,
):
    plane = lax.axis_index("plane")
    core = lax.axis_index("core")
    place = lax.axis_index("tensor")
    partner = {"core": 1 - core}
    x_side = {"plane": plane + 1 - 2 * (plane % 2)}
    y_side = {"plane": (plane + 2) % 4}
    early, late = (place + 3) // 2, 3 - 2 * (place // 2)
    turns = (early, 6 - early - late, late, 0)
    edge = (3 - place) // 3 + place // 3
    middle = jnp.logical_and(place >= 1, place <= 2)
    rows, width = gmf.shape
    own = rows // 2
    part = own // 4
    piece = width // 4
    head_cols = 2 * HD
    tile = 512
    small = 32
    gi_own = gmf
    gaf = gmf

    def remote(source, target, send, recv, to):
        return pltpu.make_async_remote_copy(
            source, target, send, recv, device_id=to, device_id_type=MESH
        )

    half_piece = piece // 2

    def block(b, j, k, h=None):
        at = slice(k * piece, (k + 1) * piece)
        if h is not None:
            at = slice(k * piece + h * half_piece, k * piece + (h + 1) * half_piece)
        if b == 2:
            return grad_c.at[j, at]
        return w.at[b + 1, j, at]

    def rows_of(h):
        return slice(h * half_piece, (h + 1) * half_piece)

    def d_copy(b, n, h):
        return remote(
            block(b, turns[n], 3, h), d_got.at[b % 2, n, rows_of(h)], d_s.at[b, n, h], d_r.at[b, n, h],
            (x_side, y_side)[h],
        )

    def x_copy(b, n, h):
        return remote(
            block(b, turns[n], 1, h), rx.at[b, n, rows_of(h)], x_s.at[b, n, h], x_r.at[b, n, h], x_side
        )

    def y_copy(b, n, h):
        return remote(
            block(b, turns[n], 2, h), ry.at[b, n, rows_of(h)], y_s.at[b, n, h], y_r.at[b, n, h], y_side
        )

    def z_copy(b, n):
        step = 1 - 2 * ((place % 2) if n == 1 else (place // 2))
        end = 3 + (1 - step) // 2
        outer, inner = ((0, 1), (2, end), (end, end))[n]
        slot = edge * outer + (1 - edge) * inner
        return remote(
            block(b, turns[n], 0), rz.at[b, slot], z_s.at[b, n], z_r.at[b, slot],
            {"tensor": (place + step + 4) % 4},
        )

    def z_got(b, slot):
        return remote(
            block(b, 0, 0), rz.at[b, slot], z_s.at[b, 0], z_r.at[b, slot],
            {"tensor": (place + 1) % 4},
        )

    cols = w.shape[3]
    mine_at = pl.ds(core * half_piece, half_piece)
    theirs_at = pl.ds((1 - core) * half_piece, half_piece)

    def home_parts(n, which):
        at = pl.ds(which * half_piece, half_piece)
        turned_at = pl.ds(pl.multiple_of(piece + which * half_piece, half_piece), half_piece)
        heads = pl.ds(pl.multiple_of(core * head_cols, head_cols), head_cols)
        wide = pl.ds(pl.multiple_of(core * cols, cols), cols)
        if n < 3:
            return home.at[0, at, n * head_cols : (n + 1) * head_cols], (gq_ref, gk_ref, gv_ref)[n].at[:, heads]
        if n == 3:
            return n1.at[0:head_cols, turned_at], go_ref.at[heads]
        if n == 4:
            return home.at[1, at], gw_ref.at[:, wide]
        return n1.at[0:cols, at], gb_ref.at[wide]

    def home_copy(n):
        source, target = home_parts(n, 1 - core)
        return remote(source, target, h_s.at[n], h_r.at[n], partner)

    def home_keep(n):
        source, target = home_parts(n, core)
        return pltpu.make_async_copy(source, target, h_l.at[n])

    def send_first(b, n):
        for h in range(2):
            d_copy(b, n, h).start()
        x_copy(b, n, 0).start()
        y_copy(b, n, 1).start()

    def send_second(b, n):
        for h, k in ((0, 2), (1, 1)):
            d_copy(b, n, h).wait_recv()
            here = block(b, turns[n], k, h)
            arrived = d_got[b % 2, n, rows_of(h)]
            here[...] = (here[...].astype(f32) + arrived.astype(f32)).astype(bf16)
        y_copy(b, n, 0).start()
        x_copy(b, n, 1).start()

    def add_slot(b, slot, cond):
        @pl.when(cond)
        def _():
            z_got(b, slot).wait_recv()
            home[b] = home[b] + rz[b, slot].astype(f32)

    def send_third(b, n):
        for h in range(2):
            x_copy(b, n, h).wait_recv()
            y_copy(b, n, h).wait_recv()
        here = block(b, turns[n], 0)
        home[b] = here[...].astype(f32) + rx[b, n].astype(f32) + ry[b, n].astype(f32)
        if n < 3:
            add_slot(b, n, middle)
            here[...] = home[b].astype(bf16)
            z_copy(b, n).start()
        else:
            add_slot(b, 3, place >= 1)
            add_slot(b, 4, place <= 2)
            if b == 0:
                n1[0:head_cols, piece : 2 * piece] = home[b, :, 3 * head_cols : 4 * head_cols].T
            if b == 2:
                n1[0:cols, 0:piece] = home[b].T
            for m in ((0, 1, 2, 3), (4,), (5,))[b]:
                home_copy(m).start()
                home_keep(m).start()

    def exchange(source, target, n):
        return remote(source, target, e_s.at[n], e_r.at[n], partner)

    def back_parts(source, target, s):
        at = pl.ds(core * part, part)
        return source.at[s * part : (s + 1) * part], target.at[place % 2, at]

    def back(source, target, send, recv, s):
        here, there = back_parts(source, target, s)
        to = {"core": place // 2, "tensor": s}
        return remote(here, there, send.at[s], recv.at[2 * (place % 2) + core], to)

    def back_local(source, target, recv, s):
        here, there = back_parts(source, target, s)
        return pltpu.make_async_copy(here, there, recv.at[2 * (place % 2) + core])

    def is_home(s):
        return jnp.logical_and(core == place // 2, place == s)

    def back_start(source, target, send, recv):
        for s in range(4):
            @pl.when(is_home(s))
            def _():
                back_local(source, target, recv, s).start()

            @pl.when(jnp.logical_not(is_home(s)))
            def _():
                back(source, target, send, recv, s).start()

    def back_end(source, target, send, recv):
        for s in range(4):
            @pl.when(jnp.logical_not(is_home(s)))
            def _():
                back(source, target, send, recv, s).wait_send()
        for s in range(4):
            pltpu.make_async_copy(
                source.at[0:part], target.at[s // 2, pl.ds((s % 2) * part, part)], recv.at[s]
            ).wait()

    def v_copy(j):
        to = {"tensor": (place + 4 - j) % 4}
        return remote(vz.at[j], zg.at[place], v_s.at[j - 1], v_r.at[place], to)

    def v_got(j):
        source = (place + j) % 4
        to = {"tensor": (place + 1) % 4}
        return remote(vz.at[j], zg.at[source], v_s.at[j - 1], v_r.at[source], to)

    coming = {}

    def fetch(name, source, target):
        copy = pltpu.make_async_copy(source, target, l_s.at[len(coming)])
        copy.start()
        coming[name] = copy

    fetch("gm", gm_ref, gm)
    for n in range(4):
        fetch(("hid", n), hid_ref.at[turns[n]], pad.at[turns[n]])
    for j in range(4):
        fetch(("w2", j), w_ref.at[2, j], w.at[2, j])
        fetch(("dg", j), dg_ref.at[j], pre.at[j])
    fetch("w1", w_ref.at[1], w.at[1])
    fetch("n1", n1_ref, n1)
    fetch("ff", ff_ref, act)
    fetch("w0", w_ref.at[0], w.at[0])

    barrier = pltpu.get_barrier_semaphore()
    friends = [x_side, y_side, partner]
    for s in range(1, 4):
        friends.append({"tensor": (place + s) % 4})
        friends.append({"tensor": (place + s) % 4, "core": 1 - core})
    for friend in friends:
        pl.semaphore_signal(barrier, inc=1, device_id=friend, device_id_type=MESH)

    coming["gm"].wait()

    def round_body(i, _):
        at = pl.ds(pl.multiple_of(i * 128, 128), 128)
        gmf[at, :] = gm[at, :].astype(bf16)
        return 0

    lax.fori_loop(0, own // 128, round_body, 0)
    pl.semaphore_wait(barrier, len(friends))
    share_gm = exchange(gmf.at[0:own], gmf.at[own : 2 * own], 0)
    share_gm.start()
    back_start(lo_own, lo_ref, lo_s, lo_r)
    vz[...] = jnp.zeros_like(vz)

    def turn(source, first, last):
        def body(i, _):
            at = pl.ds(pl.multiple_of(i * tile, tile), tile)
            turned[:, at] = source[at, :].T
            return 0

        lax.fori_loop(first, last, body, 0)

    def weight_grad(b, n, source, columns):
        j = turns[n]

        def body(k, _):
            at = pl.ds(pl.multiple_of(k * tile, tile), tile)
            value = nn(turned[at, :], source[j, :, columns]).astype(bf16)
            if b == 2:
                grad_c[j, at, columns] = value
            else:
                w[b + 1, j, at, columns] = value
            return 0

        lax.fori_loop(0, width // tile, body, 0)

    every = slice(None)
    turn(gmf, 0, own // tile)
    share_gm.wait_recv()
    turn(gmf, own // tile, rows // tile)
    for n in range(4):
        coming[("hid", n)].wait()
        weight_grad(2, n, pad, every)
        send_first(2, n)

    def slope_rows(j):
        coming[("w2", j)].wait()
        coming[("dg", j)].wait()

        def body(i, _):
            at = pl.ds(pl.multiple_of(i * tile, tile), tile)
            value = (nn(gmf[at, :], w[2, j]) * pre[j, at, :].astype(f32)).astype(bf16)
            pre[j, at, :] = value
            vz[j, 8:9, 2 * head_cols : 2 * head_cols + value.shape[1]] += jnp.sum(
                value.astype(f32), axis=0, keepdims=True
            )
            return 0

        lax.fori_loop(0, rows // tile, body, 0)

    slope_rows(0)
    slope_rows(1)
    send_second(2, 0)
    slope_rows(2)
    send_second(2, 1)
    slope_rows(3)
    send_second(2, 2)
    for j in range(4):
        fetch(("ctx", j), ctx_ref.at[j], pad.at[j, :, pl.ds(3 * head_cols, head_cols)])
    coming["w1"].wait()

    def first_rows(start, target):
        def body(i, _):
            at = pl.ds(pl.multiple_of(start + i * tile, tile), tile)
            to = pl.ds(pl.multiple_of(i * tile, tile), tile)
            total = nt(pre[0, at, :], w[1, 0])
            for j in range(1, 4):
                total += nt(pre[j, at, :], w[1, j])
            target[to, :] = total.astype(target.dtype)
            return 0

        lax.fori_loop(0, own // tile, body, 0)

    first_rows(own, other)
    share_first = exchange(other, got, 1)
    share_first.start()
    send_second(2, 3)
    first_rows(0, own_part)
    coming["n1"].wait()
    share_first.wait_recv()

    def mean(value):
        return jnp.sum(value, axis=-1, keepdims=True) * (1.0 / value.shape[-1])

    share_gm.wait_send()

    def norm_body(i, _):
        at = pl.ds(pl.multiple_of(i * small, small), small)
        grad = gm[at, :] + (own_part[at, :] + got[at, :].astype(f32))
        normed = n1[at, :]
        e = grad * vec_ref[1:2, :]
        value = (e - mean(e) - normed * mean(e * normed)) * inv1_ref[at, :]
        gm[at, :] = value
        gaf[at, :] = value.astype(bf16)
        vz[0, 0:1, :] += jnp.sum(value, axis=0, keepdims=True)
        vz[0, 1:2, :] += jnp.sum(grad * normed, axis=0, keepdims=True)
        vz[0, 2:3, :] += jnp.sum(grad, axis=0, keepdims=True)
        return 0

    lax.fori_loop(0, own // small, norm_body, 0)
    share_att = exchange(gaf.at[0:own], gaf.at[own : 2 * own], 2)
    share_att.start()
    vz[0, 3:6, :] = sums_ref[0:3, :]
    for j in range(1, 4):
        vz[j, 0:8, :] = vz[0, 0:8, :]
    coming["ff"].wait()
    turn(act, 0, rows // tile)
    fetch("xf", xf_ref, act)
    for n in range(4):
        weight_grad(1, n, pre, every)
        send_first(1, n)
        if n == 2:
            send_third(2, 0)
    for j in range(4):
        fetch(("qkv", j), qkv_ref.at[j], pre.at[j, :, pl.ds(0, 3 * head_cols)])
    share_att.wait_recv()
    turn(gaf, 0, rows // tile)
    coming["w0"].wait()
    last = slice(3 * head_cols, 4 * head_cols)

    def context_rows(j):
        def body(i, _):
            at = pl.ds(pl.multiple_of(i * tile, tile), tile)
            pre[j, at, last] = nn(gaf[at, :], w[0, j, :, last]).astype(bf16)
            return 0

        lax.fori_loop(0, rows // tile, body, 0)

    for j in range(4):
        context_rows(j)
        coming[("ctx", j)].wait()
    send_third(2, 1)
    weight_grad(0, 0, pad, last)
    weight_grad(0, 1, pad, last)
    send_third(2, 2)
    weight_grad(0, 2, pad, last)
    weight_grad(0, 3, pad, last)
    send_second(1, 0)
    coming["xf"].wait()
    turn(act, 0, rows // tile)
    send_third(2, 3)
    for j in range(4):
        coming[("qkv", j)].wait()

    index = lax.broadcasted_iota(jnp.int32, (rows, 1), 0)
    half = jnp.where(index < own, core, 1 - core)
    inside = index % own
    position = (inside // part) * (2 * part) + half * part + inside % part
    length = length_ref[pl.ds(place % 2, 1), 0:1]
    key_bias = jnp.where(position.astype(f32) < length, 0.0, NEGATIVE).astype(f32)
    lane = lax.broadcasted_iota(jnp.int32, (1, head_cols), 1)
    front = slice(0, 3 * head_cols)

    def attend_back(n, midway):
        j = turns[n]
        keys = pre[j, :, head_cols : 2 * head_cols]
        keys_t = keys.T
        values = pre[j, :, 2 * head_cols : 3 * head_cols]
        dk_acc[...] = jnp.zeros_like(dk_acc)
        dv_acc[...] = jnp.zeros_like(dv_acc)

        def body(start):
            at = slice(start, start + 512)
            query = pre[j, at, 0:head_cols]
            grad = pre[j, at, last]
            parts = []
            for h in range(2):
                here = lane // HD == h
                query_h = jnp.where(here, query, jnp.zeros_like(query))
                grad_h = jnp.where(here, grad, jnp.zeros_like(grad))
                scores = nt(keys, query_h) + key_bias
                chances = jnp.exp(scores - lse_ref[2 * j + h, :, at])
                grad_chances = nt(values, grad_h)
                inner = jnp.sum(chances * grad_chances, axis=0, keepdims=True)
                grad_scores = (chances * (grad_chances - inner)).astype(bf16)
                dv_acc[...] += nn(chances.astype(bf16), grad_h)
                dk_acc[...] += nn(grad_scores, query_h)
                parts.append(nn(keys_t[h * HD : (h + 1) * HD], grad_scores))
            low = jnp.concatenate(parts, axis=0).T.astype(bf16).astype(f32) * HD ** (-0.5)
            pad[j, at, 0:head_cols] = low.astype(bf16)
            vz[j, 8:9, 0:head_cols] += jnp.sum(low, axis=0, keepdims=True)

        for start in range(0, rows, 512):
            if start:
                midway()
            body(start)
        pad[j, :, head_cols : 2 * head_cols] = dk_acc[...].astype(bf16)
        low = dv_acc[...].astype(bf16)
        pad[j, :, 2 * head_cols : 3 * head_cols] = low
        vz[j, 8:9, head_cols : 2 * head_cols] = jnp.sum(low.astype(f32), axis=0, keepdims=True)

    between = (
        lambda: send_second(1, 1),
        lambda: send_second(1, 2),
        lambda: send_second(1, 3),
        lambda: send_third(1, 0),
    )
    for n in range(4):
        attend_back(n, between[n])
        weight_grad(0, n, pad, front)
        send_first(0, n)
        if n == 3:
            send_second(0, 0)
    for j in range(1, 4):
        v_copy(j).start()
    zg[place] = vz[0]

    def input_rows(start, target):
        def body(i, _):
            at = pl.ds(pl.multiple_of(start + i * tile, tile), tile)
            to = pl.ds(pl.multiple_of(i * tile, tile), tile)
            total = nt(pad[0, at, front], w[0, 0, :, front])
            for j in range(1, 4):
                total += nt(pad[j, at, front], w[0, j, :, front])
            target[to, :] = total.astype(target.dtype)
            return 0

        lax.fori_loop(0, own // tile, body, 0)

    share_att.wait_send()
    share_first.wait_send()
    input_rows(own, other)
    share_in = exchange(other, got, 3)
    share_in.start()
    send_third(1, 1)
    input_rows(0, own_part)
    send_second(0, 1)
    share_in.wait_recv()

    def input_body(i, _):
        at = pl.ds(pl.multiple_of(i * small, small), small)
        value = gm[at, :] + (own_part[at, :] + got[at, :].astype(f32))
        low = value.astype(bf16)
        for k in range(4):
            number = (plane, plane + 1 - 2 * (plane % 2), (plane + 2) % 4, 3 - plane)[k]
            to = pl.ds(pl.multiple_of(number * piece, piece), piece)
            gi_own[at, to] = low[:, k * piece : (k + 1) * piece]
        return 0

    lax.fori_loop(0, own // small, input_body, 0)
    send_third(1, 2)
    send_second(0, 2)
    back_start(gi_own, gi_ref, g_s, g_r)

    def fold(n, m, arrived, flip):
        for k in range(4):
            here = slice(k * piece, (k + 1) * piece)
            there = slice((k ^ flip) * piece, ((k ^ flip) + 1) * piece)
            tot[n, 0:8, here] = tot[m, 0:8, here] + arrived[0:8, there]
        tot[n, 8:16, :] = tot[m, 8:16, :] + arrived[8:16, :]

    for j in range(1, 4):
        v_got(j).wait_recv()
    tot[0] = ((zg[0] + zg[1]) + zg[2]) + zg[3]
    v_x = remote(tot.at[0], xg, e_s.at[4], e_r.at[4], x_side)
    v_x.start()
    v_x.wait_recv()
    fold(1, 0, xg, 1)
    v_y = remote(tot.at[1], yg, e_s.at[5], e_r.at[5], y_side)
    v_y.start()
    send_second(0, 3)
    v_y.wait_recv()
    fold(2, 1, yg, 2)
    v_c = exchange(tot.at[2], cg, 6)
    v_c.start()
    send_third(1, 3)
    for n in range(4):
        send_third(0, n)
    v_c.wait_recv()
    for k in range(4):
        number = (plane, plane + 1 - 2 * (plane % 2), (plane + 2) % 4, 3 - plane)[k]
        to = pl.ds(pl.multiple_of(number * piece, piece), piece)
        here = slice(k * piece, (k + 1) * piece)
        total_ref[0:8, to] = tot[2, 0:8, here] + cg[0:8, here]
    own_row = tot[2, 8:9, :]
    their_row = cg[8:9, :]
    total_ref[8:9, :] = jnp.where(core == 0, own_row, their_row)
    total_ref[9:10, :] = jnp.where(core == 0, their_row, own_row)

    for b in range(3):
        for n in range(4):
            for h in range(2):
                d_copy(b, n, h).wait_send()
                x_copy(b, n, h).wait_send()
                y_copy(b, n, h).wait_send()
            if n < 3:
                z_copy(b, n).wait_send()
    for n in range(6):
        home_keep(n).wait()
        home_copy(n).wait_send()
        home_copy(n).wait_recv()
    for j in range(1, 4):
        v_copy(j).wait_send()
    for copy in (share_in, v_x, v_y, v_c):
        copy.wait_send()
    back_end(lo_own, lo_ref, lo_s, lo_r)
    back_end(gi_own, gi_ref, g_s, g_r)


def backward(w_all, xf, qkv, lse, ctx, ff, hid, dg, n1, inv1, gm, vec, sums, length, lo):
    rows, width = xf.shape
    own = rows // 2
    part = own // 4
    piece = width // 4
    cols = hid.shape[2]
    head_cols = 2 * HD
    any_ = pl.BlockSpec(memory_space=pltpu.HBM)
    vm = pl.BlockSpec(memory_space=pltpu.VMEM)
    shape = jax.ShapeDtypeStruct
    dma = pltpu.SemaphoreType.DMA
    flops = 2 * rows * width * cols * 24 + 40 * rows * rows * HD * 4
    return pl.pallas_call(
        backward_kernel,
        in_specs=[
            any_, any_, any_, vm, any_, any_, any_, any_, any_, vm, any_, vm, vm, vm, any_
        ],
        out_specs=[any_] * 8 + [vm],
        out_shape=[
            shape((2, 2 * part, width), bf16),
            shape((2, 2 * part, width), bf16),
            shape((piece // 2, 2 * head_cols), f32),
            shape((piece // 2, 2 * head_cols), f32),
            shape((piece // 2, 2 * head_cols), f32),
            shape((2 * head_cols, piece // 2), f32),
            shape((piece // 2, 2 * cols), f32),
            shape((2 * cols, piece // 2), f32),
            shape((16, width), f32),
        ],
        scratch_shapes=[
            pltpu.VMEM((3, 4, width, cols), bf16),
            pltpu.VMEM((4, width, cols), bf16),
            pltpu.VMEM((4, rows, cols), bf16),
            pltpu.VMEM((4, rows, cols), bf16),
            pltpu.VMEM((rows, width), bf16),
            pltpu.VMEM((rows, width), bf16),
            pltpu.VMEM((width, rows), bf16),
            pltpu.VMEM((own, width), f32),
            pltpu.VMEM((own, width), f32),
            pltpu.VMEM((own, width), f32),
            pltpu.VMEM((own, width), bf16),
            pltpu.VMEM((own, width), bf16),
            pltpu.VMEM((2, 4, piece, cols), bf16),
            pltpu.VMEM((3, 4, piece, cols), bf16),
            pltpu.VMEM((3, 4, piece, cols), bf16),
            pltpu.VMEM((3, 5, piece, cols), bf16),
            pltpu.VMEM((3, piece, cols), f32),
            pltpu.VMEM((rows, head_cols), f32),
            pltpu.VMEM((rows, head_cols), f32),
            pltpu.VMEM((4, 16, width), f32),
            pltpu.VMEM((4, 16, width), f32),
            pltpu.VMEM((16, width), f32),
            pltpu.VMEM((16, width), f32),
            pltpu.VMEM((16, width), f32),
            pltpu.VMEM((3, 16, width), f32),
            dma((3, 4, 2)), dma((3, 4, 2)), dma((3, 4, 2)), dma((3, 4, 2)), dma((3, 4, 2)), dma((3, 4, 2)),
            dma((3, 3)), dma((3, 5)), dma((6,)), dma((6,)), dma((6,)), dma((8,)), dma((8,)),
            dma((4,)), dma((4,)), dma((3,)), dma((4,)), dma((32,)),
            dma((4,)), dma((4,)),
        ],
        compiler_params=pltpu.CompilerParams(
            collective_id=1, has_side_effects=True, vmem_limit_bytes=60 << 20
        ),
        cost_estimate=pl.CostEstimate(
            flops=flops, bytes_accessed=60 << 20, transcendentals=8 * rows * rows
        ),
        name="backward_layer",
    )(w_all, xf, qkv, lse, ctx, ff, hid, dg, n1, inv1, gm, vec, sums, length, lo)


def swap_cores(value):
    return lax.ppermute(value, "core", SWAP)


def on_device(
    inputs,
    lengths,
    w_query,
    w_key,
    w_value,
    b_query,
    b_value,
    w_out,
    b_out,
    gain_one,
    shift_one,
    w_in,
    b_in,
    w_back,
    b_back,
    gain_two,
    shift_two,
    cotangent,
):
    planes = lax.axis_size("plane")
    n_t = lax.axis_size("tensor")
    plane = lax.axis_index("plane")
    core = lax.axis_index("core")
    place = lax.axis_index("tensor")
    seqs, slots_here, width = inputs.shape
    slots = slots_here * n_t
    half_slots = slots_here // 2
    own = slots // 2
    assert seqs * 2 == n_t
    head_cols = w_query.shape[1] // 2
    ff_cols = w_in.shape[1] // 2
    scale = HD ** (-0.5)
    quad = planes == 4
    if quad:
        row = jnp.stack(
            [
                value.astype(f32)
                for value in (
                    b_out, gain_one, shift_one, b_back, gain_two, shift_two, b_in,
                    jnp.concatenate([b_query, b_value, jnp.zeros((width // 2,), bf16)]),
                )
            ]
        )
        lens = jnp.broadcast_to(
            jnp.concatenate([lengths.astype(f32)] * (8 // seqs))[:, None], (8, 128)
        )
        (w_all, x_full, qkv4, lse8, ctx4, first_full, hid4, dg4, normed_one, inverse_one,
         grad_mixed, lo, second_sums, vec, length_rows) = forward(
            lens, row, inputs, cotangent, w_query, w_key, w_value, w_out, w_in, w_back
        )
        (layer_out, gi, grad_w_query, grad_w_key, grad_w_value, grad_w_out, grad_w_in,
         grad_w_back, totals) = backward(
            w_all, x_full, qkv4, lse8, ctx4, first_full, hid4, dg4, normed_one, inverse_one,
            grad_mixed, vec, second_sums, length_rows, lo,
        )
        n_bias = 2 * head_cols + ff_cols
        biases_out = totals[8:10, :n_bias]
        return (
            layer_out,
            gi.astype(f32),
            grad_w_query,
            grad_w_key,
            grad_w_value,
            biases_out[:, :head_cols].reshape(-1),
            biases_out[:, head_cols : 2 * head_cols].reshape(-1),
            grad_w_out,
            totals[0],
            totals[1],
            totals[2],
            grad_w_in,
            biases_out[:, 2 * head_cols :].reshape(-1),
            grad_w_back,
            totals[3],
            totals[4],
            totals[5],
        )

    ring = [(i, (i + 1) % n_t) for i in range(n_t)]
    x_pairs = [(i, i ^ 1) for i in range(planes)]
    y_pairs = [(i, i ^ 2) for i in range(planes)]

    def reorder(value, axis):
        if not quad:
            return value
        size = value.shape[axis] // 4
        return jnp.concatenate(
            [lax.dynamic_slice_in_dim(value, (plane ^ k) * size, size, axis) for k in range(4)],
            axis=axis,
        )

    def by_core(mine, theirs, axis=0):
        first = jnp.where(core == 0, mine, theirs)
        second = jnp.where(core == 0, theirs, mine)
        return jnp.concatenate([first, second], axis=axis)

    def to_chip(rows_here):
        value = reorder(rows_here, 2).reshape(seqs, 2, half_slots, width)
        mine = lax.dynamic_index_in_dim(value, core, 1, keepdims=False)
        other = lax.dynamic_index_in_dim(value, 1 - core, 1, keepdims=False)
        both = by_core(mine, swap_cores(other))
        return lax.all_to_all(both, "tensor", 0, 0, tiled=True).reshape(own, width)

    def from_chip(rows_own):
        value = rows_own.reshape(n_t, half_slots, width)
        value = lax.all_to_all(value, "tensor", 0, 0, tiled=True)
        value = value.reshape(2, seqs, half_slots, width)
        mine = lax.dynamic_index_in_dim(value, core, 0, keepdims=False)
        other = lax.dynamic_index_in_dim(value, 1 - core, 0, keepdims=False)
        got = swap_cores(other)
        value = jnp.stack(
            [jnp.where(core == 0, mine, got), jnp.where(core == 0, got, mine)], axis=1
        )
        return reorder(value.reshape(seqs, slots_here, width), 2)

    their_lengths = swap_cores(lengths)
    all_lengths = by_core(lengths, their_lengths)
    length = lax.dynamic_index_in_dim(all_lengths, place, 0, keepdims=False)
    index = jnp.arange(slots)
    position = (
        (index % own) // half_slots * slots_here
        + ((index // own) ^ core) * half_slots
        + index % half_slots
    )
    valid = position < length
    key_bias = jnp.where(valid, 0.0, NEGATIVE).astype(f32)[:, None]
    own_valid = valid[:own, None]

    def halves(value, cols):
        return (
            lax.dynamic_slice_in_dim(value, core * cols, cols, 1),
            lax.dynamic_slice_in_dim(value, (1 - core) * cols, cols, 1),
        )

    pieces = [
        halves(w_query, head_cols),
        halves(w_key, head_cols),
        halves(w_value, head_cols),
        halves(w_out.T, head_cols),
        halves(w_in, ff_cols),
        halves(w_back.T, ff_cols),
    ]
    keep = jnp.concatenate([piece[0] for piece in pieces], axis=1)
    give = jnp.concatenate([piece[1] for piece in pieces], axis=1)
    cuts = (4 * head_cols, 4 * head_cols + ff_cols)

    def flat(gathered):
        return jnp.concatenate([gathered[j] for j in range(n_t)], axis=1)

    out_bias = reorder(b_out, 0).astype(f32)
    back_bias = reorder(b_back, 0).astype(f32)
    gain_first = reorder(gain_one, 0).astype(f32)
    shift_first = reorder(shift_one, 0).astype(f32)
    gain_second = reorder(gain_two, 0).astype(f32)
    shift_second = reorder(shift_two, 0).astype(f32)
    bias_row = jnp.concatenate(
        [
            lax.dynamic_slice_in_dim(b_query, core * head_cols, head_cols),
            lax.dynamic_slice_in_dim(b_value, core * head_cols, head_cols),
            lax.dynamic_slice_in_dim(b_in, core * ff_cols, ff_cols),
        ]
    )[None]
    qkv_scale = jnp.tile(
        jnp.concatenate([jnp.full((head_cols,), scale, f32), jnp.ones((2 * head_cols,), f32)]), n_t
    )[None]
    def both_rows(value):
        return jnp.concatenate([value, swap_cores(value)], axis=0)

    def own_sum(partial):
        return partial[:own] + swap_cores(partial[own:])

    def normalize(value):
        average = jnp.mean(value, axis=-1, keepdims=True)
        centered = value - average
        variance = jnp.mean(centered * centered, axis=-1, keepdims=True)
        inverse = lax.rsqrt(variance + EPSILON)
        return centered * inverse, inverse

    def normalize_back(grad, gain, normed, inverse):
        e = grad * gain
        return (
            e
            - jnp.mean(e, axis=-1, keepdims=True)
            - normed * jnp.mean(e * normed, axis=-1, keepdims=True)
        ) * inverse

    packed = by_core(keep, swap_cores(give))
    bundle_a = packed[:, : cuts[0]]
    bundle_b = packed[:, cuts[0] : cuts[1]]
    bundle_c = packed[:, cuts[1] :]
    def gather_z(own_piece):
        got = [own_piece]
        for _ in range(n_t - 1):
            got.append(lax.ppermute(got[-1], "tensor", ring))
        return jnp.stack(got)

    def gather_planes(mine):
        if not quad:
            return lax.all_gather(mine, "plane", axis=1, tiled=True)
        half = n_t // 2
        from_x = lax.ppermute(mine, "plane", x_pairs)
        from_y = lax.ppermute(mine, "plane", y_pairs)
        low = lax.ppermute(from_y[:half], "plane", x_pairs)
        high = lax.ppermute(from_x[half:], "plane", y_pairs)
        return jnp.concatenate([mine, from_x, from_y, jnp.concatenate([low, high])], axis=1)

    biases = gather_z(bias_row)[:, 0].astype(f32)
    z_a = gather_z(bundle_a)
    full_a = gather_planes(z_a)
    w_qkv = flat(full_a[:, :, : 3 * head_cols])
    w_o = flat(full_a[:, :, 3 * head_cols :])
    w_1 = flat(gather_planes(gather_z(bundle_b)))
    w_2 = flat(gather_planes(gather_z(bundle_c)))

    zeros_k = jnp.zeros((n_t, head_cols), f32)
    qkv_bias = jnp.concatenate(
        [biases[:, :head_cols], zeros_k, biases[:, head_cols : 2 * head_cols]], axis=1
    ).reshape(1, -1)
    in_bias = biases[:, 2 * head_cols :].reshape(1, -1)

    own_x = to_chip(inputs)
    x_full = both_rows(own_x)
    qkv = ((nn(x_full, w_qkv) + qkv_bias) * qkv_scale).astype(bf16)
    context, lse = attend_fwd(qkv, key_bias)
    attended = own_sum(nt(context, w_o))
    normed_one, inverse_one = normalize(own_x.astype(f32) + attended + out_bias)
    first_norm = normed_one * gain_first + shift_first
    first_full = both_rows(first_norm.astype(bf16))
    pre_act = nn(first_full, w_1) + in_bias
    activated, slope = gelu_and_slope(pre_act)
    hidden = activated.astype(bf16)
    mixed = own_sum(nt(hidden, w_2))
    normed_two, inverse_two = normalize(first_norm + mixed + back_bias)
    second = normed_two * gain_second + shift_second
    layer_out = from_chip(jnp.where(own_valid, second, 0.0).astype(bf16))

    grad_second = jnp.where(own_valid, to_chip(cotangent).astype(f32), 0.0)
    grad_mixed = normalize_back(grad_second, gain_second, normed_two, inverse_two)

    grad_mixed_full = both_rows(grad_mixed.astype(bf16))
    grad_w2 = tn(grad_mixed_full, hidden)
    grad_pre_low = (nn(grad_mixed_full, w_2) * slope.astype(f32)).astype(bf16)
    grad_w1 = tn(first_full, grad_pre_low)
    grad_first = grad_mixed + own_sum(nt(grad_pre_low, w_1))
    grad_att = normalize_back(grad_first, gain_first, normed_one, inverse_one)
    grad_att_full = both_rows(grad_att.astype(bf16))
    grad_context = nn(grad_att_full, w_o).astype(bf16)
    grad_wo = tn(grad_att_full, context)
    grad_qkv = attend_bwd(qkv, grad_context, lse, key_bias)
    grad_qkv = grad_qkv * qkv_scale.astype(bf16)
    grad_wqkv = tn(x_full, grad_qkv)
    grad_rows = grad_att + own_sum(nt(grad_qkv, w_qkv))
    grad_inputs = from_chip(grad_rows.astype(bf16)).astype(f32)

    def scatter(grad):
        cols = grad.shape[1] // n_t
        if quad:
            rows = width // 4
            blocks = grad.reshape(4, rows, n_t, cols).transpose(0, 2, 1, 3)
            half = n_t // 2
            low = lax.ppermute(blocks[3, :half].astype(bf16), "plane", x_pairs)
            high = lax.ppermute(blocks[3, half:].astype(bf16), "plane", y_pairs)
            for_y = jnp.concatenate([blocks[2, :half] + low.astype(f32), blocks[2, half:]])
            for_x = jnp.concatenate([blocks[1, :half], blocks[1, half:] + high.astype(f32)])
            from_x = lax.ppermute(for_x.astype(bf16), "plane", x_pairs)
            from_y = lax.ppermute(for_y.astype(bf16), "plane", y_pairs)
            mine = blocks[0] + from_x.astype(f32) + from_y.astype(f32)
        else:
            blocks = grad.reshape(width, n_t, cols).transpose(1, 0, 2)
            mine = lax.psum_scatter(
                blocks.astype(bf16), "plane", scatter_dimension=1, tiled=True
            ).astype(f32)
        back = [(b, a) for a, b in ring]
        total = mine[n_t - 1]
        for j in range(n_t - 2, -1, -1):
            total = mine[j] + lax.ppermute(total.astype(bf16), "tensor", back).astype(f32)
        return total

    home_c = scatter(grad_w2)
    home_b = scatter(grad_w1)
    grad_a = jnp.concatenate(
        [
            grad_wqkv.reshape(width, n_t, 3 * head_cols),
            grad_wo.reshape(width, n_t, head_cols),
        ],
        axis=2,
    ).reshape(width, -1)
    home_a = scatter(grad_a)
    home = jnp.concatenate([home_a, home_b, home_c], axis=1)
    home = home.reshape(2, -1, home.shape[1])
    mine = lax.dynamic_index_in_dim(home, core, 0, keepdims=False)
    other = lax.dynamic_index_in_dim(home, 1 - core, 0, keepdims=False)
    got = swap_cores(other)

    def row_sum(value):
        return reorder(jnp.sum(value, axis=0), 0)

    second_rows = [row_sum(grad_mixed), row_sum(grad_second * normed_two), row_sum(grad_second)]
    norm_sums = jnp.concatenate(
        [
            row_sum(grad_att),
            row_sum(grad_first * normed_one),
            row_sum(grad_first),
            *second_rows,
        ]
    )
    qkv_sum = jnp.sum(grad_qkv.astype(f32), axis=0).reshape(n_t, 3 * head_cols)
    pre_sum = jnp.sum(grad_pre_low.astype(f32), axis=0).reshape(n_t, ff_cols)
    bias_sum = jnp.concatenate([qkv_sum[:, :head_cols], qkv_sum[:, 2 * head_cols :], pre_sum], axis=1)
    at_home = lax.rem(place - jnp.arange(n_t) + n_t, n_t)
    spread = (at_home[:, None] == jnp.arange(n_t)[None]).astype(f32)
    by_place = jnp.sum(spread[:, :, None] * bias_sum[:, None, :], axis=0)
    both = jnp.where(
        (jnp.arange(2) == core)[None, :, None], by_place[:, None, :], 0.0
    )
    sums = lax.psum(jnp.concatenate([norm_sums, both.reshape(-1)]), ("plane", "core", "tensor"))
    norms = sums[: 6 * width].reshape(6, width)
    biases_out = lax.dynamic_index_in_dim(
        sums[6 * width :].reshape(n_t, 2, -1), place, 0, keepdims=False
    )
    def columns(start, cols):
        return by_core(mine[:, start : start + cols], got[:, start : start + cols], axis=1)

    grad_w_query = columns(0, head_cols)
    grad_w_key = columns(head_cols, head_cols)
    grad_w_value = columns(2 * head_cols, head_cols)
    grad_w_out = columns(3 * head_cols, head_cols).T
    grad_w_in = columns(cuts[0], ff_cols)
    grad_w_back = columns(cuts[1], ff_cols).T

    grad_b_query = biases_out[:, :head_cols].reshape(-1)
    grad_b_value = biases_out[:, head_cols : 2 * head_cols].reshape(-1)
    grad_b_in = biases_out[:, 2 * head_cols :].reshape(-1)
    return (
        layer_out,
        grad_inputs,
        grad_w_query,
        grad_w_key,
        grad_w_value,
        grad_b_query,
        grad_b_value,
        grad_w_out,
        norms[0],
        norms[1],
        norms[2],
        grad_w_in,
        grad_b_in,
        grad_w_back,
        norms[3],
        norms[4],
        norms[5],
    )


def solution(mesh):
    devices = mesh.devices.reshape(mesh.shape["dp"] // 2, 2, mesh.shape["tensor"])
    inner = Mesh(devices, ("plane", "core", "tensor"))
    dp = ("plane", "core")
    row = P(dp, "tensor")
    column = P("tensor", dp)
    rows3 = P(dp, "tensor", None)
    shard = P("tensor")
    whole = P()
    return jax.shard_map(
        on_device,
        mesh=inner,
        in_specs=(
            rows3, P(dp), row, row, row, shard, shard, column, whole, whole, whole,
            row, shard, column, whole, whole, whole, rows3,
        ),
        out_specs=(
            rows3, rows3, row, row, row, shard, shard, column, whole, whole, whole,
            row, shard, column, whole, whole, whole,
        ),
        check_vma=False,
    )
```

```python
import jax
import jax.numpy as jnp
from jax import lax
from jax.experimental import pallas as pl
from jax.experimental.pallas import tpu as pltpu
from jax.sharding import Mesh, PartitionSpec as P

HD = 64
EPSILON = 1e-05
NEGATIVE = -1e30
f32 = jnp.float32
bf16 = jnp.bfloat16
SWAP = [(0, 1), (1, 0)]


def nt(a, b):
    return lax.dot_general(a, b, (((1,), (1,)), ((), ())), preferred_element_type=f32)


def tn(a, b):
    return lax.dot_general(a, b, (((0,), (0,)), ((), ())), preferred_element_type=f32)


def nn(a, b):
    return lax.dot_general(a, b, (((1,), (0,)), ((), ())), preferred_element_type=f32)


def attend_fwd_kernel(block, qkv_ref, kb_ref, ctx_ref, lse_ref):
    rows = qkv_ref.shape[0]
    lane = lax.broadcasted_iota(jnp.int32, (1, 2 * HD), 1)
    keys = qkv_ref[:, 2 * HD : 4 * HD]
    values_t = qkv_ref[:, 4 * HD : 6 * HD].T
    key_bias = kb_ref[...]
    for start in range(0, rows, block):
        query = qkv_ref[start : start + block, 0 : 2 * HD]
        parts = []
        for h in range(2):
            query_h = jnp.where(lane // HD == h, query, jnp.zeros_like(query))
            scores = nt(keys, query_h) + key_bias
            largest = jnp.max(scores, axis=0, keepdims=True)
            weights = jnp.exp(scores - largest)
            total = jnp.sum(weights, axis=0, keepdims=True)
            part = nn(values_t[h * HD : (h + 1) * HD], weights.astype(bf16))
            parts.append(part / total)
            lse_ref[0, h : h + 1, start : start + block] = largest + jnp.log(total)
        ctx_ref[start : start + block, :] = jnp.concatenate(parts, axis=0).T.astype(bf16)


def attend_fwd(qkv, key_bias):
    rows = qkv.shape[0]
    groups = qkv.shape[1] // (6 * HD)
    block = min(512, rows)
    return pl.pallas_call(
        lambda *refs: attend_fwd_kernel(block, *refs),
        grid=(groups,),
        in_specs=[
            pl.BlockSpec((rows, 6 * HD), lambda j: (0, j)),
            pl.BlockSpec((rows, 1), lambda j: (0, 0)),
        ],
        out_specs=[
            pl.BlockSpec((rows, 2 * HD), lambda j: (0, j)),
            pl.BlockSpec((1, 2, rows), lambda j: (j, 0, 0)),
        ],
        out_shape=[
            jax.ShapeDtypeStruct((rows, groups * 2 * HD), bf16),
            jax.ShapeDtypeStruct((groups, 2, rows), f32),
        ],
        compiler_params=pltpu.CompilerParams(vmem_limit_bytes=48 << 20),
        cost_estimate=pl.CostEstimate(
            flops=groups * 8 * rows * rows * HD * 4,
            bytes_accessed=rows * groups * 8 * HD * 2,
            transcendentals=groups * 2 * rows * rows,
        ),
        name="attend_fwd",
    )(qkv, key_bias)


def attend_bwd_kernel(block, qkv_ref, g_ref, lse_ref, kb_ref, d_ref, dk_acc, dv_acc):
    rows = qkv_ref.shape[0]
    lane = lax.broadcasted_iota(jnp.int32, (1, 2 * HD), 1)
    keys = qkv_ref[:, 2 * HD : 4 * HD]
    keys_t = keys.T
    values = qkv_ref[:, 4 * HD : 6 * HD]
    key_bias = kb_ref[...]
    for start in range(0, rows, block):
        query = qkv_ref[start : start + block, 0 : 2 * HD]
        grad = g_ref[start : start + block, :]
        parts = []
        for h in range(2):
            here = lane // HD == h
            query_h = jnp.where(here, query, jnp.zeros_like(query))
            grad_h = jnp.where(here, grad, jnp.zeros_like(grad))
            scores = nt(keys, query_h) + key_bias
            chances = jnp.exp(scores - lse_ref[0, h : h + 1, start : start + block])
            grad_chances = nt(values, grad_h)
            inner = jnp.sum(chances * grad_chances, axis=0, keepdims=True)
            grad_scores = (chances * (grad_chances - inner)).astype(bf16)
            dv = nn(chances.astype(bf16), grad_h)
            dk = nn(grad_scores, query_h)
            if start == 0 and h == 0:
                dv_acc[...] = dv
                dk_acc[...] = dk
            else:
                dv_acc[...] += dv
                dk_acc[...] += dk
            parts.append(nn(keys_t[h * HD : (h + 1) * HD], grad_scores))
        d_ref[start : start + block, 0 : 2 * HD] = jnp.concatenate(parts, axis=0).T.astype(bf16)
    d_ref[:, 2 * HD : 4 * HD] = dk_acc[...].astype(bf16)
    d_ref[:, 4 * HD : 6 * HD] = dv_acc[...].astype(bf16)


def attend_bwd(qkv, grad_context, lse, key_bias):
    rows = qkv.shape[0]
    groups = qkv.shape[1] // (6 * HD)
    block = min(512, rows)
    return pl.pallas_call(
        lambda *refs: attend_bwd_kernel(block, *refs),
        grid=(groups,),
        in_specs=[
            pl.BlockSpec((rows, 6 * HD), lambda j: (0, j)),
            pl.BlockSpec((rows, 2 * HD), lambda j: (0, j)),
            pl.BlockSpec((1, 2, rows), lambda j: (j, 0, 0)),
            pl.BlockSpec((rows, 1), lambda j: (0, 0)),
        ],
        out_specs=pl.BlockSpec((rows, 6 * HD), lambda j: (0, j)),
        out_shape=jax.ShapeDtypeStruct((rows, groups * 6 * HD), bf16),
        scratch_shapes=[pltpu.VMEM((rows, 2 * HD), f32), pltpu.VMEM((rows, 2 * HD), f32)],
        compiler_params=pltpu.CompilerParams(vmem_limit_bytes=48 << 20),
        cost_estimate=pl.CostEstimate(
            flops=groups * 20 * rows * rows * HD * 4,
            bytes_accessed=rows * groups * 14 * HD * 2,
            transcendentals=groups * 2 * rows * rows,
        ),
        name="attend_bwd",
    )(qkv, grad_context, lse, key_bias)

POLY = (
    0.30995978221815235,
    0.31100346478903146,
    0.2699660979585953,
    0.2765467936611628,
    -0.03831584737802812,
    0.38967711658103854,
    -0.3554874111653827,
    0.08996434684501212,
)
POLY_AT = 0.31
DENSITY = 0.3989422804014327
MESH = pl.DeviceIdType.MESH


def gelu_and_slope(v):
    density = jnp.exp(-0.5 * v * v) * DENSITY
    t = 1.0 / (1.0 + POLY_AT * jnp.abs(v))
    tail = jnp.full_like(v, POLY[-1])
    for coefficient in POLY[-2::-1]:
        tail = tail * t + coefficient
    tail = tail * t * density
    below = jnp.where(v > 0, 1.0 - tail, tail)
    return v * below, below + v * density


def forward_kernel(
    lens_ref, row_ref, x_ref, c_ref, wq_ref, wk_ref, wv_ref, wo_ref, wi_ref, wb_ref,
    w_out, xf_out, qkv_out, lse_ref, ctx_out, ff_out, hid_out, dg_out, n1_out, inv1_ref, gm_ref,
    lo_ref, sums_ref, vec_ref, length_ref,
    w, xs, xf, bias, qkv, ctx, ff, hid, dg, n1, first, other_acc, other_part, own_part, att_got, mix_got, cot,
    wo_here, wb_here, wo_give, wb_give, lens, parts_of,
    z_s, z_r, zl_s, zl_r, x_s, x_r, y_s, y_r, f_s, f_r, pre_l, pre_s, pre_r, b_s, b_r,
    xa_s, xa_r, ca_s, ca_r, e_s, e_r, o_s,
):
    plane = lax.axis_index("plane")
    core = lax.axis_index("core")
    place = lax.axis_index("tensor")
    partner = {"core": 1 - core}
    x_side = {"plane": plane + 1 - 2 * (plane % 2)}
    y_side = {"plane": (plane + 2) % 4}
    z_right = {"tensor": (place + 1) % 4}
    z_left = {"tensor": (place + 3) % 4}
    first_end = (3 - place) // 3
    last_end = place // 3
    turns = (0, 1 + 2 * first_end, 3 - first_end - last_end, 2 - first_end + last_end)
    rows = xf.shape[0]
    own = rows // 2
    part = own // 4
    piece = w.shape[2] // 4

    def remote(source, target, send, recv, to):
        return pltpu.make_async_remote_copy(
            source, target, send, recv, device_id=to, device_id_type=MESH
        )

    def right_copy(b, n):
        return remote(
            w.at[b, n - 1, 0:piece], w.at[b, n, 0:piece], z_s.at[b, n - 1], z_r.at[b, n - 1], z_right
        )

    def left_copy(b, n):
        return remote(
            w.at[b, (5 - n) % 4, 0:piece], w.at[b, 4 - n, 0:piece],
            zl_s.at[b, n - 1], zl_r.at[b, n - 1], z_left,
        )

    def line_do(b, n, act):
        @pl.when(jnp.logical_and(place <= 2, place >= n - 1))
        def _():
            act(right_copy(b, n))

        @pl.when(jnp.logical_and(place >= 1, place + n <= 4))
        def _():
            act(left_copy(b, n))

    def line_start(b, n):
        line_do(b, n, lambda copy: copy.start())

    def line_wait(b, n):
        @pl.when(place >= n)
        def _():
            right_copy(b, n).wait_recv()

        @pl.when(place + n <= 3)
        def _():
            left_copy(b, n).wait_recv()

    def x_copy(b, n):
        j = turns[n]
        return remote(
            w.at[b, j, 0:piece], w.at[b, j, piece : 2 * piece], x_s.at[b, n], x_r.at[b, n], x_side
        )

    def y_copy(b, n):
        j = turns[n]
        return remote(
            w.at[b, j, 0:piece], w.at[b, j, 2 * piece : 3 * piece], y_s.at[b, n], y_r.at[b, n], y_side
        )

    def fx_copy(b, n):
        j, half = turns[n], piece // 2
        return remote(
            w.at[b, j, 2 * piece : 2 * piece + half], w.at[b, j, 3 * piece : 3 * piece + half],
            f_s.at[b, n, 0], f_r.at[b, n, 0], x_side,
        )

    def fy_copy(b, n):
        j, half = turns[n], piece // 2
        return remote(
            w.at[b, j, piece + half : 2 * piece], w.at[b, j, 3 * piece + half : 4 * piece],
            f_s.at[b, n, 1], f_r.at[b, n, 1], y_side,
        )

    def cross(b, n):
        x_copy(b, n).start()
        y_copy(b, n).start()

    def forward_on(b, n):
        y_copy(b, n).wait_recv()
        fx_copy(b, n).start()
        x_copy(b, n).wait_recv()
        fy_copy(b, n).start()

    def ready(b, n):
        fx_copy(b, n).wait_recv()
        fy_copy(b, n).wait_recv()
        save(w.at[b, turns[n]], w_out.at[b, turns[n]])

    half_piece = piece // 2
    head_cols = 2 * HD
    mine_at = pl.ds(core * half_piece, half_piece)
    theirs_at = pl.ds((1 - core) * half_piece, half_piece)
    cols = w.shape[3]

    def head_half(which):
        return pl.ds(pl.multiple_of(which * head_cols, head_cols), head_cols)

    def wide_half(which):
        return pl.ds(pl.multiple_of(which * cols, cols), cols)

    def keep_copy(n):
        if n < 3:
            source = (wq_ref, wk_ref, wv_ref)[n].at[:, head_half(core)]
            target = w.at[0, 0, mine_at, n * head_cols : (n + 1) * head_cols]
        elif n == 3:
            source, target = wo_ref, wo_here
        elif n == 4:
            source, target = wi_ref.at[:, wide_half(core)], w.at[1, 0, mine_at]
        else:
            source, target = wb_ref, wb_here
        return pltpu.make_async_copy(source, target, pre_l.at[n])

    def pre_copy(n, at):
        if n < 3:
            source = (wq_ref, wk_ref, wv_ref)[n].at[:, head_half(1 - core)]
            target = w.at[0, 0, at, n * head_cols : (n + 1) * head_cols]
        elif n == 3:
            source, target = wo_give, w.at[0, 0, at, 3 * head_cols : 4 * head_cols]
        elif n == 4:
            source, target = wi_ref.at[:, wide_half(1 - core)], w.at[1, 0, at]
        else:
            source, target = wb_give, w.at[2, 0, at]
        return remote(source, target, pre_s.at[n], pre_r.at[n], partner)

    def bias_copy(s):
        return remote(
            bias.at[0], bias.at[s], b_s.at[s], b_r.at[s], {"tensor": (place + s) % 4}
        )

    def spread(source, target, send, recv, l, h):
        at = pl.ds(place * part, part)
        to = {"core": h, "tensor": 2 * core + l}
        return remote(
            source.at[l, h * part : (h + 1) * part], target.at[at], send.at[2 * l + h],
            recv.at[place], to,
        )

    def spread_local(source, target, recv, l, h):
        at = pl.ds(place * part, part)
        return pltpu.make_async_copy(
            source.at[l, h * part : (h + 1) * part], target.at[at], recv.at[place]
        )

    def is_here(l, h):
        return jnp.logical_and(core == h, place == 2 * core + l)

    def spread_start(source, target, send, recv):
        for l in range(2):
            for h in range(2):
                @pl.when(is_here(l, h))
                def _():
                    spread_local(source, target, recv, l, h).start()

                @pl.when(jnp.logical_not(is_here(l, h)))
                def _():
                    spread(source, target, send, recv, l, h).start()

    def spread_wait(source, target, recv):
        for s in range(4):
            pltpu.make_async_copy(
                source.at[0, 0:part], target.at[s * part : (s + 1) * part], recv.at[s]
            ).wait()

    def spread_sent(source, target, send, recv):
        for l in range(2):
            for h in range(2):
                @pl.when(jnp.logical_not(is_here(l, h)))
                def _():
                    spread(source, target, send, recv, l, h).wait_send()

    def exchange(source, target, n):
        return remote(source, target, e_s.at[n], e_r.at[n], partner)

    outs = []

    def save(source, target):
        copy = pltpu.make_async_copy(source, target, o_s.at[len(outs)])
        copy.start()
        outs.append(copy)

    barrier = pltpu.get_barrier_semaphore()
    friends = [x_side, y_side, partner]
    for s in range(1, 4):
        friends.append({"tensor": (place + s) % 4})
        friends.append({"tensor": (place + s) % 4, "core": 1 - core})
    for friend in friends:
        pl.semaphore_signal(barrier, inc=1, device_id=friend, device_id_type=MESH)
    for n in (3, 0, 1, 2, 4, 5):
        keep_copy(n).start()
    pl.semaphore_wait(barrier, len(friends))

    def block_at(k):
        number = (plane, plane + 1 - 2 * (plane % 2), (plane + 2) % 4, 3 - plane)[k]
        return pl.ds(pl.multiple_of(number * piece, piece), piece)

    for n in range(3):
        pre_copy(n, mine_at).start()
    keep_copy(3).wait()
    wo_give[...] = wo_here[head_half(1 - core), :].T
    pre_copy(3, mine_at).start()
    w[0, 0, mine_at, 3 * head_cols : 4 * head_cols] = wo_here[head_half(core), :].T
    pre_copy(4, mine_at).start()
    for n in range(3):
        keep_copy(n).wait()
    for n in range(4):
        pre_copy(n, theirs_at).wait_recv()
    line_start(0, 1)
    cross(0, 0)
    spread_start(x_ref, xs, xa_s, xa_r)
    keep_copy(5).wait()
    wb_give[...] = wb_here[wide_half(1 - core), :].T
    pre_copy(5, mine_at).start()
    w[2, 0, mine_at, :] = wb_here[wide_half(core), :].T
    keep_copy(4).wait()
    pre_copy(4, theirs_at).wait_recv()
    cross(1, 0)
    pre_copy(5, theirs_at).wait_recv()
    cross(2, 0)

    zero_row = jnp.zeros((1, head_cols), f32)
    heads_q = jnp.where(core == 0, row_ref[7:8, 0:head_cols], row_ref[7:8, head_cols : 2 * head_cols])
    heads_v = jnp.where(
        core == 0, row_ref[7:8, 2 * head_cols : 3 * head_cols], row_ref[7:8, 3 * head_cols : 4 * head_cols]
    )
    wide = jnp.where(core == 0, row_ref[6:7, 0:cols], row_ref[6:7, cols : 2 * cols])
    bias[0, 0:1, :] = jnp.concatenate([heads_q, zero_row, heads_v, zero_row, wide], axis=1)
    for k in range(4):
        vec_ref[:, k * piece : (k + 1) * piece] = row_ref[:, block_at(k)]
    for s in range(1, 4):
        bias_copy(s).start()
    lens[core] = lens_ref[...]
    share_len = remote(lens_ref, lens.at[core], e_s.at[4], e_r.at[4], partner)
    share_len.start()

    line_wait(0, 1)
    line_start(0, 2)
    line_start(1, 1)
    forward_on(0, 0)
    cross(0, 1)
    forward_on(1, 0)
    forward_on(2, 0)
    for s in range(1, 4):
        bias_copy(s).wait_recv()
    remote(lens_ref, lens.at[1 - core], e_s.at[4], e_r.at[4], partner).wait_recv()

    spread_wait(x_ref, xs, xa_r)
    for k in range(4):
        xf[0:own, k * piece : (k + 1) * piece] = xs[:, block_at(k)]
    share_x = exchange(xf.at[0:own], xf.at[own : 2 * own], 0)
    share_x.start()
    share_x.wait_recv()
    save(xf, xf_out)

    index = lax.broadcasted_iota(jnp.int32, (rows, 1), 0)
    length_ref[...] = lens[place // 2]
    length = length_ref[pl.ds(place % 2, 1), 0:1]
    half = jnp.where(index < own, core, 1 - core)
    inside = index % own
    position = (inside // part) * (2 * part) + half * part + inside % part
    key_bias = jnp.where(position.astype(f32) < length, 0.0, NEGATIVE).astype(f32)
    lane = lax.broadcasted_iota(jnp.int32, (1, 2 * HD), 1)
    tile = 512

    def project(n):
        j = turns[n]
        columns = lax.broadcasted_iota(jnp.int32, (1, 3 * head_cols), 1)
        zero = jnp.zeros((1, head_cols), f32)
        add = jnp.concatenate(
            [bias[j, 0:1, 0:head_cols], zero, bias[j, 0:1, 2 * head_cols : 3 * head_cols]], axis=1
        )
        times = jnp.where(columns < head_cols, HD ** (-0.5), 1.0).astype(f32)

        def body(i, _):
            at = pl.ds(pl.multiple_of(i * tile, tile), tile)
            value = nn(xf[at, :], w[0, j, :, 0 : 3 * head_cols])
            qkv[j, at, :] = ((value + add) * times).astype(bf16)
            return 0

        lax.fori_loop(0, rows // tile, body, 0)
        save(qkv.at[j], qkv_out.at[j])

    def attend(n, midway):
        j = turns[n]
        keys = qkv[j, :, head_cols : 2 * head_cols]
        values_t = qkv[j, :, 2 * head_cols : 3 * head_cols].T

        def body(start):
            at = slice(start, start + 512)
            query = qkv[j, at, 0:head_cols]
            parts = []
            for h in range(2):
                query_h = jnp.where(lane // HD == h, query, jnp.zeros_like(query))
                scores = nt(keys, query_h) + key_bias
                largest = jnp.max(scores, axis=0, keepdims=True)
                weights = jnp.exp(scores - largest)
                total = jnp.sum(weights, axis=0, keepdims=True)
                out = nn(values_t[h * HD : (h + 1) * HD], weights.astype(bf16))
                parts.append(out / total)
                lse_ref[2 * j + h, :, at] = largest + jnp.log(total)
            ctx[j, at, :] = jnp.concatenate(parts, axis=0).T.astype(bf16)

        for start in range(0, rows, 512):
            if start:
                midway()
            body(start)
        save(ctx.at[j], ctx_out.at[j])

    def between_1():
        line_wait(0, 3)
        cross(0, 3)
        forward_on(0, 2)

    def between_2():
        line_wait(1, 2)
        line_start(1, 3)

    def between_3():
        line_wait(2, 2)
        line_start(2, 3)

    ready(0, 0)
    project(0)
    line_wait(0, 2)
    line_start(0, 3)
    line_start(2, 1)
    cross(0, 2)
    forward_on(0, 1)
    attend(0, lambda: None)
    line_wait(1, 1)
    line_start(1, 2)
    ready(0, 1)
    project(1)
    attend(1, between_1)
    cross(1, 1)
    line_wait(2, 1)
    line_start(2, 2)
    forward_on(0, 3)
    ready(0, 2)
    project(2)
    attend(2, between_2)
    cross(1, 2)
    forward_on(1, 1)
    ready(0, 3)
    project(3)
    attend(3, between_3)
    line_wait(1, 3)
    cross(1, 3)
    forward_on(1, 2)

    def out_rows(start, target):
        def body(i, _):
            at = pl.ds(pl.multiple_of(start + i * tile, tile), tile)
            to = pl.ds(pl.multiple_of(i * tile, tile), tile)
            total = nt(ctx[0, at, :], w[0, 0, :, 3 * head_cols :])
            for j in range(1, 4):
                total += nt(ctx[j, at, :], w[0, j, :, 3 * head_cols :])
            target[to, :] = total.astype(target.dtype)
            return 0

        lax.fori_loop(0, own // tile, body, 0)

    out_rows(own, other_part)
    share_att = exchange(other_part, att_got, 1)
    share_att.start()
    out_rows(0, own_part)
    cross(2, 1)
    line_wait(2, 3)
    spread_start(c_ref, cot, ca_s, ca_r)
    share_att.wait_recv()
    small = 32

    def mean(value):
        return jnp.sum(value, axis=-1, keepdims=True) * (1.0 / value.shape[-1])

    def first_body(i, _):
        at = pl.ds(pl.multiple_of(i * small, small), small)
        total = xf[at, :].astype(f32) + (own_part[at, :] + att_got[at, :].astype(f32)) + vec_ref[0:1, :]
        centered = total - mean(total)
        inverse = lax.rsqrt(mean(centered * centered) + EPSILON)
        normed = centered * inverse
        n1[at, :] = normed
        inv1_ref[at, :] = inverse
        value = normed * vec_ref[1:2, :] + vec_ref[2:3, :]
        first[at, :] = value
        ff[at, :] = value.astype(bf16)
        return 0

    lax.fori_loop(0, own // small, first_body, 0)
    share_first = exchange(ff.at[0:own], ff.at[own : 2 * own], 2)
    share_first.start()
    save(n1, n1_out)
    share_first.wait_recv()
    save(ff, ff_out)

    def expand(n):
        j = turns[n]
        add = bias[j, 0:1, 4 * head_cols : 4 * head_cols + cols]

        def body(i, _):
            at = pl.ds(pl.multiple_of(i * tile, tile), tile)
            value = nn(ff[at, :], w[1, j]) + add
            active, slope = gelu_and_slope(value)
            hid[j, at, :] = active.astype(bf16)
            dg[j, at, :] = slope.astype(bf16)
            return 0

        lax.fori_loop(0, rows // tile, body, 0)
        save(hid.at[j], hid_out.at[j])
        save(dg.at[j], dg_out.at[j])

    ready(1, 0)
    expand(0)
    cross(2, 2)
    forward_on(1, 3)
    ready(1, 1)
    expand(1)
    ready(1, 2)
    expand(2)
    cross(2, 3)
    forward_on(2, 1)
    ready(1, 3)
    expand(3)
    forward_on(2, 2)
    share_att.wait_send()

    def contract(ns, start, target, source):
        def body(i, _):
            at = pl.ds(pl.multiple_of(start + i * tile, tile), tile)
            to = pl.ds(pl.multiple_of(i * tile, tile), tile)
            total = nt(hid[turns[ns[0]], at, :], w[2, turns[ns[0]]])
            for n in ns[1:]:
                total += nt(hid[turns[n], at, :], w[2, turns[n]])
            if source is not None:
                total += source[to, :]
            target[to, :] = total.astype(target.dtype)
            return 0

        lax.fori_loop(0, own // tile, body, 0)

    ready(2, 0)
    ready(2, 1)
    contract((0, 1), own, other_acc, None)
    contract((0, 1), 0, own_part, None)
    forward_on(2, 3)
    ready(2, 2)
    contract((2,), own, other_acc, other_acc)
    contract((2,), 0, own_part, own_part)
    ready(2, 3)
    contract((3,), own, other_part, other_acc)
    share_mix = exchange(other_part, mix_got, 3)
    share_mix.start()
    contract((3,), 0, own_part, own_part)
    spread_wait(c_ref, cot, ca_r)
    share_mix.wait_recv()
    sums_ref[...] = jnp.zeros_like(sums_ref)

    def second_body(i, _):
        at = pl.ds(pl.multiple_of(i * small, small), small)
        spot = i * small + lax.broadcasted_iota(jnp.int32, (small, 1), 0)
        where = (spot // part) * (2 * part) + core * part + spot % part
        alive = where.astype(f32) < length
        total = first[at, :] + (own_part[at, :] + mix_got[at, :].astype(f32)) + vec_ref[3:4, :]
        centered = total - mean(total)
        inverse = lax.rsqrt(mean(centered * centered) + EPSILON)
        normed = centered * inverse
        value = normed * vec_ref[4:5, :] + vec_ref[5:6, :]
        shown = jnp.where(alive, value, 0.0).astype(bf16)
        for k in range(4):
            lo_ref[at, block_at(k)] = shown[:, k * piece : (k + 1) * piece]
        given = jnp.concatenate([cot[at, block_at(k)] for k in range(4)], axis=1)
        grad = jnp.where(alive, given.astype(f32), 0.0)
        e = grad * vec_ref[4:5, :]
        back = (e - mean(e) - normed * mean(e * normed)) * inverse
        gm_ref[at, :] = back
        for m, value in enumerate((back, grad * normed, grad)):
            eights = value[0:8, :]
            for q in range(8, small, 8):
                eights += value[q : q + 8, :]
            parts_of[m] += eights
        return 0

    parts_of[...] = jnp.zeros_like(parts_of)
    lax.fori_loop(0, own // small, second_body, 0)
    for m in range(3):
        sums_ref[m : m + 1, :] = jnp.sum(parts_of[m], axis=0, keepdims=True)
    for n in range(6):
        pre_copy(n, mine_at).wait_send()
    share_len.wait_send()
    for b in range(3):
        for n in range(1, 4):
            line_do(b, n, lambda copy: copy.wait_send())
        for n in range(4):
            x_copy(b, n).wait_send()
            y_copy(b, n).wait_send()
            fx_copy(b, n).wait_send()
            fy_copy(b, n).wait_send()
    for s in range(1, 4):
        bias_copy(s).wait_send()
    spread_sent(x_ref, xs, xa_s, xa_r)
    spread_sent(c_ref, cot, ca_s, ca_r)
    share_x.wait_send()
    share_first.wait_send()
    share_mix.wait_send()
    for copy in outs:
        copy.wait()


def forward(lens, row, inputs, cotangent, w_query, w_key, w_value, w_out, w_in, w_back):
    part, width = inputs.shape[1] // 2, inputs.shape[2]
    own = 4 * part
    rows = 2 * own
    cols = w_in.shape[1] // 2
    head_cols = 2 * HD
    any_ = pl.BlockSpec(memory_space=pltpu.HBM)
    vm = pl.BlockSpec(memory_space=pltpu.VMEM)
    shape = jax.ShapeDtypeStruct
    dma = pltpu.SemaphoreType.DMA
    flops = 2 * rows * width * cols * 12 + 16 * rows * rows * HD * 4
    return pl.pallas_call(
        forward_kernel,
        in_specs=[vm, vm] + [any_] * 8,
        out_specs=[
            any_, any_, any_, vm, any_, any_, any_, any_, any_, vm, vm, vm, vm, vm, vm
        ],
        out_shape=[
            shape((3, 4, width, cols), bf16),
            shape((rows, width), bf16),
            shape((4, rows, 3 * head_cols), bf16),
            shape((8, 1, rows), f32),
            shape((4, rows, head_cols), bf16),
            shape((rows, width), bf16),
            shape((4, rows, cols), bf16),
            shape((4, rows, cols), bf16),
            shape((own, width), f32),
            shape((own, 1), f32),
            shape((own, width), f32),
            shape((own, width), bf16),
            shape((8, width), f32),
            shape((8, width), f32),
            shape((8, 128), f32),
        ],
        scratch_shapes=[
            pltpu.VMEM((3, 4, width, cols), bf16),
            pltpu.VMEM((own, width), bf16),
            pltpu.VMEM((rows, width), bf16),
            pltpu.VMEM((4, 8, 4 * head_cols + cols), f32),
            pltpu.VMEM((4, rows, 3 * head_cols), bf16),
            pltpu.VMEM((4, rows, head_cols), bf16),
            pltpu.VMEM((rows, width), bf16),
            pltpu.VMEM((4, rows, cols), bf16),
            pltpu.VMEM((4, rows, cols), bf16),
            pltpu.VMEM((own, width), f32),
            pltpu.VMEM((own, width), f32),
            pltpu.VMEM((own, width), f32),
            pltpu.VMEM((own, width), bf16),
            pltpu.VMEM((own, width), f32),
            pltpu.VMEM((own, width), bf16),
            pltpu.VMEM((own, width), bf16),
            pltpu.VMEM((own, width), bf16),
            pltpu.VMEM(w_out.shape, bf16),
            pltpu.VMEM(w_back.shape, bf16),
            pltpu.VMEM((w_out.shape[1], head_cols), bf16),
            pltpu.VMEM((w_back.shape[1], cols), bf16),
            pltpu.VMEM((2, 8, 128), f32),
            pltpu.VMEM((3, 8, width), f32),
            dma((3, 3)), dma((3, 3)), dma((3, 3)), dma((3, 3)),
            dma((3, 4)), dma((3, 4)), dma((3, 4)), dma((3, 4)),
            dma((3, 4, 2)), dma((3, 4, 2)), dma((6,)), dma((6,)), dma((6,)), dma((4,)), dma((4,)),
            dma((4,)), dma((4,)), dma((4,)), dma((4,)),
            dma((5,)), dma((5,)), dma((32,)),
        ],
        compiler_params=pltpu.CompilerParams(
            collective_id=0, has_side_effects=True, vmem_limit_bytes=60 << 20
        ),
        cost_estimate=pl.CostEstimate(
            flops=flops, bytes_accessed=60 << 20, transcendentals=8 * rows * rows
        ),
        name="forward_layer",
    )(lens, row, inputs, cotangent, w_query, w_key, w_value, w_out, w_in, w_back)


def backward_kernel(
    w_ref, xf_ref, qkv_ref, lse_ref, ctx_ref, ff_ref, hid_ref, dg_ref, n1_ref, inv1_ref, gm_ref,
    vec_ref, sums_ref, length_ref, lo_own,
    lo_ref, gi_ref, gq_ref, gk_ref, gv_ref, go_ref, gw_ref, gb_ref, total_ref,
    w, grad_c, pad, pre, gmf, act, turned, gm, n1, own_part, other, got,
    d_got, rx, ry, rz, home, dk_acc, dv_acc, vz, zg, xg, yg, cg, tot,
    d_s, d_r, x_s, x_r, y_s, y_r, z_s, z_r, h_s, h_r, h_l, e_s, e_r, g_s, g_r, v_s, v_r, l_s,
    lo_s, lo_r,
):
    plane = lax.axis_index("plane")
    core = lax.axis_index("core")
    place = lax.axis_index("tensor")
    partner = {"core": 1 - core}
    x_side = {"plane": plane + 1 - 2 * (plane % 2)}
    y_side = {"plane": (plane + 2) % 4}
    early, late = (place + 3) // 2, 3 - 2 * (place // 2)
    turns = (early, 6 - early - late, late, 0)
    edge = (3 - place) // 3 + place // 3
    rows, width = gmf.shape
    own = rows // 2
    part = own // 4
    piece = width // 4
    head_cols = 2 * HD
    tile = 512
    small = 32
    gi_own = gmf
    gaf = gmf

    def remote(source, target, send, recv, to):
        return pltpu.make_async_remote_copy(
            source, target, send, recv, device_id=to, device_id_type=MESH
        )

    half_piece = piece // 2

    def block(b, j, k, h=None):
        at = slice(k * piece, (k + 1) * piece)
        if h is not None:
            at = slice(k * piece + h * half_piece, k * piece + (h + 1) * half_piece)
        if b == 2:
            return grad_c.at[j, at]
        return w.at[b + 1, j, at]

    def rows_of(h):
        return slice(h * half_piece, (h + 1) * half_piece)

    def d_copy(b, n, h):
        return remote(
            block(b, turns[n], 3, h), d_got.at[b % 2, n, rows_of(h)], d_s.at[b, n, h], d_r.at[b, n, h],
            (x_side, y_side)[h],
        )

    def x_copy(b, n, h):
        return remote(
            block(b, turns[n], 1, h), rx.at[b, n, rows_of(h)], x_s.at[b, n, h], x_r.at[b, n, h], x_side
        )

    def y_copy(b, n, h):
        return remote(
            block(b, turns[n], 2, h), ry.at[b, n, rows_of(h)], y_s.at[b, n, h], y_r.at[b, n, h], y_side
        )

    def z_copy(b, n):
        step = 1 - 2 * ((place % 2) if n == 1 else (place // 2))
        end = 3 + (1 - step) // 2
        outer, inner = ((0, 1), (2, end), (end, end))[n]
        slot = edge * outer + (1 - edge) * inner
        return remote(
            block(b, turns[n], 0), rz.at[b, slot], z_s.at[b, n], z_r.at[b, slot],
            {"tensor": (place + step + 4) % 4},
        )

    def z_got(b, slot):
        return remote(
            block(b, 0, 0), rz.at[b, slot], z_s.at[b, 0], z_r.at[b, slot],
            {"tensor": (place + 1) % 4},
        )

    cols = w.shape[3]
    mine_at = pl.ds(core * half_piece, half_piece)
    theirs_at = pl.ds((1 - core) * half_piece, half_piece)

    def home_parts(n, which):
        at = pl.ds(which * half_piece, half_piece)
        turned_at = pl.ds(pl.multiple_of(piece + which * half_piece, half_piece), half_piece)
        heads = pl.ds(pl.multiple_of(core * head_cols, head_cols), head_cols)
        wide = pl.ds(pl.multiple_of(core * cols, cols), cols)
        if n < 3:
            return home.at[0, at, n * head_cols : (n + 1) * head_cols], (gq_ref, gk_ref, gv_ref)[n].at[:, heads]
        if n == 3:
            return n1.at[0:head_cols, turned_at], go_ref.at[heads]
        if n == 4:
            return home.at[1, at], gw_ref.at[:, wide]
        return n1.at[0:cols, at], gb_ref.at[wide]

    def home_copy(n):
        source, target = home_parts(n, 1 - core)
        return remote(source, target, h_s.at[n], h_r.at[n], partner)

    def home_keep(n):
        source, target = home_parts(n, core)
        return pltpu.make_async_copy(source, target, h_l.at[n])

    def send_first(b, n):
        for h in range(2):
            d_copy(b, n, h).start()
        x_copy(b, n, 0).start()
        y_copy(b, n, 1).start()

    def send_second(b, n):
        for h, k in ((0, 2), (1, 1)):
            d_copy(b, n, h).wait_recv()
            here = block(b, turns[n], k, h)
            arrived = d_got[b % 2, n, rows_of(h)]
            here[...] = (here[...].astype(f32) + arrived.astype(f32)).astype(bf16)
        y_copy(b, n, 0).start()
        x_copy(b, n, 1).start()

    def add_slot(b, slot, cond):
        @pl.when(cond)
        def _():
            z_got(b, slot).wait_recv()
            home[b] = home[b] + rz[b, slot].astype(f32)

    def gather_piece(b, n):
        for h in range(2):
            x_copy(b, n, h).wait_recv()
            y_copy(b, n, h).wait_recv()
        here = block(b, turns[n], 0)
        home[b] = here[...].astype(f32) + rx[b, n].astype(f32) + ry[b, n].astype(f32)

    def pass_piece(b, n):
        block(b, turns[n], 0)[...] = home[b].astype(bf16)
        z_copy(b, n).start()

    def stage(b, k):
        if k < 3:
            @pl.when(edge == 1)
            def _():
                gather_piece(b, k)
                pass_piece(b, k)

        if 1 <= k <= 3:
            @pl.when(edge == 0)
            def _():
                gather_piece(b, k - 1)
                z_got(b, k - 1).wait_recv()
                home[b] = home[b] + rz[b, k - 1].astype(f32)
                pass_piece(b, k - 1)

        if k == 4:
            gather_piece(b, 3)
            add_slot(b, 3, place >= 1)
            add_slot(b, 4, place <= 2)
            if b == 0:
                n1[0:head_cols, piece : 2 * piece] = home[b, :, 3 * head_cols : 4 * head_cols].T
            if b == 2:
                n1[0:cols, 0:piece] = home[b].T
            for m in ((0, 1, 2, 3), (4,), (5,))[b]:
                home_copy(m).start()
                home_keep(m).start()

    def exchange(source, target, n):
        return remote(source, target, e_s.at[n], e_r.at[n], partner)

    def back_parts(source, target, s):
        at = pl.ds(core * part, part)
        return source.at[s * part : (s + 1) * part], target.at[place % 2, at]

    def back(source, target, send, recv, s):
        here, there = back_parts(source, target, s)
        to = {"core": place // 2, "tensor": s}
        return remote(here, there, send.at[s], recv.at[2 * (place % 2) + core], to)

    def back_local(source, target, recv, s):
        here, there = back_parts(source, target, s)
        return pltpu.make_async_copy(here, there, recv.at[2 * (place % 2) + core])

    def is_home(s):
        return jnp.logical_and(core == place // 2, place == s)

    def back_start(source, target, send, recv):
        for s in range(4):
            @pl.when(is_home(s))
            def _():
                back_local(source, target, recv, s).start()

            @pl.when(jnp.logical_not(is_home(s)))
            def _():
                back(source, target, send, recv, s).start()

    def back_end(source, target, send, recv):
        for s in range(4):
            @pl.when(jnp.logical_not(is_home(s)))
            def _():
                back(source, target, send, recv, s).wait_send()
        for s in range(4):
            pltpu.make_async_copy(
                source.at[0:part], target.at[s // 2, pl.ds((s % 2) * part, part)], recv.at[s]
            ).wait()

    def v_copy(j):
        to = {"tensor": (place + 4 - j) % 4}
        return remote(vz.at[j], zg.at[place], v_s.at[j - 1], v_r.at[place], to)

    def v_got(j):
        source = (place + j) % 4
        to = {"tensor": (place + 1) % 4}
        return remote(vz.at[j], zg.at[source], v_s.at[j - 1], v_r.at[source], to)

    coming = {}

    def fetch(name, source, target):
        copy = pltpu.make_async_copy(source, target, l_s.at[len(coming)])
        copy.start()
        coming[name] = copy

    fetch("gm", gm_ref, gm)
    for n in range(4):
        fetch(("hid", n), hid_ref.at[turns[n]], pad.at[turns[n]])
    for j in range(4):
        fetch(("w2", j), w_ref.at[2, j], w.at[2, j])
        fetch(("dg", j), dg_ref.at[j], pre.at[j])
    fetch("w1", w_ref.at[1], w.at[1])
    fetch("n1", n1_ref, n1)
    fetch("ff", ff_ref, act)
    fetch("w0", w_ref.at[0], w.at[0])

    barrier = pltpu.get_barrier_semaphore()
    friends = [x_side, y_side, partner]
    for s in range(1, 4):
        friends.append({"tensor": (place + s) % 4})
        friends.append({"tensor": (place + s) % 4, "core": 1 - core})
    for friend in friends:
        pl.semaphore_signal(barrier, inc=1, device_id=friend, device_id_type=MESH)

    coming["gm"].wait()

    def round_body(i, _):
        at = pl.ds(pl.multiple_of(i * 128, 128), 128)
        gmf[at, :] = gm[at, :].astype(bf16)
        return 0

    lax.fori_loop(0, own // 128, round_body, 0)
    pl.semaphore_wait(barrier, len(friends))
    share_gm = exchange(gmf.at[0:own], gmf.at[own : 2 * own], 0)
    share_gm.start()
    back_start(lo_own, lo_ref, lo_s, lo_r)
    vz[...] = jnp.zeros_like(vz)

    def turn(source, first, last):
        def body(i, _):
            at = pl.ds(pl.multiple_of(i * tile, tile), tile)
            turned[:, at] = source[at, :].T
            return 0

        lax.fori_loop(first, last, body, 0)

    def weight_grad(b, n, source, columns):
        j = turns[n]

        def body(k, _):
            at = pl.ds(pl.multiple_of(k * tile, tile), tile)
            value = nn(turned[at, :], source[j, :, columns]).astype(bf16)
            if b == 2:
                grad_c[j, at, columns] = value
            else:
                w[b + 1, j, at, columns] = value
            return 0

        lax.fori_loop(0, width // tile, body, 0)

    every = slice(None)
    turn(gmf, 0, own // tile)
    share_gm.wait_recv()
    turn(gmf, own // tile, rows // tile)
    for n in range(4):
        coming[("hid", n)].wait()
        weight_grad(2, n, pad, every)
        send_first(2, n)

    def slope_rows(j):
        coming[("w2", j)].wait()
        coming[("dg", j)].wait()

        def body(i, _):
            at = pl.ds(pl.multiple_of(i * tile, tile), tile)
            value = (nn(gmf[at, :], w[2, j]) * pre[j, at, :].astype(f32)).astype(bf16)
            pre[j, at, :] = value
            vz[j, 8:9, 2 * head_cols : 2 * head_cols + value.shape[1]] += jnp.sum(
                value.astype(f32), axis=0, keepdims=True
            )
            return 0

        lax.fori_loop(0, rows // tile, body, 0)

    slope_rows(0)
    slope_rows(1)
    send_second(2, 0)
    slope_rows(2)
    send_second(2, 1)
    slope_rows(3)
    for j in range(4):
        fetch(("ctx", j), ctx_ref.at[j], pad.at[j, :, pl.ds(3 * head_cols, head_cols)])
    coming["w1"].wait()

    def first_rows(start, target):
        def body(i, _):
            at = pl.ds(pl.multiple_of(start + i * tile, tile), tile)
            to = pl.ds(pl.multiple_of(i * tile, tile), tile)
            total = nt(pre[0, at, :], w[1, 0])
            for j in range(1, 4):
                total += nt(pre[j, at, :], w[1, j])
            target[to, :] = total.astype(target.dtype)
            return 0

        lax.fori_loop(0, own // tile, body, 0)

    first_rows(own, other)
    share_first = exchange(other, got, 1)
    share_first.start()
    send_second(2, 2)
    first_rows(0, own_part)
    coming["n1"].wait()
    share_first.wait_recv()

    def mean(value):
        return jnp.sum(value, axis=-1, keepdims=True) * (1.0 / value.shape[-1])

    share_gm.wait_send()

    def norm_body(i, _):
        at = pl.ds(pl.multiple_of(i * small, small), small)
        grad = gm[at, :] + (own_part[at, :] + got[at, :].astype(f32))
        normed = n1[at, :]
        e = grad * vec_ref[1:2, :]
        value = (e - mean(e) - normed * mean(e * normed)) * inv1_ref[at, :]
        gm[at, :] = value
        gaf[at, :] = value.astype(bf16)
        vz[0, 0:1, :] += jnp.sum(value, axis=0, keepdims=True)
        vz[0, 1:2, :] += jnp.sum(grad * normed, axis=0, keepdims=True)
        vz[0, 2:3, :] += jnp.sum(grad, axis=0, keepdims=True)
        return 0

    lax.fori_loop(0, own // small, norm_body, 0)
    share_att = exchange(gaf.at[0:own], gaf.at[own : 2 * own], 2)
    share_att.start()
    send_second(2, 3)
    vz[0, 3:6, :] = sums_ref[0:3, :]
    for j in range(1, 4):
        vz[j, 0:8, :] = vz[0, 0:8, :]
    coming["ff"].wait()
    turn(act, 0, rows // tile)
    fetch("xf", xf_ref, act)
    for n in range(4):
        weight_grad(1, n, pre, every)
        send_first(1, n)
    for j in range(4):
        fetch(("qkv", j), qkv_ref.at[j], pre.at[j, :, pl.ds(0, 3 * head_cols)])
    stage(2, 0)
    share_att.wait_recv()
    turn(gaf, 0, rows // tile)
    coming["w0"].wait()
    last = slice(3 * head_cols, 4 * head_cols)

    def context_rows(j):
        def body(i, _):
            at = pl.ds(pl.multiple_of(i * tile, tile), tile)
            pre[j, at, last] = nn(gaf[at, :], w[0, j, :, last]).astype(bf16)
            return 0

        lax.fori_loop(0, rows // tile, body, 0)

    for j in range(4):
        context_rows(j)
        coming[("ctx", j)].wait()
    stage(2, 1)
    weight_grad(0, 0, pad, last)
    weight_grad(0, 1, pad, last)
    weight_grad(0, 2, pad, last)
    weight_grad(0, 3, pad, last)
    coming["xf"].wait()
    turn(act, 0, rows // tile)
    for j in range(4):
        coming[("qkv", j)].wait()

    index = lax.broadcasted_iota(jnp.int32, (rows, 1), 0)
    half = jnp.where(index < own, core, 1 - core)
    inside = index % own
    position = (inside // part) * (2 * part) + half * part + inside % part
    length = length_ref[pl.ds(place % 2, 1), 0:1]
    key_bias = jnp.where(position.astype(f32) < length, 0.0, NEGATIVE).astype(f32)
    lane = lax.broadcasted_iota(jnp.int32, (1, head_cols), 1)
    front = slice(0, 3 * head_cols)

    def attend_back(n, midway):
        j = turns[n]
        keys = pre[j, :, head_cols : 2 * head_cols]
        keys_t = keys.T
        values = pre[j, :, 2 * head_cols : 3 * head_cols]
        dk_acc[...] = jnp.zeros_like(dk_acc)
        dv_acc[...] = jnp.zeros_like(dv_acc)

        def body(start):
            at = slice(start, start + 512)
            query = pre[j, at, 0:head_cols]
            grad = pre[j, at, last]
            parts = []
            for h in range(2):
                here = lane // HD == h
                query_h = jnp.where(here, query, jnp.zeros_like(query))
                grad_h = jnp.where(here, grad, jnp.zeros_like(grad))
                scores = nt(keys, query_h) + key_bias
                chances = jnp.exp(scores - lse_ref[2 * j + h, :, at])
                grad_chances = nt(values, grad_h)
                inner = jnp.sum(chances * grad_chances, axis=0, keepdims=True)
                grad_scores = (chances * (grad_chances - inner)).astype(bf16)
                dv_acc[...] += nn(chances.astype(bf16), grad_h)
                dk_acc[...] += nn(grad_scores, query_h)
                parts.append(nn(keys_t[h * HD : (h + 1) * HD], grad_scores))
            low = jnp.concatenate(parts, axis=0).T.astype(bf16).astype(f32) * HD ** (-0.5)
            pad[j, at, 0:head_cols] = low.astype(bf16)
            vz[j, 8:9, 0:head_cols] += jnp.sum(low, axis=0, keepdims=True)

        for start in range(0, rows, 512):
            if start:
                midway()
            body(start)
        pad[j, :, head_cols : 2 * head_cols] = dk_acc[...].astype(bf16)
        low = dv_acc[...].astype(bf16)
        pad[j, :, 2 * head_cols : 3 * head_cols] = low
        vz[j, 8:9, head_cols : 2 * head_cols] = jnp.sum(low.astype(f32), axis=0, keepdims=True)

    def after_0():
        send_second(1, 0)
        stage(2, 2)

    def after_1():
        send_second(1, 1)
        send_second(1, 2)
        send_first(0, 0)
        send_first(0, 1)
        stage(2, 3)

    def after_2():
        send_second(1, 3)
        send_first(0, 2)
        stage(2, 4)

    between = (lambda: None, lambda: None, lambda: None, lambda: stage(1, 0))
    after = (after_0, after_1, after_2, lambda: send_first(0, 3))
    for n in range(4):
        attend_back(n, between[n])
        weight_grad(0, n, pad, front)
        after[n]()
    for j in range(1, 4):
        v_copy(j).start()
    zg[place] = vz[0]

    def input_rows(start, target):
        def body(i, _):
            at = pl.ds(pl.multiple_of(start + i * tile, tile), tile)
            to = pl.ds(pl.multiple_of(i * tile, tile), tile)
            total = nt(pad[0, at, front], w[0, 0, :, front])
            for j in range(1, 4):
                total += nt(pad[j, at, front], w[0, j, :, front])
            target[to, :] = total.astype(target.dtype)
            return 0

        lax.fori_loop(0, own // tile, body, 0)

    share_att.wait_send()
    share_first.wait_send()
    input_rows(own, other)
    share_in = exchange(other, got, 3)
    share_in.start()
    input_rows(0, own_part)
    send_second(0, 0)
    stage(1, 1)
    share_in.wait_recv()

    def input_body(i, _):
        at = pl.ds(pl.multiple_of(i * small, small), small)
        value = gm[at, :] + (own_part[at, :] + got[at, :].astype(f32))
        low = value.astype(bf16)
        for k in range(4):
            number = (plane, plane + 1 - 2 * (plane % 2), (plane + 2) % 4, 3 - plane)[k]
            to = pl.ds(pl.multiple_of(number * piece, piece), piece)
            gi_own[at, to] = low[:, k * piece : (k + 1) * piece]
        return 0

    lax.fori_loop(0, own // small, input_body, 0)
    back_start(gi_own, gi_ref, g_s, g_r)

    def fold(n, m, arrived, flip):
        for k in range(4):
            here = slice(k * piece, (k + 1) * piece)
            there = slice((k ^ flip) * piece, ((k ^ flip) + 1) * piece)
            tot[n, 0:8, here] = tot[m, 0:8, here] + arrived[0:8, there]
        tot[n, 8:16, :] = tot[m, 8:16, :] + arrived[8:16, :]

    for j in range(1, 4):
        v_got(j).wait_recv()
    tot[0] = ((zg[0] + zg[1]) + zg[2]) + zg[3]
    v_x = remote(tot.at[0], xg, e_s.at[4], e_r.at[4], x_side)
    v_x.start()
    send_second(0, 1)
    v_x.wait_recv()
    fold(1, 0, xg, 1)
    v_y = remote(tot.at[1], yg, e_s.at[5], e_r.at[5], y_side)
    v_y.start()
    stage(1, 2)
    send_second(0, 2)
    v_y.wait_recv()
    fold(2, 1, yg, 2)
    v_c = exchange(tot.at[2], cg, 6)
    v_c.start()
    send_second(0, 3)
    stage(1, 3)
    stage(0, 0)
    stage(0, 1)
    stage(1, 4)
    stage(0, 2)
    stage(0, 3)
    stage(0, 4)
    v_c.wait_recv()
    for k in range(4):
        number = (plane, plane + 1 - 2 * (plane % 2), (plane + 2) % 4, 3 - plane)[k]
        to = pl.ds(pl.multiple_of(number * piece, piece), piece)
        here = slice(k * piece, (k + 1) * piece)
        total_ref[0:8, to] = tot[2, 0:8, here] + cg[0:8, here]
    own_row = tot[2, 8:9, :]
    their_row = cg[8:9, :]
    total_ref[8:9, :] = jnp.where(core == 0, own_row, their_row)
    total_ref[9:10, :] = jnp.where(core == 0, their_row, own_row)

    for b in range(3):
        for n in range(4):
            for h in range(2):
                d_copy(b, n, h).wait_send()
                x_copy(b, n, h).wait_send()
                y_copy(b, n, h).wait_send()
            if n < 3:
                z_copy(b, n).wait_send()
    for n in range(6):
        home_keep(n).wait()
        home_copy(n).wait_send()
        home_copy(n).wait_recv()
    for j in range(1, 4):
        v_copy(j).wait_send()
    for copy in (share_in, v_x, v_y, v_c):
        copy.wait_send()
    back_end(lo_own, lo_ref, lo_s, lo_r)
    back_end(gi_own, gi_ref, g_s, g_r)


def backward(w_all, xf, qkv, lse, ctx, ff, hid, dg, n1, inv1, gm, vec, sums, length, lo):
    rows, width = xf.shape
    own = rows // 2
    part = own // 4
    piece = width // 4
    cols = hid.shape[2]
    head_cols = 2 * HD
    any_ = pl.BlockSpec(memory_space=pltpu.HBM)
    vm = pl.BlockSpec(memory_space=pltpu.VMEM)
    shape = jax.ShapeDtypeStruct
    dma = pltpu.SemaphoreType.DMA
    flops = 2 * rows * width * cols * 24 + 40 * rows * rows * HD * 4
    return pl.pallas_call(
        backward_kernel,
        in_specs=[
            any_, any_, any_, vm, any_, any_, any_, any_, any_, vm, any_, vm, vm, vm, any_
        ],
        out_specs=[any_] * 8 + [vm],
        out_shape=[
            shape((2, 2 * part, width), bf16),
            shape((2, 2 * part, width), bf16),
            shape((piece // 2, 2 * head_cols), f32),
            shape((piece // 2, 2 * head_cols), f32),
            shape((piece // 2, 2 * head_cols), f32),
            shape((2 * head_cols, piece // 2), f32),
            shape((piece // 2, 2 * cols), f32),
            shape((2 * cols, piece // 2), f32),
            shape((16, width), f32),
        ],
        scratch_shapes=[
            pltpu.VMEM((3, 4, width, cols), bf16),
            pltpu.VMEM((4, width, cols), bf16),
            pltpu.VMEM((4, rows, cols), bf16),
            pltpu.VMEM((4, rows, cols), bf16),
            pltpu.VMEM((rows, width), bf16),
            pltpu.VMEM((rows, width), bf16),
            pltpu.VMEM((width, rows), bf16),
            pltpu.VMEM((own, width), f32),
            pltpu.VMEM((own, width), f32),
            pltpu.VMEM((own, width), f32),
            pltpu.VMEM((own, width), bf16),
            pltpu.VMEM((own, width), bf16),
            pltpu.VMEM((2, 4, piece, cols), bf16),
            pltpu.VMEM((3, 4, piece, cols), bf16),
            pltpu.VMEM((3, 4, piece, cols), bf16),
            pltpu.VMEM((3, 5, piece, cols), bf16),
            pltpu.VMEM((3, piece, cols), f32),
            pltpu.VMEM((rows, head_cols), f32),
            pltpu.VMEM((rows, head_cols), f32),
            pltpu.VMEM((4, 16, width), f32),
            pltpu.VMEM((4, 16, width), f32),
            pltpu.VMEM((16, width), f32),
            pltpu.VMEM((16, width), f32),
            pltpu.VMEM((16, width), f32),
            pltpu.VMEM((3, 16, width), f32),
            dma((3, 4, 2)), dma((3, 4, 2)), dma((3, 4, 2)), dma((3, 4, 2)), dma((3, 4, 2)), dma((3, 4, 2)),
            dma((3, 3)), dma((3, 5)), dma((6,)), dma((6,)), dma((6,)), dma((8,)), dma((8,)),
            dma((4,)), dma((4,)), dma((3,)), dma((4,)), dma((32,)),
            dma((4,)), dma((4,)),
        ],
        compiler_params=pltpu.CompilerParams(
            collective_id=1, has_side_effects=True, vmem_limit_bytes=60 << 20
        ),
        cost_estimate=pl.CostEstimate(
            flops=flops, bytes_accessed=60 << 20, transcendentals=8 * rows * rows
        ),
        name="backward_layer",
    )(w_all, xf, qkv, lse, ctx, ff, hid, dg, n1, inv1, gm, vec, sums, length, lo)


def swap_cores(value):
    return lax.ppermute(value, "core", SWAP)


def on_device(
    inputs,
    lengths,
    w_query,
    w_key,
    w_value,
    b_query,
    b_value,
    w_out,
    b_out,
    gain_one,
    shift_one,
    w_in,
    b_in,
    w_back,
    b_back,
    gain_two,
    shift_two,
    cotangent,
):
    planes = lax.axis_size("plane")
    n_t = lax.axis_size("tensor")
    plane = lax.axis_index("plane")
    core = lax.axis_index("core")
    place = lax.axis_index("tensor")
    seqs, slots_here, width = inputs.shape
    slots = slots_here * n_t
    half_slots = slots_here // 2
    own = slots // 2
    assert seqs * 2 == n_t
    head_cols = w_query.shape[1] // 2
    ff_cols = w_in.shape[1] // 2
    scale = HD ** (-0.5)
    quad = planes == 4
    if quad:
        row = jnp.stack(
            [
                value.astype(f32)
                for value in (
                    b_out, gain_one, shift_one, b_back, gain_two, shift_two, b_in,
                    jnp.concatenate([b_query, b_value, jnp.zeros((width // 2,), bf16)]),
                )
            ]
        )
        lens = jnp.broadcast_to(
            jnp.concatenate([lengths.astype(f32)] * (8 // seqs))[:, None], (8, 128)
        )
        (w_all, x_full, qkv4, lse8, ctx4, first_full, hid4, dg4, normed_one, inverse_one,
         grad_mixed, lo, second_sums, vec, length_rows) = forward(
            lens, row, inputs, cotangent, w_query, w_key, w_value, w_out, w_in, w_back
        )
        (layer_out, gi, grad_w_query, grad_w_key, grad_w_value, grad_w_out, grad_w_in,
         grad_w_back, totals) = backward(
            w_all, x_full, qkv4, lse8, ctx4, first_full, hid4, dg4, normed_one, inverse_one,
            grad_mixed, vec, second_sums, length_rows, lo,
        )
        n_bias = 2 * head_cols + ff_cols
        biases_out = totals[8:10, :n_bias]
        return (
            layer_out,
            gi.astype(f32),
            grad_w_query,
            grad_w_key,
            grad_w_value,
            biases_out[:, :head_cols].reshape(-1),
            biases_out[:, head_cols : 2 * head_cols].reshape(-1),
            grad_w_out,
            totals[0],
            totals[1],
            totals[2],
            grad_w_in,
            biases_out[:, 2 * head_cols :].reshape(-1),
            grad_w_back,
            totals[3],
            totals[4],
            totals[5],
        )

    ring = [(i, (i + 1) % n_t) for i in range(n_t)]
    x_pairs = [(i, i ^ 1) for i in range(planes)]
    y_pairs = [(i, i ^ 2) for i in range(planes)]

    def reorder(value, axis):
        if not quad:
            return value
        size = value.shape[axis] // 4
        return jnp.concatenate(
            [lax.dynamic_slice_in_dim(value, (plane ^ k) * size, size, axis) for k in range(4)],
            axis=axis,
        )

    def by_core(mine, theirs, axis=0):
        first = jnp.where(core == 0, mine, theirs)
        second = jnp.where(core == 0, theirs, mine)
        return jnp.concatenate([first, second], axis=axis)

    def to_chip(rows_here):
        value = reorder(rows_here, 2).reshape(seqs, 2, half_slots, width)
        mine = lax.dynamic_index_in_dim(value, core, 1, keepdims=False)
        other = lax.dynamic_index_in_dim(value, 1 - core, 1, keepdims=False)
        both = by_core(mine, swap_cores(other))
        return lax.all_to_all(both, "tensor", 0, 0, tiled=True).reshape(own, width)

    def from_chip(rows_own):
        value = rows_own.reshape(n_t, half_slots, width)
        value = lax.all_to_all(value, "tensor", 0, 0, tiled=True)
        value = value.reshape(2, seqs, half_slots, width)
        mine = lax.dynamic_index_in_dim(value, core, 0, keepdims=False)
        other = lax.dynamic_index_in_dim(value, 1 - core, 0, keepdims=False)
        got = swap_cores(other)
        value = jnp.stack(
            [jnp.where(core == 0, mine, got), jnp.where(core == 0, got, mine)], axis=1
        )
        return reorder(value.reshape(seqs, slots_here, width), 2)

    their_lengths = swap_cores(lengths)
    all_lengths = by_core(lengths, their_lengths)
    length = lax.dynamic_index_in_dim(all_lengths, place, 0, keepdims=False)
    index = jnp.arange(slots)
    position = (
        (index % own) // half_slots * slots_here
        + ((index // own) ^ core) * half_slots
        + index % half_slots
    )
    valid = position < length
    key_bias = jnp.where(valid, 0.0, NEGATIVE).astype(f32)[:, None]
    own_valid = valid[:own, None]

    def halves(value, cols):
        return (
            lax.dynamic_slice_in_dim(value, core * cols, cols, 1),
            lax.dynamic_slice_in_dim(value, (1 - core) * cols, cols, 1),
        )

    pieces = [
        halves(w_query, head_cols),
        halves(w_key, head_cols),
        halves(w_value, head_cols),
        halves(w_out.T, head_cols),
        halves(w_in, ff_cols),
        halves(w_back.T, ff_cols),
    ]
    keep = jnp.concatenate([piece[0] for piece in pieces], axis=1)
    give = jnp.concatenate([piece[1] for piece in pieces], axis=1)
    cuts = (4 * head_cols, 4 * head_cols + ff_cols)

    def flat(gathered):
        return jnp.concatenate([gathered[j] for j in range(n_t)], axis=1)

    out_bias = reorder(b_out, 0).astype(f32)
    back_bias = reorder(b_back, 0).astype(f32)
    gain_first = reorder(gain_one, 0).astype(f32)
    shift_first = reorder(shift_one, 0).astype(f32)
    gain_second = reorder(gain_two, 0).astype(f32)
    shift_second = reorder(shift_two, 0).astype(f32)
    bias_row = jnp.concatenate(
        [
            lax.dynamic_slice_in_dim(b_query, core * head_cols, head_cols),
            lax.dynamic_slice_in_dim(b_value, core * head_cols, head_cols),
            lax.dynamic_slice_in_dim(b_in, core * ff_cols, ff_cols),
        ]
    )[None]
    qkv_scale = jnp.tile(
        jnp.concatenate([jnp.full((head_cols,), scale, f32), jnp.ones((2 * head_cols,), f32)]), n_t
    )[None]
    def both_rows(value):
        return jnp.concatenate([value, swap_cores(value)], axis=0)

    def own_sum(partial):
        return partial[:own] + swap_cores(partial[own:])

    def normalize(value):
        average = jnp.mean(value, axis=-1, keepdims=True)
        centered = value - average
        variance = jnp.mean(centered * centered, axis=-1, keepdims=True)
        inverse = lax.rsqrt(variance + EPSILON)
        return centered * inverse, inverse

    def normalize_back(grad, gain, normed, inverse):
        e = grad * gain
        return (
            e
            - jnp.mean(e, axis=-1, keepdims=True)
            - normed * jnp.mean(e * normed, axis=-1, keepdims=True)
        ) * inverse

    packed = by_core(keep, swap_cores(give))
    bundle_a = packed[:, : cuts[0]]
    bundle_b = packed[:, cuts[0] : cuts[1]]
    bundle_c = packed[:, cuts[1] :]
    def gather_z(own_piece):
        got = [own_piece]
        for _ in range(n_t - 1):
            got.append(lax.ppermute(got[-1], "tensor", ring))
        return jnp.stack(got)

    def gather_planes(mine):
        if not quad:
            return lax.all_gather(mine, "plane", axis=1, tiled=True)
        half = n_t // 2
        from_x = lax.ppermute(mine, "plane", x_pairs)
        from_y = lax.ppermute(mine, "plane", y_pairs)
        low = lax.ppermute(from_y[:half], "plane", x_pairs)
        high = lax.ppermute(from_x[half:], "plane", y_pairs)
        return jnp.concatenate([mine, from_x, from_y, jnp.concatenate([low, high])], axis=1)

    biases = gather_z(bias_row)[:, 0].astype(f32)
    z_a = gather_z(bundle_a)
    full_a = gather_planes(z_a)
    w_qkv = flat(full_a[:, :, : 3 * head_cols])
    w_o = flat(full_a[:, :, 3 * head_cols :])
    w_1 = flat(gather_planes(gather_z(bundle_b)))
    w_2 = flat(gather_planes(gather_z(bundle_c)))

    zeros_k = jnp.zeros((n_t, head_cols), f32)
    qkv_bias = jnp.concatenate(
        [biases[:, :head_cols], zeros_k, biases[:, head_cols : 2 * head_cols]], axis=1
    ).reshape(1, -1)
    in_bias = biases[:, 2 * head_cols :].reshape(1, -1)

    own_x = to_chip(inputs)
    x_full = both_rows(own_x)
    qkv = ((nn(x_full, w_qkv) + qkv_bias) * qkv_scale).astype(bf16)
    context, lse = attend_fwd(qkv, key_bias)
    attended = own_sum(nt(context, w_o))
    normed_one, inverse_one = normalize(own_x.astype(f32) + attended + out_bias)
    first_norm = normed_one * gain_first + shift_first
    first_full = both_rows(first_norm.astype(bf16))
    pre_act = nn(first_full, w_1) + in_bias
    activated, slope = gelu_and_slope(pre_act)
    hidden = activated.astype(bf16)
    mixed = own_sum(nt(hidden, w_2))
    normed_two, inverse_two = normalize(first_norm + mixed + back_bias)
    second = normed_two * gain_second + shift_second
    layer_out = from_chip(jnp.where(own_valid, second, 0.0).astype(bf16))

    grad_second = jnp.where(own_valid, to_chip(cotangent).astype(f32), 0.0)
    grad_mixed = normalize_back(grad_second, gain_second, normed_two, inverse_two)

    grad_mixed_full = both_rows(grad_mixed.astype(bf16))
    grad_w2 = tn(grad_mixed_full, hidden)
    grad_pre_low = (nn(grad_mixed_full, w_2) * slope.astype(f32)).astype(bf16)
    grad_w1 = tn(first_full, grad_pre_low)
    grad_first = grad_mixed + own_sum(nt(grad_pre_low, w_1))
    grad_att = normalize_back(grad_first, gain_first, normed_one, inverse_one)
    grad_att_full = both_rows(grad_att.astype(bf16))
    grad_context = nn(grad_att_full, w_o).astype(bf16)
    grad_wo = tn(grad_att_full, context)
    grad_qkv = attend_bwd(qkv, grad_context, lse, key_bias)
    grad_qkv = grad_qkv * qkv_scale.astype(bf16)
    grad_wqkv = tn(x_full, grad_qkv)
    grad_rows = grad_att + own_sum(nt(grad_qkv, w_qkv))
    grad_inputs = from_chip(grad_rows.astype(bf16)).astype(f32)

    def scatter(grad):
        cols = grad.shape[1] // n_t
        if quad:
            rows = width // 4
            blocks = grad.reshape(4, rows, n_t, cols).transpose(0, 2, 1, 3)
            half = n_t // 2
            low = lax.ppermute(blocks[3, :half].astype(bf16), "plane", x_pairs)
            high = lax.ppermute(blocks[3, half:].astype(bf16), "plane", y_pairs)
            for_y = jnp.concatenate([blocks[2, :half] + low.astype(f32), blocks[2, half:]])
            for_x = jnp.concatenate([blocks[1, :half], blocks[1, half:] + high.astype(f32)])
            from_x = lax.ppermute(for_x.astype(bf16), "plane", x_pairs)
            from_y = lax.ppermute(for_y.astype(bf16), "plane", y_pairs)
            mine = blocks[0] + from_x.astype(f32) + from_y.astype(f32)
        else:
            blocks = grad.reshape(width, n_t, cols).transpose(1, 0, 2)
            mine = lax.psum_scatter(
                blocks.astype(bf16), "plane", scatter_dimension=1, tiled=True
            ).astype(f32)
        back = [(b, a) for a, b in ring]
        total = mine[n_t - 1]
        for j in range(n_t - 2, -1, -1):
            total = mine[j] + lax.ppermute(total.astype(bf16), "tensor", back).astype(f32)
        return total

    home_c = scatter(grad_w2)
    home_b = scatter(grad_w1)
    grad_a = jnp.concatenate(
        [
            grad_wqkv.reshape(width, n_t, 3 * head_cols),
            grad_wo.reshape(width, n_t, head_cols),
        ],
        axis=2,
    ).reshape(width, -1)
    home_a = scatter(grad_a)
    home = jnp.concatenate([home_a, home_b, home_c], axis=1)
    home = home.reshape(2, -1, home.shape[1])
    mine = lax.dynamic_index_in_dim(home, core, 0, keepdims=False)
    other = lax.dynamic_index_in_dim(home, 1 - core, 0, keepdims=False)
    got = swap_cores(other)

    def row_sum(value):
        return reorder(jnp.sum(value, axis=0), 0)

    second_rows = [row_sum(grad_mixed), row_sum(grad_second * normed_two), row_sum(grad_second)]
    norm_sums = jnp.concatenate(
        [
            row_sum(grad_att),
            row_sum(grad_first * normed_one),
            row_sum(grad_first),
            *second_rows,
        ]
    )
    qkv_sum = jnp.sum(grad_qkv.astype(f32), axis=0).reshape(n_t, 3 * head_cols)
    pre_sum = jnp.sum(grad_pre_low.astype(f32), axis=0).reshape(n_t, ff_cols)
    bias_sum = jnp.concatenate([qkv_sum[:, :head_cols], qkv_sum[:, 2 * head_cols :], pre_sum], axis=1)
    at_home = lax.rem(place - jnp.arange(n_t) + n_t, n_t)
    spread = (at_home[:, None] == jnp.arange(n_t)[None]).astype(f32)
    by_place = jnp.sum(spread[:, :, None] * bias_sum[:, None, :], axis=0)
    both = jnp.where(
        (jnp.arange(2) == core)[None, :, None], by_place[:, None, :], 0.0
    )
    sums = lax.psum(jnp.concatenate([norm_sums, both.reshape(-1)]), ("plane", "core", "tensor"))
    norms = sums[: 6 * width].reshape(6, width)
    biases_out = lax.dynamic_index_in_dim(
        sums[6 * width :].reshape(n_t, 2, -1), place, 0, keepdims=False
    )
    def columns(start, cols):
        return by_core(mine[:, start : start + cols], got[:, start : start + cols], axis=1)

    grad_w_query = columns(0, head_cols)
    grad_w_key = columns(head_cols, head_cols)
    grad_w_value = columns(2 * head_cols, head_cols)
    grad_w_out = columns(3 * head_cols, head_cols).T
    grad_w_in = columns(cuts[0], ff_cols)
    grad_w_back = columns(cuts[1], ff_cols).T

    grad_b_query = biases_out[:, :head_cols].reshape(-1)
    grad_b_value = biases_out[:, head_cols : 2 * head_cols].reshape(-1)
    grad_b_in = biases_out[:, 2 * head_cols :].reshape(-1)
    return (
        layer_out,
        grad_inputs,
        grad_w_query,
        grad_w_key,
        grad_w_value,
        grad_b_query,
        grad_b_value,
        grad_w_out,
        norms[0],
        norms[1],
        norms[2],
        grad_w_in,
        grad_b_in,
        grad_w_back,
        norms[3],
        norms[4],
        norms[5],
    )


def solution(mesh):
    devices = mesh.devices.reshape(mesh.shape["dp"] // 2, 2, mesh.shape["tensor"])
    inner = Mesh(devices, ("plane", "core", "tensor"))
    dp = ("plane", "core")
    row = P(dp, "tensor")
    column = P("tensor", dp)
    rows3 = P(dp, "tensor", None)
    shard = P("tensor")
    whole = P()
    return jax.shard_map(
        on_device,
        mesh=inner,
        in_specs=(
            rows3, P(dp), row, row, row, shard, shard, column, whole, whole, whole,
            row, shard, column, whole, whole, whole, rows3,
        ),
        out_specs=(
            rows3, rows3, row, row, row, shard, shard, column, whole, whole, whole,
            row, shard, column, whole, whole, whole,
        ),
        check_vma=False,
    )
```

```python
import jax
import jax.numpy as jnp
from jax import lax
from jax.experimental import pallas as pl
from jax.experimental.pallas import tpu as pltpu
from jax.sharding import Mesh, PartitionSpec as P

HD = 64
EPSILON = 1e-05
NEGATIVE = -1e30
f32 = jnp.float32
bf16 = jnp.bfloat16
SWAP = [(0, 1), (1, 0)]


def nt(a, b):
    return lax.dot_general(a, b, (((1,), (1,)), ((), ())), preferred_element_type=f32)


def tn(a, b):
    return lax.dot_general(a, b, (((0,), (0,)), ((), ())), preferred_element_type=f32)


def nn(a, b):
    return lax.dot_general(a, b, (((1,), (0,)), ((), ())), preferred_element_type=f32)


def attend_fwd_kernel(block, qkv_ref, kb_ref, ctx_ref, lse_ref):
    rows = qkv_ref.shape[0]
    lane = lax.broadcasted_iota(jnp.int32, (1, 2 * HD), 1)
    keys = qkv_ref[:, 2 * HD : 4 * HD]
    values_t = qkv_ref[:, 4 * HD : 6 * HD].T
    key_bias = kb_ref[...]
    for start in range(0, rows, block):
        query = qkv_ref[start : start + block, 0 : 2 * HD]
        parts = []
        for h in range(2):
            query_h = jnp.where(lane // HD == h, query, jnp.zeros_like(query))
            scores = nt(keys, query_h) + key_bias
            largest = jnp.max(scores, axis=0, keepdims=True)
            weights = jnp.exp(scores - largest)
            total = jnp.sum(weights, axis=0, keepdims=True)
            part = nn(values_t[h * HD : (h + 1) * HD], weights.astype(bf16))
            parts.append(part / total)
            lse_ref[0, h : h + 1, start : start + block] = largest + jnp.log(total)
        ctx_ref[start : start + block, :] = jnp.concatenate(parts, axis=0).T.astype(bf16)


def attend_fwd(qkv, key_bias):
    rows = qkv.shape[0]
    groups = qkv.shape[1] // (6 * HD)
    block = min(512, rows)
    return pl.pallas_call(
        lambda *refs: attend_fwd_kernel(block, *refs),
        grid=(groups,),
        in_specs=[
            pl.BlockSpec((rows, 6 * HD), lambda j: (0, j)),
            pl.BlockSpec((rows, 1), lambda j: (0, 0)),
        ],
        out_specs=[
            pl.BlockSpec((rows, 2 * HD), lambda j: (0, j)),
            pl.BlockSpec((1, 2, rows), lambda j: (j, 0, 0)),
        ],
        out_shape=[
            jax.ShapeDtypeStruct((rows, groups * 2 * HD), bf16),
            jax.ShapeDtypeStruct((groups, 2, rows), f32),
        ],
        compiler_params=pltpu.CompilerParams(vmem_limit_bytes=48 << 20),
        cost_estimate=pl.CostEstimate(
            flops=groups * 8 * rows * rows * HD * 4,
            bytes_accessed=rows * groups * 8 * HD * 2,
            transcendentals=groups * 2 * rows * rows,
        ),
        name="attend_fwd",
    )(qkv, key_bias)


def attend_bwd_kernel(block, qkv_ref, g_ref, lse_ref, kb_ref, d_ref, dk_acc, dv_acc):
    rows = qkv_ref.shape[0]
    lane = lax.broadcasted_iota(jnp.int32, (1, 2 * HD), 1)
    keys = qkv_ref[:, 2 * HD : 4 * HD]
    keys_t = keys.T
    values = qkv_ref[:, 4 * HD : 6 * HD]
    key_bias = kb_ref[...]
    for start in range(0, rows, block):
        query = qkv_ref[start : start + block, 0 : 2 * HD]
        grad = g_ref[start : start + block, :]
        parts = []
        for h in range(2):
            here = lane // HD == h
            query_h = jnp.where(here, query, jnp.zeros_like(query))
            grad_h = jnp.where(here, grad, jnp.zeros_like(grad))
            scores = nt(keys, query_h) + key_bias
            chances = jnp.exp(scores - lse_ref[0, h : h + 1, start : start + block])
            grad_chances = nt(values, grad_h)
            inner = jnp.sum(chances * grad_chances, axis=0, keepdims=True)
            grad_scores = (chances * (grad_chances - inner)).astype(bf16)
            dv = nn(chances.astype(bf16), grad_h)
            dk = nn(grad_scores, query_h)
            if start == 0 and h == 0:
                dv_acc[...] = dv
                dk_acc[...] = dk
            else:
                dv_acc[...] += dv
                dk_acc[...] += dk
            parts.append(nn(keys_t[h * HD : (h + 1) * HD], grad_scores))
        d_ref[start : start + block, 0 : 2 * HD] = jnp.concatenate(parts, axis=0).T.astype(bf16)
    d_ref[:, 2 * HD : 4 * HD] = dk_acc[...].astype(bf16)
    d_ref[:, 4 * HD : 6 * HD] = dv_acc[...].astype(bf16)


def attend_bwd(qkv, grad_context, lse, key_bias):
    rows = qkv.shape[0]
    groups = qkv.shape[1] // (6 * HD)
    block = min(512, rows)
    return pl.pallas_call(
        lambda *refs: attend_bwd_kernel(block, *refs),
        grid=(groups,),
        in_specs=[
            pl.BlockSpec((rows, 6 * HD), lambda j: (0, j)),
            pl.BlockSpec((rows, 2 * HD), lambda j: (0, j)),
            pl.BlockSpec((1, 2, rows), lambda j: (j, 0, 0)),
            pl.BlockSpec((rows, 1), lambda j: (0, 0)),
        ],
        out_specs=pl.BlockSpec((rows, 6 * HD), lambda j: (0, j)),
        out_shape=jax.ShapeDtypeStruct((rows, groups * 6 * HD), bf16),
        scratch_shapes=[pltpu.VMEM((rows, 2 * HD), f32), pltpu.VMEM((rows, 2 * HD), f32)],
        compiler_params=pltpu.CompilerParams(vmem_limit_bytes=48 << 20),
        cost_estimate=pl.CostEstimate(
            flops=groups * 20 * rows * rows * HD * 4,
            bytes_accessed=rows * groups * 14 * HD * 2,
            transcendentals=groups * 2 * rows * rows,
        ),
        name="attend_bwd",
    )(qkv, grad_context, lse, key_bias)

POLY = (
    0.30995978221815235,
    0.31100346478903146,
    0.2699660979585953,
    0.2765467936611628,
    -0.03831584737802812,
    0.38967711658103854,
    -0.3554874111653827,
    0.08996434684501212,
)
POLY_AT = 0.31
DENSITY = 0.3989422804014327
MESH = pl.DeviceIdType.MESH


def gelu_and_slope(v):
    density = jnp.exp(-0.5 * v * v) * DENSITY
    t = 1.0 / (1.0 + POLY_AT * jnp.abs(v))
    tail = jnp.full_like(v, POLY[-1])
    for coefficient in POLY[-2::-1]:
        tail = tail * t + coefficient
    tail = tail * t * density
    below = jnp.where(v > 0, 1.0 - tail, tail)
    return v * below, below + v * density


def forward_kernel(
    lens_ref, bo_ref, g1_ref, s1_ref, bb_ref, g2_ref, s2_ref, bi_ref, bq_ref, bv_ref, x_ref, c_ref, wq_ref, wk_ref, wv_ref, wo_ref, wi_ref, wb_ref,
    w_out, xf_out, qkv_out, lse_ref, ctx_out, ff_out, hid_out, dg_out, n1_out, inv1_ref, gm_ref,
    lo_ref, sums_ref, vec_ref, length_ref,
    w, xs, xf, bias, qkv, ctx, ff, hid, dg, n1, first, other_acc, other_part, own_part, att_got, mix_got, cot,
    wo_here, wb_here, wo_give, wb_give, lens, parts_of, row_ref,
    z_s, z_r, zl_s, zl_r, x_s, x_r, y_s, y_r, f_s, f_r, pre_l, pre_s, pre_r, b_s, b_r,
    xa_s, xa_r, ca_s, ca_r, e_s, e_r, o_s,
):
    plane = lax.axis_index("plane")
    core = lax.axis_index("core")
    place = lax.axis_index("tensor")
    partner = {"core": 1 - core}
    x_side = {"plane": plane + 1 - 2 * (plane % 2)}
    y_side = {"plane": (plane + 2) % 4}
    z_right = {"tensor": (place + 1) % 4}
    z_left = {"tensor": (place + 3) % 4}
    first_end = (3 - place) // 3
    last_end = place // 3
    turns = (0, 1 + 2 * first_end, 3 - first_end - last_end, 2 - first_end + last_end)
    rows = xf.shape[0]
    own = rows // 2
    part = own // 4
    piece = w.shape[2] // 4

    def remote(source, target, send, recv, to):
        return pltpu.make_async_remote_copy(
            source, target, send, recv, device_id=to, device_id_type=MESH
        )

    def right_copy(b, n):
        return remote(
            w.at[b, n - 1, 0:piece], w.at[b, n, 0:piece], z_s.at[b, n - 1], z_r.at[b, n - 1], z_right
        )

    def left_copy(b, n):
        return remote(
            w.at[b, (5 - n) % 4, 0:piece], w.at[b, 4 - n, 0:piece],
            zl_s.at[b, n - 1], zl_r.at[b, n - 1], z_left,
        )

    def line_do(b, n, act):
        @pl.when(jnp.logical_and(place <= 2, place >= n - 1))
        def _():
            act(right_copy(b, n))

        @pl.when(jnp.logical_and(place >= 1, place + n <= 4))
        def _():
            act(left_copy(b, n))

    def line_start(b, n):
        line_do(b, n, lambda copy: copy.start())

    def line_wait(b, n):
        @pl.when(place >= n)
        def _():
            right_copy(b, n).wait_recv()

        @pl.when(place + n <= 3)
        def _():
            left_copy(b, n).wait_recv()

    def x_copy(b, n):
        j = turns[n]
        return remote(
            w.at[b, j, 0:piece], w.at[b, j, piece : 2 * piece], x_s.at[b, n], x_r.at[b, n], x_side
        )

    def y_copy(b, n):
        j = turns[n]
        return remote(
            w.at[b, j, 0:piece], w.at[b, j, 2 * piece : 3 * piece], y_s.at[b, n], y_r.at[b, n], y_side
        )

    def fx_copy(b, n):
        j, half = turns[n], piece // 2
        return remote(
            w.at[b, j, 2 * piece : 2 * piece + half], w.at[b, j, 3 * piece : 3 * piece + half],
            f_s.at[b, n, 0], f_r.at[b, n, 0], x_side,
        )

    def fy_copy(b, n):
        j, half = turns[n], piece // 2
        return remote(
            w.at[b, j, piece + half : 2 * piece], w.at[b, j, 3 * piece + half : 4 * piece],
            f_s.at[b, n, 1], f_r.at[b, n, 1], y_side,
        )

    def cross(b, n):
        x_copy(b, n).start()
        y_copy(b, n).start()

    def forward_on(b, n):
        y_copy(b, n).wait_recv()
        fx_copy(b, n).start()
        x_copy(b, n).wait_recv()
        fy_copy(b, n).start()

    def ready(b, n):
        fx_copy(b, n).wait_recv()
        fy_copy(b, n).wait_recv()
        save(w.at[b, turns[n]], w_out.at[b, turns[n]])

    half_piece = piece // 2
    head_cols = 2 * HD
    mine_at = pl.ds(core * half_piece, half_piece)
    theirs_at = pl.ds((1 - core) * half_piece, half_piece)
    cols = w.shape[3]

    def head_half(which):
        return pl.ds(pl.multiple_of(which * head_cols, head_cols), head_cols)

    def wide_half(which):
        return pl.ds(pl.multiple_of(which * cols, cols), cols)

    def keep_copy(n):
        if n < 3:
            source = (wq_ref, wk_ref, wv_ref)[n].at[:, head_half(core)]
            target = w.at[0, 0, mine_at, n * head_cols : (n + 1) * head_cols]
        elif n == 3:
            source, target = wo_ref, wo_here
        elif n == 4:
            source, target = wi_ref.at[:, wide_half(core)], w.at[1, 0, mine_at]
        else:
            source, target = wb_ref, wb_here
        return pltpu.make_async_copy(source, target, pre_l.at[n])

    def pre_copy(n, at):
        if n < 3:
            source = (wq_ref, wk_ref, wv_ref)[n].at[:, head_half(1 - core)]
            target = w.at[0, 0, at, n * head_cols : (n + 1) * head_cols]
        elif n == 3:
            source, target = wo_give, w.at[0, 0, at, 3 * head_cols : 4 * head_cols]
        elif n == 4:
            source, target = wi_ref.at[:, wide_half(1 - core)], w.at[1, 0, at]
        else:
            source, target = wb_give, w.at[2, 0, at]
        return remote(source, target, pre_s.at[n], pre_r.at[n], partner)

    def bias_copy(s):
        return remote(
            bias.at[0], bias.at[s], b_s.at[s], b_r.at[s], {"tensor": (place + s) % 4}
        )

    def spread(source, target, send, recv, l, h):
        at = pl.ds(place * part, part)
        to = {"core": h, "tensor": 2 * core + l}
        return remote(
            source.at[l, h * part : (h + 1) * part], target.at[at], send.at[2 * l + h],
            recv.at[place], to,
        )

    def spread_local(source, target, recv, l, h):
        at = pl.ds(place * part, part)
        return pltpu.make_async_copy(
            source.at[l, h * part : (h + 1) * part], target.at[at], recv.at[place]
        )

    def is_here(l, h):
        return jnp.logical_and(core == h, place == 2 * core + l)

    def spread_start(source, target, send, recv):
        for l in range(2):
            for h in range(2):
                @pl.when(is_here(l, h))
                def _():
                    spread_local(source, target, recv, l, h).start()

                @pl.when(jnp.logical_not(is_here(l, h)))
                def _():
                    spread(source, target, send, recv, l, h).start()

    def spread_wait(source, target, recv):
        for s in range(4):
            pltpu.make_async_copy(
                source.at[0, 0:part], target.at[s * part : (s + 1) * part], recv.at[s]
            ).wait()

    def spread_sent(source, target, send, recv):
        for l in range(2):
            for h in range(2):
                @pl.when(jnp.logical_not(is_here(l, h)))
                def _():
                    spread(source, target, send, recv, l, h).wait_send()

    def exchange(source, target, n):
        return remote(source, target, e_s.at[n], e_r.at[n], partner)

    outs = []

    def save(source, target):
        copy = pltpu.make_async_copy(source, target, o_s.at[len(outs)])
        copy.start()
        outs.append(copy)

    barrier = pltpu.get_barrier_semaphore()
    friends = [x_side, y_side, partner]
    for s in range(1, 4):
        friends.append({"tensor": (place + s) % 4})
        friends.append({"tensor": (place + s) % 4, "core": 1 - core})
    for friend in friends:
        pl.semaphore_signal(barrier, inc=1, device_id=friend, device_id_type=MESH)
    for n in (3, 0, 1, 2, 4, 5):
        keep_copy(n).start()
    pl.semaphore_wait(barrier, len(friends))

    def block_at(k):
        number = (plane, plane + 1 - 2 * (plane % 2), (plane + 2) % 4, 3 - plane)[k]
        return pl.ds(pl.multiple_of(number * piece, piece), piece)

    for n in range(3):
        pre_copy(n, mine_at).start()
    keep_copy(3).wait()
    wo_give[...] = wo_here[head_half(1 - core), :].T
    pre_copy(3, mine_at).start()
    w[0, 0, mine_at, 3 * head_cols : 4 * head_cols] = wo_here[head_half(core), :].T
    pre_copy(4, mine_at).start()
    for n in range(3):
        keep_copy(n).wait()
    for n in range(4):
        pre_copy(n, theirs_at).wait_recv()
    line_start(0, 1)
    cross(0, 0)
    spread_start(x_ref, xs, xa_s, xa_r)
    keep_copy(5).wait()
    wb_give[...] = wb_here[wide_half(1 - core), :].T
    pre_copy(5, mine_at).start()
    w[2, 0, mine_at, :] = wb_here[wide_half(core), :].T
    keep_copy(4).wait()
    pre_copy(4, theirs_at).wait_recv()
    cross(1, 0)
    pre_copy(5, theirs_at).wait_recv()
    cross(2, 0)

    for m, given in enumerate((bo_ref, g1_ref, s1_ref, bb_ref, g2_ref, s2_ref, bi_ref)):
        row_ref[m : m + 1, :] = given[...].astype(f32).reshape(1, -1)
    row_ref[7:8, 0 : 2 * head_cols] = bq_ref[...].astype(f32).reshape(1, -1)
    row_ref[7:8, 2 * head_cols : 4 * head_cols] = bv_ref[...].astype(f32).reshape(1, -1)
    zero_row = jnp.zeros((1, head_cols), f32)
    heads_q = jnp.where(core == 0, row_ref[7:8, 0:head_cols], row_ref[7:8, head_cols : 2 * head_cols])
    heads_v = jnp.where(
        core == 0, row_ref[7:8, 2 * head_cols : 3 * head_cols], row_ref[7:8, 3 * head_cols : 4 * head_cols]
    )
    wide = jnp.where(core == 0, row_ref[6:7, 0:cols], row_ref[6:7, cols : 2 * cols])
    bias[0, 0:1, :] = jnp.concatenate([heads_q, zero_row, heads_v, zero_row, wide], axis=1)
    for k in range(4):
        vec_ref[0:6, k * piece : (k + 1) * piece] = row_ref[0:6, block_at(k)]
    for s in range(1, 4):
        bias_copy(s).start()
    lens[core] = lens_ref[...]
    share_len = remote(lens_ref, lens.at[core], e_s.at[4], e_r.at[4], partner)
    share_len.start()

    line_wait(0, 1)
    line_start(0, 2)
    line_start(1, 1)
    forward_on(0, 0)
    cross(0, 1)
    forward_on(1, 0)
    forward_on(2, 0)
    for s in range(1, 4):
        bias_copy(s).wait_recv()
    remote(lens_ref, lens.at[1 - core], e_s.at[4], e_r.at[4], partner).wait_recv()

    spread_wait(x_ref, xs, xa_r)
    for k in range(4):
        xf[0:own, k * piece : (k + 1) * piece] = xs[:, block_at(k)]
    share_x = exchange(xf.at[0:own], xf.at[own : 2 * own], 0)
    share_x.start()
    share_x.wait_recv()
    save(xf, xf_out)

    index = lax.broadcasted_iota(jnp.int32, (rows, 1), 0)
    length_ref[...] = lens[place // 2]
    length = length_ref[pl.ds(place % 2, 1), 0:1]
    half = jnp.where(index < own, core, 1 - core)
    inside = index % own
    position = (inside // part) * (2 * part) + half * part + inside % part
    key_bias = jnp.where(position.astype(f32) < length, 0.0, NEGATIVE).astype(f32)
    lane = lax.broadcasted_iota(jnp.int32, (1, 2 * HD), 1)
    tile = 512

    def project(n):
        j = turns[n]
        columns = lax.broadcasted_iota(jnp.int32, (1, 3 * head_cols), 1)
        zero = jnp.zeros((1, head_cols), f32)
        add = jnp.concatenate(
            [bias[j, 0:1, 0:head_cols], zero, bias[j, 0:1, 2 * head_cols : 3 * head_cols]], axis=1
        )
        times = jnp.where(columns < head_cols, HD ** (-0.5), 1.0).astype(f32)

        def body(i, _):
            at = pl.ds(pl.multiple_of(i * tile, tile), tile)
            value = nn(xf[at, :], w[0, j, :, 0 : 3 * head_cols])
            qkv[j, at, :] = ((value + add) * times).astype(bf16)
            return 0

        lax.fori_loop(0, rows // tile, body, 0)
        save(qkv.at[j], qkv_out.at[j])

    def attend(n, midway):
        j = turns[n]
        keys = qkv[j, :, head_cols : 2 * head_cols]
        values_t = qkv[j, :, 2 * head_cols : 3 * head_cols].T

        def body(start):
            at = slice(start, start + 512)
            query = qkv[j, at, 0:head_cols]
            parts = []
            for h in range(2):
                query_h = jnp.where(lane // HD == h, query, jnp.zeros_like(query))
                scores = nt(keys, query_h) + key_bias
                largest = jnp.max(scores, axis=0, keepdims=True)
                weights = jnp.exp(scores - largest)
                total = jnp.sum(weights, axis=0, keepdims=True)
                out = nn(values_t[h * HD : (h + 1) * HD], weights.astype(bf16))
                parts.append(out / total)
                lse_ref[2 * j + h, :, at] = largest + jnp.log(total)
            ctx[j, at, :] = jnp.concatenate(parts, axis=0).T.astype(bf16)

        for start in range(0, rows, 512):
            if start:
                midway()
            body(start)
        save(ctx.at[j], ctx_out.at[j])

    def between_1():
        line_wait(0, 3)
        cross(0, 3)
        forward_on(0, 2)

    def between_2():
        line_wait(1, 2)
        line_start(1, 3)

    def between_3():
        line_wait(2, 2)
        line_start(2, 3)

    ready(0, 0)
    project(0)
    line_wait(0, 2)
    line_start(0, 3)
    line_start(2, 1)
    cross(0, 2)
    forward_on(0, 1)
    attend(0, lambda: None)
    line_wait(1, 1)
    line_start(1, 2)
    ready(0, 1)
    project(1)
    attend(1, between_1)
    cross(1, 1)
    line_wait(2, 1)
    line_start(2, 2)
    forward_on(0, 3)
    ready(0, 2)
    project(2)
    attend(2, between_2)
    cross(1, 2)
    forward_on(1, 1)
    ready(0, 3)
    project(3)
    attend(3, between_3)
    line_wait(1, 3)
    cross(1, 3)
    forward_on(1, 2)

    def out_rows(start, target):
        def body(i, _):
            at = pl.ds(pl.multiple_of(start + i * tile, tile), tile)
            to = pl.ds(pl.multiple_of(i * tile, tile), tile)
            total = nt(ctx[0, at, :], w[0, 0, :, 3 * head_cols :])
            for j in range(1, 4):
                total += nt(ctx[j, at, :], w[0, j, :, 3 * head_cols :])
            target[to, :] = total.astype(target.dtype)
            return 0

        lax.fori_loop(0, own // tile, body, 0)

    out_rows(own, other_part)
    share_att = exchange(other_part, att_got, 1)
    share_att.start()
    out_rows(0, own_part)
    cross(2, 1)
    line_wait(2, 3)
    spread_start(c_ref, cot, ca_s, ca_r)
    share_att.wait_recv()
    small = 32

    def mean(value):
        return jnp.sum(value, axis=-1, keepdims=True) * (1.0 / value.shape[-1])

    def first_body(i, _):
        at = pl.ds(pl.multiple_of(i * small, small), small)
        total = xf[at, :].astype(f32) + (own_part[at, :] + att_got[at, :].astype(f32)) + vec_ref[0:1, :]
        centered = total - mean(total)
        inverse = lax.rsqrt(mean(centered * centered) + EPSILON)
        normed = centered * inverse
        n1[at, :] = normed
        inv1_ref[at, :] = inverse
        value = normed * vec_ref[1:2, :] + vec_ref[2:3, :]
        first[at, :] = value
        ff[at, :] = value.astype(bf16)
        return 0

    lax.fori_loop(0, own // small, first_body, 0)
    share_first = exchange(ff.at[0:own], ff.at[own : 2 * own], 2)
    share_first.start()
    save(n1, n1_out)
    share_first.wait_recv()
    save(ff, ff_out)

    def expand(n):
        j = turns[n]
        add = bias[j, 0:1, 4 * head_cols : 4 * head_cols + cols]

        def body(i, _):
            at = pl.ds(pl.multiple_of(i * tile, tile), tile)
            value = nn(ff[at, :], w[1, j]) + add
            active, slope = gelu_and_slope(value)
            hid[j, at, :] = active.astype(bf16)
            dg[j, at, :] = slope.astype(bf16)
            return 0

        lax.fori_loop(0, rows // tile, body, 0)
        save(hid.at[j], hid_out.at[j])
        save(dg.at[j], dg_out.at[j])

    ready(1, 0)
    expand(0)
    cross(2, 2)
    forward_on(1, 3)
    ready(1, 1)
    expand(1)
    ready(1, 2)
    expand(2)
    cross(2, 3)
    forward_on(2, 1)
    ready(1, 3)
    expand(3)
    forward_on(2, 2)
    share_att.wait_send()

    def contract(ns, start, target, source):
        def body(i, _):
            at = pl.ds(pl.multiple_of(start + i * tile, tile), tile)
            to = pl.ds(pl.multiple_of(i * tile, tile), tile)
            total = nt(hid[turns[ns[0]], at, :], w[2, turns[ns[0]]])
            for n in ns[1:]:
                total += nt(hid[turns[n], at, :], w[2, turns[n]])
            if source is not None:
                total += source[to, :]
            target[to, :] = total.astype(target.dtype)
            return 0

        lax.fori_loop(0, own // tile, body, 0)

    ready(2, 0)
    ready(2, 1)
    contract((0, 1), own, other_acc, None)
    contract((0, 1), 0, own_part, None)
    forward_on(2, 3)
    ready(2, 2)
    contract((2,), own, other_acc, other_acc)
    contract((2,), 0, own_part, own_part)
    ready(2, 3)
    contract((3,), own, other_part, other_acc)
    share_mix = exchange(other_part, mix_got, 3)
    share_mix.start()
    contract((3,), 0, own_part, own_part)
    spread_wait(c_ref, cot, ca_r)
    share_mix.wait_recv()
    sums_ref[...] = jnp.zeros_like(sums_ref)

    def second_body(i, _):
        at = pl.ds(pl.multiple_of(i * small, small), small)
        spot = i * small + lax.broadcasted_iota(jnp.int32, (small, 1), 0)
        where = (spot // part) * (2 * part) + core * part + spot % part
        alive = where.astype(f32) < length
        total = first[at, :] + (own_part[at, :] + mix_got[at, :].astype(f32)) + vec_ref[3:4, :]
        centered = total - mean(total)
        inverse = lax.rsqrt(mean(centered * centered) + EPSILON)
        normed = centered * inverse
        value = normed * vec_ref[4:5, :] + vec_ref[5:6, :]
        shown = jnp.where(alive, value, 0.0).astype(bf16)
        for k in range(4):
            lo_ref[at, block_at(k)] = shown[:, k * piece : (k + 1) * piece]
        given = jnp.concatenate([cot[at, block_at(k)] for k in range(4)], axis=1)
        grad = jnp.where(alive, given.astype(f32), 0.0)
        e = grad * vec_ref[4:5, :]
        back = (e - mean(e) - normed * mean(e * normed)) * inverse
        gm_ref[at, :] = back
        for m, value in enumerate((back, grad * normed, grad)):
            eights = value[0:8, :]
            for q in range(8, small, 8):
                eights += value[q : q + 8, :]
            parts_of[m] += eights
        return 0

    parts_of[...] = jnp.zeros_like(parts_of)
    lax.fori_loop(0, own // small, second_body, 0)
    for m in range(3):
        sums_ref[m : m + 1, :] = jnp.sum(parts_of[m], axis=0, keepdims=True)
    for n in range(6):
        pre_copy(n, mine_at).wait_send()
    share_len.wait_send()
    for b in range(3):
        for n in range(1, 4):
            line_do(b, n, lambda copy: copy.wait_send())
        for n in range(4):
            x_copy(b, n).wait_send()
            y_copy(b, n).wait_send()
            fx_copy(b, n).wait_send()
            fy_copy(b, n).wait_send()
    for s in range(1, 4):
        bias_copy(s).wait_send()
    spread_sent(x_ref, xs, xa_s, xa_r)
    spread_sent(c_ref, cot, ca_s, ca_r)
    share_x.wait_send()
    share_first.wait_send()
    share_mix.wait_send()
    for copy in outs:
        copy.wait()


def forward(lens, vectors, inputs, cotangent, w_query, w_key, w_value, w_out, w_in, w_back):
    part, width = inputs.shape[1] // 2, inputs.shape[2]
    own = 4 * part
    rows = 2 * own
    cols = w_in.shape[1] // 2
    head_cols = 2 * HD
    any_ = pl.BlockSpec(memory_space=pltpu.HBM)
    vm = pl.BlockSpec(memory_space=pltpu.VMEM)
    shape = jax.ShapeDtypeStruct
    dma = pltpu.SemaphoreType.DMA
    flops = 2 * rows * width * cols * 12 + 16 * rows * rows * HD * 4
    return pl.pallas_call(
        forward_kernel,
        in_specs=[vm] * 10 + [any_] * 8,
        out_specs=[
            any_, any_, any_, vm, any_, any_, any_, any_, any_, vm, vm, vm, vm, vm, vm
        ],
        out_shape=[
            shape((3, 4, width, cols), bf16),
            shape((rows, width), bf16),
            shape((4, rows, 3 * head_cols), bf16),
            shape((8, 1, rows), f32),
            shape((4, rows, head_cols), bf16),
            shape((rows, width), bf16),
            shape((4, rows, cols), bf16),
            shape((4, rows, cols), bf16),
            shape((own, width), f32),
            shape((own, 1), f32),
            shape((own, width), f32),
            shape((own, width), bf16),
            shape((8, width), f32),
            shape((8, width), f32),
            shape((8, 128), f32),
        ],
        scratch_shapes=[
            pltpu.VMEM((3, 4, width, cols), bf16),
            pltpu.VMEM((own, width), bf16),
            pltpu.VMEM((rows, width), bf16),
            pltpu.VMEM((4, 8, 4 * head_cols + cols), f32),
            pltpu.VMEM((4, rows, 3 * head_cols), bf16),
            pltpu.VMEM((4, rows, head_cols), bf16),
            pltpu.VMEM((rows, width), bf16),
            pltpu.VMEM((4, rows, cols), bf16),
            pltpu.VMEM((4, rows, cols), bf16),
            pltpu.VMEM((own, width), f32),
            pltpu.VMEM((own, width), f32),
            pltpu.VMEM((own, width), f32),
            pltpu.VMEM((own, width), bf16),
            pltpu.VMEM((own, width), f32),
            pltpu.VMEM((own, width), bf16),
            pltpu.VMEM((own, width), bf16),
            pltpu.VMEM((own, width), bf16),
            pltpu.VMEM(w_out.shape, bf16),
            pltpu.VMEM(w_back.shape, bf16),
            pltpu.VMEM((w_out.shape[1], head_cols), bf16),
            pltpu.VMEM((w_back.shape[1], cols), bf16),
            pltpu.VMEM((2, 8, 128), f32),
            pltpu.VMEM((3, 8, width), f32),
            pltpu.VMEM((8, width), f32),
            dma((3, 3)), dma((3, 3)), dma((3, 3)), dma((3, 3)),
            dma((3, 4)), dma((3, 4)), dma((3, 4)), dma((3, 4)),
            dma((3, 4, 2)), dma((3, 4, 2)), dma((6,)), dma((6,)), dma((6,)), dma((4,)), dma((4,)),
            dma((4,)), dma((4,)), dma((4,)), dma((4,)),
            dma((5,)), dma((5,)), dma((32,)),
        ],
        compiler_params=pltpu.CompilerParams(
            collective_id=0, has_side_effects=True, vmem_limit_bytes=60 << 20
        ),
        cost_estimate=pl.CostEstimate(
            flops=flops, bytes_accessed=60 << 20, transcendentals=8 * rows * rows
        ),
        name="forward_layer",
    )(lens, *vectors, inputs, cotangent, w_query, w_key, w_value, w_out, w_in, w_back)


def backward_kernel(
    w_ref, xf_ref, qkv_ref, lse_ref, ctx_ref, ff_ref, hid_ref, dg_ref, n1_ref, inv1_ref, gm_ref,
    vec_ref, sums_ref, length_ref, lo_own,
    lo_ref, gi_ref, gq_ref, gk_ref, gv_ref, go_ref, gw_ref, gb_ref, total_ref,
    w, grad_c, pad, pre, gmf, act, turned, gm, n1, own_part, other, got,
    d_got, rx, ry, rz, home, dk_acc, dv_acc, vz, zg, xg, yg, cg, tot,
    d_s, d_r, x_s, x_r, y_s, y_r, z_s, z_r, h_s, h_r, h_l, e_s, e_r, g_s, g_r, v_s, v_r, l_s,
    lo_s, lo_r,
):
    plane = lax.axis_index("plane")
    core = lax.axis_index("core")
    place = lax.axis_index("tensor")
    partner = {"core": 1 - core}
    x_side = {"plane": plane + 1 - 2 * (plane % 2)}
    y_side = {"plane": (plane + 2) % 4}
    early, late = (place + 3) // 2, 3 - 2 * (place // 2)
    turns = (early, 6 - early - late, late, 0)
    edge = (3 - place) // 3 + place // 3
    rows, width = gmf.shape
    own = rows // 2
    part = own // 4
    piece = width // 4
    head_cols = 2 * HD
    tile = 512
    small = 32
    gi_own = gmf
    gaf = gmf

    def remote(source, target, send, recv, to):
        return pltpu.make_async_remote_copy(
            source, target, send, recv, device_id=to, device_id_type=MESH
        )

    half_piece = piece // 2

    def block(b, j, k, h=None):
        at = slice(k * piece, (k + 1) * piece)
        if h is not None:
            at = slice(k * piece + h * half_piece, k * piece + (h + 1) * half_piece)
        if b == 2:
            return grad_c.at[j, at]
        return w.at[b + 1, j, at]

    def rows_of(h):
        return slice(h * half_piece, (h + 1) * half_piece)

    def d_copy(b, n, h):
        return remote(
            block(b, turns[n], 3, h), d_got.at[b % 2, n, rows_of(h)], d_s.at[b, n, h], d_r.at[b, n, h],
            (x_side, y_side)[h],
        )

    def x_copy(b, n, h):
        return remote(
            block(b, turns[n], 1, h), rx.at[b, n, rows_of(h)], x_s.at[b, n, h], x_r.at[b, n, h], x_side
        )

    def y_copy(b, n, h):
        return remote(
            block(b, turns[n], 2, h), ry.at[b, n, rows_of(h)], y_s.at[b, n, h], y_r.at[b, n, h], y_side
        )

    def z_copy(b, n):
        step = 1 - 2 * ((place % 2) if n == 1 else (place // 2))
        end = 3 + (1 - step) // 2
        outer, inner = ((0, 1), (2, end), (end, end))[n]
        slot = edge * outer + (1 - edge) * inner
        return remote(
            block(b, turns[n], 0), rz.at[b, slot], z_s.at[b, n], z_r.at[b, slot],
            {"tensor": (place + step + 4) % 4},
        )

    def z_got(b, slot):
        return remote(
            block(b, 0, 0), rz.at[b, slot], z_s.at[b, 0], z_r.at[b, slot],
            {"tensor": (place + 1) % 4},
        )

    cols = w.shape[3]
    mine_at = pl.ds(core * half_piece, half_piece)
    theirs_at = pl.ds((1 - core) * half_piece, half_piece)

    def home_parts(n, which):
        at = pl.ds(which * half_piece, half_piece)
        turned_at = pl.ds(pl.multiple_of(piece + which * half_piece, half_piece), half_piece)
        heads = pl.ds(pl.multiple_of(core * head_cols, head_cols), head_cols)
        wide = pl.ds(pl.multiple_of(core * cols, cols), cols)
        if n < 3:
            return home.at[0, at, n * head_cols : (n + 1) * head_cols], (gq_ref, gk_ref, gv_ref)[n].at[:, heads]
        if n == 3:
            return n1.at[0:head_cols, turned_at], go_ref.at[heads]
        if n == 4:
            return home.at[1, at], gw_ref.at[:, wide]
        return n1.at[0:cols, at], gb_ref.at[wide]

    def home_copy(n):
        source, target = home_parts(n, 1 - core)
        return remote(source, target, h_s.at[n], h_r.at[n], partner)

    def home_keep(n):
        source, target = home_parts(n, core)
        return pltpu.make_async_copy(source, target, h_l.at[n])

    def send_first(b, n):
        for h in range(2):
            d_copy(b, n, h).start()
        x_copy(b, n, 0).start()
        y_copy(b, n, 1).start()

    def send_second(b, n):
        for h, k in ((0, 2), (1, 1)):
            d_copy(b, n, h).wait_recv()
            here = block(b, turns[n], k, h)
            arrived = d_got[b % 2, n, rows_of(h)]
            here[...] = (here[...].astype(f32) + arrived.astype(f32)).astype(bf16)
        y_copy(b, n, 0).start()
        x_copy(b, n, 1).start()

    def add_slot(b, slot, cond):
        @pl.when(cond)
        def _():
            z_got(b, slot).wait_recv()
            home[b] = home[b] + rz[b, slot].astype(f32)

    def gather_piece(b, n):
        for h in range(2):
            x_copy(b, n, h).wait_recv()
            y_copy(b, n, h).wait_recv()
        here = block(b, turns[n], 0)
        home[b] = here[...].astype(f32) + rx[b, n].astype(f32) + ry[b, n].astype(f32)

    def pass_piece(b, n):
        block(b, turns[n], 0)[...] = home[b].astype(bf16)
        z_copy(b, n).start()

    def stage(b, k):
        if k < 3:
            @pl.when(edge == 1)
            def _():
                gather_piece(b, k)
                pass_piece(b, k)

        if 1 <= k <= 3:
            @pl.when(edge == 0)
            def _():
                gather_piece(b, k - 1)
                z_got(b, k - 1).wait_recv()
                home[b] = home[b] + rz[b, k - 1].astype(f32)
                pass_piece(b, k - 1)

        if k == 4:
            gather_piece(b, 3)
            add_slot(b, 3, place >= 1)
            add_slot(b, 4, place <= 2)
            if b == 0:
                n1[0:head_cols, piece : 2 * piece] = home[b, :, 3 * head_cols : 4 * head_cols].T
            if b == 2:
                n1[0:cols, 0:piece] = home[b].T
            for m in ((0, 1, 2, 3), (4,), (5,))[b]:
                home_copy(m).start()
                home_keep(m).start()

    def exchange(source, target, n):
        return remote(source, target, e_s.at[n], e_r.at[n], partner)

    def back_parts(source, target, s):
        at = pl.ds(core * part, part)
        return source.at[s * part : (s + 1) * part], target.at[place % 2, at]

    def back(source, target, send, recv, s):
        here, there = back_parts(source, target, s)
        to = {"core": place // 2, "tensor": s}
        return remote(here, there, send.at[s], recv.at[2 * (place % 2) + core], to)

    def back_local(source, target, recv, s):
        here, there = back_parts(source, target, s)
        return pltpu.make_async_copy(here, there, recv.at[2 * (place % 2) + core])

    def is_home(s):
        return jnp.logical_and(core == place // 2, place == s)

    def back_start(source, target, send, recv):
        for s in range(4):
            @pl.when(is_home(s))
            def _():
                back_local(source, target, recv, s).start()

            @pl.when(jnp.logical_not(is_home(s)))
            def _():
                back(source, target, send, recv, s).start()

    def back_end(source, target, send, recv):
        for s in range(4):
            @pl.when(jnp.logical_not(is_home(s)))
            def _():
                back(source, target, send, recv, s).wait_send()
        for s in range(4):
            pltpu.make_async_copy(
                source.at[0:part], target.at[s // 2, pl.ds((s % 2) * part, part)], recv.at[s]
            ).wait()

    def v_copy(j):
        to = {"tensor": (place + 4 - j) % 4}
        return remote(vz.at[j], zg.at[place], v_s.at[j - 1], v_r.at[place], to)

    def v_got(j):
        source = (place + j) % 4
        to = {"tensor": (place + 1) % 4}
        return remote(vz.at[j], zg.at[source], v_s.at[j - 1], v_r.at[source], to)

    coming = {}

    def fetch(name, source, target):
        copy = pltpu.make_async_copy(source, target, l_s.at[len(coming)])
        copy.start()
        coming[name] = copy

    fetch("gm", gm_ref, gm)
    for n in range(4):
        fetch(("hid", n), hid_ref.at[turns[n]], pad.at[turns[n]])
    for j in range(4):
        fetch(("w2", j), w_ref.at[2, j], w.at[2, j])
        fetch(("dg", j), dg_ref.at[j], pre.at[j])
    fetch("w1", w_ref.at[1], w.at[1])
    fetch("n1", n1_ref, n1)
    fetch("ff", ff_ref, act)
    fetch("w0", w_ref.at[0], w.at[0])

    barrier = pltpu.get_barrier_semaphore()
    friends = [x_side, y_side, partner]
    for s in range(1, 4):
        friends.append({"tensor": (place + s) % 4})
        friends.append({"tensor": (place + s) % 4, "core": 1 - core})
    for friend in friends:
        pl.semaphore_signal(barrier, inc=1, device_id=friend, device_id_type=MESH)

    coming["gm"].wait()

    def round_body(i, _):
        at = pl.ds(pl.multiple_of(i * 128, 128), 128)
        gmf[at, :] = gm[at, :].astype(bf16)
        return 0

    lax.fori_loop(0, own // 128, round_body, 0)
    pl.semaphore_wait(barrier, len(friends))
    share_gm = exchange(gmf.at[0:own], gmf.at[own : 2 * own], 0)
    share_gm.start()
    back_start(lo_own, lo_ref, lo_s, lo_r)
    vz[...] = jnp.zeros_like(vz)

    def turn(source, first, last):
        def body(i, _):
            at = pl.ds(pl.multiple_of(i * tile, tile), tile)
            turned[:, at] = source[at, :].T
            return 0

        lax.fori_loop(first, last, body, 0)

    def weight_grad(b, n, source, columns):
        j = turns[n]

        def body(k, _):
            at = pl.ds(pl.multiple_of(k * tile, tile), tile)
            value = nn(turned[at, :], source[j, :, columns]).astype(bf16)
            if b == 2:
                grad_c[j, at, columns] = value
            else:
                w[b + 1, j, at, columns] = value
            return 0

        lax.fori_loop(0, width // tile, body, 0)

    every = slice(None)
    turn(gmf, 0, own // tile)
    share_gm.wait_recv()
    turn(gmf, own // tile, rows // tile)
    for n in range(4):
        coming[("hid", n)].wait()
        weight_grad(2, n, pad, every)
        send_first(2, n)

    def slope_rows(j):
        coming[("w2", j)].wait()
        coming[("dg", j)].wait()

        def body(i, _):
            at = pl.ds(pl.multiple_of(i * tile, tile), tile)
            value = (nn(gmf[at, :], w[2, j]) * pre[j, at, :].astype(f32)).astype(bf16)
            pre[j, at, :] = value
            vz[j, 8:9, 2 * head_cols : 2 * head_cols + value.shape[1]] += jnp.sum(
                value.astype(f32), axis=0, keepdims=True
            )
            return 0

        lax.fori_loop(0, rows // tile, body, 0)

    slope_rows(0)
    slope_rows(1)
    send_second(2, 0)
    slope_rows(2)
    send_second(2, 1)
    slope_rows(3)
    for j in range(4):
        fetch(("ctx", j), ctx_ref.at[j], pad.at[j, :, pl.ds(3 * head_cols, head_cols)])
    coming["w1"].wait()

    def first_rows(start, target):
        def body(i, _):
            at = pl.ds(pl.multiple_of(start + i * tile, tile), tile)
            to = pl.ds(pl.multiple_of(i * tile, tile), tile)
            total = nt(pre[0, at, :], w[1, 0])
            for j in range(1, 4):
                total += nt(pre[j, at, :], w[1, j])
            target[to, :] = total.astype(target.dtype)
            return 0

        lax.fori_loop(0, own // tile, body, 0)

    first_rows(own, other)
    share_first = exchange(other, got, 1)
    share_first.start()
    send_second(2, 2)
    first_rows(0, own_part)
    coming["n1"].wait()
    share_first.wait_recv()

    def mean(value):
        return jnp.sum(value, axis=-1, keepdims=True) * (1.0 / value.shape[-1])

    share_gm.wait_send()

    def norm_body(i, _):
        at = pl.ds(pl.multiple_of(i * small, small), small)
        grad = gm[at, :] + (own_part[at, :] + got[at, :].astype(f32))
        normed = n1[at, :]
        e = grad * vec_ref[1:2, :]
        value = (e - mean(e) - normed * mean(e * normed)) * inv1_ref[at, :]
        gm[at, :] = value
        gaf[at, :] = value.astype(bf16)
        vz[0, 0:1, :] += jnp.sum(value, axis=0, keepdims=True)
        vz[0, 1:2, :] += jnp.sum(grad * normed, axis=0, keepdims=True)
        vz[0, 2:3, :] += jnp.sum(grad, axis=0, keepdims=True)
        return 0

    lax.fori_loop(0, own // small, norm_body, 0)
    share_att = exchange(gaf.at[0:own], gaf.at[own : 2 * own], 2)
    share_att.start()
    send_second(2, 3)
    vz[0, 3:6, :] = sums_ref[0:3, :]
    for j in range(1, 4):
        vz[j, 0:8, :] = vz[0, 0:8, :]
    coming["ff"].wait()
    turn(act, 0, rows // tile)
    fetch("xf", xf_ref, act)
    for n in range(4):
        weight_grad(1, n, pre, every)
        send_first(1, n)
    for j in range(4):
        fetch(("qkv", j), qkv_ref.at[j], pre.at[j, :, pl.ds(0, 3 * head_cols)])
    stage(2, 0)
    share_att.wait_recv()
    turn(gaf, 0, rows // tile)
    coming["w0"].wait()
    last = slice(3 * head_cols, 4 * head_cols)

    def context_rows(j):
        def body(i, _):
            at = pl.ds(pl.multiple_of(i * tile, tile), tile)
            pre[j, at, last] = nn(gaf[at, :], w[0, j, :, last]).astype(bf16)
            return 0

        lax.fori_loop(0, rows // tile, body, 0)

    for j in range(4):
        context_rows(j)
        coming[("ctx", j)].wait()
    stage(2, 1)
    weight_grad(0, 0, pad, last)
    weight_grad(0, 1, pad, last)
    weight_grad(0, 2, pad, last)
    weight_grad(0, 3, pad, last)
    coming["xf"].wait()
    turn(act, 0, rows // tile)
    for j in range(4):
        coming[("qkv", j)].wait()

    index = lax.broadcasted_iota(jnp.int32, (rows, 1), 0)
    half = jnp.where(index < own, core, 1 - core)
    inside = index % own
    position = (inside // part) * (2 * part) + half * part + inside % part
    length = length_ref[pl.ds(place % 2, 1), 0:1]
    key_bias = jnp.where(position.astype(f32) < length, 0.0, NEGATIVE).astype(f32)
    lane = lax.broadcasted_iota(jnp.int32, (1, head_cols), 1)
    front = slice(0, 3 * head_cols)

    def attend_back(n, midway):
        j = turns[n]
        keys = pre[j, :, head_cols : 2 * head_cols]
        keys_t = keys.T
        values = pre[j, :, 2 * head_cols : 3 * head_cols]
        dk_acc[...] = jnp.zeros_like(dk_acc)
        dv_acc[...] = jnp.zeros_like(dv_acc)

        def body(start):
            at = slice(start, start + 512)
            query = pre[j, at, 0:head_cols]
            grad = pre[j, at, last]
            parts = []
            for h in range(2):
                here = lane // HD == h
                query_h = jnp.where(here, query, jnp.zeros_like(query))
                grad_h = jnp.where(here, grad, jnp.zeros_like(grad))
                scores = nt(keys, query_h) + key_bias
                chances = jnp.exp(scores - lse_ref[2 * j + h, :, at])
                grad_chances = nt(values, grad_h)
                inner = jnp.sum(chances * grad_chances, axis=0, keepdims=True)
                grad_scores = (chances * (grad_chances - inner)).astype(bf16)
                dv_acc[...] += nn(chances.astype(bf16), grad_h)
                dk_acc[...] += nn(grad_scores, query_h)
                parts.append(nn(keys_t[h * HD : (h + 1) * HD], grad_scores))
            low = jnp.concatenate(parts, axis=0).T.astype(bf16).astype(f32) * HD ** (-0.5)
            pad[j, at, 0:head_cols] = low.astype(bf16)
            vz[j, 8:9, 0:head_cols] += jnp.sum(low, axis=0, keepdims=True)

        for start in range(0, rows, 512):
            if start:
                midway()
            body(start)
        pad[j, :, head_cols : 2 * head_cols] = dk_acc[...].astype(bf16)
        low = dv_acc[...].astype(bf16)
        pad[j, :, 2 * head_cols : 3 * head_cols] = low
        vz[j, 8:9, head_cols : 2 * head_cols] = jnp.sum(low.astype(f32), axis=0, keepdims=True)

    def after_0():
        send_second(1, 0)
        stage(2, 2)

    def after_1():
        send_second(1, 1)
        send_second(1, 2)
        send_first(0, 0)
        send_first(0, 1)
        stage(2, 3)

    def after_2():
        send_second(1, 3)
        send_first(0, 2)
        stage(2, 4)

    between = (lambda: None, lambda: None, lambda: None, lambda: stage(1, 0))
    after = (after_0, after_1, after_2, lambda: send_first(0, 3))
    for n in range(4):
        attend_back(n, between[n])
        weight_grad(0, n, pad, front)
        after[n]()
    for j in range(1, 4):
        v_copy(j).start()
    zg[place] = vz[0]

    def input_rows(start, target):
        def body(i, _):
            at = pl.ds(pl.multiple_of(start + i * tile, tile), tile)
            to = pl.ds(pl.multiple_of(i * tile, tile), tile)
            total = nt(pad[0, at, front], w[0, 0, :, front])
            for j in range(1, 4):
                total += nt(pad[j, at, front], w[0, j, :, front])
            target[to, :] = total.astype(target.dtype)
            return 0

        lax.fori_loop(0, own // tile, body, 0)

    share_att.wait_send()
    share_first.wait_send()
    input_rows(own, other)
    share_in = exchange(other, got, 3)
    share_in.start()
    input_rows(0, own_part)
    send_second(0, 0)
    stage(1, 1)
    share_in.wait_recv()

    def input_body(i, _):
        at = pl.ds(pl.multiple_of(i * small, small), small)
        value = gm[at, :] + (own_part[at, :] + got[at, :].astype(f32))
        low = value.astype(bf16)
        for k in range(4):
            number = (plane, plane + 1 - 2 * (plane % 2), (plane + 2) % 4, 3 - plane)[k]
            to = pl.ds(pl.multiple_of(number * piece, piece), piece)
            gi_own[at, to] = low[:, k * piece : (k + 1) * piece]
        return 0

    lax.fori_loop(0, own // small, input_body, 0)
    back_start(gi_own, gi_ref, g_s, g_r)

    def fold(n, m, arrived, flip):
        for k in range(4):
            here = slice(k * piece, (k + 1) * piece)
            there = slice((k ^ flip) * piece, ((k ^ flip) + 1) * piece)
            tot[n, 0:8, here] = tot[m, 0:8, here] + arrived[0:8, there]
        tot[n, 8:16, :] = tot[m, 8:16, :] + arrived[8:16, :]

    for j in range(1, 4):
        v_got(j).wait_recv()
    tot[0] = ((zg[0] + zg[1]) + zg[2]) + zg[3]
    v_x = remote(tot.at[0], xg, e_s.at[4], e_r.at[4], x_side)
    v_x.start()
    send_second(0, 1)
    v_x.wait_recv()
    fold(1, 0, xg, 1)
    v_y = remote(tot.at[1], yg, e_s.at[5], e_r.at[5], y_side)
    v_y.start()
    stage(1, 2)
    send_second(0, 2)
    v_y.wait_recv()
    fold(2, 1, yg, 2)
    v_c = exchange(tot.at[2], cg, 6)
    v_c.start()
    send_second(0, 3)
    stage(1, 3)
    stage(0, 0)
    stage(0, 1)
    stage(1, 4)
    stage(0, 2)
    stage(0, 3)
    stage(0, 4)
    v_c.wait_recv()
    for k in range(4):
        number = (plane, plane + 1 - 2 * (plane % 2), (plane + 2) % 4, 3 - plane)[k]
        to = pl.ds(pl.multiple_of(number * piece, piece), piece)
        here = slice(k * piece, (k + 1) * piece)
        total_ref[0:8, to] = tot[2, 0:8, here] + cg[0:8, here]
    own_row = tot[2, 8:9, :]
    their_row = cg[8:9, :]
    total_ref[8:9, :] = jnp.where(core == 0, own_row, their_row)
    total_ref[9:10, :] = jnp.where(core == 0, their_row, own_row)

    for b in range(3):
        for n in range(4):
            for h in range(2):
                d_copy(b, n, h).wait_send()
                x_copy(b, n, h).wait_send()
                y_copy(b, n, h).wait_send()
            if n < 3:
                z_copy(b, n).wait_send()
    for n in range(6):
        home_keep(n).wait()
        home_copy(n).wait_send()
        home_copy(n).wait_recv()
    for j in range(1, 4):
        v_copy(j).wait_send()
    for copy in (share_in, v_x, v_y, v_c):
        copy.wait_send()
    back_end(lo_own, lo_ref, lo_s, lo_r)
    back_end(gi_own, gi_ref, g_s, g_r)


def backward(w_all, xf, qkv, lse, ctx, ff, hid, dg, n1, inv1, gm, vec, sums, length, lo):
    rows, width = xf.shape
    own = rows // 2
    part = own // 4
    piece = width // 4
    cols = hid.shape[2]
    head_cols = 2 * HD
    any_ = pl.BlockSpec(memory_space=pltpu.HBM)
    vm = pl.BlockSpec(memory_space=pltpu.VMEM)
    shape = jax.ShapeDtypeStruct
    dma = pltpu.SemaphoreType.DMA
    flops = 2 * rows * width * cols * 24 + 40 * rows * rows * HD * 4
    return pl.pallas_call(
        backward_kernel,
        in_specs=[
            any_, any_, any_, vm, any_, any_, any_, any_, any_, vm, any_, vm, vm, vm, any_
        ],
        out_specs=[any_] * 8 + [vm],
        out_shape=[
            shape((2, 2 * part, width), bf16),
            shape((2, 2 * part, width), bf16),
            shape((piece // 2, 2 * head_cols), f32),
            shape((piece // 2, 2 * head_cols), f32),
            shape((piece // 2, 2 * head_cols), f32),
            shape((2 * head_cols, piece // 2), f32),
            shape((piece // 2, 2 * cols), f32),
            shape((2 * cols, piece // 2), f32),
            shape((16, width), f32),
        ],
        scratch_shapes=[
            pltpu.VMEM((3, 4, width, cols), bf16),
            pltpu.VMEM((4, width, cols), bf16),
            pltpu.VMEM((4, rows, cols), bf16),
            pltpu.VMEM((4, rows, cols), bf16),
            pltpu.VMEM((rows, width), bf16),
            pltpu.VMEM((rows, width), bf16),
            pltpu.VMEM((width, rows), bf16),
            pltpu.VMEM((own, width), f32),
            pltpu.VMEM((own, width), f32),
            pltpu.VMEM((own, width), f32),
            pltpu.VMEM((own, width), bf16),
            pltpu.VMEM((own, width), bf16),
            pltpu.VMEM((2, 4, piece, cols), bf16),
            pltpu.VMEM((3, 4, piece, cols), bf16),
            pltpu.VMEM((3, 4, piece, cols), bf16),
            pltpu.VMEM((3, 5, piece, cols), bf16),
            pltpu.VMEM((3, piece, cols), f32),
            pltpu.VMEM((rows, head_cols), f32),
            pltpu.VMEM((rows, head_cols), f32),
            pltpu.VMEM((4, 16, width), f32),
            pltpu.VMEM((4, 16, width), f32),
            pltpu.VMEM((16, width), f32),
            pltpu.VMEM((16, width), f32),
            pltpu.VMEM((16, width), f32),
            pltpu.VMEM((3, 16, width), f32),
            dma((3, 4, 2)), dma((3, 4, 2)), dma((3, 4, 2)), dma((3, 4, 2)), dma((3, 4, 2)), dma((3, 4, 2)),
            dma((3, 3)), dma((3, 5)), dma((6,)), dma((6,)), dma((6,)), dma((8,)), dma((8,)),
            dma((4,)), dma((4,)), dma((3,)), dma((4,)), dma((32,)),
            dma((4,)), dma((4,)),
        ],
        compiler_params=pltpu.CompilerParams(
            collective_id=1, has_side_effects=True, vmem_limit_bytes=60 << 20
        ),
        cost_estimate=pl.CostEstimate(
            flops=flops, bytes_accessed=60 << 20, transcendentals=8 * rows * rows
        ),
        name="backward_layer",
    )(w_all, xf, qkv, lse, ctx, ff, hid, dg, n1, inv1, gm, vec, sums, length, lo)


def swap_cores(value):
    return lax.ppermute(value, "core", SWAP)


def on_device(
    inputs,
    lengths,
    w_query,
    w_key,
    w_value,
    b_query,
    b_value,
    w_out,
    b_out,
    gain_one,
    shift_one,
    w_in,
    b_in,
    w_back,
    b_back,
    gain_two,
    shift_two,
    cotangent,
):
    planes = lax.axis_size("plane")
    n_t = lax.axis_size("tensor")
    plane = lax.axis_index("plane")
    core = lax.axis_index("core")
    place = lax.axis_index("tensor")
    seqs, slots_here, width = inputs.shape
    slots = slots_here * n_t
    half_slots = slots_here // 2
    own = slots // 2
    assert seqs * 2 == n_t
    head_cols = w_query.shape[1] // 2
    ff_cols = w_in.shape[1] // 2
    scale = HD ** (-0.5)
    quad = planes == 4
    if quad:
        vectors = [
            value
            for value in (
                b_out, gain_one, shift_one, b_back, gain_two, shift_two, b_in, b_query, b_value
            )
        ]
        lens = jnp.broadcast_to(
            jnp.concatenate([lengths.astype(f32)] * (8 // seqs))[:, None], (8, 128)
        )
        (w_all, x_full, qkv4, lse8, ctx4, first_full, hid4, dg4, normed_one, inverse_one,
         grad_mixed, lo, second_sums, vec, length_rows) = forward(
            lens, vectors, inputs, cotangent, w_query, w_key, w_value, w_out, w_in, w_back
        )
        (layer_out, gi, grad_w_query, grad_w_key, grad_w_value, grad_w_out, grad_w_in,
         grad_w_back, totals) = backward(
            w_all, x_full, qkv4, lse8, ctx4, first_full, hid4, dg4, normed_one, inverse_one,
            grad_mixed, vec, second_sums, length_rows, lo,
        )
        n_bias = 2 * head_cols + ff_cols
        biases_out = totals[8:10, :n_bias]
        return (
            layer_out,
            gi.astype(f32),
            grad_w_query,
            grad_w_key,
            grad_w_value,
            biases_out[:, :head_cols].reshape(-1),
            biases_out[:, head_cols : 2 * head_cols].reshape(-1),
            grad_w_out,
            totals[0],
            totals[1],
            totals[2],
            grad_w_in,
            biases_out[:, 2 * head_cols :].reshape(-1),
            grad_w_back,
            totals[3],
            totals[4],
            totals[5],
        )

    ring = [(i, (i + 1) % n_t) for i in range(n_t)]
    x_pairs = [(i, i ^ 1) for i in range(planes)]
    y_pairs = [(i, i ^ 2) for i in range(planes)]

    def reorder(value, axis):
        if not quad:
            return value
        size = value.shape[axis] // 4
        return jnp.concatenate(
            [lax.dynamic_slice_in_dim(value, (plane ^ k) * size, size, axis) for k in range(4)],
            axis=axis,
        )

    def by_core(mine, theirs, axis=0):
        first = jnp.where(core == 0, mine, theirs)
        second = jnp.where(core == 0, theirs, mine)
        return jnp.concatenate([first, second], axis=axis)

    def to_chip(rows_here):
        value = reorder(rows_here, 2).reshape(seqs, 2, half_slots, width)
        mine = lax.dynamic_index_in_dim(value, core, 1, keepdims=False)
        other = lax.dynamic_index_in_dim(value, 1 - core, 1, keepdims=False)
        both = by_core(mine, swap_cores(other))
        return lax.all_to_all(both, "tensor", 0, 0, tiled=True).reshape(own, width)

    def from_chip(rows_own):
        value = rows_own.reshape(n_t, half_slots, width)
        value = lax.all_to_all(value, "tensor", 0, 0, tiled=True)
        value = value.reshape(2, seqs, half_slots, width)
        mine = lax.dynamic_index_in_dim(value, core, 0, keepdims=False)
        other = lax.dynamic_index_in_dim(value, 1 - core, 0, keepdims=False)
        got = swap_cores(other)
        value = jnp.stack(
            [jnp.where(core == 0, mine, got), jnp.where(core == 0, got, mine)], axis=1
        )
        return reorder(value.reshape(seqs, slots_here, width), 2)

    their_lengths = swap_cores(lengths)
    all_lengths = by_core(lengths, their_lengths)
    length = lax.dynamic_index_in_dim(all_lengths, place, 0, keepdims=False)
    index = jnp.arange(slots)
    position = (
        (index % own) // half_slots * slots_here
        + ((index // own) ^ core) * half_slots
        + index % half_slots
    )
    valid = position < length
    key_bias = jnp.where(valid, 0.0, NEGATIVE).astype(f32)[:, None]
    own_valid = valid[:own, None]

    def halves(value, cols):
        return (
            lax.dynamic_slice_in_dim(value, core * cols, cols, 1),
            lax.dynamic_slice_in_dim(value, (1 - core) * cols, cols, 1),
        )

    pieces = [
        halves(w_query, head_cols),
        halves(w_key, head_cols),
        halves(w_value, head_cols),
        halves(w_out.T, head_cols),
        halves(w_in, ff_cols),
        halves(w_back.T, ff_cols),
    ]
    keep = jnp.concatenate([piece[0] for piece in pieces], axis=1)
    give = jnp.concatenate([piece[1] for piece in pieces], axis=1)
    cuts = (4 * head_cols, 4 * head_cols + ff_cols)

    def flat(gathered):
        return jnp.concatenate([gathered[j] for j in range(n_t)], axis=1)

    out_bias = reorder(b_out, 0).astype(f32)
    back_bias = reorder(b_back, 0).astype(f32)
    gain_first = reorder(gain_one, 0).astype(f32)
    shift_first = reorder(shift_one, 0).astype(f32)
    gain_second = reorder(gain_two, 0).astype(f32)
    shift_second = reorder(shift_two, 0).astype(f32)
    bias_row = jnp.concatenate(
        [
            lax.dynamic_slice_in_dim(b_query, core * head_cols, head_cols),
            lax.dynamic_slice_in_dim(b_value, core * head_cols, head_cols),
            lax.dynamic_slice_in_dim(b_in, core * ff_cols, ff_cols),
        ]
    )[None]
    qkv_scale = jnp.tile(
        jnp.concatenate([jnp.full((head_cols,), scale, f32), jnp.ones((2 * head_cols,), f32)]), n_t
    )[None]
    def both_rows(value):
        return jnp.concatenate([value, swap_cores(value)], axis=0)

    def own_sum(partial):
        return partial[:own] + swap_cores(partial[own:])

    def normalize(value):
        average = jnp.mean(value, axis=-1, keepdims=True)
        centered = value - average
        variance = jnp.mean(centered * centered, axis=-1, keepdims=True)
        inverse = lax.rsqrt(variance + EPSILON)
        return centered * inverse, inverse

    def normalize_back(grad, gain, normed, inverse):
        e = grad * gain
        return (
            e
            - jnp.mean(e, axis=-1, keepdims=True)
            - normed * jnp.mean(e * normed, axis=-1, keepdims=True)
        ) * inverse

    packed = by_core(keep, swap_cores(give))
    bundle_a = packed[:, : cuts[0]]
    bundle_b = packed[:, cuts[0] : cuts[1]]
    bundle_c = packed[:, cuts[1] :]
    def gather_z(own_piece):
        got = [own_piece]
        for _ in range(n_t - 1):
            got.append(lax.ppermute(got[-1], "tensor", ring))
        return jnp.stack(got)

    def gather_planes(mine):
        if not quad:
            return lax.all_gather(mine, "plane", axis=1, tiled=True)
        half = n_t // 2
        from_x = lax.ppermute(mine, "plane", x_pairs)
        from_y = lax.ppermute(mine, "plane", y_pairs)
        low = lax.ppermute(from_y[:half], "plane", x_pairs)
        high = lax.ppermute(from_x[half:], "plane", y_pairs)
        return jnp.concatenate([mine, from_x, from_y, jnp.concatenate([low, high])], axis=1)

    biases = gather_z(bias_row)[:, 0].astype(f32)
    z_a = gather_z(bundle_a)
    full_a = gather_planes(z_a)
    w_qkv = flat(full_a[:, :, : 3 * head_cols])
    w_o = flat(full_a[:, :, 3 * head_cols :])
    w_1 = flat(gather_planes(gather_z(bundle_b)))
    w_2 = flat(gather_planes(gather_z(bundle_c)))

    zeros_k = jnp.zeros((n_t, head_cols), f32)
    qkv_bias = jnp.concatenate(
        [biases[:, :head_cols], zeros_k, biases[:, head_cols : 2 * head_cols]], axis=1
    ).reshape(1, -1)
    in_bias = biases[:, 2 * head_cols :].reshape(1, -1)

    own_x = to_chip(inputs)
    x_full = both_rows(own_x)
    qkv = ((nn(x_full, w_qkv) + qkv_bias) * qkv_scale).astype(bf16)
    context, lse = attend_fwd(qkv, key_bias)
    attended = own_sum(nt(context, w_o))
    normed_one, inverse_one = normalize(own_x.astype(f32) + attended + out_bias)
    first_norm = normed_one * gain_first + shift_first
    first_full = both_rows(first_norm.astype(bf16))
    pre_act = nn(first_full, w_1) + in_bias
    activated, slope = gelu_and_slope(pre_act)
    hidden = activated.astype(bf16)
    mixed = own_sum(nt(hidden, w_2))
    normed_two, inverse_two = normalize(first_norm + mixed + back_bias)
    second = normed_two * gain_second + shift_second
    layer_out = from_chip(jnp.where(own_valid, second, 0.0).astype(bf16))

    grad_second = jnp.where(own_valid, to_chip(cotangent).astype(f32), 0.0)
    grad_mixed = normalize_back(grad_second, gain_second, normed_two, inverse_two)

    grad_mixed_full = both_rows(grad_mixed.astype(bf16))
    grad_w2 = tn(grad_mixed_full, hidden)
    grad_pre_low = (nn(grad_mixed_full, w_2) * slope.astype(f32)).astype(bf16)
    grad_w1 = tn(first_full, grad_pre_low)
    grad_first = grad_mixed + own_sum(nt(grad_pre_low, w_1))
    grad_att = normalize_back(grad_first, gain_first, normed_one, inverse_one)
    grad_att_full = both_rows(grad_att.astype(bf16))
    grad_context = nn(grad_att_full, w_o).astype(bf16)
    grad_wo = tn(grad_att_full, context)
    grad_qkv = attend_bwd(qkv, grad_context, lse, key_bias)
    grad_qkv = grad_qkv * qkv_scale.astype(bf16)
    grad_wqkv = tn(x_full, grad_qkv)
    grad_rows = grad_att + own_sum(nt(grad_qkv, w_qkv))
    grad_inputs = from_chip(grad_rows.astype(bf16)).astype(f32)

    def scatter(grad):
        cols = grad.shape[1] // n_t
        if quad:
            rows = width // 4
            blocks = grad.reshape(4, rows, n_t, cols).transpose(0, 2, 1, 3)
            half = n_t // 2
            low = lax.ppermute(blocks[3, :half].astype(bf16), "plane", x_pairs)
            high = lax.ppermute(blocks[3, half:].astype(bf16), "plane", y_pairs)
            for_y = jnp.concatenate([blocks[2, :half] + low.astype(f32), blocks[2, half:]])
            for_x = jnp.concatenate([blocks[1, :half], blocks[1, half:] + high.astype(f32)])
            from_x = lax.ppermute(for_x.astype(bf16), "plane", x_pairs)
            from_y = lax.ppermute(for_y.astype(bf16), "plane", y_pairs)
            mine = blocks[0] + from_x.astype(f32) + from_y.astype(f32)
        else:
            blocks = grad.reshape(width, n_t, cols).transpose(1, 0, 2)
            mine = lax.psum_scatter(
                blocks.astype(bf16), "plane", scatter_dimension=1, tiled=True
            ).astype(f32)
        back = [(b, a) for a, b in ring]
        total = mine[n_t - 1]
        for j in range(n_t - 2, -1, -1):
            total = mine[j] + lax.ppermute(total.astype(bf16), "tensor", back).astype(f32)
        return total

    home_c = scatter(grad_w2)
    home_b = scatter(grad_w1)
    grad_a = jnp.concatenate(
        [
            grad_wqkv.reshape(width, n_t, 3 * head_cols),
            grad_wo.reshape(width, n_t, head_cols),
        ],
        axis=2,
    ).reshape(width, -1)
    home_a = scatter(grad_a)
    home = jnp.concatenate([home_a, home_b, home_c], axis=1)
    home = home.reshape(2, -1, home.shape[1])
    mine = lax.dynamic_index_in_dim(home, core, 0, keepdims=False)
    other = lax.dynamic_index_in_dim(home, 1 - core, 0, keepdims=False)
    got = swap_cores(other)

    def row_sum(value):
        return reorder(jnp.sum(value, axis=0), 0)

    second_rows = [row_sum(grad_mixed), row_sum(grad_second * normed_two), row_sum(grad_second)]
    norm_sums = jnp.concatenate(
        [
            row_sum(grad_att),
            row_sum(grad_first * normed_one),
            row_sum(grad_first),
            *second_rows,
        ]
    )
    qkv_sum = jnp.sum(grad_qkv.astype(f32), axis=0).reshape(n_t, 3 * head_cols)
    pre_sum = jnp.sum(grad_pre_low.astype(f32), axis=0).reshape(n_t, ff_cols)
    bias_sum = jnp.concatenate([qkv_sum[:, :head_cols], qkv_sum[:, 2 * head_cols :], pre_sum], axis=1)
    at_home = lax.rem(place - jnp.arange(n_t) + n_t, n_t)
    spread = (at_home[:, None] == jnp.arange(n_t)[None]).astype(f32)
    by_place = jnp.sum(spread[:, :, None] * bias_sum[:, None, :], axis=0)
    both = jnp.where(
        (jnp.arange(2) == core)[None, :, None], by_place[:, None, :], 0.0
    )
    sums = lax.psum(jnp.concatenate([norm_sums, both.reshape(-1)]), ("plane", "core", "tensor"))
    norms = sums[: 6 * width].reshape(6, width)
    biases_out = lax.dynamic_index_in_dim(
        sums[6 * width :].reshape(n_t, 2, -1), place, 0, keepdims=False
    )
    def columns(start, cols):
        return by_core(mine[:, start : start + cols], got[:, start : start + cols], axis=1)

    grad_w_query = columns(0, head_cols)
    grad_w_key = columns(head_cols, head_cols)
    grad_w_value = columns(2 * head_cols, head_cols)
    grad_w_out = columns(3 * head_cols, head_cols).T
    grad_w_in = columns(cuts[0], ff_cols)
    grad_w_back = columns(cuts[1], ff_cols).T

    grad_b_query = biases_out[:, :head_cols].reshape(-1)
    grad_b_value = biases_out[:, head_cols : 2 * head_cols].reshape(-1)
    grad_b_in = biases_out[:, 2 * head_cols :].reshape(-1)
    return (
        layer_out,
        grad_inputs,
        grad_w_query,
        grad_w_key,
        grad_w_value,
        grad_b_query,
        grad_b_value,
        grad_w_out,
        norms[0],
        norms[1],
        norms[2],
        grad_w_in,
        grad_b_in,
        grad_w_back,
        norms[3],
        norms[4],
        norms[5],
    )


def solution(mesh):
    devices = mesh.devices.reshape(mesh.shape["dp"] // 2, 2, mesh.shape["tensor"])
    inner = Mesh(devices, ("plane", "core", "tensor"))
    dp = ("plane", "core")
    row = P(dp, "tensor")
    column = P("tensor", dp)
    rows3 = P(dp, "tensor", None)
    shard = P("tensor")
    whole = P()
    return jax.shard_map(
        on_device,
        mesh=inner,
        in_specs=(
            rows3, P(dp), row, row, row, shard, shard, column, whole, whole, whole,
            row, shard, column, whole, whole, whole, rows3,
        ),
        out_specs=(
            rows3, rows3, row, row, row, shard, shard, column, whole, whole, whole,
            row, shard, column, whole, whole, whole,
        ),
        check_vma=False,
    )
```
